32 devices in a mesh: dp: 8 (over y, x, core), tensor: 4 (over z).
Axes of the slice: x: 2, y: 2, z: 4, core: 2. Of those that a mesh axis runs over, the one named last changes fastest.
Arguments:
- tokens: bfloat16 [16384, 1024], P(('dp', 'tensor')), may hold values from -6 to 6
- enc_states: bfloat16 [4096, 1024], P(('dp', 'tensor')), may hold values from -6 to 6
- enc_len: int32 [8], P('dp'), may hold values from 1 to 512, 3072 in all
- cont_lengths: int32 [8, 8], P('dp'), may hold values from 1 to 256, 1024 in all within a row
- cotangent: bfloat16 [16384, 1024], P(('dp', 'tensor')), may hold values from -6 to 6
- self_qkv: bfloat16 [3, 1024, 1024], P(None, 'dp', 'tensor'), may hold values from -0.1875 to 0.1875
- self_out: bfloat16 [1024, 1024], P('tensor', 'dp'), may hold values from -1.5 to 1.5
- cross_qkv: bfloat16 [3, 1024, 1024], P(None, 'dp', 'tensor'), may hold values from -0.1875 to 0.1875
- cross_out: bfloat16 [1024, 1024], P('tensor', 'dp'), may hold values from -1.5 to 1.5
- ff_in: bfloat16 [1024, 8192], P('dp', 'tensor'), may hold values from -0.1875 to 0.1875
- ff_out: bfloat16 [8192, 1024], P('tensor', 'dp'), may hold values from -0.25 to 0.25
- head_bias: bfloat16 [4, 1024], P(None, ('tensor', 'dp')), may hold values from -1.796875 to 1.796875
- ff_bias: bfloat16 [8192], P(('tensor', 'dp')), may hold values from -1.796875 to 1.796875
- vec_params: bfloat16 [9, 1024], P(None, 'dp'), may hold values from -0.9 to 1.9, as said below
Outputs:
- layer_out: bfloat16 [16384, 1024], P(('dp', 'tensor'))
- input_grad: float32 [16384, 1024], P(('dp', 'tensor'))
- enc_grad: float32 [4096, 1024], P(('dp', 'tensor'))
- self_qkv_grad: float32 [3, 1024, 1024], P(None, 'dp', 'tensor')
- self_out_grad: float32 [1024, 1024], P('tensor', 'dp')
- cross_qkv_grad: float32 [3, 1024, 1024], P(None, 'dp', 'tensor')
- cross_out_grad: float32 [1024, 1024], P('tensor', 'dp')
- ff_in_grad: float32 [1024, 8192], P('dp', 'tensor')
- ff_out_grad: float32 [8192, 1024], P('tensor', 'dp')
- head_bias_grad: float32 [4, 1024], P(None, ('tensor', 'dp'))
- ff_bias_grad: float32 [8192], P(('tensor', 'dp'))
- vec_params_grad: float32 [9, 1024], P(None, 'dp')
The draws below stay inside these ranges and needn't reach their ends.
Inputs may be any that keep to these rules, and one draw needn't show every extreme that they name: `cont_lengths`: each row sums to 1024. `vec_params`: rows 0 to 2 lie near one, rows 3 to 8 near zero.
All inputs are finite; a program needn't handle non-finite values. No bound on the sum of `enc_len` on one device may be relied on, other than what follows from the above.
Results may differ from the reference program's by a relative error of at most 0.025.
Values may be sent and summed in bfloat16 or wider, within the bound.
A program may use at most 256 MiB of HBM per device.

```python
import math
import jax
import jax.numpy as jnp
import numpy as np
from jax import lax

D = 1024
H = 16
HD = 64
FF = 8192
PROMPT = 1024
CONT = 8
CONT_TOK = 1024
CONT_MOST = 256
ENC = 512
SEQ = 2048
GROUPS = 8
TOKENS = 16384
ENC_ROWS = 4096


def draw_vec_params(key, part):
    base = jnp.concatenate([jnp.ones((3, D), jnp.float32), jnp.zeros((6, D), jnp.float32)], axis=0)
    noise = jnp.clip(0.3 * jax.random.normal(key, (9, D), jnp.float32), -0.9, 0.9)
    return (base + noise).astype(jnp.bfloat16)


def steps_of(own_key, extent, shards, low, largest):
    factor_of, own = 1.0, jax.random.fold_in(own_key, 6)
    for dim, shards_of in shards:
        draws = jnp.exp(jax.random.uniform(jax.random.fold_in(own, dim), (shards_of,), jnp.float32, low / len(shards), largest / len(shards)))
        factor_of = factor_of * jnp.repeat(draws, extent[dim] // shards_of).reshape([-1 if axis == dim else 1 for axis in range(len(extent))])
    return factor_of


def profile(number_of, total, most, skew):
    loads = [(1 << 20) // math.isqrt(standing ** skew) + 1 for standing in range(2, number_of + 1)]
    spare, holding = total - most - (number_of - 1), [1] * (number_of - 1)
    while spare > 0:
        candidates = [i for i in range(number_of - 1) if holding[i] < most]
        pool, remaining = sum([loads[i] for i in candidates]), spare
        for i in candidates:
            addition = min(most - holding[i], max(1, remaining * loads[i] // pool), spare)
            holding[i] = holding[i] + addition
            spare = spare - addition
    return np.array([most] + holding)


def ragged_sizes(stream_key, amount, total, reach, slope):
    if amount == 2:
        one = jax.random.randint(stream_key, (), max(1, total - reach), min(reach, total - 1) + 1)
        return jnp.stack([one, total - one])
    lengths = jnp.asarray(profile(amount, total, reach, slope), jnp.int32)
    pairs = (amount - 1) // 2
    giver, taker = lengths[1:1 + 2 * pairs:2], lengths[2:2 + 2 * pairs:2]
    room = jnp.minimum(giver - 1, reach - taker)
    passed = jax.random.randint(jax.random.fold_in(stream_key, 1), (pairs,), 0, 1 << 20) % (room + 1)
    lengths = lengths.at[1:1 + 2 * pairs:2].set(giver - passed).at[2:2 + 2 * pairs:2].set(taker + passed)
    return lengths[jax.random.permutation(jax.random.fold_in(stream_key, 2), amount)]


def normal_values(rng, dims, deviation, most, split=(), kind=jnp.bfloat16):
    gain = steps_of(rng, dims, split, -0.22, 0.18) if split else 1.0
    values = jax.random.normal(rng, dims, jnp.float32) * deviation * gain
    return jnp.minimum(jnp.maximum(values, -most), most).astype(kind)


def setup_inputs(seed: int = 0) -> dict:
    keys = jax.random.split(jax.random.key(seed), 15)
    tokens = normal_values(keys[0], (TOKENS, D), 1.0, 6.0, ((0, 32),))
    enc_states = normal_values(keys[1], (ENC_ROWS, D), 1.0, 6.0, ((0, 32),))
    enc_len = ragged_sizes(keys[2], GROUPS, (3 * ENC // 4) * GROUPS, ENC, 1).astype(jnp.int32)
    cont_lengths = jax.vmap(lambda own: ragged_sizes(own, CONT, CONT_TOK, CONT_MOST, 1))(jax.random.split(keys[3], GROUPS)).reshape((GROUPS, CONT)).astype(jnp.int32)
    cotangent = normal_values(keys[4], (TOKENS, D), 1.0, 6.0, ((0, 32),))
    self_qkv = normal_values(keys[5], (3, D, D), D ** -0.5, 0.1875, ((1, 8), (2, 4)))
    self_out = normal_values(keys[6], (D, D), (D // 64) ** -0.5, 1.5, ((0, 4), (1, 8)))
    cross_qkv = normal_values(keys[7], (3, D, D), D ** -0.5, 0.1875, ((1, 8), (2, 4)))
    cross_out = normal_values(keys[8], (D, D), (D // 64) ** -0.5, 1.5, ((0, 4), (1, 8)))
    ff_in = normal_values(keys[9], (D, FF), D ** -0.5, 0.1875, ((0, 8), (1, 4)))
    ff_out = normal_values(keys[10], (FF, D), (FF // 16) ** -0.5, 0.25, ((0, 4), (1, 8)))
    head_bias = normal_values(keys[11], (4, D), 0.3, 1.796875, ((1, 32),))
    ff_bias = normal_values(keys[12], (FF,), 0.3, 1.796875, ((0, 32),))
    vec_params = draw_vec_params(jax.random.fold_in(keys[14], 71), 0)
    return {"tokens": tokens, "enc_states": enc_states, "enc_len": enc_len, "cont_lengths": cont_lengths, "cotangent": cotangent, "self_qkv": self_qkv, "self_out": self_out, "cross_qkv": cross_qkv, "cross_out": cross_out, "ff_in": ff_in, "ff_out": ff_out, "head_bias": head_bias, "ff_bias": ff_bias, "vec_params": vec_params}


@jax.custom_vjp
def low(v):
    return lax.optimization_barrier(v.astype(jnp.bfloat16)).astype(jnp.float32)

@jax.custom_vjp
def low_back(v):
    return v

def low_keep(v):
    return (low(v), None)

def low_pass(kept, grad):
    return (grad,)

def back_keep(v):
    return (v, None)

def back_low(kept, grad):
    return (low(grad),)
low.defvjp(low_keep, low_pass)
low_back.defvjp(back_keep, back_low)
EPSILON = 1e-05
MASKED = 1e+30
HIGHEST = lax.Precision.HIGHEST

def matmul(left, right):
    return jnp.dot(left, right, precision=HIGHEST)

def layer_norm(values, gain_vec, shift_vec):
    row_mean = lax.optimization_barrier(jnp.mean(values, axis=-1, keepdims=True))
    centred = values - row_mean
    variance = lax.optimization_barrier(jnp.mean(centred * centred, axis=-1, keepdims=True))
    return centred * lax.rsqrt(variance + EPSILON) * gain_vec + shift_vec

def attend(queries, key_rows, value_rows, allowed):
    count = queries.shape[0]
    scores = jnp.einsum('qhd,khd->hqk', queries.reshape(count, H, HD), key_rows.reshape(-1, H, HD), precision=HIGHEST)
    scores = jnp.where(allowed[None], low_back(scores), -MASKED)
    row_max = lax.optimization_barrier(jnp.max(scores, axis=2, keepdims=True))
    exponent = jnp.exp(scores - row_max)
    probs = low(exponent / lax.optimization_barrier(jnp.sum(exponent, axis=2, keepdims=True)))
    mixed = jnp.einsum('hqk,khd->qhd', probs, value_rows.reshape(-1, H, HD), precision=HIGHEST)
    return mixed.reshape(count, D)

def group_layer(resid, encoder, cont_len, enc_count, weights):
    self_qkv, self_out, cross_qkv, cross_out, ff_in, ff_out, head_bias, ff_bias, vectors = weights
    scaling = HD ** (-0.5)
    positions = jnp.arange(SEQ, dtype=jnp.int32)
    bounds = PROMPT + jnp.cumsum(cont_len)
    segment = lax.optimization_barrier(jnp.sum((positions[:, None] >= bounds[None, :]).astype(jnp.int32), axis=1))
    self_ok = (positions[None, :] <= positions[:, None]) & ((positions[None, :] < PROMPT) | (segment[None, :] == segment[:, None]))
    cross_ok = jnp.broadcast_to((jnp.arange(ENC, dtype=jnp.int32) < enc_count)[None, :], (SEQ, ENC))
    attn_in = low(layer_norm(resid, vectors[0], vectors[3]))
    queries = low_back(low((matmul(attn_in, self_qkv[0]) + head_bias[0]) * scaling))
    key_rows = low_back(low(matmul(attn_in, self_qkv[1])))
    value_rows = low_back(low(matmul(attn_in, self_qkv[2]) + head_bias[1]))
    mixed = low_back(low(attend(queries, key_rows, value_rows, self_ok)))
    after_one = resid + low_back(matmul(mixed, self_out) + vectors[6])
    cross_in = low(layer_norm(after_one, vectors[1], vectors[4]))
    cross_queries = low_back(low((matmul(cross_in, cross_qkv[0]) + head_bias[2]) * scaling))
    cross_keys = low_back(low(matmul(encoder, cross_qkv[1])))
    cross_values = low_back(low(matmul(encoder, cross_qkv[2]) + head_bias[3]))
    cross_mixed = low_back(low(attend(cross_queries, cross_keys, cross_values, cross_ok)))
    after_two = after_one + low_back(matmul(cross_mixed, cross_out) + vectors[7])
    mlp_in = low(layer_norm(after_two, vectors[2], vectors[5]))
    pre_act = low_back(matmul(mlp_in, ff_in) + ff_bias)
    hidden = low(jax.nn.gelu(pre_act, approximate=True))
    return after_two + low_back(matmul(hidden, ff_out) + vectors[8])

def reference(tokens, enc_states, enc_len, cont_lengths, cotangent, self_qkv, self_out, cross_qkv, cross_out, ff_in, ff_out, head_bias, ff_bias, vec_params):
    weights = tuple((weight.astype(jnp.float32) for weight in (self_qkv, self_out, cross_qkv, cross_out, ff_in, ff_out, head_bias, ff_bias, vec_params)))
    resid = tokens.astype(jnp.float32).reshape(GROUPS, SEQ, D)
    encoder = enc_states.astype(jnp.float32).reshape(GROUPS, ENC, D)
    saved_layer = jax.checkpoint(group_layer)

    def forward(resid, encoder, weights):

        def per_group(pieces):
            return saved_layer(pieces[0], pieces[1], pieces[2], pieces[3], weights)
        return lax.map(per_group, (resid, encoder, cont_lengths, enc_len))
    layer_out, pullback = jax.vjp(forward, resid, encoder, weights)
    input_grad, enc_grad, weight_grads = pullback(cotangent.astype(jnp.float32).reshape(GROUPS, SEQ, D))
    return (layer_out.reshape(TOKENS, D).astype(jnp.bfloat16), input_grad.reshape(TOKENS, D), enc_grad.reshape(ENC_ROWS, D), weight_grads[0], weight_grads[1], weight_grads[2], weight_grads[3], weight_grads[4], weight_grads[5], weight_grads[6], weight_grads[7], weight_grads[8])
```

```python
import functools
import math

import jax
import jax.numpy as jnp
from jax import lax
from jax.experimental import pallas as pl
from jax.experimental.pallas import tpu as pltpu
from jax.sharding import Mesh
from jax.sharding import PartitionSpec as P

HD = 64
PROMPT = 1024
CONT_TOK = 1024
ENC = 512
BLOCK = 256
PAIR = 2 * HD
AXES = ("y", "x", "core", "zhi", "zlo")


def lane_half():
    return lax.broadcasted_iota(jnp.int32, (1, PAIR), 1) < HD


def one_head(rows, head):
    keep = lane_half() if head == 0 else jnp.logical_not(lane_half())
    return rows * jnp.where(keep, 1.0, 0.0).astype(rows.dtype)


def dot_nt(left, right):
    return lax.dot_general(left, right, (((1,), (1,)), ((), ())), preferred_element_type=jnp.float32)


def dot_nn(left, right):
    return jnp.dot(left, right, preferred_element_type=jnp.float32)


def dot_tn(left, right):
    return lax.dot_general(left, right, (((0,), (0,)), ((), ())), preferred_element_type=jnp.float32)


def self_sections(meta_ref, segments):
    def at(block):
        return pl.multiple_of(meta_ref[block], 512)

    def place(index):
        return pl.multiple_of(meta_ref[index >> 1] + (index & 1) * BLOCK, BLOCK)

    def causal(row, col):
        return col <= row

    def banded(row, col):
        start = jnp.full(row.shape, meta_ref[4], jnp.int32)
        for segment in range(1, segments):
            bound = meta_ref[4 + segment]
            start = jnp.where(row >= bound, bound, start)
        return (col <= row) & (col >= start)

    def early(index):
        return [(at(0), 512, 0, causal)]

    def middle(index):
        return [(at(0), 512, 0, None), (at(1), 512, 512, causal)]

    def late(index):
        return [
            (at(0), 512, 0, None),
            (at(1), 512, 512, None),
            (place(index - 1), BLOCK, (index - 1) * BLOCK, banded),
            (place(index), BLOCK, index * BLOCK, banded),
        ]

    return place, ((0, 2, early), (2, 4, middle), (4, 8, late))


def cross_sections(meta_ref, blocks):
    def place(index):
        return pl.multiple_of(index * BLOCK, BLOCK)

    def usable(row, col):
        return col < meta_ref[0]

    def every(index):
        return [(0, ENC, 0, usable)]

    return place, ((0, blocks, every),)


def forward_kernel(sections, meta_ref, q_ref, k_ref, v_ref, o_ref, lse_ref):
    place, ranges = sections(meta_ref)

    for low, high, parts_of in ranges:

        def step(index, carry, parts_of=parts_of):
            rows = pl.ds(place(index), BLOCK)
            parts = parts_of(index)
            queries = q_ref[rows, :]
            row = index * BLOCK + lax.broadcasted_iota(jnp.int32, (BLOCK, 1), 0)
            allowed = [
                None if rule is None else rule(row, first + lax.broadcasted_iota(jnp.int32, (1, size), 1))
                for _, size, first, rule in parts
            ]
            outs, totals = [], []
            for head in range(2):
                query = one_head(queries, head)
                scores = []
                for (where, size, _, _), ok in zip(parts, allowed):
                    score = dot_nt(query, k_ref[pl.ds(where, size), :])
                    scores.append(score if ok is None else jnp.where(ok, score, -1e30))
                top = functools.reduce(jnp.maximum, [jnp.max(s, axis=1, keepdims=True) for s in scores])
                exps = [jnp.exp(s - top) for s in scores]
                total = sum(jnp.sum(e, axis=1, keepdims=True) for e in exps)
                mixed = sum(
                    dot_nn(e.astype(jnp.bfloat16), v_ref[pl.ds(where, size), :])
                    for (where, size, _, _), e in zip(parts, exps)
                )
                outs.append(mixed * (1.0 / total))
                totals.append(top + jnp.log(total))
            o_ref[rows, :] = jnp.where(lane_half(), outs[0], outs[1]).astype(o_ref.dtype)
            lse_ref[rows, :] = jnp.where(lane_half(), totals[0], totals[1])
            return carry

        lax.fori_loop(low, high, step, 0)


def backward_kernel(
    sections, meta_ref, q_ref, k_ref, v_ref, o_ref, do_ref, lse_ref, dq_ref, dk_ref, dv_ref, dk_sum, dv_sum
):
    place, ranges = sections(meta_ref)
    dk_sum[...] = jnp.zeros_like(dk_sum)
    dv_sum[...] = jnp.zeros_like(dv_sum)

    for low, high, parts_of in ranges:

        def step(index, carry, parts_of=parts_of):
            rows = pl.ds(place(index), BLOCK)
            parts = parts_of(index)
            queries, grads = q_ref[rows, :], do_ref[rows, :]
            row = index * BLOCK + lax.broadcasted_iota(jnp.int32, (1, BLOCK), 1)
            allowed = [
                None if rule is None else rule(row, first + lax.broadcasted_iota(jnp.int32, (size, 1), 0))
                for _, size, first, rule in parts
            ]
            logs = jnp.transpose(lse_ref[rows, :])
            spread = jnp.transpose(grads.astype(jnp.float32) * o_ref[rows, :].astype(jnp.float32))
            key_parts = [k_ref[pl.ds(where, size), :] for where, size, _, _ in parts]
            value_parts = [v_ref[pl.ds(where, size), :] for where, size, _, _ in parts]
            query_grads = []
            for head in range(2):
                query, grad = one_head(queries, head), one_head(grads, head)
                log = logs[head * HD : head * HD + 1, :]
                delta = jnp.sum(spread[head * HD : (head + 1) * HD, :], axis=0, keepdims=True)
                query_grad = None
                for (where, size, _, _), ok, keys, values in zip(parts, allowed, key_parts, value_parts):
                    score = dot_nt(keys, query)
                    if ok is not None:
                        score = jnp.where(ok, score, -1e30)
                    probs = jnp.exp(score - log)
                    score_grad = (probs * (dot_nt(values, grad) - delta)).astype(jnp.bfloat16)
                    dv_sum[pl.ds(where, size), :] += dot_nn(probs.astype(jnp.bfloat16), grad)
                    dk_sum[pl.ds(where, size), :] += dot_nn(score_grad, query)
                    term = dot_tn(score_grad, keys)
                    query_grad = term if query_grad is None else query_grad + term
                query_grads.append(query_grad)
            both = jnp.where(lane_half(), query_grads[0], query_grads[1])
            dq_ref[rows, :] = both.astype(jnp.bfloat16) * jnp.asarray(HD**-0.5, jnp.bfloat16)
            return carry

        lax.fori_loop(low, high, step, 0)
    dk_ref[...] = dk_sum[...].astype(dk_ref.dtype)
    dv_ref[...] = dv_sum[...].astype(dv_ref.dtype)


def columns(rows, first):
    return pl.BlockSpec((rows, PAIR), lambda pair, meta: (0, first + pair))


def attend(sections, meta, q, q_at, keys, k_at, v_at, pairs, weight):
    count, key_rows = q.shape[0], keys.shape[0]
    return pl.pallas_call(
        functools.partial(forward_kernel, sections),
        grid_spec=pltpu.PrefetchScalarGridSpec(
            num_scalar_prefetch=1,
            grid=(pairs,),
            in_specs=[columns(count, q_at), columns(key_rows, k_at), columns(key_rows, v_at)],
            out_specs=[columns(count, 0), columns(count, 0)],
        ),
        out_shape=[
            jax.ShapeDtypeStruct((count, pairs * PAIR), jnp.bfloat16),
            jax.ShapeDtypeStruct((count, pairs * PAIR), jnp.float32),
        ],
        cost_estimate=pl.CostEstimate(
            flops=2 * 4 * 4 * count * weight * pairs * PAIR,
            bytes_accessed=10 * count * pairs * PAIR,
            transcendentals=2 * pairs * count * weight,
        ),
    )(meta, q, keys, keys)


def attend_back(sections, meta, q, q_at, keys, k_at, v_at, out, out_grad, lse, pairs, weight):
    count, key_rows = q.shape[0], keys.shape[0]
    return pl.pallas_call(
        functools.partial(backward_kernel, sections),
        grid_spec=pltpu.PrefetchScalarGridSpec(
            num_scalar_prefetch=1,
            grid=(pairs,),
            in_specs=[
                columns(count, q_at),
                columns(key_rows, k_at),
                columns(key_rows, v_at),
                columns(count, 0),
                columns(count, 0),
                columns(count, 0),
            ],
            out_specs=[columns(count, 0), columns(key_rows, 0), columns(key_rows, 0)],
            scratch_shapes=[pltpu.VMEM((key_rows, PAIR), jnp.float32)] * 2,
        ),
        out_shape=[
            jax.ShapeDtypeStruct((count, pairs * PAIR), jnp.bfloat16),
            jax.ShapeDtypeStruct((key_rows, pairs * PAIR), jnp.bfloat16),
            jax.ShapeDtypeStruct((key_rows, pairs * PAIR), jnp.bfloat16),
        ],
        cost_estimate=pl.CostEstimate(
            flops=5 * 4 * 4 * count * weight * pairs * PAIR,
            bytes_accessed=20 * count * pairs * PAIR,
            transcendentals=2 * pairs * count * weight,
        ),
    )(meta, q, keys, keys, out, out_grad, lse)


EPSILON = 1e-05
MASKED = 1e30
GELU_C = math.sqrt(2.0 / math.pi)
GELU_A = 0.044715


def gelu_value(values):
    inner = jnp.tanh(GELU_C * (values + GELU_A * values * values * values))
    return 0.5 * values * (1.0 + inner)


def gelu_slope(values):
    inner = jnp.tanh(GELU_C * (values + GELU_A * values * values * values))
    return 0.5 * (1.0 + inner) + 0.5 * values * (1.0 - inner * inner) * GELU_C * (
        1.0 + 3.0 * GELU_A * values * values
    )


def norm_forward(values, gain_vec, shift_vec):
    row_mean = jnp.mean(values, axis=1, keepdims=True)
    centred = values - row_mean
    inverse = lax.rsqrt(jnp.mean(centred * centred, axis=1, keepdims=True) + EPSILON)
    normed = centred * inverse
    return (normed * gain_vec + shift_vec, normed, inverse)


def norm_backward(gradient, normed, inverse, gain_vec):
    scaled = gradient * gain_vec
    inner = (
        scaled
        - jnp.mean(scaled, axis=1, keepdims=True)
        - normed * jnp.mean(scaled * normed, axis=1, keepdims=True)
    )
    return (inner * inverse, jnp.sum(gradient * normed, axis=0), jnp.sum(gradient, axis=0))


def product(left, right):
    return jnp.dot(left, right, preferred_element_type=jnp.float32)


def product_left_t(left, right):
    return lax.dot_general(
        left, right, (((0,), (0,)), ((), ())), preferred_element_type=jnp.float32
    )


def product_right_t(left, right):
    return lax.dot_general(
        left, right, (((1,), (1,)), ((), ())), preferred_element_type=jnp.float32
    )


def attend_forward(queries, key_rows, value_rows, rule, block_rows):
    seq_rows, local_width = queries.shape
    local_heads = local_width // HD
    query_blocks = queries.reshape(seq_rows // block_rows, block_rows, local_heads, HD)
    key_heads = key_rows.reshape(-1, local_heads, HD)
    value_heads = value_rows.reshape(-1, local_heads, HD)
    block_starts = jnp.arange(seq_rows // block_rows, dtype=jnp.int32) * block_rows

    def attend_block(pieces):
        query_block, offset = pieces
        scores = jnp.einsum(
            "qhd,khd->hqk", query_block, key_heads, preferred_element_type=jnp.float32
        )
        scores = jnp.where(rule(offset, block_rows)[None], scores, -MASKED)
        row_max = jnp.max(scores, axis=2, keepdims=True)
        exponent = jnp.exp(scores - row_max)
        row_total = jnp.sum(exponent, axis=2, keepdims=True)
        probs_low = (exponent / row_total).astype(jnp.bfloat16)
        mixed = jnp.einsum(
            "hqk,khd->qhd", probs_low, value_heads, preferred_element_type=jnp.float32
        )
        return (
            mixed.astype(jnp.bfloat16).reshape(block_rows, local_width),
            (row_max + jnp.log(row_total))[:, :, 0],
        )

    outputs, log_total = lax.map(attend_block, (query_blocks, block_starts))
    return (outputs.reshape(seq_rows, local_width), log_total)


def attend_backward(queries, key_rows, value_rows, out_grad, log_total, rule, block_rows):
    seq_rows, local_width = queries.shape
    local_heads = local_width // HD
    key_count = key_rows.shape[0]
    query_blocks = queries.reshape(seq_rows // block_rows, block_rows, local_heads, HD)
    grad_blocks = out_grad.reshape(seq_rows // block_rows, block_rows, local_heads, HD)
    key_heads = key_rows.reshape(key_count, local_heads, HD)
    value_heads = value_rows.reshape(key_count, local_heads, HD)
    block_starts = jnp.arange(seq_rows // block_rows, dtype=jnp.int32) * block_rows

    def back_block(running, pieces):
        key_sum, value_sum = running
        query_block, grad_block, block_total, offset = pieces
        scores = jnp.einsum(
            "qhd,khd->hqk", query_block, key_heads, preferred_element_type=jnp.float32
        )
        probs = jnp.where(
            rule(offset, block_rows)[None], jnp.exp(scores - block_total[:, :, None]), 0.0
        )
        probs_low = probs.astype(jnp.bfloat16)
        prob_grad = jnp.einsum(
            "qhd,khd->hqk", grad_block, value_heads, preferred_element_type=jnp.float32
        )
        row_delta = jnp.sum(probs * prob_grad, axis=2, keepdims=True)
        score_grad = (probs * (prob_grad - row_delta)).astype(jnp.bfloat16)
        query_grad = jnp.einsum(
            "hqk,khd->qhd", score_grad, key_heads, preferred_element_type=jnp.float32
        )
        key_sum = key_sum + jnp.einsum(
            "hqk,qhd->khd", score_grad, query_block, preferred_element_type=jnp.float32
        )
        value_sum = value_sum + jnp.einsum(
            "hqk,qhd->khd", probs_low, grad_block, preferred_element_type=jnp.float32
        )
        return (
            (key_sum, value_sum),
            query_grad.astype(jnp.bfloat16).reshape(block_rows, local_width),
        )

    zero_sum = jnp.zeros((key_count, local_heads, HD), jnp.float32)
    (key_sum, value_sum), query_grads = lax.scan(
        back_block, (zero_sum, zero_sum), (query_blocks, grad_blocks, log_total, block_starts)
    )
    return (
        query_grads.reshape(seq_rows, local_width),
        key_sum.astype(jnp.bfloat16).reshape(key_count, local_width),
        value_sum.astype(jnp.bfloat16).reshape(key_count, local_width),
    )


def attend_groups(queries, key_rows, value_rows, rules, block_rows):
    results, totals = ([], [])
    for which_group, rule in enumerate(rules):
        mixed, log_total = attend_forward(queries, key_rows, value_rows, rule, block_rows)
        results.append(mixed)
        totals.append(log_total)
    return (results[0], totals)


def back_groups(queries, key_rows, value_rows, out_grad, totals, rules, block_rows):
    query_list, key_list, value_list = ([], [], [])
    for which_group, rule in enumerate(rules):
        query_grad, key_grad, value_grad = attend_backward(
            queries, key_rows, value_rows, out_grad, totals[which_group], rule, block_rows
        )
        query_list.append(query_grad)
        key_list.append(key_grad)
        value_list.append(value_grad)
    return (query_list[0], key_list[0], value_list[0])


def shards(
    tokens,
    enc_states,
    enc_len,
    cont_lengths,
    cotangent,
    self_qkv,
    self_out,
    cross_qkv,
    cross_out,
    ff_in,
    ff_out,
    head_bias,
    ff_bias,
    vec_params,
):
    gathered = (
        lax.all_gather(self_qkv, "dp", axis=1, tiled=True),
        lax.all_gather(self_out, "dp", axis=1, tiled=True),
        lax.all_gather(cross_qkv, "dp", axis=1, tiled=True),
        lax.all_gather(cross_out, "dp", axis=1, tiled=True),
        lax.all_gather(ff_in, "dp", axis=0, tiled=True),
        lax.all_gather(ff_out, "dp", axis=1, tiled=True),
        lax.all_gather(head_bias, "dp", axis=1, tiled=True),
        lax.all_gather(ff_bias, "dp", axis=0, tiled=True),
        lax.all_gather(vec_params, "dp", axis=1, tiled=True),
    )
    (
        w_self,
        w_self_out,
        w_cross,
        w_cross_out,
        w_hidden_in,
        w_hidden_out,
        bias_heads,
        bias_hidden,
        vectors,
    ) = gathered
    vectors = vectors.astype(jnp.float32)
    bias_heads = bias_heads.astype(jnp.float32)
    bias_hidden = bias_hidden.astype(jnp.float32)
    seq_rows = PROMPT + CONT_TOK
    block_rows = min(512, seq_rows)
    scaling = HD ** (-0.5)
    rows_dev = tokens.shape[0]

    def self_rule(which_group):
        bounds = PROMPT + jnp.cumsum(cont_lengths[which_group])
        positions = jnp.arange(seq_rows, dtype=jnp.int32)
        segment = jnp.sum((positions[:, None] >= bounds[None, :]).astype(jnp.int32), axis=1)

        def self_allowed(offset, number):
            row_ids = offset + jnp.arange(number, dtype=jnp.int32)
            row_segment = lax.dynamic_slice_in_dim(segment, offset, number)
            return (positions[None, :] <= row_ids[:, None]) & (
                (positions[None, :] < PROMPT) | (segment[None, :] == row_segment[:, None])
            )

        return self_allowed

    def cross_rule(which_group):
        usable = jnp.arange(ENC, dtype=jnp.int32) < enc_len[which_group]

        def cross_allowed(offset, number):
            return jnp.broadcast_to(usable[None, :], (number, ENC))

        return cross_allowed

    def spread(low_rows):
        return lax.all_gather(low_rows, "tensor", axis=0, tiled=True)

    def head_branch(values, weight):

        def term(offset, number):
            return product(values, weight)

        return lax.psum_scatter(
            term(jnp.int32(0), rows_dev * lax.axis_size("tensor")),
            "tensor",
            scatter_dimension=0,
            tiled=True,
        )

    def widen(low_rows):
        return lax.all_gather(low_rows, "tensor", axis=0, tiled=True)

    def narrow(term):
        return lax.psum_scatter(
            term(jnp.int32(0), rows_dev * lax.axis_size("tensor")),
            "tensor",
            scatter_dimension=0,
            tiled=True,
        )

    self_rules = [self_rule(0)]
    cross_rules = [cross_rule(0)]
    resid = tokens.astype(jnp.float32)
    enc_full = lax.all_gather(enc_states, "tensor", axis=0, tiled=True)
    normed_in, hat_one, inv_one = norm_forward(resid, vectors[0], vectors[3])
    attn_low = normed_in.astype(jnp.bfloat16)
    attn_full = spread(attn_low)
    queries = ((product(attn_full, w_self[0]) + bias_heads[0]) * scaling).astype(jnp.bfloat16)
    key_rows = product(attn_full, w_self[1]).astype(jnp.bfloat16)
    value_rows = (product(attn_full, w_self[2]) + bias_heads[1]).astype(jnp.bfloat16)
    mixed, self_totals = attend_groups(queries, key_rows, value_rows, self_rules, block_rows)
    after_one = resid + (head_branch(mixed, w_self_out) + vectors[6])
    normed_mid, hat_two, inv_two = norm_forward(after_one, vectors[1], vectors[4])
    cross_low = normed_mid.astype(jnp.bfloat16)
    cross_full = spread(cross_low)
    cross_queries = ((product(cross_full, w_cross[0]) + bias_heads[2]) * scaling).astype(
        jnp.bfloat16
    )
    cross_keys = product(enc_full, w_cross[1]).astype(jnp.bfloat16)
    cross_values = (product(enc_full, w_cross[2]) + bias_heads[3]).astype(jnp.bfloat16)
    cross_mixed, cross_totals = attend_groups(
        cross_queries, cross_keys, cross_values, cross_rules, block_rows
    )
    after_two = after_one + (head_branch(cross_mixed, w_cross_out) + vectors[7])
    normed_out, hat_three, inv_three = norm_forward(after_two, vectors[2], vectors[5])
    hidden_low = normed_out.astype(jnp.bfloat16)
    hidden_full = spread(hidden_low)
    pre_act = product(hidden_full, w_hidden_in) + bias_hidden
    activation = gelu_value(pre_act).astype(jnp.bfloat16)

    def term(offset, number):
        return product(activation, w_hidden_out)

    after_three = after_two + (
        lax.psum_scatter(
            term(jnp.int32(0), rows_dev * lax.axis_size("tensor")),
            "tensor",
            scatter_dimension=0,
            tiled=True,
        )
        + vectors[8]
    )
    layer_out = after_three.astype(jnp.bfloat16)
    gradient = cotangent.astype(jnp.float32)
    grad_low = gradient.astype(jnp.bfloat16)
    bias_out_three = jnp.sum(grad_low.astype(jnp.float32), axis=0)
    grad_full = widen(grad_low)
    act_grad = (product_right_t(grad_full, w_hidden_out) * gelu_slope(pre_act)).astype(jnp.bfloat16)
    grad_hidden_out = product_left_t(activation, grad_full)
    grad_hidden_in = product_left_t(hidden_full, act_grad)
    grad_bias_hidden = jnp.sum(act_grad.astype(jnp.float32), axis=0)

    def hidden_term(offset, number):
        return product_right_t(act_grad, w_hidden_in)

    input_part, gain_three, shift_three = norm_backward(
        narrow(hidden_term), hat_three, inv_three, vectors[2]
    )
    gradient = gradient + input_part
    grad_low = gradient.astype(jnp.bfloat16)
    bias_out_two = jnp.sum(grad_low.astype(jnp.float32), axis=0)
    grad_full = widen(grad_low)
    grad_cross_out = product_left_t(cross_mixed, grad_full)
    mixed_grad = product_right_t(grad_full, w_cross_out).astype(jnp.bfloat16)
    cross_query_grad, cross_key_grad, cross_value_grad = back_groups(
        cross_queries, cross_keys, cross_values, mixed_grad, cross_totals, cross_rules, block_rows
    )
    grad_cross = jnp.stack(
        [
            product_left_t(cross_full, cross_query_grad) * scaling,
            product_left_t(enc_full, cross_key_grad),
            product_left_t(enc_full, cross_value_grad),
        ]
    )
    bias_cross_query = jnp.sum(cross_query_grad.astype(jnp.float32), axis=0) * scaling
    bias_cross_value = jnp.sum(cross_value_grad.astype(jnp.float32), axis=0)
    enc_grad = lax.psum_scatter(
        product_right_t(cross_key_grad, w_cross[1]) + product_right_t(cross_value_grad, w_cross[2]),
        "tensor",
        scatter_dimension=0,
        tiled=True,
    )

    def cross_term(offset, number):
        return product_right_t(cross_query_grad, w_cross[0]) * scaling

    input_part, gain_two, shift_two = norm_backward(
        narrow(cross_term), hat_two, inv_two, vectors[1]
    )
    gradient = gradient + input_part
    grad_low = gradient.astype(jnp.bfloat16)
    bias_out_one = jnp.sum(grad_low.astype(jnp.float32), axis=0)
    grad_full = widen(grad_low)
    grad_self_out = product_left_t(mixed, grad_full)
    self_mixed_grad = product_right_t(grad_full, w_self_out).astype(jnp.bfloat16)
    query_grad, key_grad, value_grad = back_groups(
        queries, key_rows, value_rows, self_mixed_grad, self_totals, self_rules, block_rows
    )
    grad_self = jnp.stack(
        [
            product_left_t(attn_full, query_grad) * scaling,
            product_left_t(attn_full, key_grad),
            product_left_t(attn_full, value_grad),
        ]
    )
    bias_self_query = jnp.sum(query_grad.astype(jnp.float32), axis=0) * scaling
    bias_self_value = jnp.sum(value_grad.astype(jnp.float32), axis=0)

    def self_term(offset, number):
        return (
            product_right_t(query_grad, w_self[0]) * scaling
            + product_right_t(key_grad, w_self[1])
            + product_right_t(value_grad, w_self[2])
        )

    input_part, gain_one, shift_one = norm_backward(narrow(self_term), hat_one, inv_one, vectors[0])
    input_grad = gradient + input_part
    vector_grads = jnp.stack(
        [
            gain_one,
            gain_two,
            gain_three,
            shift_one,
            shift_two,
            shift_three,
            bias_out_one,
            bias_out_two,
            bias_out_three,
        ]
    )
    head_grads = jnp.stack([bias_self_query, bias_self_value, bias_cross_query, bias_cross_value])
    results = (
        lax.psum_scatter(grad_self, "dp", scatter_dimension=1, tiled=True),
        lax.psum_scatter(grad_self_out, "dp", scatter_dimension=1, tiled=True),
        lax.psum_scatter(grad_cross, "dp", scatter_dimension=1, tiled=True),
        lax.psum_scatter(grad_cross_out, "dp", scatter_dimension=1, tiled=True),
        lax.psum_scatter(grad_hidden_in, "dp", scatter_dimension=0, tiled=True),
        lax.psum_scatter(grad_hidden_out, "dp", scatter_dimension=1, tiled=True),
        lax.psum_scatter(head_grads, "dp", scatter_dimension=1, tiled=True),
        lax.psum_scatter(grad_bias_hidden, "dp", scatter_dimension=0, tiled=True),
        lax.psum_scatter(vector_grads, "dp", scatter_dimension=1, tiled=True),
    )
    vector_total = lax.psum(results[8], "tensor")
    return (
        layer_out,
        input_grad,
        enc_grad,
        results[0],
        results[1],
        results[2],
        results[3],
        results[4],
        results[5],
        results[6],
        results[7],
        vector_total,
    )


def trade(rows, axis):
    return lax.ppermute(rows, axis, [(0, 1), (1, 0)])


def regroup(rows):
    return lax.ppermute(rows, ("core", "zhi"), [(0, 0), (1, 2), (2, 1), (3, 3)])


def in_order(index, own, other, axis):
    return jnp.concatenate(
        [jnp.where(index == 0, own, other), jnp.where(index == 0, other, own)], axis=axis
    )


def low(values):
    return values.astype(jnp.bfloat16)


def half_of(values, index, axis):
    size = values.shape[axis] // 2
    return lax.dynamic_slice_in_dim(values, index * size, size, axis)


def over_chips(rows):
    return lax.all_gather(rows, ("y", "x"), axis=0, tiled=True)


def sum_over_chips(partial):
    return lax.psum_scatter(partial, ("y", "x"), scatter_dimension=0, tiled=True)


def spread_rows(rows):
    beyond = trade(rows, "zlo")
    return (
        jnp.concatenate([rows, trade(rows, "core")], axis=0),
        jnp.concatenate([beyond, trade(beyond, "core")], axis=0),
    )


def sum_rows(near, far, term):
    size = near.shape[0] // 2
    far_sum = term(far[:size]) + trade(low(term(far[size:])), "core")
    from_far = trade(low(far_sum), "zlo")
    near_other = trade(low(term(near[size:])), "core")
    return term(near[:size]) + near_other + from_far


def fast_layer(
    tokens,
    enc_states,
    enc_len,
    cont_lengths,
    cotangent,
    self_qkv,
    self_out,
    cross_qkv,
    cross_out,
    ff_in,
    ff_out,
    head_bias,
    ff_bias,
    vec_params,
):
    core, zhi, zlo = lax.axis_index("core"), lax.axis_index("zhi"), lax.axis_index("zlo")
    scaling = HD**-0.5
    model = tokens.shape[1]
    segments = cont_lengths.shape[1]

    flat = jnp.concatenate([vec_params.reshape(-1), head_bias.reshape(-1), ff_bias])
    sizes = (vec_params.size, head_bias.size, ff_bias.size)
    small = lax.all_gather(flat, AXES, axis=0).reshape(8, 4, -1).astype(jnp.float32)
    vec_part, head_part, ff_part = jnp.split(small, [sizes[0], sizes[0] + sizes[1]], axis=2)
    vectors = vec_part[:, 0].reshape(8, 9, -1).transpose(1, 0, 2).reshape(9, model)
    heads = head_part.reshape(8, 4, 4, -1).transpose(2, 1, 0, 3).reshape(4, 2, 2, 2, -1)
    self_bias = lax.dynamic_index_in_dim(
        lax.dynamic_index_in_dim(heads[:2], zlo, 2, False), core, 2, False
    ).reshape(2, -1)
    cross_bias = lax.dynamic_index_in_dim(heads[2:], core, 3, False).reshape(2, -1)
    hidden_bias = ff_part.transpose(1, 0, 2).reshape(2, 2, 2, -1)
    hidden_bias = lax.dynamic_index_in_dim(
        lax.dynamic_index_in_dim(hidden_bias, zlo, 1, False), core, 1, False
    ).reshape(-1)

    token_rows = regroup(tokens)
    grad_rows = regroup(cotangent)
    lengths = regroup(jnp.concatenate([cont_lengths[0], enc_len]))
    places = jnp.stack(
        [512 * ((core != block // 2) + 2 * (zlo != block % 2)) for block in range(4)]
    ).astype(jnp.int32)
    bounds = PROMPT + jnp.concatenate(
        [jnp.zeros((1,), jnp.int32), jnp.cumsum(lengths[:segments]).astype(jnp.int32)]
    )
    self_meta = jnp.concatenate([places, bounds])
    cross_meta = lengths[segments:]

    attention = jnp.concatenate([self_qkv, self_out.T[None], cross_qkv, cross_out.T[None]], axis=0)
    mine, theirs = half_of(attention, core, 2), half_of(attention, 1 - core, 2)
    attention = in_order(core, mine, trade(theirs, "core"), 1)
    rows_of = attention.shape[1]
    own = attention[:4].transpose(1, 0, 2)[:, :, None]
    own = in_order(zhi, own, trade(own, "zhi"), 2)
    w_self = over_chips(own.reshape(rows_of, -1))
    own = attention[4:].transpose(1, 0, 2)[:, :, None]
    own = in_order(zlo, own, trade(own, "zlo"), 2)[:, :, None]
    own = in_order(zhi, own, trade(own, "zhi"), 2)
    w_cross = over_chips(own.reshape(rows_of, -1))
    hidden = jnp.stack([ff_in, ff_out.T])
    mine, theirs = half_of(hidden, core, 2), half_of(hidden, 1 - core, 2)
    hidden = in_order(core, mine, trade(theirs, "core"), 1)
    hidden = in_order(zhi, hidden, trade(hidden, "zhi"), 2)
    w_in = over_chips(hidden[0])
    w_out = over_chips(hidden[1])
    width = w_self.shape[1] // 4
    pairs = width // PAIR
    cross_width = w_cross.shape[1] // 4
    cross_pairs = cross_width // PAIR

    enc_rows = regroup(enc_states)
    enc_both = in_order(zlo, enc_rows, trade(enc_rows, "zlo"), 0)
    enc_full = in_order(core, enc_both, trade(enc_both, "core"), 0)

    resid = token_rows.astype(jnp.float32)
    normed_in, hat_one, inv_one = norm_forward(resid, vectors[0], vectors[3])
    attn_near, attn_far = spread_rows(low(normed_in))
    qkv_bias = jnp.concatenate([self_bias[0], jnp.zeros((width,), jnp.float32), self_bias[1]])
    qkv_scale = jnp.concatenate([jnp.full((width,), scaling), jnp.ones((2 * width,))]).astype(jnp.float32)
    w_qkv, w_so = w_self[:, : 3 * width], w_self[:, 3 * width :]

    def project(rows):
        return low((product(rows, w_qkv) + qkv_bias) * qkv_scale)

    qkv = jnp.concatenate([project(attn_near), project(attn_far)], axis=0)
    count = qkv.shape[0]
    self_plan = functools.partial(self_sections, segments=segments)
    mixed, self_lse = attend(self_plan, self_meta, qkv, 0, qkv, pairs, 2 * pairs, pairs, 1152)
    near, far = mixed[: count // 2], mixed[count // 2 :]
    branch = sum_rows(near, far, lambda rows: product_right_t(rows, w_so))
    after_one = resid + (branch + vectors[6])

    normed_mid, hat_two, inv_two = norm_forward(after_one, vectors[1], vectors[4])
    cross_low = low(normed_mid)
    cross_rows = jnp.concatenate([cross_low, trade(cross_low, "core")], axis=0)
    own_rows = cross_low.shape[0]
    w_cq = w_cross[:, :cross_width]
    w_ckv = w_cross[:, cross_width : 3 * cross_width]
    w_co = w_cross[:, 3 * cross_width :]
    cross_kv = low(
        product(enc_full, w_ckv)
        + jnp.concatenate([jnp.zeros((cross_width,), jnp.float32), cross_bias[1]])
    )
    cross_q = low((product(cross_rows, w_cq) + cross_bias[0]) * scaling)
    cross_plan = functools.partial(cross_sections, blocks=cross_q.shape[0] // BLOCK)
    cross_mixed, cross_lse = attend(
        cross_plan, cross_meta, cross_q, 0, cross_kv, 0, cross_pairs, cross_pairs, ENC
    )
    other = trade(low(product_right_t(cross_mixed[own_rows:], w_co)), "core")
    branch = product_right_t(cross_mixed[:own_rows], w_co) + other
    after_two = after_one + (branch + vectors[7])

    normed_out, hat_three, inv_three = norm_forward(after_two, vectors[2], vectors[5])
    mlp_near, mlp_far = spread_rows(low(normed_out))
    grad_near, grad_far = spread_rows(grad_rows)
    pre_near = product(mlp_near, w_in) + hidden_bias
    pre_far = product(mlp_far, w_in) + hidden_bias
    act_near, act_far = low(gelu_value(pre_near)), low(gelu_value(pre_far))
    dpre_near = low(product(grad_near, w_out) * gelu_slope(pre_near))
    dpre_far = low(product(grad_far, w_out) * gelu_slope(pre_far))
    gradient = grad_rows.astype(jnp.float32)
    bias_out_three = jnp.sum(gradient, axis=0)
    mlp_term = sum_rows(dpre_near, dpre_far, lambda rows: product_right_t(rows, w_in))
    branch = sum_rows(act_near, act_far, lambda rows: product_right_t(rows, w_out))
    layer_out = regroup(low(after_two + (branch + vectors[8])))
    grad_w_out = product_left_t(grad_near, act_near) + product_left_t(grad_far, act_far)
    grad_w_in = product_left_t(mlp_near, dpre_near) + product_left_t(mlp_far, dpre_far)
    grad_hidden_bias = jnp.sum(dpre_near.astype(jnp.float32), axis=0) + jnp.sum(
        dpre_far.astype(jnp.float32), axis=0
    )
    part, gain_three, shift_three = norm_backward(mlp_term, hat_three, inv_three, vectors[2])
    gradient = gradient + part

    grad_low = low(gradient)
    bias_out_two = jnp.sum(grad_low.astype(jnp.float32), axis=0)
    grad_both = jnp.concatenate([grad_low, trade(grad_low, "core")], axis=0)
    cross_mixed_grad = low(product(grad_both, w_co))
    cross_dq, cross_dk, cross_dv = attend_back(
        cross_plan,
        cross_meta,
        cross_q,
        0,
        cross_kv,
        0,
        cross_pairs,
        cross_mixed,
        cross_mixed_grad,
        cross_lse,
        cross_pairs,
        ENC,
    )
    other = trade(low(product_right_t(cross_dq[own_rows:], w_cq)), "core")
    part, gain_two, shift_two = norm_backward(
        product_right_t(cross_dq[:own_rows], w_cq) + other, hat_two, inv_two, vectors[1]
    )
    gradient = gradient + part
    grad_cross = jnp.concatenate(
        [
            low(product_left_t(cross_rows, cross_dq)),
            low(product_left_t(enc_full, cross_dk)),
            low(product_left_t(enc_full, cross_dv)),
            low(product_left_t(grad_both, cross_mixed)),
        ],
        axis=1,
    )
    bias_cross_query = jnp.sum(cross_dq.astype(jnp.float32), axis=0)
    bias_cross_value = jnp.sum(cross_dv.astype(jnp.float32), axis=0)

    def enc_term(rows):
        return product_right_t(half_of(cross_dk, rows, 0), w_ckv[:, :cross_width]) + product_right_t(
            half_of(cross_dv, rows, 0), w_ckv[:, cross_width:]
        )

    enc_half = enc_term(core) + trade(low(enc_term(1 - core)), "core")
    enc_sum = half_of(enc_half, zlo, 0) + trade(low(half_of(enc_half, 1 - zlo, 0)), "zlo")
    enc_grad = regroup(low(enc_sum)).astype(jnp.float32)

    grad_low = low(gradient)
    bias_out_one = jnp.sum(grad_low.astype(jnp.float32), axis=0)
    grad_near, grad_far = spread_rows(grad_low)
    mixed_grad = jnp.concatenate([low(product(grad_near, w_so)), low(product(grad_far, w_so))], axis=0)
    dq, dk, dv = attend_back(
        self_plan, self_meta, qkv, 0, qkv, pairs, 2 * pairs, mixed, mixed_grad, self_lse, pairs, 1152
    )
    dqkv = jnp.concatenate([dq, dk, dv], axis=1)
    d_near, d_far = dqkv[: count // 2], dqkv[count // 2 :]
    part, gain_one, shift_one = norm_backward(
        sum_rows(d_near, d_far, lambda rows: product_right_t(rows, w_qkv)), hat_one, inv_one, vectors[0]
    )
    input_grad = regroup(low(gradient + part)).astype(jnp.float32)
    grad_self = jnp.concatenate(
        [
            low(product_left_t(attn_near, d_near) + product_left_t(attn_far, d_far)),
            low(product_left_t(grad_near, near) + product_left_t(grad_far, far)),
        ],
        axis=1,
    )
    bias_self_query = jnp.sum(dq.astype(jnp.float32), axis=0)
    bias_self_value = jnp.sum(dv.astype(jnp.float32), axis=0)

    def keep_half(values, index, axis, axis_name):
        kept = half_of(values, index, axis).astype(jnp.float32)
        return kept + trade(half_of(values, 1 - index, axis), axis_name).astype(jnp.float32)

    def to_shards(values):
        kept, sent = half_of(values, core, 0), half_of(values, 1 - core, 0)
        return in_order(core, kept, trade(low(sent), "core").astype(jnp.float32), values.ndim - 1)

    def hidden_shard(partial):
        total = sum_over_chips(low(partial))
        return to_shards(keep_half(total, zhi, 1, "zhi"))

    ff_in_grad = hidden_shard(grad_w_in)
    ff_out_grad = hidden_shard(grad_w_out).T
    total = sum_over_chips(grad_cross).reshape(rows_of, 4, 2, -1)
    total = low(keep_half(total, zhi, 2, "zhi")).reshape(rows_of, 4, 2, -1)
    cross_grad = to_shards(keep_half(total, zlo, 2, "zlo").reshape(rows_of, 4, -1))
    total = sum_over_chips(grad_self).reshape(rows_of, 4, 2, -1)
    self_grad = to_shards(keep_half(total, zhi, 2, "zhi").reshape(rows_of, 4, -1))

    vec_sums = jnp.stack(
        [
            gain_one,
            gain_two,
            gain_three,
            shift_one,
            shift_two,
            shift_three,
            bias_out_one,
            bias_out_two,
            bias_out_three,
        ]
    )
    at_zlo = (jnp.arange(2) == zlo).astype(jnp.float32)
    at_core = (jnp.arange(2) == core).astype(jnp.float32)
    quarter = (at_zlo[:, None] * at_core[None, :])[:, :, None]
    self_sums = jnp.stack([bias_self_query, bias_self_value]).reshape(2, 2, 1, 1, -1) * quarter
    cross_sums = jnp.stack([bias_cross_query, bias_cross_value]).reshape(2, 2, 2, 1, -1) * at_core[:, None]
    head_sums = jnp.concatenate([self_sums, cross_sums], axis=0)
    hidden_sums = grad_hidden_bias.reshape(2, 1, 1, -1) * quarter
    vec_sums = jnp.broadcast_to(vec_sums.reshape(9, 8, -1).transpose(1, 0, 2).reshape(8, 1, -1), (8, 4, sizes[0]))
    head_sums = head_sums.reshape(4, 4, 8, -1).transpose(2, 1, 0, 3).reshape(8, 4, -1)
    hidden_sums = hidden_sums.reshape(4, 8, -1).transpose(1, 0, 2)
    sums = jnp.concatenate([vec_sums, head_sums, hidden_sums], axis=2).reshape(32, -1)
    sums = lax.psum_scatter(sums, AXES, scatter_dimension=0, tiled=True).reshape(-1)
    vec_grad, head_grad, ff_bias_grad = jnp.split(sums, [sizes[0], sizes[0] + sizes[1]])
    return (
        layer_out,
        input_grad,
        enc_grad,
        self_grad[:, :3].transpose(1, 0, 2),
        self_grad[:, 3].T,
        cross_grad[:, :3].transpose(1, 0, 2),
        cross_grad[:, 3].T,
        ff_in_grad,
        ff_out_grad,
        head_grad.reshape(head_bias.shape),
        ff_bias_grad,
        vec_grad.reshape(vec_params.shape),
    )


def solution(mesh):
    fast = tuple(mesh.shape[axis] for axis in ("dp", "tensor")) == (8, 4)
    dp, tensor = (AXES[:3], AXES[3:]) if fast else (("dp",), ("tensor",))
    both = dp + tensor
    rows = P(both, None)
    qkv = P(None, dp, tensor)
    out = P(tensor, dp)
    in_specs = (
        rows,
        rows,
        P(dp),
        P(dp, None),
        rows,
        qkv,
        out,
        qkv,
        out,
        P(dp, tensor),
        out,
        P(None, tensor + dp),
        P(tensor + dp),
        P(None, dp),
    )
    out_specs = (
        rows,
        rows,
        rows,
        qkv,
        out,
        qkv,
        out,
        P(dp, tensor),
        out,
        P(None, tensor + dp),
        P(tensor + dp),
        P(None, dp),
    )
    if fast:
        mesh = Mesh(mesh.devices.reshape(2, 2, 2, 2, 2), AXES)
    return jax.shard_map(
        fast_layer if fast else shards, mesh=mesh, in_specs=in_specs, out_specs=out_specs, check_vma=False
    )
```

```python
import functools
import math

import jax
import jax.numpy as jnp
from jax import lax
from jax.experimental import pallas as pl
from jax.experimental.pallas import tpu as pltpu
from jax.sharding import Mesh
from jax.sharding import PartitionSpec as P

HD = 64
PROMPT = 1024
CONT_TOK = 1024
ENC = 512
BLOCK = 256
PAIR = 2 * HD
AXES = ("y", "x", "core", "zhi", "zlo")


def lane_half():
    return lax.broadcasted_iota(jnp.int32, (1, PAIR), 1) < HD


def one_head(rows, head):
    keep = lane_half() if head == 0 else jnp.logical_not(lane_half())
    return rows * jnp.where(keep, 1.0, 0.0).astype(rows.dtype)


def dot_nt(left, right):
    return lax.dot_general(left, right, (((1,), (1,)), ((), ())), preferred_element_type=jnp.float32)


def dot_nn(left, right):
    return jnp.dot(left, right, preferred_element_type=jnp.float32)


def dot_tn(left, right):
    return lax.dot_general(left, right, (((0,), (0,)), ((), ())), preferred_element_type=jnp.float32)


def self_sections(meta_ref, segments):
    def at(block):
        return pl.multiple_of(meta_ref[block], 512)

    def place(index):
        return pl.multiple_of(meta_ref[index >> 1] + (index & 1) * BLOCK, BLOCK)

    def causal(row, col):
        return col <= row

    def banded(row, col):
        start = jnp.full(row.shape, meta_ref[4], jnp.int32)
        for segment in range(1, segments):
            bound = meta_ref[4 + segment]
            start = jnp.where(row >= bound, bound, start)
        return (col <= row) & (col >= start)

    def early(index):
        return [(at(0), 512, 0, causal)]

    def middle(index):
        return [(at(0), 512, 0, None), (at(1), 512, 512, causal)]

    def late(index):
        return [
            (at(0), 512, 0, None),
            (at(1), 512, 512, None),
            (place(index - 1), BLOCK, (index - 1) * BLOCK, banded),
            (place(index), BLOCK, index * BLOCK, banded),
        ]

    return place, ((0, 2, early), (2, 4, middle), (4, 8, late))


def cross_sections(meta_ref, blocks):
    def place(index):
        return pl.multiple_of(index * BLOCK, BLOCK)

    def usable(row, col):
        return col < meta_ref[0]

    def every(index):
        return [(0, ENC, 0, usable)]

    return place, ((0, blocks, every),)


def forward_kernel(sections, meta_ref, q_ref, k_ref, v_ref, o_ref, lse_ref):
    place, ranges = sections(meta_ref)

    for low, high, parts_of in ranges:

        def step(index, carry, parts_of=parts_of):
            rows = pl.ds(place(index), BLOCK)
            parts = parts_of(index)
            queries = q_ref[rows, :]
            row = index * BLOCK + lax.broadcasted_iota(jnp.int32, (BLOCK, 1), 0)
            allowed = [
                None if rule is None else rule(row, first + lax.broadcasted_iota(jnp.int32, (1, size), 1))
                for _, size, first, rule in parts
            ]
            outs, totals = [], []
            for head in range(2):
                query = one_head(queries, head)
                scores = []
                for (where, size, _, _), ok in zip(parts, allowed):
                    score = dot_nt(query, k_ref[pl.ds(where, size), :])
                    scores.append(score if ok is None else jnp.where(ok, score, -1e30))
                top = functools.reduce(jnp.maximum, [jnp.max(s, axis=1, keepdims=True) for s in scores])
                exps = [jnp.exp(s - top) for s in scores]
                total = sum(jnp.sum(e, axis=1, keepdims=True) for e in exps)
                mixed = sum(
                    dot_nn(e.astype(jnp.bfloat16), v_ref[pl.ds(where, size), :])
                    for (where, size, _, _), e in zip(parts, exps)
                )
                outs.append(mixed * (1.0 / total))
                totals.append(top + jnp.log(total))
            o_ref[rows, :] = jnp.where(lane_half(), outs[0], outs[1]).astype(o_ref.dtype)
            lse_ref[rows, :] = jnp.where(lane_half(), totals[0], totals[1])
            return carry

        lax.fori_loop(low, high, step, 0)


def backward_kernel(
    sections, meta_ref, q_ref, k_ref, v_ref, o_ref, do_ref, lse_ref, dq_ref, dk_ref, dv_ref, dk_sum, dv_sum
):
    place, ranges = sections(meta_ref)
    dk_sum[...] = jnp.zeros_like(dk_sum)
    dv_sum[...] = jnp.zeros_like(dv_sum)

    for low, high, parts_of in ranges:

        def step(index, carry, parts_of=parts_of):
            rows = pl.ds(place(index), BLOCK)
            parts = parts_of(index)
            queries, grads = q_ref[rows, :], do_ref[rows, :]
            row = index * BLOCK + lax.broadcasted_iota(jnp.int32, (1, BLOCK), 1)
            allowed = [
                None if rule is None else rule(row, first + lax.broadcasted_iota(jnp.int32, (size, 1), 0))
                for _, size, first, rule in parts
            ]
            logs = jnp.transpose(lse_ref[rows, :])
            spread = jnp.transpose(grads.astype(jnp.float32) * o_ref[rows, :].astype(jnp.float32))
            key_parts = [k_ref[pl.ds(where, size), :] for where, size, _, _ in parts]
            value_parts = [v_ref[pl.ds(where, size), :] for where, size, _, _ in parts]
            query_grads = []
            for head in range(2):
                query, grad = one_head(queries, head), one_head(grads, head)
                log = logs[head * HD : head * HD + 1, :]
                delta = jnp.sum(spread[head * HD : (head + 1) * HD, :], axis=0, keepdims=True)
                query_grad = None
                for (where, size, _, _), ok, keys, values in zip(parts, allowed, key_parts, value_parts):
                    score = dot_nt(keys, query)
                    if ok is not None:
                        score = jnp.where(ok, score, -1e30)
                    probs = jnp.exp(score - log)
                    score_grad = (probs * (dot_nt(values, grad) - delta)).astype(jnp.bfloat16)
                    dv_sum[pl.ds(where, size), :] += dot_nn(probs.astype(jnp.bfloat16), grad)
                    dk_sum[pl.ds(where, size), :] += dot_nn(score_grad, query)
                    term = dot_tn(score_grad, keys)
                    query_grad = term if query_grad is None else query_grad + term
                query_grads.append(query_grad)
            both = jnp.where(lane_half(), query_grads[0], query_grads[1])
            dq_ref[rows, :] = both.astype(jnp.bfloat16) * jnp.asarray(HD**-0.5, jnp.bfloat16)
            return carry

        lax.fori_loop(low, high, step, 0)
    dk_ref[...] = dk_sum[...].astype(dk_ref.dtype)
    dv_ref[...] = dv_sum[...].astype(dv_ref.dtype)


def columns(rows, first):
    return pl.BlockSpec((rows, PAIR), lambda pair, meta: (0, first + pair))


def attend(sections, meta, q, q_at, keys, k_at, v_at, pairs, weight):
    count, key_rows = q.shape[0], keys.shape[0]
    return pl.pallas_call(
        functools.partial(forward_kernel, sections),
        grid_spec=pltpu.PrefetchScalarGridSpec(
            num_scalar_prefetch=1,
            grid=(pairs,),
            in_specs=[columns(count, q_at), columns(key_rows, k_at), columns(key_rows, v_at)],
            out_specs=[columns(count, 0), columns(count, 0)],
        ),
        out_shape=[
            jax.ShapeDtypeStruct((count, pairs * PAIR), jnp.bfloat16),
            jax.ShapeDtypeStruct((count, pairs * PAIR), jnp.float32),
        ],
        cost_estimate=pl.CostEstimate(
            flops=2 * 4 * 4 * count * weight * pairs * PAIR,
            bytes_accessed=10 * count * pairs * PAIR,
            transcendentals=2 * pairs * count * weight,
        ),
    )(meta, q, keys, keys)


def attend_back(sections, meta, q, q_at, keys, k_at, v_at, out, out_grad, lse, pairs, weight):
    count, key_rows = q.shape[0], keys.shape[0]
    return pl.pallas_call(
        functools.partial(backward_kernel, sections),
        grid_spec=pltpu.PrefetchScalarGridSpec(
            num_scalar_prefetch=1,
            grid=(pairs,),
            in_specs=[
                columns(count, q_at),
                columns(key_rows, k_at),
                columns(key_rows, v_at),
                columns(count, 0),
                columns(count, 0),
                columns(count, 0),
            ],
            out_specs=[columns(count, 0), columns(key_rows, 0), columns(key_rows, 0)],
            scratch_shapes=[pltpu.VMEM((key_rows, PAIR), jnp.float32)] * 2,
        ),
        out_shape=[
            jax.ShapeDtypeStruct((count, pairs * PAIR), jnp.bfloat16),
            jax.ShapeDtypeStruct((key_rows, pairs * PAIR), jnp.bfloat16),
            jax.ShapeDtypeStruct((key_rows, pairs * PAIR), jnp.bfloat16),
        ],
        cost_estimate=pl.CostEstimate(
            flops=5 * 4 * 4 * count * weight * pairs * PAIR,
            bytes_accessed=20 * count * pairs * PAIR,
            transcendentals=2 * pairs * count * weight,
        ),
    )(meta, q, keys, keys, out, out_grad, lse)


EPSILON = 1e-05
MASKED = 1e30
GELU_C = math.sqrt(2.0 / math.pi)
GELU_A = 0.044715


def gelu_value(values):
    inner = jnp.tanh(GELU_C * (values + GELU_A * values * values * values))
    return 0.5 * values * (1.0 + inner)


def gelu_slope(values):
    inner = jnp.tanh(GELU_C * (values + GELU_A * values * values * values))
    return 0.5 * (1.0 + inner) + 0.5 * values * (1.0 - inner * inner) * GELU_C * (
        1.0 + 3.0 * GELU_A * values * values
    )


def norm_forward(values, gain_vec, shift_vec):
    row_mean = jnp.mean(values, axis=1, keepdims=True)
    centred = values - row_mean
    inverse = lax.rsqrt(jnp.mean(centred * centred, axis=1, keepdims=True) + EPSILON)
    normed = centred * inverse
    return (normed * gain_vec + shift_vec, normed, inverse)


def norm_backward(gradient, normed, inverse, gain_vec):
    scaled = gradient * gain_vec
    inner = (
        scaled
        - jnp.mean(scaled, axis=1, keepdims=True)
        - normed * jnp.mean(scaled * normed, axis=1, keepdims=True)
    )
    return (inner * inverse, jnp.sum(gradient * normed, axis=0), jnp.sum(gradient, axis=0))


def product(left, right):
    return jnp.dot(left, right, preferred_element_type=jnp.float32)


def product_left_t(left, right):
    return lax.dot_general(
        left, right, (((0,), (0,)), ((), ())), preferred_element_type=jnp.float32
    )


def product_right_t(left, right):
    return lax.dot_general(
        left, right, (((1,), (1,)), ((), ())), preferred_element_type=jnp.float32
    )


def attend_forward(queries, key_rows, value_rows, rule, block_rows):
    seq_rows, local_width = queries.shape
    local_heads = local_width // HD
    query_blocks = queries.reshape(seq_rows // block_rows, block_rows, local_heads, HD)
    key_heads = key_rows.reshape(-1, local_heads, HD)
    value_heads = value_rows.reshape(-1, local_heads, HD)
    block_starts = jnp.arange(seq_rows // block_rows, dtype=jnp.int32) * block_rows

    def attend_block(pieces):
        query_block, offset = pieces
        scores = jnp.einsum(
            "qhd,khd->hqk", query_block, key_heads, preferred_element_type=jnp.float32
        )
        scores = jnp.where(rule(offset, block_rows)[None], scores, -MASKED)
        row_max = jnp.max(scores, axis=2, keepdims=True)
        exponent = jnp.exp(scores - row_max)
        row_total = jnp.sum(exponent, axis=2, keepdims=True)
        probs_low = (exponent / row_total).astype(jnp.bfloat16)
        mixed = jnp.einsum(
            "hqk,khd->qhd", probs_low, value_heads, preferred_element_type=jnp.float32
        )
        return (
            mixed.astype(jnp.bfloat16).reshape(block_rows, local_width),
            (row_max + jnp.log(row_total))[:, :, 0],
        )

    outputs, log_total = lax.map(attend_block, (query_blocks, block_starts))
    return (outputs.reshape(seq_rows, local_width), log_total)


def attend_backward(queries, key_rows, value_rows, out_grad, log_total, rule, block_rows):
    seq_rows, local_width = queries.shape
    local_heads = local_width // HD
    key_count = key_rows.shape[0]
    query_blocks = queries.reshape(seq_rows // block_rows, block_rows, local_heads, HD)
    grad_blocks = out_grad.reshape(seq_rows // block_rows, block_rows, local_heads, HD)
    key_heads = key_rows.reshape(key_count, local_heads, HD)
    value_heads = value_rows.reshape(key_count, local_heads, HD)
    block_starts = jnp.arange(seq_rows // block_rows, dtype=jnp.int32) * block_rows

    def back_block(running, pieces):
        key_sum, value_sum = running
        query_block, grad_block, block_total, offset = pieces
        scores = jnp.einsum(
            "qhd,khd->hqk", query_block, key_heads, preferred_element_type=jnp.float32
        )
        probs = jnp.where(
            rule(offset, block_rows)[None], jnp.exp(scores - block_total[:, :, None]), 0.0
        )
        probs_low = probs.astype(jnp.bfloat16)
        prob_grad = jnp.einsum(
            "qhd,khd->hqk", grad_block, value_heads, preferred_element_type=jnp.float32
        )
        row_delta = jnp.sum(probs * prob_grad, axis=2, keepdims=True)
        score_grad = (probs * (prob_grad - row_delta)).astype(jnp.bfloat16)
        query_grad = jnp.einsum(
            "hqk,khd->qhd", score_grad, key_heads, preferred_element_type=jnp.float32
        )
        key_sum = key_sum + jnp.einsum(
            "hqk,qhd->khd", score_grad, query_block, preferred_element_type=jnp.float32
        )
        value_sum = value_sum + jnp.einsum(
            "hqk,qhd->khd", probs_low, grad_block, preferred_element_type=jnp.float32
        )
        return (
            (key_sum, value_sum),
            query_grad.astype(jnp.bfloat16).reshape(block_rows, local_width),
        )

    zero_sum = jnp.zeros((key_count, local_heads, HD), jnp.float32)
    (key_sum, value_sum), query_grads = lax.scan(
        back_block, (zero_sum, zero_sum), (query_blocks, grad_blocks, log_total, block_starts)
    )
    return (
        query_grads.reshape(seq_rows, local_width),
        key_sum.astype(jnp.bfloat16).reshape(key_count, local_width),
        value_sum.astype(jnp.bfloat16).reshape(key_count, local_width),
    )


def attend_groups(queries, key_rows, value_rows, rules, block_rows):
    results, totals = ([], [])
    for which_group, rule in enumerate(rules):
        mixed, log_total = attend_forward(queries, key_rows, value_rows, rule, block_rows)
        results.append(mixed)
        totals.append(log_total)
    return (results[0], totals)


def back_groups(queries, key_rows, value_rows, out_grad, totals, rules, block_rows):
    query_list, key_list, value_list = ([], [], [])
    for which_group, rule in enumerate(rules):
        query_grad, key_grad, value_grad = attend_backward(
            queries, key_rows, value_rows, out_grad, totals[which_group], rule, block_rows
        )
        query_list.append(query_grad)
        key_list.append(key_grad)
        value_list.append(value_grad)
    return (query_list[0], key_list[0], value_list[0])


def shards(
    tokens,
    enc_states,
    enc_len,
    cont_lengths,
    cotangent,
    self_qkv,
    self_out,
    cross_qkv,
    cross_out,
    ff_in,
    ff_out,
    head_bias,
    ff_bias,
    vec_params,
):
    gathered = (
        lax.all_gather(self_qkv, "dp", axis=1, tiled=True),
        lax.all_gather(self_out, "dp", axis=1, tiled=True),
        lax.all_gather(cross_qkv, "dp", axis=1, tiled=True),
        lax.all_gather(cross_out, "dp", axis=1, tiled=True),
        lax.all_gather(ff_in, "dp", axis=0, tiled=True),
        lax.all_gather(ff_out, "dp", axis=1, tiled=True),
        lax.all_gather(head_bias, "dp", axis=1, tiled=True),
        lax.all_gather(ff_bias, "dp", axis=0, tiled=True),
        lax.all_gather(vec_params, "dp", axis=1, tiled=True),
    )
    (
        w_self,
        w_self_out,
        w_cross,
        w_cross_out,
        w_hidden_in,
        w_hidden_out,
        bias_heads,
        bias_hidden,
        vectors,
    ) = gathered
    vectors = vectors.astype(jnp.float32)
    bias_heads = bias_heads.astype(jnp.float32)
    bias_hidden = bias_hidden.astype(jnp.float32)
    seq_rows = PROMPT + CONT_TOK
    block_rows = min(512, seq_rows)
    scaling = HD ** (-0.5)
    rows_dev = tokens.shape[0]

    def self_rule(which_group):
        bounds = PROMPT + jnp.cumsum(cont_lengths[which_group])
        positions = jnp.arange(seq_rows, dtype=jnp.int32)
        segment = jnp.sum((positions[:, None] >= bounds[None, :]).astype(jnp.int32), axis=1)

        def self_allowed(offset, number):
            row_ids = offset + jnp.arange(number, dtype=jnp.int32)
            row_segment = lax.dynamic_slice_in_dim(segment, offset, number)
            return (positions[None, :] <= row_ids[:, None]) & (
                (positions[None, :] < PROMPT) | (segment[None, :] == row_segment[:, None])
            )

        return self_allowed

    def cross_rule(which_group):
        usable = jnp.arange(ENC, dtype=jnp.int32) < enc_len[which_group]

        def cross_allowed(offset, number):
            return jnp.broadcast_to(usable[None, :], (number, ENC))

        return cross_allowed

    def spread(low_rows):
        return lax.all_gather(low_rows, "tensor", axis=0, tiled=True)

    def head_branch(values, weight):

        def term(offset, number):
            return product(values, weight)

        return lax.psum_scatter(
            term(jnp.int32(0), rows_dev * lax.axis_size("tensor")),
            "tensor",
            scatter_dimension=0,
            tiled=True,
        )

    def widen(low_rows):
        return lax.all_gather(low_rows, "tensor", axis=0, tiled=True)

    def narrow(term):
        return lax.psum_scatter(
            term(jnp.int32(0), rows_dev * lax.axis_size("tensor")),
            "tensor",
            scatter_dimension=0,
            tiled=True,
        )

    self_rules = [self_rule(0)]
    cross_rules = [cross_rule(0)]
    resid = tokens.astype(jnp.float32)
    enc_full = lax.all_gather(enc_states, "tensor", axis=0, tiled=True)
    normed_in, hat_one, inv_one = norm_forward(resid, vectors[0], vectors[3])
    attn_low = normed_in.astype(jnp.bfloat16)
    attn_full = spread(attn_low)
    queries = ((product(attn_full, w_self[0]) + bias_heads[0]) * scaling).astype(jnp.bfloat16)
    key_rows = product(attn_full, w_self[1]).astype(jnp.bfloat16)
    value_rows = (product(attn_full, w_self[2]) + bias_heads[1]).astype(jnp.bfloat16)
    mixed, self_totals = attend_groups(queries, key_rows, value_rows, self_rules, block_rows)
    after_one = resid + (head_branch(mixed, w_self_out) + vectors[6])
    normed_mid, hat_two, inv_two = norm_forward(after_one, vectors[1], vectors[4])
    cross_low = normed_mid.astype(jnp.bfloat16)
    cross_full = spread(cross_low)
    cross_queries = ((product(cross_full, w_cross[0]) + bias_heads[2]) * scaling).astype(
        jnp.bfloat16
    )
    cross_keys = product(enc_full, w_cross[1]).astype(jnp.bfloat16)
    cross_values = (product(enc_full, w_cross[2]) + bias_heads[3]).astype(jnp.bfloat16)
    cross_mixed, cross_totals = attend_groups(
        cross_queries, cross_keys, cross_values, cross_rules, block_rows
    )
    after_two = after_one + (head_branch(cross_mixed, w_cross_out) + vectors[7])
    normed_out, hat_three, inv_three = norm_forward(after_two, vectors[2], vectors[5])
    hidden_low = normed_out.astype(jnp.bfloat16)
    hidden_full = spread(hidden_low)
    pre_act = product(hidden_full, w_hidden_in) + bias_hidden
    activation = gelu_value(pre_act).astype(jnp.bfloat16)

    def term(offset, number):
        return product(activation, w_hidden_out)

    after_three = after_two + (
        lax.psum_scatter(
            term(jnp.int32(0), rows_dev * lax.axis_size("tensor")),
            "tensor",
            scatter_dimension=0,
            tiled=True,
        )
        + vectors[8]
    )
    layer_out = after_three.astype(jnp.bfloat16)
    gradient = cotangent.astype(jnp.float32)
    grad_low = gradient.astype(jnp.bfloat16)
    bias_out_three = jnp.sum(grad_low.astype(jnp.float32), axis=0)
    grad_full = widen(grad_low)
    act_grad = (product_right_t(grad_full, w_hidden_out) * gelu_slope(pre_act)).astype(jnp.bfloat16)
    grad_hidden_out = product_left_t(activation, grad_full)
    grad_hidden_in = product_left_t(hidden_full, act_grad)
    grad_bias_hidden = jnp.sum(act_grad.astype(jnp.float32), axis=0)

    def hidden_term(offset, number):
        return product_right_t(act_grad, w_hidden_in)

    input_part, gain_three, shift_three = norm_backward(
        narrow(hidden_term), hat_three, inv_three, vectors[2]
    )
    gradient = gradient + input_part
    grad_low = gradient.astype(jnp.bfloat16)
    bias_out_two = jnp.sum(grad_low.astype(jnp.float32), axis=0)
    grad_full = widen(grad_low)
    grad_cross_out = product_left_t(cross_mixed, grad_full)
    mixed_grad = product_right_t(grad_full, w_cross_out).astype(jnp.bfloat16)
    cross_query_grad, cross_key_grad, cross_value_grad = back_groups(
        cross_queries, cross_keys, cross_values, mixed_grad, cross_totals, cross_rules, block_rows
    )
    grad_cross = jnp.stack(
        [
            product_left_t(cross_full, cross_query_grad) * scaling,
            product_left_t(enc_full, cross_key_grad),
            product_left_t(enc_full, cross_value_grad),
        ]
    )
    bias_cross_query = jnp.sum(cross_query_grad.astype(jnp.float32), axis=0) * scaling
    bias_cross_value = jnp.sum(cross_value_grad.astype(jnp.float32), axis=0)
    enc_grad = lax.psum_scatter(
        product_right_t(cross_key_grad, w_cross[1]) + product_right_t(cross_value_grad, w_cross[2]),
        "tensor",
        scatter_dimension=0,
        tiled=True,
    )

    def cross_term(offset, number):
        return product_right_t(cross_query_grad, w_cross[0]) * scaling

    input_part, gain_two, shift_two = norm_backward(
        narrow(cross_term), hat_two, inv_two, vectors[1]
    )
    gradient = gradient + input_part
    grad_low = gradient.astype(jnp.bfloat16)
    bias_out_one = jnp.sum(grad_low.astype(jnp.float32), axis=0)
    grad_full = widen(grad_low)
    grad_self_out = product_left_t(mixed, grad_full)
    self_mixed_grad = product_right_t(grad_full, w_self_out).astype(jnp.bfloat16)
    query_grad, key_grad, value_grad = back_groups(
        queries, key_rows, value_rows, self_mixed_grad, self_totals, self_rules, block_rows
    )
    grad_self = jnp.stack(
        [
            product_left_t(attn_full, query_grad) * scaling,
            product_left_t(attn_full, key_grad),
            product_left_t(attn_full, value_grad),
        ]
    )
    bias_self_query = jnp.sum(query_grad.astype(jnp.float32), axis=0) * scaling
    bias_self_value = jnp.sum(value_grad.astype(jnp.float32), axis=0)

    def self_term(offset, number):
        return (
            product_right_t(query_grad, w_self[0]) * scaling
            + product_right_t(key_grad, w_self[1])
            + product_right_t(value_grad, w_self[2])
        )

    input_part, gain_one, shift_one = norm_backward(narrow(self_term), hat_one, inv_one, vectors[0])
    input_grad = gradient + input_part
    vector_grads = jnp.stack(
        [
            gain_one,
            gain_two,
            gain_three,
            shift_one,
            shift_two,
            shift_three,
            bias_out_one,
            bias_out_two,
            bias_out_three,
        ]
    )
    head_grads = jnp.stack([bias_self_query, bias_self_value, bias_cross_query, bias_cross_value])
    results = (
        lax.psum_scatter(grad_self, "dp", scatter_dimension=1, tiled=True),
        lax.psum_scatter(grad_self_out, "dp", scatter_dimension=1, tiled=True),
        lax.psum_scatter(grad_cross, "dp", scatter_dimension=1, tiled=True),
        lax.psum_scatter(grad_cross_out, "dp", scatter_dimension=1, tiled=True),
        lax.psum_scatter(grad_hidden_in, "dp", scatter_dimension=0, tiled=True),
        lax.psum_scatter(grad_hidden_out, "dp", scatter_dimension=1, tiled=True),
        lax.psum_scatter(head_grads, "dp", scatter_dimension=1, tiled=True),
        lax.psum_scatter(grad_bias_hidden, "dp", scatter_dimension=0, tiled=True),
        lax.psum_scatter(vector_grads, "dp", scatter_dimension=1, tiled=True),
    )
    vector_total = lax.psum(results[8], "tensor")
    return (
        layer_out,
        input_grad,
        enc_grad,
        results[0],
        results[1],
        results[2],
        results[3],
        results[4],
        results[5],
        results[6],
        results[7],
        vector_total,
    )


MESH = pl.DeviceIdType.MESH
LINKS = ("core", "x", "y", "zhi", "zlo")


def start_kernel(
    tokens,
    enc,
    w_self,
    w_cross,
    w_in,
    w_out,
    small,
    token_rows,
    attn,
    g_self,
    g_cross,
    hidden,
    enc_full,
    small_all,
    held,
    normed,
    gathered,
    send,
    recv,
    local,
):
    y, x, core, zhi, zlo = (lax.axis_index(axis) for axis in AXES)
    crossing = core != zhi
    rows = tokens.shape[0]
    part = w_self.shape[1]
    counts = {"sent": 0, "local": 0}

    def push(source, target, axis):
        index = counts["sent"]
        counts["sent"] += 1
        copy = pltpu.make_async_remote_copy(
            src_ref=source,
            dst_ref=target,
            send_sem=send.at[index],
            recv_sem=recv.at[index],
            device_id={axis: 1 - lax.axis_index(axis)},
            device_id_type=MESH,
        )
        copy.start()
        return copy

    def keep(source, target):
        index = counts["local"]
        counts["local"] += 1
        copy = pltpu.make_async_copy(source, target, local.at[index])
        copy.start()
        return copy

    def moving(source, target, source_here, target_here):
        index, index_here = counts["sent"], counts["local"]
        counts["sent"] += 1
        counts["local"] += 1

        def remote():
            return pltpu.make_async_remote_copy(
                src_ref=source,
                dst_ref=target,
                send_sem=send.at[index],
                recv_sem=recv.at[index],
                device_id={"core": zhi, "zhi": core},
                device_id_type=MESH,
            )

        def here():
            return pltpu.make_async_copy(source_here, target_here, local.at[index_here])

        @pl.when(crossing)
        def _():
            remote().start()

        @pl.when(jnp.logical_not(crossing))
        def _():
            here().start()

        def wait():
            @pl.when(crossing)
            def _():
                remote().wait()

            @pl.when(jnp.logical_not(crossing))
            def _():
                here().wait()

        return wait

    def lanes(block, size):
        return pl.ds(pl.multiple_of(block * size, size), size)

    barrier = pltpu.get_barrier_semaphore()
    for axis in LINKS:
        pl.semaphore_signal(barrier, inc=1, device_id={axis: 1 - lax.axis_index(axis)}, device_id_type=MESH)

    @pl.when(crossing)
    def _():
        pl.semaphore_signal(barrier, inc=1, device_id={"core": zhi, "zhi": core}, device_id_type=MESH)

    pl.semaphore_wait(barrier, len(LINKS) + crossing.astype(jnp.int32))

    wait_tokens = moving(tokens, held, tokens, held)
    own_small = keep(small, gathered.at[y, x, core, zhi, zlo])
    own_rows = pl.ds(pl.multiple_of(core * part, part), part)
    quarter = 2 * zhi + zlo

    def from_shard(shard, target, block, size):
        own = keep(shard.at[:, :, lanes(core, size)], target.at[:, y, x, own_rows, lanes(block, size)])
        other = push(
            shard.at[:, :, lanes(1 - core, size)], target.at[:, y, x, own_rows, lanes(block, size)], "core"
        )
        return own, other

    self_width = w_self.shape[2] // 2
    hidden_width = w_in.shape[1] // 2
    cross_core = from_shard(w_cross, g_cross, quarter, self_width)
    own_small.wait()
    small_core = push(gathered.at[y, x, core, zhi, zlo], gathered.at[y, x, core, zhi, zlo], "core")
    self_core = from_shard(w_self, g_self, zhi, self_width)
    hidden_core = []
    for plane, shard in enumerate((w_in, w_out)):
        target = hidden.at[plane, own_rows, lanes(zhi, hidden_width)]
        hidden_core.append(keep(shard.at[:, lanes(core, hidden_width)], target))
        hidden_core.append(push(shard.at[:, lanes(1 - core, hidden_width)], target, "core"))
    for copy in cross_core:
        copy.wait()
    region = g_cross.at[:, y, x, :, lanes(quarter, self_width)]
    cross_zlo = push(region, region, "zlo")
    small_core.wait()
    region = gathered.at[y, x, :, zhi, zlo]
    small_x = push(region, region, "x")
    for copy in self_core:
        copy.wait()
    small_x.wait()
    region = gathered.at[y, :, :, zhi, zlo]
    small_y = push(region, region, "y")
    cross_zlo.wait()
    small_y.wait()

    def over_plane(target, width):
        first, second = pl.ds(0, width), pl.ds(width, width)
        region_a, region_b = target.at[:, y, x, :, first], target.at[:, y, x, :, second]
        steps = (push(region_a, region_a, "x"), push(region_b, region_b, "y"))

        def second_steps():
            steps[0].wait()
            region_a = target.at[:, y, :, :, first]
            step_a = push(region_a, region_a, "y")
            steps[1].wait()
            region_b = target.at[:, :, x, :, second]
            return step_a, push(region_b, region_b, "x")

        return second_steps

    wait_tokens()
    keep_tokens = keep(held, token_rows)
    region = gathered.at[:, :, :, zhi, zlo]
    small_zhi = push(region, region, "zhi")
    region = g_self.at[:, y, x, :, lanes(zhi, self_width)]
    self_zhi = push(region, region, "zhi")
    gain = jnp.concatenate([gathered[d // 4, d // 2 % 2, d % 2, zhi, zlo, 0:1, :] for d in range(8)], axis=1)
    shift = jnp.concatenate([gathered[d // 4, d // 2 % 2, d % 2, zhi, zlo, 3:4, :] for d in range(8)], axis=1)

    def norm_step(step, carry):
        block = pl.ds(pl.multiple_of(step * 64, 64), 64)
        values = held[block, :].astype(jnp.float32)
        centred = values - jnp.mean(values, axis=1, keepdims=True)
        inverse = lax.rsqrt(jnp.mean(centred * centred, axis=1, keepdims=True) + EPSILON)
        normed[block, :] = (centred * inverse * gain + shift).astype(normed.dtype)
        return carry

    lax.fori_loop(0, rows // 64, norm_step, 0)
    attn_zlo = push(normed, attn.at[pl.ds(2 * rows, rows)], "zlo")
    attn_core = push(normed, attn.at[pl.ds(rows, rows)], "core")
    attn_own = keep(normed, attn.at[pl.ds(0, rows)])

    self_zhi.wait()
    region = g_cross.at[:, y, x, :, lanes(zhi, 2 * self_width)]
    cross_zhi = push(region, region, "zhi")
    self_second = over_plane(g_self, self_width)
    self_last = self_second()
    small_zhi.wait()
    region = gathered.at[:, :, :, :, zlo]
    small_zlo = push(region, region, "zlo")
    for copy in hidden_core:
        copy.wait()
    cross_zhi.wait()
    region = hidden.at[0, :, lanes(zhi, hidden_width)]
    hidden_zhi = push(region, region, "zhi")
    wait_enc = moving(enc, enc_full.at[2 * zhi + zlo], enc, enc_full.at[2 * core + zlo])
    cross_second = over_plane(g_cross, 2 * self_width)
    attn_zlo.wait()
    attn_diagonal = push(attn.at[pl.ds(2 * rows, rows)], attn.at[pl.ds(3 * rows, rows)], "core")
    cross_last = cross_second()
    wait_enc()
    region = enc_full.at[2 * core + zlo]
    enc_zlo = push(region, region, "zlo")
    enc_core = push(region, region, "core")
    enc_zlo.wait()
    region = enc_full.at[2 * core + 1 - zlo]
    enc_diagonal = push(region, region, "core")
    small_zlo.wait()
    keep_small = keep(gathered, small_all)
    for copy in (
        *self_last,
        *cross_last,
        hidden_zhi,
        attn_core,
        attn_diagonal,
        enc_core,
        enc_diagonal,
        attn_own,
        keep_tokens,
        keep_small,
    ):
        copy.wait()


def start_exchange(tokens, enc, w_self, w_cross, w_in, w_out, small):
    rows, model = tokens.shape
    part = w_self.shape[1]
    low_type = tokens.dtype
    shapes = [
        jax.ShapeDtypeStruct((rows, model), low_type),
        jax.ShapeDtypeStruct((4 * rows, model), low_type),
        jax.ShapeDtypeStruct((4, 2, 2, 2 * part, w_self.shape[2]), low_type),
        jax.ShapeDtypeStruct((4, 2, 2, 2 * part, 2 * w_cross.shape[2]), low_type),
        jax.ShapeDtypeStruct((2, 2 * part, w_in.shape[1]), low_type),
        jax.ShapeDtypeStruct((4, enc.shape[0], model), low_type),
        jax.ShapeDtypeStruct((2,) * 5 + small.shape, small.dtype),
    ]
    anywhere = pl.BlockSpec(memory_space=pl.ANY)
    return pl.pallas_call(
        start_kernel,
        out_shape=shapes,
        in_specs=[anywhere] * 7,
        out_specs=[anywhere] * len(shapes),
        scratch_shapes=[
            pltpu.VMEM((rows, model), low_type),
            pltpu.VMEM((rows, model), low_type),
            pltpu.VMEM((2,) * 5 + small.shape, small.dtype),
            pltpu.SemaphoreType.DMA((30,)),
            pltpu.SemaphoreType.DMA((30,)),
            pltpu.SemaphoreType.DMA((12,)),
        ],
        compiler_params=pltpu.CompilerParams(collective_id=0, has_side_effects=True),
    )(tokens, enc, w_self, w_cross, w_in, w_out, small)


def finish_kernel(spread, hidden, attention, small, *refs):
    y, x, core, zhi, zlo = (lax.axis_index(axis) for axis in AXES)
    crossing = core != zhi
    refs = list(refs)

    def take(number):
        taken, refs[:number] = refs[:number], []
        return taken

    links = ("core", "zhi")
    if spread or attention or small:
        links += ("zlo",)
    if attention or small:
        links += ("x", "y")
    rows_in = take(1) if spread else []
    hidden_in = take(hidden)
    attention_in = take(3) if attention else []
    small_in = take(small)
    rows_out = take(1) if spread else []
    hidden_out = take(hidden)
    attention_out = take(3) if attention else []
    small_out = take(small)
    hidden_kept = [take(3) for _ in range(hidden)]
    if attention:
        enc_own, enc_got, enc_sum, enc_far, enc_low = take(5)
        kept, got, total, low_part, got_low, total_low = take(6)
        self_own, self_got, self_low, self_got_low, self_total, self_send, self_last = take(7)
    if small:
        small_sum, *small_got = take(1 + len(AXES))
    send, recv, local = take(3)
    counts = {"sent": 0, "local": 0}

    def push(source, target, axis):
        index = counts["sent"]
        counts["sent"] += 1
        copy = pltpu.make_async_remote_copy(
            src_ref=source,
            dst_ref=target,
            send_sem=send.at[index],
            recv_sem=recv.at[index],
            device_id={axis: 1 - lax.axis_index(axis)},
            device_id_type=MESH,
        )
        copy.start()
        return copy

    def keep(source, target):
        index = counts["local"]
        counts["local"] += 1
        copy = pltpu.make_async_copy(source, target, local.at[index])
        copy.start()
        return copy

    def lanes(block, size):
        return pl.ds(pl.multiple_of(block * size, size), size)

    def moving(source, target, source_here, target_here):
        index, index_here = counts["sent"], counts["local"]
        counts["sent"] += 1
        counts["local"] += 1

        def remote():
            return pltpu.make_async_remote_copy(
                src_ref=source,
                dst_ref=target,
                send_sem=send.at[index],
                recv_sem=recv.at[index],
                device_id={"core": zhi, "zhi": core},
                device_id_type=MESH,
            )

        def here():
            return pltpu.make_async_copy(source_here, target_here, local.at[index_here])

        @pl.when(crossing)
        def _():
            remote().start()

        @pl.when(jnp.logical_not(crossing))
        def _():
            here().start()

        def wait():
            @pl.when(crossing)
            def _():
                remote().wait()

            @pl.when(jnp.logical_not(crossing))
            def _():
                here().wait()

        return wait

    def add(target, left, right, columns_of=slice(None)):
        def step(index, carry):
            rows = pl.ds(pl.multiple_of(index * 64, 64), 64)
            value = left[rows, columns_of].astype(jnp.float32) + right[rows, :].astype(jnp.float32)
            target[rows, :] = value.astype(target.dtype)
            return carry

        lax.fori_loop(0, target.shape[0] // 64, step, 0)

    def narrow(target, source, columns_of=slice(None)):
        def step(index, carry):
            rows = pl.ds(pl.multiple_of(index * 64, 64), 64)
            target[rows, :] = source[rows, columns_of].astype(target.dtype)
            return carry

        lax.fori_loop(0, target.shape[0] // 64, step, 0)

    barrier = pltpu.get_barrier_semaphore()
    for axis in links:
        pl.semaphore_signal(barrier, inc=1, device_id={axis: 1 - lax.axis_index(axis)}, device_id_type=MESH)
    if attention:

        @pl.when(crossing)
        def _():
            pl.semaphore_signal(barrier, inc=1, device_id={"core": zhi, "zhi": core}, device_id_type=MESH)

        pl.semaphore_wait(barrier, len(links) + crossing.astype(jnp.int32))
    else:
        pl.semaphore_wait(barrier, len(links))

    small_first, small_size = 0, 32

    def small_send(stage):
        half, got = small_size // 2, small_got[stage]
        away = small_first + (1 - lax.axis_index(AXES[stage])) * half
        return push(small_sum.at[pl.ds(away, half)], got, AXES[stage])

    def small_add(stage, copy):
        copy.wait()
        half, got = small_size // 2, small_got[stage]
        mine = small_first + lax.axis_index(AXES[stage]) * half

        def step(index, carry):
            small_sum[mine + index] += got[index]
            return carry

        lax.fori_loop(0, half, step, 0)
        return mine, half

    last = []

    def to_cores(values, out):
        part, width = values.shape[0] // 2, values.shape[1]
        there = pl.ds(pl.multiple_of((1 - core) * part, part), part)
        here = pl.ds(pl.multiple_of(core * part, part), part)
        last.append(push(values.at[there], out.at[:, lanes(core, width)], "core"))
        last.append(keep(values.at[here], out.at[:, lanes(core, width)]))

    if spread:
        rows = rows_in[0].shape[0]
        out = rows_out[0]
        spread_zlo = push(rows_in[0], out.at[pl.ds(2 * rows, rows)], "zlo")
        last.append(push(rows_in[0], out.at[pl.ds(rows, rows)], "core"))
        last.append(keep(rows_in[0], out.at[pl.ds(0, rows)]))
    steps = []
    for partial, (mine, theirs, _) in zip(hidden_in, hidden_kept):
        width = mine.shape[1]
        steps.append(
            (push(partial.at[:, lanes(1 - zhi, width)], theirs, "zhi"), keep(partial.at[:, lanes(zhi, width)], mine))
        )
    if small:
        keep(small_in[0], small_sum).wait()
        for stage in range(len(AXES)):
            small_first, small_size = small_add(stage, small_send(stage))
        keep(small_sum.at[small_first], small_out[0]).wait()
    if attention:
        cross_part, self_part, enc_part = attention_in
        width = kept.shape[1]
        cross_zhi = push(cross_part.at[:, lanes(1 - zhi, width)], got, "zhi")
        cross_own = keep(cross_part.at[:, lanes(zhi, width)], kept)
        half = self_got.shape[3]
        first, second = pl.ds(0, half), pl.ds(half, half)
        enc_core = push(enc_part.at[1 - core], enc_got, "core")
        enc_keep = keep(enc_part.at[core], enc_own)
        self_x = push(self_part.at[:, 1 - x, :, first], self_got.at[0], "x")
        self_y = push(self_part.at[1 - y, :, :, second], self_got.at[1], "y")
        own_a = keep(self_part.at[:, x, :, first], self_own.at[0])
        own_b = keep(self_part.at[y, :, :, second], self_own.at[1])
        enc_core.wait()
        enc_keep.wait()
        add(enc_sum, enc_own.at[1 - zlo], enc_got.at[1 - zlo])
        enc_zlo = push(enc_sum, enc_far, "zlo")
        own_a.wait()
        self_x.wait()
        add(self_low, self_own.at[0, 1 - y], self_got.at[0, 1 - y])
        a_second = push(self_low, self_got_low.at[0], "y")
        own_b.wait()
        self_y.wait()
        add(self_send, self_own.at[1, 1 - x], self_got.at[1, 1 - x])
        b_second = push(self_send, self_got_low.at[1], "x")
        add(self_total.at[0], self_own.at[0, y], self_got.at[0, y])
        add(self_total.at[1], self_own.at[1, x], self_got.at[1, x])
        a_second.wait()
        add(self_total.at[0], self_total.at[0], self_got_low.at[0])
        b_second.wait()
        add(self_total.at[1], self_total.at[1], self_got_low.at[1])
        enc_zlo.wait()

        def enc_step(index, carry):
            rows = pl.ds(pl.multiple_of(index * 64, 64), 64)
            value = enc_own[zlo, rows, :].astype(jnp.float32) + enc_got[zlo, rows, :].astype(jnp.float32)
            enc_low[rows, :] = (value + enc_far[rows, :].astype(jnp.float32)).astype(enc_low.dtype)
            return carry

        lax.fori_loop(0, enc_low.shape[0] // 64, enc_step, 0)
        wait_enc = moving(enc_low, attention_out[2], enc_low, attention_out[2])
        narrow(self_low, self_total.at[1 - zhi])
        self_zhi = push(self_low, self_last, "zhi")
        cross_own.wait()
        cross_zhi.wait()
        add(total, kept, got)
        narrow(low_part, total, lanes(1 - zlo, low_part.shape[1]))
        cross_zlo = push(low_part, got_low, "zlo")
        self_zhi.wait()
        add(self_total.at[zhi], self_total.at[zhi], self_last)
        to_cores(self_total.at[zhi], attention_out[1])
        cross_zlo.wait()
        add(total_low, total, got_low, lanes(zlo, low_part.shape[1]))
        to_cores(total_low, attention_out[0])
    if spread:
        spread_zlo.wait()
        last.append(push(rows_out[0].at[pl.ds(2 * rows, rows)], rows_out[0].at[pl.ds(3 * rows, rows)], "core"))
    for copies, (mine, theirs, summed), out in zip(steps, hidden_kept, hidden_out):
        for copy in copies:
            copy.wait()
        add(summed, mine, theirs)
        to_cores(summed, out)
    if attention:
        wait_enc()
    for copy in last:
        copy.wait()


def finish(rows, hidden, attention, small, collective_id):
    operands, shapes, scratch = [], [], []
    if rows is not None:
        operands.append(rows)
        shapes.append(jax.ShapeDtypeStruct((4 * rows.shape[0], rows.shape[1]), rows.dtype))
    for partial in hidden:
        count, width = partial.shape
        operands.append(partial)
        shapes.append(jax.ShapeDtypeStruct((count // 2, width), jnp.float32))
        scratch += [pltpu.VMEM((count, width // 2), partial.dtype)] * 2
        scratch.append(pltpu.VMEM((count, width // 2), jnp.float32))
    if attention is not None:
        cross, own, enc = attention
        enc_shape = enc.shape[2:]
        count, width = cross.shape
        part, half = own.shape[2], own.shape[3] // 2
        operands += [cross, own, enc]
        shapes.append(jax.ShapeDtypeStruct((count // 2, width // 2), jnp.float32))
        shapes.append(jax.ShapeDtypeStruct((part // 2, 2 * half), jnp.float32))
        shapes.append(jax.ShapeDtypeStruct(enc_shape, enc.dtype))
        scratch += [
            pltpu.VMEM((2, *enc_shape), enc.dtype),
            pltpu.VMEM((2, *enc_shape), enc.dtype),
            pltpu.VMEM(enc_shape, enc.dtype),
            pltpu.VMEM(enc_shape, enc.dtype),
            pltpu.VMEM(enc_shape, enc.dtype),
            pltpu.VMEM((count, width // 2), cross.dtype),
            pltpu.VMEM((count, width // 2), cross.dtype),
            pltpu.VMEM((count, width // 2), jnp.float32),
            pltpu.VMEM((count, width // 4), cross.dtype),
            pltpu.VMEM((count, width // 4), cross.dtype),
            pltpu.VMEM((count, width // 4), jnp.float32),
            pltpu.VMEM((2, 2, part, half), own.dtype),
            pltpu.VMEM((2, 2, part, half), own.dtype),
            pltpu.VMEM((part, half), own.dtype),
            pltpu.VMEM((2, part, half), own.dtype),
            pltpu.VMEM((2, part, half), jnp.float32),
            pltpu.VMEM((part, half), own.dtype),
            pltpu.VMEM((part, half), own.dtype),
        ]
    if small is not None:
        operands.append(small)
        shapes.append(jax.ShapeDtypeStruct(small.shape[1:], small.dtype))
        scratch.append(pltpu.VMEM(small.shape, small.dtype))
        scratch += [pltpu.VMEM((32 >> stage, *small.shape[1:]), small.dtype) for stage in range(1, 6)]
    anywhere = pl.BlockSpec(memory_space=pl.ANY)
    return pl.pallas_call(
        functools.partial(
            finish_kernel, rows is not None, len(hidden), attention is not None, int(small is not None)
        ),
        out_shape=shapes,
        in_specs=[anywhere] * len(operands),
        out_specs=[anywhere] * len(shapes),
        scratch_shapes=scratch + [pltpu.SemaphoreType.DMA((16,))] * 3,
        compiler_params=pltpu.CompilerParams(collective_id=collective_id, has_side_effects=True),
        cost_estimate=pl.CostEstimate(flops=20_000_000_000, bytes_accessed=0, transcendentals=0),
    )(*operands)


def trade(rows, axis, name="trade"):
    with jax.named_scope(name):
        return lax.ppermute(rows, axis, [(0, 1), (1, 0)])


def after(value, *others):
    return lax.optimization_barrier((value, *others))[0]


def regroup(rows, name="regroup"):
    with jax.named_scope("re_" + name):
        return lax.ppermute(rows, ("core", "zhi"), [(0, 0), (1, 2), (2, 1), (3, 3)])


def in_order(index, own, other, axis):
    return jnp.concatenate(
        [jnp.where(index == 0, own, other), jnp.where(index == 0, other, own)], axis=axis
    )


def low(values):
    return values.astype(jnp.bfloat16)


def half_of(values, index, axis):
    size = values.shape[axis] // 2
    return lax.dynamic_slice_in_dim(values, index * size, size, axis)


def over_chips(rows):
    return lax.all_gather(rows, ("y", "x"), axis=0, tiled=True)


def sum_over_chips(partial):
    return lax.psum_scatter(partial, ("y", "x"), scatter_dimension=0, tiled=True)


def spread_rows(rows, name):
    beyond = trade(rows, "zlo", name + "_z")
    return (
        jnp.concatenate([rows, trade(rows, "core", name + "_c")], axis=0),
        jnp.concatenate([beyond, trade(beyond, "core", name + "_zc")], axis=0),
    )


def sum_rows(near, far, term, name):
    size = near.shape[0] // 2
    far_sum = term(far[:size]) + trade(low(term(far[size:])), "core", name + "_zc")
    from_far = trade(low(far_sum), "zlo", name + "_z")
    near_other = trade(low(term(near[size:])), "core", name + "_c")
    return term(near[:size]) + near_other + from_far


def fast_layer(
    tokens,
    enc_states,
    enc_len,
    cont_lengths,
    cotangent,
    self_qkv,
    self_out,
    cross_qkv,
    cross_out,
    ff_in,
    ff_out,
    head_bias,
    ff_bias,
    vec_params,
):
    core, zhi, zlo = lax.axis_index("core"), lax.axis_index("zhi"), lax.axis_index("zlo")
    scaling = HD**-0.5
    model = tokens.shape[1]
    segments = cont_lengths.shape[1]

    flat = jnp.concatenate([vec_params.reshape(-1), head_bias.reshape(-1), ff_bias]).astype(jnp.float32)
    sizes = (vec_params.size, head_bias.size, ff_bias.size)
    flat = jnp.pad(flat.reshape(-1, 128), ((0, 4), (0, 0)))
    token_rows, attn_rows, w_self, w_cross, w_hidden, enc_full, small = start_exchange(
        tokens,
        enc_states,
        jnp.concatenate([self_qkv, self_out.T[None]], axis=0),
        jnp.concatenate([cross_qkv, cross_out.T[None]], axis=0),
        ff_in,
        ff_out.T,
        flat,
    )
    w_self, w_cross = w_self.reshape(4, model, -1), w_cross.reshape(4, model, -1)
    w_in = over_chips(w_hidden[0])
    out_own = half_of(w_hidden[1], zhi, 1)
    out_beyond = trade(out_own, "zhi", "wo_zhi")
    w_qkv, w_so = jnp.concatenate([w_self[0], w_self[1], w_self[2]], axis=1), w_self[3]
    w_cq, w_ckv, w_co = w_cross[0], jnp.concatenate([w_cross[1], w_cross[2]], axis=1), w_cross[3]
    rows_of = model // 4
    width, cross_width = w_self.shape[2], w_cross.shape[2]
    pairs, cross_pairs = width // PAIR, cross_width // PAIR
    enc_full = enc_full.reshape(-1, model)
    attn_near, attn_far = attn_rows[: attn_rows.shape[0] // 2], attn_rows[attn_rows.shape[0] // 2 :]
    small = small.reshape(8, 4, -1)
    vec_part, head_part, ff_part = jnp.split(
        small[:, :, : sum(sizes)], [sizes[0], sizes[0] + sizes[1]], axis=2
    )
    vectors = vec_part[:, 0].reshape(8, 9, -1).transpose(1, 0, 2).reshape(9, model)
    heads = head_part.reshape(8, 4, 4, -1).transpose(2, 1, 0, 3).reshape(4, 2, 2, 2, -1)
    self_bias = lax.dynamic_index_in_dim(
        lax.dynamic_index_in_dim(heads[:2], zlo, 2, False), core, 2, False
    ).reshape(2, -1)
    cross_bias = lax.dynamic_index_in_dim(heads[2:], core, 3, False).reshape(2, -1)
    hidden_bias = ff_part.transpose(1, 0, 2).reshape(2, 2, 2, -1)
    hidden_bias = lax.dynamic_index_in_dim(
        lax.dynamic_index_in_dim(hidden_bias, zlo, 1, False), core, 1, False
    ).reshape(-1)

    lengths = regroup(jnp.concatenate([cont_lengths[0], enc_len]))
    places = jnp.stack(
        [512 * ((core != block // 2) + 2 * (zlo != block % 2)) for block in range(4)]
    ).astype(jnp.int32)
    bounds = PROMPT + jnp.concatenate(
        [jnp.zeros((1,), jnp.int32), jnp.cumsum(lengths[:segments]).astype(jnp.int32)]
    )
    self_meta = jnp.concatenate([places, bounds])
    cross_meta = lengths[segments:]

    resid = token_rows.astype(jnp.float32)
    _, hat_one, inv_one = norm_forward(resid, vectors[0], vectors[3])
    qkv_bias = jnp.concatenate([self_bias[0], jnp.zeros((width,), jnp.float32), self_bias[1]])
    qkv_scale = jnp.concatenate([jnp.full((width,), scaling), jnp.ones((2 * width,))]).astype(jnp.float32)
    def project(rows):
        return low((product(rows, w_qkv) + qkv_bias) * qkv_scale)

    qkv = project(attn_rows)
    count = qkv.shape[0]
    self_plan = functools.partial(self_sections, segments=segments)
    mixed, self_lse = attend(self_plan, self_meta, qkv, 0, qkv, pairs, 2 * pairs, pairs, 1152)
    mixed = after(mixed, out_beyond)
    w_out = over_chips(in_order(zhi, out_own, after(out_beyond, mixed), 1))
    near, far = mixed[: count // 2], mixed[count // 2 :]
    so_far = low(
        product_right_t(far[: count // 4], w_so)
        + trade(low(product_right_t(far[count // 4 :], w_so)), "core", "so_zc")
    )
    so_near_other = low(product_right_t(near[count // 4 :], w_so))
    so_near = product_right_t(near[: count // 4], w_so)
    grad_rows = regroup(after(cotangent, attn_rows), "cotangent")
    cross_kv = low(
        product(after(enc_full, grad_rows, so_far), w_ckv)
        + jnp.concatenate([jnp.zeros((cross_width,), jnp.float32), cross_bias[1]])
    )
    branch = so_near + trade(so_near_other, "core", "so_c") + after(trade(so_far, "zlo", "so_z"), cross_kv)
    after_one = resid + (branch + vectors[6])

    cot_beyond = trade(after(grad_rows, after_one), "zlo", "cot_z")
    cot_near = jnp.concatenate([grad_rows, trade(grad_rows, "core", "cot_c")], axis=0)

    normed_mid, hat_two, inv_two = norm_forward(after_one, vectors[1], vectors[4])
    cross_low = low(normed_mid)
    cross_rows = jnp.concatenate([cross_low, trade(cross_low, "core", "cin")], axis=0)
    own_rows = cross_low.shape[0]
    cross_q = low((product(cross_rows, w_cq) + cross_bias[0]) * scaling)
    cross_plan = functools.partial(cross_sections, blocks=cross_q.shape[0] // BLOCK)
    cross_mixed, cross_lse = attend(
        cross_plan, cross_meta, cross_q, 0, cross_kv, 0, cross_pairs, cross_pairs, ENC
    )
    cross_mixed = after(cross_mixed, cot_beyond)
    other = trade(low(product_right_t(cross_mixed[own_rows:], w_co)), "core", "co_c")
    branch = product_right_t(cross_mixed[:own_rows], w_co) + other
    after_two = after_one + (branch + vectors[7])

    normed_out, hat_three, inv_three = norm_forward(after_two, vectors[2], vectors[5])
    mlp_in = low(normed_out)
    beyond = trade(mlp_in, "zlo", "mlp_z")
    mlp_near = jnp.concatenate([mlp_in, trade(mlp_in, "core", "mlp_c")], axis=0)
    pre_near = product(mlp_near, w_in) + hidden_bias
    act_near = low(gelu_value(pre_near))
    beyond = after(beyond, act_near)
    mlp_far = jnp.concatenate([beyond, trade(beyond, "core", "mlp_zc")], axis=0)
    pre_far = product(mlp_far, w_in) + hidden_bias
    act_far = low(gelu_value(pre_far))
    cot_far = jnp.concatenate([cot_beyond, trade(cot_beyond, "core", "cot_zc")], axis=0)
    out_parts = [
        low(product_right_t(act_far[own_rows:], w_out)),
        product_right_t(act_far[:own_rows], w_out),
        low(product_right_t(act_near[own_rows:], w_out)),
        product_right_t(act_near[:own_rows], w_out),
    ]
    out_far = trade(low(out_parts[1] + trade(out_parts[0], "core", "out_zc")), "zlo", "out_z")
    out_branch = out_parts[3] + trade(out_parts[2], "core", "out_c")
    dpre_near = low(product(after(cot_near, act_far, out_branch), w_out) * gelu_slope(pre_near))
    dpre_far = low(product(after(cot_far, dpre_near), w_out) * gelu_slope(pre_far))
    gradient = grad_rows.astype(jnp.float32)
    bias_out_three = jnp.sum(gradient, axis=0)
    dmlp_far = low(
        product_right_t(dpre_far[:own_rows], w_in)
        + trade(low(product_right_t(dpre_far[own_rows:], w_in)), "core", "dmlp_zc")
    )
    mlp_term = product_right_t(dpre_near[:own_rows], w_in) + trade(
        low(product_right_t(dpre_near[own_rows:], w_in)), "core", "dmlp_c"
    )
    act_near, act_far = after(act_near, dmlp_far, mlp_term), after(act_far, dmlp_far, mlp_term)
    grad_w_out = low(product_left_t(cot_near, act_near) + product_left_t(cot_far, act_far))
    mlp_near, mlp_far = after(mlp_near, grad_w_out), after(mlp_far, grad_w_out)
    grad_w_in = low(product_left_t(mlp_near, dpre_near) + product_left_t(mlp_far, dpre_far))
    mlp_term = mlp_term + after(trade(dmlp_far, "zlo", "dmlp_z"), grad_w_in)
    part, gain_three, shift_three = norm_backward(mlp_term, hat_three, inv_three, vectors[2])
    gradient = gradient + part

    grad_low = low(gradient)
    bias_out_two = jnp.sum(grad_low.astype(jnp.float32), axis=0)
    grad_both = jnp.concatenate([grad_low, trade(grad_low, "core", "e2")], axis=0)
    cross_mixed_grad = low(product(grad_both, w_co))
    cross_dq, cross_dk, cross_dv = attend_back(
        cross_plan,
        cross_meta,
        cross_q,
        0,
        cross_kv,
        0,
        cross_pairs,
        cross_mixed,
        cross_mixed_grad,
        cross_lse,
        cross_pairs,
        ENC,
    )
    out_sum = sum_over_chips(grad_w_out)
    out_sum = half_of(out_sum, zhi, 1).astype(jnp.float32) + trade(half_of(out_sum, 1 - zhi, 1), "zhi", "go_zhi").astype(
        jnp.float32
    )
    cross_dq = after(cross_dq, out_sum)
    layer_out = regroup(low(after_two + (out_branch + after(out_far, cross_dq) + vectors[8])), "out")
    other = trade(low(product_right_t(cross_dq[own_rows:], w_cq)), "core", "dcin")
    part, gain_two, shift_two = norm_backward(
        product_right_t(cross_dq[:own_rows], w_cq) + other, hat_two, inv_two, vectors[1]
    )
    gradient = gradient + part

    grad_low = low(gradient)
    bias_out_one = jnp.sum(grad_low.astype(jnp.float32), axis=0)
    cross_parts = [
        low(product_left_t(cross_rows, after(cross_dq, grad_low))),
        low(product_left_t(enc_full, cross_dk)),
        low(product_left_t(enc_full, cross_dv)),
        low(product_left_t(grad_both, cross_mixed)),
    ]
    grad_cross = jnp.concatenate(
        [part[:, lo : lo + width // 2] for lo in range(0, cross_width, width // 2) for part in cross_parts], axis=1
    )
    e1_rows, ff_in_grad = finish(after(grad_low, grad_cross), [sum_over_chips(grad_w_in)], None, None, 1)
    lacking = trade(half_of(after(out_sum, e1_rows), 1 - core, 0), "core", "go_core")
    ff_out_grad = in_order(core, half_of(out_sum, core, 0), lacking, 1)
    cross_sum = sum_over_chips(grad_cross)
    mixed_grad = low(product(e1_rows, w_so))
    dq, dk, dv = attend_back(
        self_plan, self_meta, qkv, 0, qkv, pairs, 2 * pairs, mixed, mixed_grad, self_lse, pairs, 1152
    )
    dqkv = jnp.concatenate([dq, dk, dv], axis=1)
    d_near, d_far = dqkv[: count // 2], dqkv[count // 2 :]
    dx_far = low(
        product_right_t(d_far[: count // 4], w_qkv)
        + trade(low(product_right_t(d_far[count // 4 :], w_qkv)), "core", "dx_zc")
    )
    dx = product_right_t(d_near[: count // 4], w_qkv) + trade(
        low(product_right_t(d_near[count // 4 :], w_qkv)), "core", "dx_c"
    )
    dq, dk, dv = after(dq, dx_far), after(dk, dx_far), after(dv, dx_far)
    self_parts = [
        low(product_left_t(attn_rows, dq)),
        low(product_left_t(attn_rows, dk)),
        low(product_left_t(attn_rows, dv)),
        low(product_left_t(e1_rows, mixed)),
    ]
    grad_self = jnp.concatenate(
        [part[:, lo : lo + width // 2] for lo in range(0, width, width // 2) for part in self_parts], axis=1
    )

    enc_part = low(
        product_right_t(after(cross_dk, dq), w_ckv[:, :cross_width])
        + product_right_t(after(cross_dv, dq), w_ckv[:, cross_width:])
    )
    cross_grad, self_grad, enc_grad = finish(
        None,
        [],
        (
            after(cross_sum, dx),
            grad_self.reshape(2, 2, rows_of, -1),
            enc_part.reshape(2, 2, -1, model),
        ),
        None,
        2,
    )
    enc_grad = enc_grad.astype(jnp.float32)
    dx = dx + after(trade(dx_far, "zlo", "dx_z"), cross_grad)

    def planes(shard):
        return shard.reshape(shard.shape[0], 2, 4, -1).transpose(2, 0, 1, 3).reshape(4, shard.shape[0], -1)

    cross_grad, self_grad = planes(cross_grad), planes(self_grad)
    part, gain_one, shift_one = norm_backward(dx, hat_one, inv_one, vectors[0])
    input_part = low(gradient + part)
    input_grad = regroup(input_part, "dgrad").astype(jnp.float32)

    bias_self_query = jnp.sum(dq.astype(jnp.float32), axis=0)
    bias_self_value = jnp.sum(dv.astype(jnp.float32), axis=0)
    bias_cross_query = jnp.sum(cross_dq.astype(jnp.float32), axis=0)
    bias_cross_value = jnp.sum(cross_dv.astype(jnp.float32), axis=0)
    grad_hidden_bias = jnp.sum(dpre_near.astype(jnp.float32), axis=0) + jnp.sum(
        dpre_far.astype(jnp.float32), axis=0
    )
    vec_sums = jnp.stack(
        [
            gain_one,
            gain_two,
            gain_three,
            shift_one,
            shift_two,
            shift_three,
            bias_out_one,
            bias_out_two,
            bias_out_three,
        ]
    )
    at_zlo = (jnp.arange(2) == zlo).astype(jnp.float32)
    at_core = (jnp.arange(2) == core).astype(jnp.float32)
    quarter = (at_zlo[:, None] * at_core[None, :])[:, :, None]
    self_sums = jnp.stack([bias_self_query, bias_self_value]).reshape(2, 2, 1, 1, -1) * quarter
    cross_sums = jnp.stack([bias_cross_query, bias_cross_value]).reshape(2, 2, 2, 1, -1) * at_core[:, None]
    head_sums = jnp.concatenate([self_sums, cross_sums], axis=0)
    hidden_sums = grad_hidden_bias.reshape(2, 1, 1, -1) * quarter
    vec_sums = vec_sums.reshape(9, 8, -1).transpose(1, 0, 2).reshape(8, 1, -1)
    sums = jnp.concatenate(
        [
            jnp.broadcast_to(vec_sums, (8, 4, sizes[0])),
            head_sums.reshape(4, 4, 8, -1).transpose(2, 1, 0, 3).reshape(8, 4, -1),
            hidden_sums.reshape(4, 8, -1).transpose(1, 0, 2),
        ],
        axis=2,
    )
    sums = jnp.pad(after(sums, input_part).reshape(32, -1, 128), ((0, 0), (0, 4), (0, 0)))
    (sums,) = finish(None, [], None, sums, 3)
    sums = sums.reshape(-1)[: sum(sizes)]
    vec_grad, head_grad, ff_bias_grad = jnp.split(sums, [sizes[0], sizes[0] + sizes[1]])
    return (
        layer_out,
        input_grad,
        enc_grad,
        self_grad[:3],
        self_grad[3].T,
        cross_grad[:3],
        cross_grad[3].T,
        ff_in_grad,
        ff_out_grad.T,
        head_grad.reshape(head_bias.shape),
        ff_bias_grad,
        vec_grad.reshape(vec_params.shape),
    )


def solution(mesh):
    fast = tuple(mesh.shape[axis] for axis in ("dp", "tensor")) == (8, 4)
    dp, tensor = (AXES[:3], AXES[3:]) if fast else (("dp",), ("tensor",))
    both = dp + tensor
    rows = P(both, None)
    qkv = P(None, dp, tensor)
    out = P(tensor, dp)
    in_specs = (
        rows,
        rows,
        P(dp),
        P(dp, None),
        rows,
        qkv,
        out,
        qkv,
        out,
        P(dp, tensor),
        out,
        P(None, tensor + dp),
        P(tensor + dp),
        P(None, dp),
    )
    out_specs = (
        rows,
        rows,
        rows,
        qkv,
        out,
        qkv,
        out,
        P(dp, tensor),
        out,
        P(None, tensor + dp),
        P(tensor + dp),
        P(None, dp),
    )
    if fast:
        mesh = Mesh(mesh.devices.reshape(2, 2, 2, 2, 2), AXES)
    return jax.shard_map(
        fast_layer if fast else shards, mesh=mesh, in_specs=in_specs, out_specs=out_specs, check_vma=False
    )
```

```python
import functools
import math

import jax
import jax.numpy as jnp
from jax import lax
from jax.experimental import pallas as pl
from jax.experimental.pallas import tpu as pltpu
from jax.sharding import Mesh
from jax.sharding import PartitionSpec as P

HD = 64
PROMPT = 1024
CONT_TOK = 1024
ENC = 512
BLOCK = 256
PAIR = 2 * HD
AXES = ("y", "x", "core", "zhi", "zlo")


def lane_half():
    return lax.broadcasted_iota(jnp.int32, (1, PAIR), 1) < HD


def one_head(rows, head):
    keep = lane_half() if head == 0 else jnp.logical_not(lane_half())
    return rows * jnp.where(keep, 1.0, 0.0).astype(rows.dtype)


def dot_nt(left, right):
    return lax.dot_general(left, right, (((1,), (1,)), ((), ())), preferred_element_type=jnp.float32)


def dot_nn(left, right):
    return jnp.dot(left, right, preferred_element_type=jnp.float32)


def dot_tn(left, right):
    return lax.dot_general(left, right, (((0,), (0,)), ((), ())), preferred_element_type=jnp.float32)


def self_sections(meta_ref, segments):
    def at(block):
        return pl.multiple_of(meta_ref[block], 512)

    def place(index):
        return pl.multiple_of(meta_ref[index >> 1] + (index & 1) * BLOCK, BLOCK)

    def causal(row, col):
        return col <= row

    def banded(row, col):
        start = jnp.full(row.shape, meta_ref[4], jnp.int32)
        for segment in range(1, segments):
            bound = meta_ref[4 + segment]
            start = jnp.where(row >= bound, bound, start)
        return (col <= row) & (col >= start)

    def early(index):
        return [(at(0), 512, 0, causal)]

    def middle(index):
        return [(at(0), 512, 0, None), (at(1), 512, 512, causal)]

    def late(index):
        return [
            (at(0), 512, 0, None),
            (at(1), 512, 512, None),
            (place(index - 1), BLOCK, (index - 1) * BLOCK, banded),
            (place(index), BLOCK, index * BLOCK, banded),
        ]

    return place, ((0, 2, early), (2, 4, middle), (4, 8, late))


def cross_sections(meta_ref, blocks):
    def place(index):
        return pl.multiple_of(index * BLOCK, BLOCK)

    def usable(row, col):
        return col < meta_ref[0]

    def every(index):
        return [(0, ENC, 0, usable)]

    return place, ((0, blocks, every),)


def forward_kernel(sections, meta_ref, q_ref, k_ref, v_ref, o_ref, lse_ref):
    place, ranges = sections(meta_ref)

    for low, high, parts_of in ranges:

        def step(index, carry, parts_of=parts_of):
            rows = pl.ds(place(index), BLOCK)
            parts = parts_of(index)
            queries = q_ref[rows, :]
            row = index * BLOCK + lax.broadcasted_iota(jnp.int32, (BLOCK, 1), 0)
            allowed = [
                None if rule is None else rule(row, first + lax.broadcasted_iota(jnp.int32, (1, size), 1))
                for _, size, first, rule in parts
            ]
            outs, totals = [], []
            for head in range(2):
                query = one_head(queries, head)
                scores = []
                for (where, size, _, _), ok in zip(parts, allowed):
                    score = dot_nt(query, k_ref[pl.ds(where, size), :])
                    scores.append(score if ok is None else jnp.where(ok, score, -1e30))
                top = functools.reduce(jnp.maximum, [jnp.max(s, axis=1, keepdims=True) for s in scores])
                exps = [jnp.exp(s - top) for s in scores]
                total = sum(jnp.sum(e, axis=1, keepdims=True) for e in exps)
                mixed = sum(
                    dot_nn(e.astype(jnp.bfloat16), v_ref[pl.ds(where, size), :])
                    for (where, size, _, _), e in zip(parts, exps)
                )
                outs.append(mixed * (1.0 / total))
                totals.append(top + jnp.log(total))
            o_ref[rows, :] = jnp.where(lane_half(), outs[0], outs[1]).astype(o_ref.dtype)
            lse_ref[rows, :] = jnp.where(lane_half(), totals[0], totals[1])
            return carry

        lax.fori_loop(low, high, step, 0)


def backward_kernel(
    sections, meta_ref, q_ref, k_ref, v_ref, o_ref, do_ref, lse_ref, dq_ref, dk_ref, dv_ref, dk_sum, dv_sum
):
    place, ranges = sections(meta_ref)
    dk_sum[...] = jnp.zeros_like(dk_sum)
    dv_sum[...] = jnp.zeros_like(dv_sum)

    for low, high, parts_of in ranges:

        def step(index, carry, parts_of=parts_of):
            rows = pl.ds(place(index), BLOCK)
            parts = parts_of(index)
            queries, grads = q_ref[rows, :], do_ref[rows, :]
            row = index * BLOCK + lax.broadcasted_iota(jnp.int32, (1, BLOCK), 1)
            allowed = [
                None if rule is None else rule(row, first + lax.broadcasted_iota(jnp.int32, (size, 1), 0))
                for _, size, first, rule in parts
            ]
            logs = jnp.transpose(lse_ref[rows, :])
            spread = jnp.transpose(grads.astype(jnp.float32) * o_ref[rows, :].astype(jnp.float32))
            key_parts = [k_ref[pl.ds(where, size), :] for where, size, _, _ in parts]
            value_parts = [v_ref[pl.ds(where, size), :] for where, size, _, _ in parts]
            query_grads = []
            for head in range(2):
                query, grad = one_head(queries, head), one_head(grads, head)
                log = logs[head * HD : head * HD + 1, :]
                delta = jnp.sum(spread[head * HD : (head + 1) * HD, :], axis=0, keepdims=True)
                query_grad = None
                for (where, size, _, _), ok, keys, values in zip(parts, allowed, key_parts, value_parts):
                    score = dot_nt(keys, query)
                    if ok is not None:
                        score = jnp.where(ok, score, -1e30)
                    probs = jnp.exp(score - log)
                    score_grad = (probs * (dot_nt(values, grad) - delta)).astype(jnp.bfloat16)
                    dv_sum[pl.ds(where, size), :] += dot_nn(probs.astype(jnp.bfloat16), grad)
                    dk_sum[pl.ds(where, size), :] += dot_nn(score_grad, query)
                    term = dot_tn(score_grad, keys)
                    query_grad = term if query_grad is None else query_grad + term
                query_grads.append(query_grad)
            both = jnp.where(lane_half(), query_grads[0], query_grads[1])
            dq_ref[rows, :] = both.astype(jnp.bfloat16) * jnp.asarray(HD**-0.5, jnp.bfloat16)
            return carry

        lax.fori_loop(low, high, step, 0)
    dk_ref[...] = dk_sum[...].astype(dk_ref.dtype)
    dv_ref[...] = dv_sum[...].astype(dv_ref.dtype)


def columns(rows, first):
    return pl.BlockSpec((rows, PAIR), lambda pair, meta: (0, first + pair))


def attend(sections, meta, q, q_at, keys, k_at, v_at, pairs, weight):
    count, key_rows = q.shape[0], keys.shape[0]
    return pl.pallas_call(
        functools.partial(forward_kernel, sections),
        grid_spec=pltpu.PrefetchScalarGridSpec(
            num_scalar_prefetch=1,
            grid=(pairs,),
            in_specs=[columns(count, q_at), columns(key_rows, k_at), columns(key_rows, v_at)],
            out_specs=[columns(count, 0), columns(count, 0)],
        ),
        out_shape=[
            jax.ShapeDtypeStruct((count, pairs * PAIR), jnp.bfloat16),
            jax.ShapeDtypeStruct((count, pairs * PAIR), jnp.float32),
        ],
        cost_estimate=pl.CostEstimate(
            flops=2 * 4 * 4 * count * weight * pairs * PAIR,
            bytes_accessed=10 * count * pairs * PAIR,
            transcendentals=2 * pairs * count * weight,
        ),
    )(meta, q, keys, keys)


def attend_back(sections, meta, q, q_at, keys, k_at, v_at, out, out_grad, lse, pairs, weight):
    count, key_rows = q.shape[0], keys.shape[0]
    return pl.pallas_call(
        functools.partial(backward_kernel, sections),
        grid_spec=pltpu.PrefetchScalarGridSpec(
            num_scalar_prefetch=1,
            grid=(pairs,),
            in_specs=[
                columns(count, q_at),
                columns(key_rows, k_at),
                columns(key_rows, v_at),
                columns(count, 0),
                columns(count, 0),
                columns(count, 0),
            ],
            out_specs=[columns(count, 0), columns(key_rows, 0), columns(key_rows, 0)],
            scratch_shapes=[pltpu.VMEM((key_rows, PAIR), jnp.float32)] * 2,
        ),
        out_shape=[
            jax.ShapeDtypeStruct((count, pairs * PAIR), jnp.bfloat16),
            jax.ShapeDtypeStruct((key_rows, pairs * PAIR), jnp.bfloat16),
            jax.ShapeDtypeStruct((key_rows, pairs * PAIR), jnp.bfloat16),
        ],
        cost_estimate=pl.CostEstimate(
            flops=5 * 4 * 4 * count * weight * pairs * PAIR,
            bytes_accessed=20 * count * pairs * PAIR,
            transcendentals=2 * pairs * count * weight,
        ),
    )(meta, q, keys, keys, out, out_grad, lse)


EPSILON = 1e-05
MASKED = 1e30
GELU_C = math.sqrt(2.0 / math.pi)
GELU_A = 0.044715


def gelu_value(values):
    inner = jnp.tanh(GELU_C * (values + GELU_A * values * values * values))
    return 0.5 * values * (1.0 + inner)


def gelu_slope(values):
    inner = jnp.tanh(GELU_C * (values + GELU_A * values * values * values))
    return 0.5 * (1.0 + inner) + 0.5 * values * (1.0 - inner * inner) * GELU_C * (
        1.0 + 3.0 * GELU_A * values * values
    )


def norm_forward(values, gain_vec, shift_vec):
    row_mean = jnp.mean(values, axis=1, keepdims=True)
    centred = values - row_mean
    inverse = lax.rsqrt(jnp.mean(centred * centred, axis=1, keepdims=True) + EPSILON)
    normed = centred * inverse
    return (normed * gain_vec + shift_vec, normed, inverse)


def norm_backward(gradient, normed, inverse, gain_vec):
    scaled = gradient * gain_vec
    inner = (
        scaled
        - jnp.mean(scaled, axis=1, keepdims=True)
        - normed * jnp.mean(scaled * normed, axis=1, keepdims=True)
    )
    return (inner * inverse, jnp.sum(gradient * normed, axis=0), jnp.sum(gradient, axis=0))


def product(left, right):
    return jnp.dot(left, right, preferred_element_type=jnp.float32)


def product_left_t(left, right):
    return lax.dot_general(
        left, right, (((0,), (0,)), ((), ())), preferred_element_type=jnp.float32
    )


def product_right_t(left, right):
    return lax.dot_general(
        left, right, (((1,), (1,)), ((), ())), preferred_element_type=jnp.float32
    )


def attend_forward(queries, key_rows, value_rows, rule, block_rows):
    seq_rows, local_width = queries.shape
    local_heads = local_width // HD
    query_blocks = queries.reshape(seq_rows // block_rows, block_rows, local_heads, HD)
    key_heads = key_rows.reshape(-1, local_heads, HD)
    value_heads = value_rows.reshape(-1, local_heads, HD)
    block_starts = jnp.arange(seq_rows // block_rows, dtype=jnp.int32) * block_rows

    def attend_block(pieces):
        query_block, offset = pieces
        scores = jnp.einsum(
            "qhd,khd->hqk", query_block, key_heads, preferred_element_type=jnp.float32
        )
        scores = jnp.where(rule(offset, block_rows)[None], scores, -MASKED)
        row_max = jnp.max(scores, axis=2, keepdims=True)
        exponent = jnp.exp(scores - row_max)
        row_total = jnp.sum(exponent, axis=2, keepdims=True)
        probs_low = (exponent / row_total).astype(jnp.bfloat16)
        mixed = jnp.einsum(
            "hqk,khd->qhd", probs_low, value_heads, preferred_element_type=jnp.float32
        )
        return (
            mixed.astype(jnp.bfloat16).reshape(block_rows, local_width),
            (row_max + jnp.log(row_total))[:, :, 0],
        )

    outputs, log_total = lax.map(attend_block, (query_blocks, block_starts))
    return (outputs.reshape(seq_rows, local_width), log_total)


def attend_backward(queries, key_rows, value_rows, out_grad, log_total, rule, block_rows):
    seq_rows, local_width = queries.shape
    local_heads = local_width // HD
    key_count = key_rows.shape[0]
    query_blocks = queries.reshape(seq_rows // block_rows, block_rows, local_heads, HD)
    grad_blocks = out_grad.reshape(seq_rows // block_rows, block_rows, local_heads, HD)
    key_heads = key_rows.reshape(key_count, local_heads, HD)
    value_heads = value_rows.reshape(key_count, local_heads, HD)
    block_starts = jnp.arange(seq_rows // block_rows, dtype=jnp.int32) * block_rows

    def back_block(running, pieces):
        key_sum, value_sum = running
        query_block, grad_block, block_total, offset = pieces
        scores = jnp.einsum(
            "qhd,khd->hqk", query_block, key_heads, preferred_element_type=jnp.float32
        )
        probs = jnp.where(
            rule(offset, block_rows)[None], jnp.exp(scores - block_total[:, :, None]), 0.0
        )
        probs_low = probs.astype(jnp.bfloat16)
        prob_grad = jnp.einsum(
            "qhd,khd->hqk", grad_block, value_heads, preferred_element_type=jnp.float32
        )
        row_delta = jnp.sum(probs * prob_grad, axis=2, keepdims=True)
        score_grad = (probs * (prob_grad - row_delta)).astype(jnp.bfloat16)
        query_grad = jnp.einsum(
            "hqk,khd->qhd", score_grad, key_heads, preferred_element_type=jnp.float32
        )
        key_sum = key_sum + jnp.einsum(
            "hqk,qhd->khd", score_grad, query_block, preferred_element_type=jnp.float32
        )
        value_sum = value_sum + jnp.einsum(
            "hqk,qhd->khd", probs_low, grad_block, preferred_element_type=jnp.float32
        )
        return (
            (key_sum, value_sum),
            query_grad.astype(jnp.bfloat16).reshape(block_rows, local_width),
        )

    zero_sum = jnp.zeros((key_count, local_heads, HD), jnp.float32)
    (key_sum, value_sum), query_grads = lax.scan(
        back_block, (zero_sum, zero_sum), (query_blocks, grad_blocks, log_total, block_starts)
    )
    return (
        query_grads.reshape(seq_rows, local_width),
        key_sum.astype(jnp.bfloat16).reshape(key_count, local_width),
        value_sum.astype(jnp.bfloat16).reshape(key_count, local_width),
    )


def attend_groups(queries, key_rows, value_rows, rules, block_rows):
    results, totals = ([], [])
    for which_group, rule in enumerate(rules):
        mixed, log_total = attend_forward(queries, key_rows, value_rows, rule, block_rows)
        results.append(mixed)
        totals.append(log_total)
    return (results[0], totals)


def back_groups(queries, key_rows, value_rows, out_grad, totals, rules, block_rows):
    query_list, key_list, value_list = ([], [], [])
    for which_group, rule in enumerate(rules):
        query_grad, key_grad, value_grad = attend_backward(
            queries, key_rows, value_rows, out_grad, totals[which_group], rule, block_rows
        )
        query_list.append(query_grad)
        key_list.append(key_grad)
        value_list.append(value_grad)
    return (query_list[0], key_list[0], value_list[0])


def shards(
    tokens,
    enc_states,
    enc_len,
    cont_lengths,
    cotangent,
    self_qkv,
    self_out,
    cross_qkv,
    cross_out,
    ff_in,
    ff_out,
    head_bias,
    ff_bias,
    vec_params,
):
    gathered = (
        lax.all_gather(self_qkv, "dp", axis=1, tiled=True),
        lax.all_gather(self_out, "dp", axis=1, tiled=True),
        lax.all_gather(cross_qkv, "dp", axis=1, tiled=True),
        lax.all_gather(cross_out, "dp", axis=1, tiled=True),
        lax.all_gather(ff_in, "dp", axis=0, tiled=True),
        lax.all_gather(ff_out, "dp", axis=1, tiled=True),
        lax.all_gather(head_bias, "dp", axis=1, tiled=True),
        lax.all_gather(ff_bias, "dp", axis=0, tiled=True),
        lax.all_gather(vec_params, "dp", axis=1, tiled=True),
    )
    (
        w_self,
        w_self_out,
        w_cross,
        w_cross_out,
        w_hidden_in,
        w_hidden_out,
        bias_heads,
        bias_hidden,
        vectors,
    ) = gathered
    vectors = vectors.astype(jnp.float32)
    bias_heads = bias_heads.astype(jnp.float32)
    bias_hidden = bias_hidden.astype(jnp.float32)
    seq_rows = PROMPT + CONT_TOK
    block_rows = min(512, seq_rows)
    scaling = HD ** (-0.5)
    rows_dev = tokens.shape[0]

    def self_rule(which_group):
        bounds = PROMPT + jnp.cumsum(cont_lengths[which_group])
        positions = jnp.arange(seq_rows, dtype=jnp.int32)
        segment = jnp.sum((positions[:, None] >= bounds[None, :]).astype(jnp.int32), axis=1)

        def self_allowed(offset, number):
            row_ids = offset + jnp.arange(number, dtype=jnp.int32)
            row_segment = lax.dynamic_slice_in_dim(segment, offset, number)
            return (positions[None, :] <= row_ids[:, None]) & (
                (positions[None, :] < PROMPT) | (segment[None, :] == row_segment[:, None])
            )

        return self_allowed

    def cross_rule(which_group):
        usable = jnp.arange(ENC, dtype=jnp.int32) < enc_len[which_group]

        def cross_allowed(offset, number):
            return jnp.broadcast_to(usable[None, :], (number, ENC))

        return cross_allowed

    def spread(low_rows):
        return lax.all_gather(low_rows, "tensor", axis=0, tiled=True)

    def head_branch(values, weight):

        def term(offset, number):
            return product(values, weight)

        return lax.psum_scatter(
            term(jnp.int32(0), rows_dev * lax.axis_size("tensor")),
            "tensor",
            scatter_dimension=0,
            tiled=True,
        )

    def widen(low_rows):
        return lax.all_gather(low_rows, "tensor", axis=0, tiled=True)

    def narrow(term):
        return lax.psum_scatter(
            term(jnp.int32(0), rows_dev * lax.axis_size("tensor")),
            "tensor",
            scatter_dimension=0,
            tiled=True,
        )

    self_rules = [self_rule(0)]
    cross_rules = [cross_rule(0)]
    resid = tokens.astype(jnp.float32)
    enc_full = lax.all_gather(enc_states, "tensor", axis=0, tiled=True)
    normed_in, hat_one, inv_one = norm_forward(resid, vectors[0], vectors[3])
    attn_low = normed_in.astype(jnp.bfloat16)
    attn_full = spread(attn_low)
    queries = ((product(attn_full, w_self[0]) + bias_heads[0]) * scaling).astype(jnp.bfloat16)
    key_rows = product(attn_full, w_self[1]).astype(jnp.bfloat16)
    value_rows = (product(attn_full, w_self[2]) + bias_heads[1]).astype(jnp.bfloat16)
    mixed, self_totals = attend_groups(queries, key_rows, value_rows, self_rules, block_rows)
    after_one = resid + (head_branch(mixed, w_self_out) + vectors[6])
    normed_mid, hat_two, inv_two = norm_forward(after_one, vectors[1], vectors[4])
    cross_low = normed_mid.astype(jnp.bfloat16)
    cross_full = spread(cross_low)
    cross_queries = ((product(cross_full, w_cross[0]) + bias_heads[2]) * scaling).astype(
        jnp.bfloat16
    )
    cross_keys = product(enc_full, w_cross[1]).astype(jnp.bfloat16)
    cross_values = (product(enc_full, w_cross[2]) + bias_heads[3]).astype(jnp.bfloat16)
    cross_mixed, cross_totals = attend_groups(
        cross_queries, cross_keys, cross_values, cross_rules, block_rows
    )
    after_two = after_one + (head_branch(cross_mixed, w_cross_out) + vectors[7])
    normed_out, hat_three, inv_three = norm_forward(after_two, vectors[2], vectors[5])
    hidden_low = normed_out.astype(jnp.bfloat16)
    hidden_full = spread(hidden_low)
    pre_act = product(hidden_full, w_hidden_in) + bias_hidden
    activation = gelu_value(pre_act).astype(jnp.bfloat16)

    def term(offset, number):
        return product(activation, w_hidden_out)

    after_three = after_two + (
        lax.psum_scatter(
            term(jnp.int32(0), rows_dev * lax.axis_size("tensor")),
            "tensor",
            scatter_dimension=0,
            tiled=True,
        )
        + vectors[8]
    )
    layer_out = after_three.astype(jnp.bfloat16)
    gradient = cotangent.astype(jnp.float32)
    grad_low = gradient.astype(jnp.bfloat16)
    bias_out_three = jnp.sum(grad_low.astype(jnp.float32), axis=0)
    grad_full = widen(grad_low)
    act_grad = (product_right_t(grad_full, w_hidden_out) * gelu_slope(pre_act)).astype(jnp.bfloat16)
    grad_hidden_out = product_left_t(activation, grad_full)
    grad_hidden_in = product_left_t(hidden_full, act_grad)
    grad_bias_hidden = jnp.sum(act_grad.astype(jnp.float32), axis=0)

    def hidden_term(offset, number):
        return product_right_t(act_grad, w_hidden_in)

    input_part, gain_three, shift_three = norm_backward(
        narrow(hidden_term), hat_three, inv_three, vectors[2]
    )
    gradient = gradient + input_part
    grad_low = gradient.astype(jnp.bfloat16)
    bias_out_two = jnp.sum(grad_low.astype(jnp.float32), axis=0)
    grad_full = widen(grad_low)
    grad_cross_out = product_left_t(cross_mixed, grad_full)
    mixed_grad = product_right_t(grad_full, w_cross_out).astype(jnp.bfloat16)
    cross_query_grad, cross_key_grad, cross_value_grad = back_groups(
        cross_queries, cross_keys, cross_values, mixed_grad, cross_totals, cross_rules, block_rows
    )
    grad_cross = jnp.stack(
        [
            product_left_t(cross_full, cross_query_grad) * scaling,
            product_left_t(enc_full, cross_key_grad),
            product_left_t(enc_full, cross_value_grad),
        ]
    )
    bias_cross_query = jnp.sum(cross_query_grad.astype(jnp.float32), axis=0) * scaling
    bias_cross_value = jnp.sum(cross_value_grad.astype(jnp.float32), axis=0)
    enc_grad = lax.psum_scatter(
        product_right_t(cross_key_grad, w_cross[1]) + product_right_t(cross_value_grad, w_cross[2]),
        "tensor",
        scatter_dimension=0,
        tiled=True,
    )

    def cross_term(offset, number):
        return product_right_t(cross_query_grad, w_cross[0]) * scaling

    input_part, gain_two, shift_two = norm_backward(
        narrow(cross_term), hat_two, inv_two, vectors[1]
    )
    gradient = gradient + input_part
    grad_low = gradient.astype(jnp.bfloat16)
    bias_out_one = jnp.sum(grad_low.astype(jnp.float32), axis=0)
    grad_full = widen(grad_low)
    grad_self_out = product_left_t(mixed, grad_full)
    self_mixed_grad = product_right_t(grad_full, w_self_out).astype(jnp.bfloat16)
    query_grad, key_grad, value_grad = back_groups(
        queries, key_rows, value_rows, self_mixed_grad, self_totals, self_rules, block_rows
    )
    grad_self = jnp.stack(
        [
            product_left_t(attn_full, query_grad) * scaling,
            product_left_t(attn_full, key_grad),
            product_left_t(attn_full, value_grad),
        ]
    )
    bias_self_query = jnp.sum(query_grad.astype(jnp.float32), axis=0) * scaling
    bias_self_value = jnp.sum(value_grad.astype(jnp.float32), axis=0)

    def self_term(offset, number):
        return (
            product_right_t(query_grad, w_self[0]) * scaling
            + product_right_t(key_grad, w_self[1])
            + product_right_t(value_grad, w_self[2])
        )

    input_part, gain_one, shift_one = norm_backward(narrow(self_term), hat_one, inv_one, vectors[0])
    input_grad = gradient + input_part
    vector_grads = jnp.stack(
        [
            gain_one,
            gain_two,
            gain_three,
            shift_one,
            shift_two,
            shift_three,
            bias_out_one,
            bias_out_two,
            bias_out_three,
        ]
    )
    head_grads = jnp.stack([bias_self_query, bias_self_value, bias_cross_query, bias_cross_value])
    results = (
        lax.psum_scatter(grad_self, "dp", scatter_dimension=1, tiled=True),
        lax.psum_scatter(grad_self_out, "dp", scatter_dimension=1, tiled=True),
        lax.psum_scatter(grad_cross, "dp", scatter_dimension=1, tiled=True),
        lax.psum_scatter(grad_cross_out, "dp", scatter_dimension=1, tiled=True),
        lax.psum_scatter(grad_hidden_in, "dp", scatter_dimension=0, tiled=True),
        lax.psum_scatter(grad_hidden_out, "dp", scatter_dimension=1, tiled=True),
        lax.psum_scatter(head_grads, "dp", scatter_dimension=1, tiled=True),
        lax.psum_scatter(grad_bias_hidden, "dp", scatter_dimension=0, tiled=True),
        lax.psum_scatter(vector_grads, "dp", scatter_dimension=1, tiled=True),
    )
    vector_total = lax.psum(results[8], "tensor")
    return (
        layer_out,
        input_grad,
        enc_grad,
        results[0],
        results[1],
        results[2],
        results[3],
        results[4],
        results[5],
        results[6],
        results[7],
        vector_total,
    )


def hidden_kernel(x_ref, e_ref, w_in_ref, w_out_ref, bias_ref, act_ref, grad_ref, sum_ref):
    chunk = 256
    sum_ref[...] = jnp.zeros_like(sum_ref)

    def step(index, carry):
        rows = pl.ds(pl.multiple_of(index * chunk, chunk), chunk)
        value = dot_nn(x_ref[rows, :], w_in_ref[...]) + bias_ref[...]
        upper = dot_nn(e_ref[rows, :], w_out_ref[...])
        square = value * value
        inner = jnp.tanh(value * (GELU_C + (GELU_C * GELU_A) * square))
        half = 0.5 + 0.5 * inner
        act_ref[rows, :] = (value * half).astype(act_ref.dtype)
        slope = half + (value * (half * (1.0 - inner))) * (GELU_C + (3.0 * GELU_C * GELU_A) * square)
        grad = (upper * slope).astype(grad_ref.dtype)
        grad_ref[rows, :] = grad
        sum_ref[...] += jnp.sum(grad.astype(jnp.float32), axis=0, keepdims=True)
        return carry

    lax.fori_loop(0, x_ref.shape[0] // chunk, step, 0, unroll=2)


def hidden_units(rows, grads, w_in, w_out, bias, tile=512):
    count, model = rows.shape
    width = w_in.shape[1]
    whole = pl.BlockSpec((count, model), lambda i: (0, 0))
    weight = pl.BlockSpec((model, tile), lambda i: (0, i))
    line = pl.BlockSpec((1, tile), lambda i: (0, i))
    out = pl.BlockSpec((count, tile), lambda i: (0, i))
    return pl.pallas_call(
        hidden_kernel,
        grid=(width // tile,),
        in_specs=[whole, whole, weight, weight, line],
        out_specs=[out, out, line],
        out_shape=[
            jax.ShapeDtypeStruct((count, width), jnp.bfloat16),
            jax.ShapeDtypeStruct((count, width), jnp.bfloat16),
            jax.ShapeDtypeStruct((1, width), jnp.float32),
        ],
        cost_estimate=pl.CostEstimate(
            flops=4 * count * model * width,
            bytes_accessed=4 * (count * model + model * width + count * width),
            transcendentals=count * width,
        ),
    )(rows, grads, w_in, w_out, bias)


MESH = pl.DeviceIdType.MESH
LINKS = ("core", "x", "y", "zhi", "zlo")


def start_kernel(
    tokens,
    enc,
    w_self,
    w_cross,
    w_in,
    w_out,
    small,
    token_rows,
    attn,
    g_self,
    g_cross,
    hidden,
    enc_full,
    small_all,
    held,
    normed,
    gathered,
    send,
    recv,
    local,
):
    y, x, core, zhi, zlo = (lax.axis_index(axis) for axis in AXES)
    crossing = core != zhi
    rows = tokens.shape[0]
    part = w_self.shape[1]
    counts = {"sent": 0, "local": 0}

    def push(source, target, axis):
        index = counts["sent"]
        counts["sent"] += 1
        copy = pltpu.make_async_remote_copy(
            src_ref=source,
            dst_ref=target,
            send_sem=send.at[index],
            recv_sem=recv.at[index],
            device_id={axis: 1 - lax.axis_index(axis)},
            device_id_type=MESH,
        )
        copy.start()
        return copy

    def keep(source, target):
        index = counts["local"]
        counts["local"] += 1
        copy = pltpu.make_async_copy(source, target, local.at[index])
        copy.start()
        return copy

    def moving(source, target, source_here, target_here):
        index, index_here = counts["sent"], counts["local"]
        counts["sent"] += 1
        counts["local"] += 1

        def remote():
            return pltpu.make_async_remote_copy(
                src_ref=source,
                dst_ref=target,
                send_sem=send.at[index],
                recv_sem=recv.at[index],
                device_id={"core": zhi, "zhi": core},
                device_id_type=MESH,
            )

        def here():
            return pltpu.make_async_copy(source_here, target_here, local.at[index_here])

        @pl.when(crossing)
        def _():
            remote().start()

        @pl.when(jnp.logical_not(crossing))
        def _():
            here().start()

        def wait():
            @pl.when(crossing)
            def _():
                remote().wait()

            @pl.when(jnp.logical_not(crossing))
            def _():
                here().wait()

        return wait

    def lanes(block, size):
        return pl.ds(pl.multiple_of(block * size, size), size)

    barrier = pltpu.get_barrier_semaphore()
    for axis in LINKS:
        pl.semaphore_signal(barrier, inc=1, device_id={axis: 1 - lax.axis_index(axis)}, device_id_type=MESH)

    @pl.when(crossing)
    def _():
        pl.semaphore_signal(barrier, inc=1, device_id={"core": zhi, "zhi": core}, device_id_type=MESH)

    pl.semaphore_wait(barrier, len(LINKS) + crossing.astype(jnp.int32))

    wait_tokens = moving(tokens, held, tokens, held)
    own_small = keep(small, gathered.at[y, x, core, zhi, zlo])
    own_rows = pl.ds(pl.multiple_of(core * part, part), part)
    quarter = 2 * zhi + zlo

    def from_shard(shard, target, block, size):
        own = keep(shard.at[:, :, lanes(core, size)], target.at[:, y, x, own_rows, lanes(block, size)])
        other = push(
            shard.at[:, :, lanes(1 - core, size)], target.at[:, y, x, own_rows, lanes(block, size)], "core"
        )
        return own, other

    self_width = w_self.shape[2] // 2
    hidden_width = w_in.shape[1] // 2
    cross_core = from_shard(w_cross, g_cross, quarter, self_width)
    own_small.wait()
    small_core = push(gathered.at[y, x, core, zhi, zlo], gathered.at[y, x, core, zhi, zlo], "core")
    self_core = from_shard(w_self, g_self, zhi, self_width)
    hidden_core = []
    for plane, shard in enumerate((w_in, w_out)):
        target = hidden.at[plane, own_rows, lanes(zhi, hidden_width)]
        hidden_core.append(keep(shard.at[:, lanes(core, hidden_width)], target))
        hidden_core.append(push(shard.at[:, lanes(1 - core, hidden_width)], target, "core"))
    for copy in cross_core:
        copy.wait()
    region = g_cross.at[:, y, x, :, lanes(quarter, self_width)]
    cross_zlo = push(region, region, "zlo")
    small_core.wait()
    region = gathered.at[y, x, :, zhi, zlo]
    small_x = push(region, region, "x")
    for copy in self_core:
        copy.wait()
    small_x.wait()
    region = gathered.at[y, :, :, zhi, zlo]
    small_y = push(region, region, "y")
    cross_zlo.wait()
    small_y.wait()

    def over_plane(target, width):
        first, second = pl.ds(0, width), pl.ds(width, width)
        region_a, region_b = target.at[:, y, x, :, first], target.at[:, y, x, :, second]
        steps = (push(region_a, region_a, "x"), push(region_b, region_b, "y"))

        def second_steps():
            steps[0].wait()
            region_a = target.at[:, y, :, :, first]
            step_a = push(region_a, region_a, "y")
            steps[1].wait()
            region_b = target.at[:, :, x, :, second]
            return step_a, push(region_b, region_b, "x")

        return second_steps

    wait_tokens()
    keep_tokens = keep(held, token_rows)
    region = gathered.at[:, :, :, zhi, zlo]
    small_zhi = push(region, region, "zhi")
    region = g_self.at[:, y, x, :, lanes(zhi, self_width)]
    self_zhi = push(region, region, "zhi")
    gain = jnp.concatenate([gathered[d // 4, d // 2 % 2, d % 2, zhi, zlo, 0:1, :] for d in range(8)], axis=1)
    shift = jnp.concatenate([gathered[d // 4, d // 2 % 2, d % 2, zhi, zlo, 3:4, :] for d in range(8)], axis=1)

    def norm_step(step, carry):
        block = pl.ds(pl.multiple_of(step * 64, 64), 64)
        values = held[block, :].astype(jnp.float32)
        centred = values - jnp.mean(values, axis=1, keepdims=True)
        inverse = lax.rsqrt(jnp.mean(centred * centred, axis=1, keepdims=True) + EPSILON)
        normed[block, :] = (centred * inverse * gain + shift).astype(normed.dtype)
        return carry

    lax.fori_loop(0, rows // 64, norm_step, 0)
    attn_zlo = push(normed, attn.at[pl.ds(2 * rows, rows)], "zlo")
    attn_core = push(normed, attn.at[pl.ds(rows, rows)], "core")
    attn_own = keep(normed, attn.at[pl.ds(0, rows)])

    self_zhi.wait()
    region = g_cross.at[:, y, x, :, lanes(zhi, 2 * self_width)]
    cross_zhi = push(region, region, "zhi")
    self_second = over_plane(g_self, self_width)
    self_last = self_second()
    small_zhi.wait()
    region = gathered.at[:, :, :, :, zlo]
    small_zlo = push(region, region, "zlo")
    for copy in hidden_core:
        copy.wait()
    cross_zhi.wait()
    region = hidden.at[0, :, lanes(zhi, hidden_width)]
    hidden_zhi = push(region, region, "zhi")
    wait_enc = moving(enc, enc_full.at[2 * zhi + zlo], enc, enc_full.at[2 * core + zlo])
    cross_second = over_plane(g_cross, 2 * self_width)
    attn_zlo.wait()
    attn_diagonal = push(attn.at[pl.ds(2 * rows, rows)], attn.at[pl.ds(3 * rows, rows)], "core")
    cross_last = cross_second()
    wait_enc()
    region = enc_full.at[2 * core + zlo]
    enc_zlo = push(region, region, "zlo")
    enc_core = push(region, region, "core")
    enc_zlo.wait()
    region = enc_full.at[2 * core + 1 - zlo]
    enc_diagonal = push(region, region, "core")
    small_zlo.wait()
    keep_small = keep(gathered, small_all)
    for copy in (
        *self_last,
        *cross_last,
        hidden_zhi,
        attn_core,
        attn_diagonal,
        enc_core,
        enc_diagonal,
        attn_own,
        keep_tokens,
        keep_small,
    ):
        copy.wait()


def start_exchange(tokens, enc, w_self, w_cross, w_in, w_out, small):
    rows, model = tokens.shape
    part = w_self.shape[1]
    low_type = tokens.dtype
    shapes = [
        jax.ShapeDtypeStruct((rows, model), low_type),
        jax.ShapeDtypeStruct((4 * rows, model), low_type),
        jax.ShapeDtypeStruct((4, 2, 2, 2 * part, w_self.shape[2]), low_type),
        jax.ShapeDtypeStruct((4, 2, 2, 2 * part, 2 * w_cross.shape[2]), low_type),
        jax.ShapeDtypeStruct((2, 2 * part, w_in.shape[1]), low_type),
        jax.ShapeDtypeStruct((4, enc.shape[0], model), low_type),
        jax.ShapeDtypeStruct((2,) * 5 + small.shape, small.dtype),
    ]
    anywhere = pl.BlockSpec(memory_space=pl.ANY)
    return pl.pallas_call(
        start_kernel,
        out_shape=shapes,
        in_specs=[anywhere] * 7,
        out_specs=[anywhere] * len(shapes),
        scratch_shapes=[
            pltpu.VMEM((rows, model), low_type),
            pltpu.VMEM((rows, model), low_type),
            pltpu.VMEM((2,) * 5 + small.shape, small.dtype),
            pltpu.SemaphoreType.DMA((30,)),
            pltpu.SemaphoreType.DMA((30,)),
            pltpu.SemaphoreType.DMA((12,)),
        ],
        compiler_params=pltpu.CompilerParams(collective_id=0, has_side_effects=True),
    )(tokens, enc, w_self, w_cross, w_in, w_out, small)


def finish_kernel(
    ff_in,
    ff_out,
    cross,
    self_q,
    self_k,
    self_v,
    self_o,
    enc_part,
    small,
    ff_in_out,
    ff_out_out,
    cross_qkv_out,
    cross_out_out,
    self_qkv_out,
    self_out_out,
    enc_out,
    small_out,
    cross_own,
    cross_got,
    cross_low,
    cross_got_low,
    cross_total,
    enc_own,
    enc_got,
    enc_sum,
    enc_far,
    enc_low,
    self_own,
    self_got,
    low_a,
    low_b,
    self_got_low,
    self_total,
    self_last,
    small_sum,
    small_got_0,
    small_got_1,
    small_got_2,
    small_got_3,
    small_got_4,
    send,
    recv,
    local,
):
    y, x, core, zhi, zlo = (lax.axis_index(axis) for axis in AXES)
    crossing = core != zhi
    small_got = (small_got_0, small_got_1, small_got_2, small_got_3, small_got_4)
    counts = {"sent": 0, "local": 0}

    def push(source, target, axis):
        index = counts["sent"]
        counts["sent"] += 1
        copy = pltpu.make_async_remote_copy(
            src_ref=source,
            dst_ref=target,
            send_sem=send.at[index],
            recv_sem=recv.at[index],
            device_id={axis: 1 - lax.axis_index(axis)},
            device_id_type=MESH,
        )
        copy.start()
        return copy

    def keep(source, target):
        index = counts["local"]
        counts["local"] += 1
        copy = pltpu.make_async_copy(source, target, local.at[index])
        copy.start()
        return copy

    def moving(source, target, source_here, target_here):
        index, index_here = counts["sent"], counts["local"]
        counts["sent"] += 1
        counts["local"] += 1

        def remote():
            return pltpu.make_async_remote_copy(
                src_ref=source,
                dst_ref=target,
                send_sem=send.at[index],
                recv_sem=recv.at[index],
                device_id={"core": zhi, "zhi": core},
                device_id_type=MESH,
            )

        def here():
            return pltpu.make_async_copy(source_here, target_here, local.at[index_here])

        @pl.when(crossing)
        def _():
            remote().start()

        @pl.when(jnp.logical_not(crossing))
        def _():
            here().start()

        def wait():
            @pl.when(crossing)
            def _():
                remote().wait()

            @pl.when(jnp.logical_not(crossing))
            def _():
                here().wait()

        return wait

    def lanes(block, size):
        return pl.ds(pl.multiple_of(block * size, size), size)

    def add(target, *terms):
        def step(index, carry):
            rows = pl.ds(pl.multiple_of(index * 64, 64), 64)
            value = sum(term[rows, :].astype(jnp.float32) for term in terms)
            target[rows, :] = value.astype(target.dtype)
            return carry

        lax.fori_loop(0, target.shape[0] // 64, step, 0)

    barrier = pltpu.get_barrier_semaphore()
    for axis in LINKS:
        pl.semaphore_signal(barrier, inc=1, device_id={axis: 1 - lax.axis_index(axis)}, device_id_type=MESH)

    @pl.when(crossing)
    def _():
        pl.semaphore_signal(barrier, inc=1, device_id={"core": zhi, "zhi": core}, device_id_type=MESH)

    pl.semaphore_wait(barrier, len(LINKS) + crossing.astype(jnp.int32))

    last = []
    half = self_q.shape[3] // 2

    def to_cores(values, out):
        part, width = values.shape[0] // 2, values.shape[1]
        there, here = lanes(1 - core, part), lanes(core, part)
        last.append(push(values.at[there], out.at[:, lanes(core, width)], "core"))
        last.append(keep(values.at[here], out.at[:, lanes(core, width)]))

    def planes_to_cores(values, qkv_out, out_out):
        part = values.shape[0] // 2
        there, here = lanes(1 - core, part), lanes(core, part)
        for plane in range(4):
            columns_of = pl.ds(plane * half, half)
            out = qkv_out.at[plane, :, lanes(core, half)] if plane < 3 else out_out.at[:, lanes(core, half)]
            last.append(push(values.at[there, columns_of], out, "core"))
            last.append(keep(values.at[here, columns_of], out))

    cross_zhi, cross_keep = [], []
    for plane in range(4):
        columns_of = pl.ds(plane * 2 * half, 2 * half)
        there = pl.ds(pl.multiple_of((2 * plane + 1 - zhi) * 2 * half, 2 * half), 2 * half)
        here = pl.ds(pl.multiple_of((2 * plane + zhi) * 2 * half, 2 * half), 2 * half)
        cross_zhi.append(push(cross.at[:, there], cross_got.at[:, columns_of], "zhi"))
        cross_keep.append(keep(cross.at[:, here], cross_own.at[:, columns_of]))

    first, second = pl.ds(0, half), pl.ds(half, half)
    parts = (self_q, self_k, self_v, self_o)
    self_x, self_y, own_a, own_b = [], [], [], []
    for plane, partial in enumerate(parts):
        columns_of = pl.ds(plane * half, half)
        self_x.append(push(partial.at[:, 1 - x, :, first], self_got.at[0, :, :, columns_of], "x"))
        self_y.append(push(partial.at[1 - y, :, :, second], self_got.at[1, :, :, columns_of], "y"))
        own_a.append(keep(partial.at[:, x, :, first], self_own.at[0, :, :, columns_of]))
        own_b.append(keep(partial.at[y, :, :, second], self_own.at[1, :, :, columns_of]))
    enc_core = push(enc_part.at[1 - core], enc_got, "core")
    enc_keep = keep(enc_part.at[core], enc_own)

    to_cores(ff_in, ff_in_out)
    to_cores(ff_out, ff_out_out)

    small_first, small_size = 0, 32

    def small_send(stage):
        rows = small_size // 2
        away = small_first + (1 - lax.axis_index(AXES[stage])) * rows
        return push(small_sum.at[pl.ds(away, rows)], small_got[stage], AXES[stage])

    def small_add(stage, copy):
        copy.wait()
        rows, got = small_size // 2, small_got[stage]
        mine = small_first + lax.axis_index(AXES[stage]) * rows

        def step(index, carry):
            small_sum[mine + index] += got[index]
            return carry

        lax.fori_loop(0, rows, step, 0)
        return mine, rows

    keep(small, small_sum).wait()
    small_copy = small_send(0)
    enc_core.wait()
    enc_keep.wait()
    add(enc_sum, enc_own.at[1 - zlo], enc_got.at[1 - zlo])
    enc_zlo = push(enc_sum, enc_far, "zlo")
    small_first, small_size = small_add(0, small_copy)
    small_copy = small_send(1)
    for copy in own_a + self_x:
        copy.wait()
    add(low_a, self_own.at[0, 1 - y], self_got.at[0, 1 - y])
    a_second = push(low_a, self_got_low.at[0], "y")
    for copy in own_b + self_y:
        copy.wait()
    add(low_b, self_own.at[1, 1 - x], self_got.at[1, 1 - x])
    b_second = push(low_b, self_got_low.at[1], "x")
    small_first, small_size = small_add(1, small_copy)
    small_copy = small_send(2)
    add(self_total.at[0], self_own.at[0, y], self_got.at[0, y])
    add(self_total.at[1], self_own.at[1, x], self_got.at[1, x])
    enc_zlo.wait()
    add(enc_low, enc_own.at[zlo], enc_got.at[zlo], enc_far)
    small_first, small_size = small_add(2, small_copy)
    small_copy = small_send(3)
    a_second.wait()
    add(self_total.at[0], self_total.at[0], self_got_low.at[0])
    b_second.wait()
    add(self_total.at[1], self_total.at[1], self_got_low.at[1])
    add(low_a, self_total.at[1 - zhi])
    self_zhi = push(low_a, self_last, "zhi")
    for copy in cross_zhi + cross_keep:
        copy.wait()

    def cross_step(target, which, *others):
        def step(index, carry):
            rows = pl.ds(pl.multiple_of(index * 64, 64), 64)
            for plane in range(4):
                source = pl.ds(pl.multiple_of((2 * plane + which) * half, half), half)
                columns_of = pl.ds(plane * half, half)
                value = cross_own[rows, source].astype(jnp.float32) + cross_got[rows, source].astype(jnp.float32)
                for other in others:
                    value += other[rows, columns_of].astype(jnp.float32)
                target[rows, columns_of] = value.astype(target.dtype)
            return carry

        lax.fori_loop(0, target.shape[0] // 64, step, 0)

    cross_step(cross_low, 1 - zlo)
    cross_zlo = push(cross_low, cross_got_low, "zlo")
    wait_enc = moving(enc_low, enc_out, enc_low, enc_out)
    cross_zlo.wait()
    cross_step(cross_total, zlo, cross_got_low)
    planes_to_cores(cross_total, cross_qkv_out, cross_out_out)
    small_first, small_size = small_add(3, small_copy)
    small_copy = small_send(4)
    self_zhi.wait()
    add(self_total.at[zhi], self_total.at[zhi], self_last)
    planes_to_cores(self_total.at[zhi], self_qkv_out, self_out_out)
    small_first, small_size = small_add(4, small_copy)
    keep(small_sum.at[small_first], small_out).wait()
    wait_enc()
    for copy in last:
        copy.wait()


def finish(ff_in, ff_out, cross, self_parts, enc, small):
    rows, width = ff_in.shape
    part, half = self_parts[0].shape[2], self_parts[0].shape[3] // 2
    low_type, enc_shape = enc.dtype, enc.shape[2:]
    wide = 4 * half

    def full(*shape):
        return jax.ShapeDtypeStruct(shape, jnp.float32)

    shapes = [
        full(rows // 2, 2 * width),
        full(rows // 2, 2 * width),
        full(3, part // 2, 2 * half),
        full(part // 2, 2 * half),
        full(3, part // 2, 2 * half),
        full(part // 2, 2 * half),
        jax.ShapeDtypeStruct(enc_shape, low_type),
        jax.ShapeDtypeStruct(small.shape[1:], small.dtype),
    ]
    anywhere = pl.BlockSpec(memory_space=pl.ANY)
    return pl.pallas_call(
        finish_kernel,
        out_shape=shapes,
        in_specs=[anywhere] * 9,
        out_specs=[anywhere] * len(shapes),
        scratch_shapes=[
            pltpu.VMEM((part, 2 * wide), low_type),
            pltpu.VMEM((part, 2 * wide), low_type),
            pltpu.VMEM((part, wide), low_type),
            pltpu.VMEM((part, wide), low_type),
            pltpu.VMEM((part, wide), jnp.float32),
            pltpu.VMEM((2, *enc_shape), low_type),
            pltpu.VMEM((2, *enc_shape), low_type),
            pltpu.VMEM(enc_shape, low_type),
            pltpu.VMEM(enc_shape, low_type),
            pltpu.VMEM(enc_shape, low_type),
            pltpu.VMEM((2, 2, part, wide), low_type),
            pltpu.VMEM((2, 2, part, wide), low_type),
            pltpu.VMEM((part, wide), low_type),
            pltpu.VMEM((part, wide), low_type),
            pltpu.VMEM((2, part, wide), low_type),
            pltpu.VMEM((2, part, wide), jnp.float32),
            pltpu.VMEM((part, wide), low_type),
            pltpu.VMEM(small.shape, small.dtype),
        ]
        + [pltpu.VMEM((32 >> stage, *small.shape[1:]), small.dtype) for stage in range(1, 6)]
        + [pltpu.SemaphoreType.DMA((40,))] * 3,
        compiler_params=pltpu.CompilerParams(collective_id=1, has_side_effects=True),
        cost_estimate=pl.CostEstimate(flops=40_000_000_000, bytes_accessed=0, transcendentals=0),
    )(ff_in, ff_out, cross, *self_parts, enc, small)


def trade(rows, axis, name="trade"):
    with jax.named_scope(name):
        return lax.ppermute(rows, axis, [(0, 1), (1, 0)])


def after(value, *others):
    return lax.optimization_barrier((value, *others))[0]


def regroup(rows, name="regroup"):
    with jax.named_scope("re_" + name):
        moved = lax.ppermute(rows, ("core", "zhi"), [(1, 2), (2, 1)])
        return jnp.where(lax.axis_index("core") == lax.axis_index("zhi"), rows, moved)


def in_order(index, own, other, axis):
    return jnp.concatenate(
        [jnp.where(index == 0, own, other), jnp.where(index == 0, other, own)], axis=axis
    )


def low(values):
    return values.astype(jnp.bfloat16)


def half_of(values, index, axis):
    size = values.shape[axis] // 2
    return lax.dynamic_slice_in_dim(values, index * size, size, axis)


def over_chips(rows):
    return lax.all_gather(rows, ("y", "x"), axis=0, tiled=True)


def sum_over_chips(partial):
    return lax.psum_scatter(partial, ("y", "x"), scatter_dimension=0, tiled=True)


def spread_rows(rows, name):
    beyond = trade(rows, "zlo", name + "_z")
    return (
        jnp.concatenate([rows, trade(rows, "core", name + "_c")], axis=0),
        jnp.concatenate([beyond, trade(beyond, "core", name + "_zc")], axis=0),
    )


def sum_rows(near, far, term, name):
    size = near.shape[0] // 2
    far_sum = term(far[:size]) + trade(low(term(far[size:])), "core", name + "_zc")
    from_far = trade(low(far_sum), "zlo", name + "_z")
    near_other = trade(low(term(near[size:])), "core", name + "_c")
    return term(near[:size]) + near_other + from_far


def fast_layer(
    tokens,
    enc_states,
    enc_len,
    cont_lengths,
    cotangent,
    self_qkv,
    self_out,
    cross_qkv,
    cross_out,
    ff_in,
    ff_out,
    head_bias,
    ff_bias,
    vec_params,
):
    core, zhi, zlo = lax.axis_index("core"), lax.axis_index("zhi"), lax.axis_index("zlo")
    scaling = HD**-0.5
    model = tokens.shape[1]
    segments = cont_lengths.shape[1]

    flat = jnp.concatenate([vec_params.reshape(-1), head_bias.reshape(-1), ff_bias]).astype(jnp.float32)
    sizes = (vec_params.size, head_bias.size, ff_bias.size)
    flat = jnp.pad(flat.reshape(-1, 128), ((0, 4), (0, 0)))
    token_rows, attn_rows, w_self, w_cross, w_hidden, enc_full, small = start_exchange(
        tokens,
        enc_states,
        jnp.concatenate([self_qkv, self_out.T[None]], axis=0),
        jnp.concatenate([cross_qkv, cross_out.T[None]], axis=0),
        ff_in,
        ff_out.T,
        flat,
    )
    w_self, w_cross = w_self.reshape(4, model, -1), w_cross.reshape(4, model, -1)
    w_in = over_chips(w_hidden[0])
    out_own = half_of(w_hidden[1], zhi, 1)
    out_beyond = trade(out_own, "zhi", "wo_zhi")
    w_qkv, w_so = jnp.concatenate([w_self[0], w_self[1], w_self[2]], axis=1), w_self[3]
    w_cq, w_ckv, w_co = w_cross[0], jnp.concatenate([w_cross[1], w_cross[2]], axis=1), w_cross[3]
    rows_of = model // 4
    width, cross_width = w_self.shape[2], w_cross.shape[2]
    pairs, cross_pairs = width // PAIR, cross_width // PAIR
    enc_full = enc_full.reshape(-1, model)
    attn_near, attn_far = attn_rows[: attn_rows.shape[0] // 2], attn_rows[attn_rows.shape[0] // 2 :]
    small = small.reshape(8, 4, -1)
    vec_part, head_part, ff_part = jnp.split(
        small[:, :, : sum(sizes)], [sizes[0], sizes[0] + sizes[1]], axis=2
    )
    vectors = vec_part[:, 0].reshape(8, 9, -1).transpose(1, 0, 2).reshape(9, model)
    heads = head_part.reshape(8, 4, 4, -1).transpose(2, 1, 0, 3).reshape(4, 2, 2, 2, -1)
    self_bias = lax.dynamic_index_in_dim(
        lax.dynamic_index_in_dim(heads[:2], zlo, 2, False), core, 2, False
    ).reshape(2, -1)
    cross_bias = lax.dynamic_index_in_dim(heads[2:], core, 3, False).reshape(2, -1)
    hidden_bias = ff_part.transpose(1, 0, 2).reshape(2, 2, 2, -1)
    hidden_bias = lax.dynamic_index_in_dim(
        lax.dynamic_index_in_dim(hidden_bias, zlo, 1, False), core, 1, False
    ).reshape(-1)

    lengths = regroup(jnp.concatenate([cont_lengths[0], enc_len]))
    places = jnp.stack(
        [512 * ((core != block // 2) + 2 * (zlo != block % 2)) for block in range(4)]
    ).astype(jnp.int32)
    bounds = PROMPT + jnp.concatenate(
        [jnp.zeros((1,), jnp.int32), jnp.cumsum(lengths[:segments]).astype(jnp.int32)]
    )
    self_meta = jnp.concatenate([places, bounds])
    cross_meta = lengths[segments:]

    resid = token_rows.astype(jnp.float32)
    _, hat_one, inv_one = norm_forward(resid, vectors[0], vectors[3])
    qkv_bias = jnp.concatenate([self_bias[0], jnp.zeros((width,), jnp.float32), self_bias[1]])
    qkv_scale = jnp.concatenate([jnp.full((width,), scaling), jnp.ones((2 * width,))]).astype(jnp.float32)
    def project(rows):
        return low((product(rows, w_qkv) + qkv_bias) * qkv_scale)

    qkv = project(attn_rows)
    count = qkv.shape[0]
    self_plan = functools.partial(self_sections, segments=segments)
    mixed, self_lse = attend(self_plan, self_meta, qkv, 0, qkv, pairs, 2 * pairs, pairs, 1152)
    mixed = after(mixed, out_beyond)
    w_out = over_chips(in_order(zhi, out_own, after(out_beyond, mixed), 1))
    near, far = mixed[: count // 2], mixed[count // 2 :]
    so_far = low(
        product_right_t(far[: count // 4], w_so)
        + trade(low(product_right_t(far[count // 4 :], w_so)), "core", "so_zc")
    )
    so_near_other = low(product_right_t(near[count // 4 :], w_so))
    so_near = product_right_t(near[: count // 4], w_so)
    grad_rows = regroup(after(cotangent, attn_rows), "cotangent")
    cross_kv = low(
        product(after(enc_full, grad_rows, so_far), w_ckv)
        + jnp.concatenate([jnp.zeros((cross_width,), jnp.float32), cross_bias[1]])
    )
    branch = so_near + trade(so_near_other, "core", "so_c") + after(trade(so_far, "zlo", "so_z"), cross_kv)
    after_one = resid + (branch + vectors[6])

    cot_beyond = trade(after(grad_rows, after_one), "zlo", "cot_z")
    cot_near = jnp.concatenate([grad_rows, trade(grad_rows, "core", "cot_c")], axis=0)

    normed_mid, hat_two, inv_two = norm_forward(after_one, vectors[1], vectors[4])
    cross_low = low(normed_mid)
    cross_rows = jnp.concatenate([cross_low, trade(cross_low, "core", "cin")], axis=0)
    own_rows = cross_low.shape[0]
    cross_q = low((product(cross_rows, w_cq) + cross_bias[0]) * scaling)
    cross_plan = functools.partial(cross_sections, blocks=cross_q.shape[0] // BLOCK)
    cross_mixed, cross_lse = attend(
        cross_plan, cross_meta, cross_q, 0, cross_kv, 0, cross_pairs, cross_pairs, ENC
    )
    cross_mixed = after(cross_mixed, cot_beyond)
    other = trade(low(product_right_t(cross_mixed[own_rows:], w_co)), "core", "co_c")
    branch = product_right_t(cross_mixed[:own_rows], w_co) + other
    after_two = after_one + (branch + vectors[7])

    normed_out, hat_three, inv_three = norm_forward(after_two, vectors[2], vectors[5])
    mlp_in = low(normed_out)
    beyond = trade(mlp_in, "zlo", "mlp_z")
    mlp_near = jnp.concatenate([mlp_in, trade(mlp_in, "core", "mlp_c")], axis=0)
    act_near, dpre_near, sum_near = hidden_units(mlp_near, cot_near, w_in, w_out, hidden_bias[None])
    beyond = after(beyond, act_near)
    mlp_far = jnp.concatenate([beyond, trade(beyond, "core", "mlp_zc")], axis=0)
    cot_far = jnp.concatenate([cot_beyond, trade(cot_beyond, "core", "cot_zc")], axis=0)
    act_far, dpre_far, sum_far = hidden_units(mlp_far, cot_far, w_in, w_out, hidden_bias[None])
    gradient = grad_rows.astype(jnp.float32)
    bias_out_three = jnp.sum(gradient, axis=0)
    dmlp_far = low(
        product_right_t(dpre_far[:own_rows], w_in)
        + trade(low(product_right_t(dpre_far[own_rows:], w_in)), "core", "dmlp_zc")
    )
    mlp_term = product_right_t(dpre_near[:own_rows], w_in) + trade(
        low(product_right_t(dpre_near[own_rows:], w_in)), "core", "dmlp_c"
    )
    act_near, act_far = after(act_near, dmlp_far, mlp_term), after(act_far, dmlp_far, mlp_term)
    out_parts = [
        low(product_right_t(act_far[own_rows:], w_out)),
        product_right_t(act_far[:own_rows], w_out),
        low(product_right_t(act_near[own_rows:], w_out)),
        product_right_t(act_near[:own_rows], w_out),
    ]
    out_far = low(out_parts[1] + trade(out_parts[0], "core", "out_zc"))
    out_branch = out_parts[3] + trade(out_parts[2], "core", "out_c")
    grad_w_out = low(product_left_t(cot_near, act_near) + product_left_t(cot_far, act_far))
    mlp_near, mlp_far = after(mlp_near, grad_w_out), after(mlp_far, grad_w_out)
    grad_w_in = low(product_left_t(mlp_near, dpre_near) + product_left_t(mlp_far, dpre_far))
    mlp_term = mlp_term + after(trade(dmlp_far, "zlo", "dmlp_z"), grad_w_in, grad_w_out)
    out_far = trade(after(out_far, mlp_term), "zlo", "out_z")
    part, gain_three, shift_three = norm_backward(mlp_term, hat_three, inv_three, vectors[2])
    gradient = gradient + part

    grad_low = low(gradient)
    bias_out_two = jnp.sum(grad_low.astype(jnp.float32), axis=0)
    grad_both = jnp.concatenate([grad_low, trade(grad_low, "core", "e2")], axis=0)
    cross_mixed_grad = low(product(grad_both, w_co))
    cross_dq, cross_dk, cross_dv = attend_back(
        cross_plan,
        cross_meta,
        cross_q,
        0,
        cross_kv,
        0,
        cross_pairs,
        cross_mixed,
        cross_mixed_grad,
        cross_lse,
        cross_pairs,
        ENC,
    )
    cross_dq = after(cross_dq, out_far)
    layer_out = regroup(low(after_two + (out_branch + after(out_far, cross_dq) + vectors[8])), "out")
    other = trade(low(product_right_t(cross_dq[own_rows:], w_cq)), "core", "dcin")
    part, gain_two, shift_two = norm_backward(
        product_right_t(cross_dq[:own_rows], w_cq) + other, hat_two, inv_two, vectors[1]
    )
    gradient = gradient + part

    grad_low = low(gradient)
    bias_out_one = jnp.sum(grad_low.astype(jnp.float32), axis=0)
    def zhi_sum(partial, axis, name):
        mine, theirs = half_of(partial, zhi, axis), half_of(partial, 1 - zhi, axis)
        return mine.astype(jnp.float32) + trade(theirs, "zhi", name).astype(jnp.float32)

    beyond = trade(grad_low, "zlo", "e1_z")
    grad_near = jnp.concatenate([grad_low, trade(grad_low, "core", "e1_c")], axis=0)
    mixed_grad = low(product(grad_near, w_so))
    cross_parts = [
        low(product_left_t(cross_rows, after(cross_dq, grad_low))),
        low(product_left_t(enc_full, after(cross_dk, grad_low))),
        low(product_left_t(enc_full, after(cross_dv, grad_low))),
        low(product_left_t(after(grad_both, grad_low), cross_mixed)),
    ]
    grad_cross = jnp.concatenate(cross_parts, axis=1)
    beyond = after(beyond, mixed_grad, grad_cross, layer_out)
    cross_sum = sum_over_chips(grad_cross)
    grad_far = jnp.concatenate([beyond, trade(beyond, "core", "e1_zc")], axis=0)
    mixed_grad = jnp.concatenate([mixed_grad, low(product(grad_far, w_so))], axis=0)

    out_sum = zhi_sum(sum_over_chips(grad_w_out), 1, "go_zhi")
    in_sum = zhi_sum(sum_over_chips(grad_w_in), 1, "gi_zhi")
    dq, dk, dv = attend_back(
        self_plan, self_meta, qkv, 0, qkv, pairs, 2 * pairs, mixed, mixed_grad, self_lse, pairs, 1152
    )
    dq, dk, dv = after(dq, in_sum, out_sum), after(dk, in_sum, out_sum), after(dv, in_sum, out_sum)
    dqkv = jnp.concatenate([dq, dk, dv], axis=1)
    d_near, d_far = dqkv[: count // 2], dqkv[count // 2 :]
    dx_far = low(
        product_right_t(d_far[: count // 4], w_qkv)
        + trade(low(product_right_t(d_far[count // 4 :], w_qkv)), "core", "dx_zc")
    )
    dx = product_right_t(d_near[: count // 4], w_qkv) + trade(
        low(product_right_t(d_near[count // 4 :], w_qkv)), "core", "dx_c"
    )
    dq, dk, dv = after(dq, dx_far), after(dk, dx_far), after(dv, dx_far)
    self_parts = [
        low(product_left_t(attn_rows, dq)),
        low(product_left_t(attn_rows, dk)),
        low(product_left_t(attn_rows, dv)),
        low(product_left_t(grad_near, near) + product_left_t(grad_far, far)),
    ]
    enc_part = low(
        product_right_t(after(cross_dk, dq), w_ckv[:, :cross_width])
        + product_right_t(after(cross_dv, dq), w_ckv[:, cross_width:])
    )
    dx = dx + after(trade(dx_far, "zlo", "dx_z"), enc_part, *self_parts)
    part, gain_one, shift_one = norm_backward(dx, hat_one, inv_one, vectors[0])
    input_part = low(gradient + part)
    input_grad = regroup(input_part, "dgrad").astype(jnp.float32)

    bias_self_query = jnp.sum(dq.astype(jnp.float32), axis=0)
    bias_self_value = jnp.sum(dv.astype(jnp.float32), axis=0)
    bias_cross_query = jnp.sum(cross_dq.astype(jnp.float32), axis=0)
    bias_cross_value = jnp.sum(cross_dv.astype(jnp.float32), axis=0)
    grad_hidden_bias = (sum_near + sum_far)[0]
    vec_sums = jnp.stack(
        [
            gain_one,
            gain_two,
            gain_three,
            shift_one,
            shift_two,
            shift_three,
            bias_out_one,
            bias_out_two,
            bias_out_three,
        ]
    )
    at_zlo = (jnp.arange(2) == zlo).astype(jnp.float32)
    at_core = (jnp.arange(2) == core).astype(jnp.float32)
    quarter = (at_zlo[:, None] * at_core[None, :])[:, :, None]
    self_sums = jnp.stack([bias_self_query, bias_self_value]).reshape(2, 2, 1, 1, -1) * quarter
    cross_sums = jnp.stack([bias_cross_query, bias_cross_value]).reshape(2, 2, 2, 1, -1) * at_core[:, None]
    head_sums = jnp.concatenate([self_sums, cross_sums], axis=0)
    hidden_sums = grad_hidden_bias.reshape(2, 1, 1, -1) * quarter
    vec_sums = vec_sums.reshape(9, 8, -1).transpose(1, 0, 2).reshape(8, 1, -1)
    sums = jnp.concatenate(
        [
            jnp.broadcast_to(vec_sums, (8, 4, sizes[0])),
            head_sums.reshape(4, 4, 8, -1).transpose(2, 1, 0, 3).reshape(8, 4, -1),
            hidden_sums.reshape(4, 8, -1).transpose(1, 0, 2),
        ],
        axis=2,
    )
    sums = jnp.pad(after(sums, input_part).reshape(32, -1, 128), ((0, 0), (0, 4), (0, 0)))
    ff_in_grad, ff_out_grad, cross_qkv_grad, cross_out_grad, self_qkv_grad, self_out_grad, enc_grad, sums = finish(
        in_sum,
        out_sum,
        cross_sum,
        [part.reshape(2, 2, rows_of, -1) for part in self_parts],
        enc_part.reshape(2, 2, -1, model),
        sums,
    )
    sums = sums.reshape(-1)[: sum(sizes)]
    vec_grad, head_grad, ff_bias_grad = jnp.split(sums, [sizes[0], sizes[0] + sizes[1]])
    return (
        layer_out,
        input_grad,
        enc_grad.astype(jnp.float32),
        self_qkv_grad,
        self_out_grad.T,
        cross_qkv_grad,
        cross_out_grad.T,
        ff_in_grad,
        ff_out_grad.T,
        head_grad.reshape(head_bias.shape),
        ff_bias_grad,
        vec_grad.reshape(vec_params.shape),
    )


def solution(mesh):
    fast = tuple(mesh.shape[axis] for axis in ("dp", "tensor")) == (8, 4)
    dp, tensor = (AXES[:3], AXES[3:]) if fast else (("dp",), ("tensor",))
    both = dp + tensor
    rows = P(both, None)
    qkv = P(None, dp, tensor)
    out = P(tensor, dp)
    in_specs = (
        rows,
        rows,
        P(dp),
        P(dp, None),
        rows,
        qkv,
        out,
        qkv,
        out,
        P(dp, tensor),
        out,
        P(None, tensor + dp),
        P(tensor + dp),
        P(None, dp),
    )
    out_specs = (
        rows,
        rows,
        rows,
        qkv,
        out,
        qkv,
        out,
        P(dp, tensor),
        out,
        P(None, tensor + dp),
        P(tensor + dp),
        P(None, dp),
    )
    if fast:
        mesh = Mesh(mesh.devices.reshape(2, 2, 2, 2, 2), AXES)
    return jax.shard_map(
        fast_layer if fast else shards, mesh=mesh, in_specs=in_specs, out_specs=out_specs, check_vma=False
    )
```

```python
import functools
import math

import jax
import jax.numpy as jnp
from jax import lax
from jax.experimental import pallas as pl
from jax.experimental.pallas import tpu as pltpu
from jax.sharding import Mesh
from jax.sharding import PartitionSpec as P

HD = 64
PROMPT = 1024
CONT_TOK = 1024
ENC = 512
BLOCK = 256
PAIR = 2 * HD
AXES = ("y", "x", "core", "zhi", "zlo")


def lane_half():
    return lax.broadcasted_iota(jnp.int32, (1, PAIR), 1) < HD


def one_head(rows, head):
    keep = lane_half() if head == 0 else jnp.logical_not(lane_half())
    return rows * jnp.where(keep, 1.0, 0.0).astype(rows.dtype)


def dot_nt(left, right):
    return lax.dot_general(left, right, (((1,), (1,)), ((), ())), preferred_element_type=jnp.float32)


def dot_nn(left, right):
    return jnp.dot(left, right, preferred_element_type=jnp.float32)


def dot_tn(left, right):
    return lax.dot_general(left, right, (((0,), (0,)), ((), ())), preferred_element_type=jnp.float32)


def self_sections(meta_ref, segments):
    def at(block):
        return pl.multiple_of(meta_ref[block], 512)

    def place(index):
        return pl.multiple_of(meta_ref[index >> 1] + (index & 1) * BLOCK, BLOCK)

    def causal(row, col):
        return col <= row

    def banded(row, col):
        start = jnp.full(row.shape, meta_ref[4], jnp.int32)
        for segment in range(1, segments):
            bound = meta_ref[4 + segment]
            start = jnp.where(row >= bound, bound, start)
        return (col <= row) & (col >= start)

    def early(index):
        return [(at(0), 512, 0, causal)]

    def middle(index):
        return [(at(0), 512, 0, None), (at(1), 512, 512, causal)]

    def late(index):
        return [
            (at(0), 512, 0, None),
            (at(1), 512, 512, None),
            (place(index - 1), BLOCK, (index - 1) * BLOCK, banded),
            (place(index), BLOCK, index * BLOCK, banded),
        ]

    return place, ((0, 2, early), (2, 4, middle), (4, 8, late))


def cross_sections(meta_ref, blocks):
    def place(index):
        return pl.multiple_of(index * BLOCK, BLOCK)

    def usable(row, col):
        return col < meta_ref[0]

    def every(index):
        return [(0, ENC, 0, usable)]

    return place, ((0, blocks, every),)


def forward_kernel(sections, meta_ref, q_ref, k_ref, v_ref, o_ref, lse_ref):
    place, ranges = sections(meta_ref)

    for low, high, parts_of in ranges:

        def step(index, carry, parts_of=parts_of):
            rows = pl.ds(place(index), BLOCK)
            parts = parts_of(index)
            queries = q_ref[rows, :]
            row = index * BLOCK + lax.broadcasted_iota(jnp.int32, (BLOCK, 1), 0)
            allowed = [
                None if rule is None else rule(row, first + lax.broadcasted_iota(jnp.int32, (1, size), 1))
                for _, size, first, rule in parts
            ]
            outs, totals = [], []
            for head in range(2):
                query = one_head(queries, head)
                scores = []
                for (where, size, _, _), ok in zip(parts, allowed):
                    score = dot_nt(query, k_ref[pl.ds(where, size), :])
                    scores.append(score if ok is None else jnp.where(ok, score, -1e30))
                top = functools.reduce(jnp.maximum, [jnp.max(s, axis=1, keepdims=True) for s in scores])
                exps = [jnp.exp(s - top) for s in scores]
                total = sum(jnp.sum(e, axis=1, keepdims=True) for e in exps)
                mixed = sum(
                    dot_nn(e.astype(jnp.bfloat16), v_ref[pl.ds(where, size), :])
                    for (where, size, _, _), e in zip(parts, exps)
                )
                outs.append(mixed * (1.0 / total))
                totals.append(top + jnp.log(total))
            o_ref[rows, :] = jnp.where(lane_half(), outs[0], outs[1]).astype(o_ref.dtype)
            lse_ref[rows, :] = jnp.where(lane_half(), totals[0], totals[1])
            return carry

        lax.fori_loop(low, high, step, 0)


def backward_kernel(
    sections, meta_ref, q_ref, k_ref, v_ref, o_ref, do_ref, lse_ref, dq_ref, dk_ref, dv_ref, dk_sum, dv_sum
):
    place, ranges = sections(meta_ref)
    dk_sum[...] = jnp.zeros_like(dk_sum)
    dv_sum[...] = jnp.zeros_like(dv_sum)

    for low, high, parts_of in ranges:

        def step(index, carry, parts_of=parts_of):
            rows = pl.ds(place(index), BLOCK)
            parts = parts_of(index)
            queries, grads = q_ref[rows, :], do_ref[rows, :]
            row = index * BLOCK + lax.broadcasted_iota(jnp.int32, (1, BLOCK), 1)
            allowed = [
                None if rule is None else rule(row, first + lax.broadcasted_iota(jnp.int32, (size, 1), 0))
                for _, size, first, rule in parts
            ]
            logs = jnp.transpose(lse_ref[rows, :])
            spread = jnp.transpose(grads.astype(jnp.float32) * o_ref[rows, :].astype(jnp.float32))
            key_parts = [k_ref[pl.ds(where, size), :] for where, size, _, _ in parts]
            value_parts = [v_ref[pl.ds(where, size), :] for where, size, _, _ in parts]
            query_grads = []
            for head in range(2):
                query, grad = one_head(queries, head), one_head(grads, head)
                log = logs[head * HD : head * HD + 1, :]
                delta = jnp.sum(spread[head * HD : (head + 1) * HD, :], axis=0, keepdims=True)
                query_grad = None
                for (where, size, _, _), ok, keys, values in zip(parts, allowed, key_parts, value_parts):
                    score = dot_nt(keys, query)
                    if ok is not None:
                        score = jnp.where(ok, score, -1e30)
                    probs = jnp.exp(score - log)
                    score_grad = (probs * (dot_nt(values, grad) - delta)).astype(jnp.bfloat16)
                    dv_sum[pl.ds(where, size), :] += dot_nn(probs.astype(jnp.bfloat16), grad)
                    dk_sum[pl.ds(where, size), :] += dot_nn(score_grad, query)
                    term = dot_tn(score_grad, keys)
                    query_grad = term if query_grad is None else query_grad + term
                query_grads.append(query_grad)
            both = jnp.where(lane_half(), query_grads[0], query_grads[1])
            dq_ref[rows, :] = both.astype(jnp.bfloat16) * jnp.asarray(HD**-0.5, jnp.bfloat16)
            return carry

        lax.fori_loop(low, high, step, 0)
    dk_ref[...] = dk_sum[...].astype(dk_ref.dtype)
    dv_ref[...] = dv_sum[...].astype(dv_ref.dtype)


def columns(rows, first):
    return pl.BlockSpec((rows, PAIR), lambda pair, meta: (0, first + pair))


def attend(sections, meta, q, q_at, keys, k_at, v_at, pairs, weight):
    count, key_rows = q.shape[0], keys.shape[0]
    return pl.pallas_call(
        functools.partial(forward_kernel, sections),
        grid_spec=pltpu.PrefetchScalarGridSpec(
            num_scalar_prefetch=1,
            grid=(pairs,),
            in_specs=[columns(count, q_at), columns(key_rows, k_at), columns(key_rows, v_at)],
            out_specs=[columns(count, 0), columns(count, 0)],
        ),
        out_shape=[
            jax.ShapeDtypeStruct((count, pairs * PAIR), jnp.bfloat16),
            jax.ShapeDtypeStruct((count, pairs * PAIR), jnp.float32),
        ],
        cost_estimate=pl.CostEstimate(
            flops=2 * 4 * 4 * count * weight * pairs * PAIR,
            bytes_accessed=10 * count * pairs * PAIR,
            transcendentals=2 * pairs * count * weight,
        ),
    )(meta, q, keys, keys)


def attend_back(sections, meta, q, q_at, keys, k_at, v_at, out, out_grad, lse, pairs, weight):
    count, key_rows = q.shape[0], keys.shape[0]
    return pl.pallas_call(
        functools.partial(backward_kernel, sections),
        grid_spec=pltpu.PrefetchScalarGridSpec(
            num_scalar_prefetch=1,
            grid=(pairs,),
            in_specs=[
                columns(count, q_at),
                columns(key_rows, k_at),
                columns(key_rows, v_at),
                columns(count, 0),
                columns(count, 0),
                columns(count, 0),
            ],
            out_specs=[columns(count, 0), columns(key_rows, 0), columns(key_rows, 0)],
            scratch_shapes=[pltpu.VMEM((key_rows, PAIR), jnp.float32)] * 2,
        ),
        out_shape=[
            jax.ShapeDtypeStruct((count, pairs * PAIR), jnp.bfloat16),
            jax.ShapeDtypeStruct((key_rows, pairs * PAIR), jnp.bfloat16),
            jax.ShapeDtypeStruct((key_rows, pairs * PAIR), jnp.bfloat16),
        ],
        cost_estimate=pl.CostEstimate(
            flops=5 * 4 * 4 * count * weight * pairs * PAIR,
            bytes_accessed=20 * count * pairs * PAIR,
            transcendentals=2 * pairs * count * weight,
        ),
    )(meta, q, keys, keys, out, out_grad, lse)


EPSILON = 1e-05
MASKED = 1e30
GELU_C = math.sqrt(2.0 / math.pi)
GELU_A = 0.044715


def gelu_value(values):
    inner = jnp.tanh(GELU_C * (values + GELU_A * values * values * values))
    return 0.5 * values * (1.0 + inner)


def gelu_slope(values):
    inner = jnp.tanh(GELU_C * (values + GELU_A * values * values * values))
    return 0.5 * (1.0 + inner) + 0.5 * values * (1.0 - inner * inner) * GELU_C * (
        1.0 + 3.0 * GELU_A * values * values
    )


def norm_forward(values, gain_vec, shift_vec):
    row_mean = jnp.mean(values, axis=1, keepdims=True)
    centred = values - row_mean
    inverse = lax.rsqrt(jnp.mean(centred * centred, axis=1, keepdims=True) + EPSILON)
    normed = centred * inverse
    return (normed * gain_vec + shift_vec, normed, inverse)


def norm_backward(gradient, normed, inverse, gain_vec):
    scaled = gradient * gain_vec
    inner = (
        scaled
        - jnp.mean(scaled, axis=1, keepdims=True)
        - normed * jnp.mean(scaled * normed, axis=1, keepdims=True)
    )
    return (inner * inverse, jnp.sum(gradient * normed, axis=0), jnp.sum(gradient, axis=0))


def product(left, right):
    return jnp.dot(left, right, preferred_element_type=jnp.float32)


def product_left_t(left, right):
    return lax.dot_general(
        left, right, (((0,), (0,)), ((), ())), preferred_element_type=jnp.float32
    )


def product_right_t(left, right):
    return lax.dot_general(
        left, right, (((1,), (1,)), ((), ())), preferred_element_type=jnp.float32
    )


def attend_forward(queries, key_rows, value_rows, rule, block_rows):
    seq_rows, local_width = queries.shape
    local_heads = local_width // HD
    query_blocks = queries.reshape(seq_rows // block_rows, block_rows, local_heads, HD)
    key_heads = key_rows.reshape(-1, local_heads, HD)
    value_heads = value_rows.reshape(-1, local_heads, HD)
    block_starts = jnp.arange(seq_rows // block_rows, dtype=jnp.int32) * block_rows

    def attend_block(pieces):
        query_block, offset = pieces
        scores = jnp.einsum(
            "qhd,khd->hqk", query_block, key_heads, preferred_element_type=jnp.float32
        )
        scores = jnp.where(rule(offset, block_rows)[None], scores, -MASKED)
        row_max = jnp.max(scores, axis=2, keepdims=True)
        exponent = jnp.exp(scores - row_max)
        row_total = jnp.sum(exponent, axis=2, keepdims=True)
        probs_low = (exponent / row_total).astype(jnp.bfloat16)
        mixed = jnp.einsum(
            "hqk,khd->qhd", probs_low, value_heads, preferred_element_type=jnp.float32
        )
        return (
            mixed.astype(jnp.bfloat16).reshape(block_rows, local_width),
            (row_max + jnp.log(row_total))[:, :, 0],
        )

    outputs, log_total = lax.map(attend_block, (query_blocks, block_starts))
    return (outputs.reshape(seq_rows, local_width), log_total)


def attend_backward(queries, key_rows, value_rows, out_grad, log_total, rule, block_rows):
    seq_rows, local_width = queries.shape
    local_heads = local_width // HD
    key_count = key_rows.shape[0]
    query_blocks = queries.reshape(seq_rows // block_rows, block_rows, local_heads, HD)
    grad_blocks = out_grad.reshape(seq_rows // block_rows, block_rows, local_heads, HD)
    key_heads = key_rows.reshape(key_count, local_heads, HD)
    value_heads = value_rows.reshape(key_count, local_heads, HD)
    block_starts = jnp.arange(seq_rows // block_rows, dtype=jnp.int32) * block_rows

    def back_block(running, pieces):
        key_sum, value_sum = running
        query_block, grad_block, block_total, offset = pieces
        scores = jnp.einsum(
            "qhd,khd->hqk", query_block, key_heads, preferred_element_type=jnp.float32
        )
        probs = jnp.where(
            rule(offset, block_rows)[None], jnp.exp(scores - block_total[:, :, None]), 0.0
        )
        probs_low = probs.astype(jnp.bfloat16)
        prob_grad = jnp.einsum(
            "qhd,khd->hqk", grad_block, value_heads, preferred_element_type=jnp.float32
        )
        row_delta = jnp.sum(probs * prob_grad, axis=2, keepdims=True)
        score_grad = (probs * (prob_grad - row_delta)).astype(jnp.bfloat16)
        query_grad = jnp.einsum(
            "hqk,khd->qhd", score_grad, key_heads, preferred_element_type=jnp.float32
        )
        key_sum = key_sum + jnp.einsum(
            "hqk,qhd->khd", score_grad, query_block, preferred_element_type=jnp.float32
        )
        value_sum = value_sum + jnp.einsum(
            "hqk,qhd->khd", probs_low, grad_block, preferred_element_type=jnp.float32
        )
        return (
            (key_sum, value_sum),
            query_grad.astype(jnp.bfloat16).reshape(block_rows, local_width),
        )

    zero_sum = jnp.zeros((key_count, local_heads, HD), jnp.float32)
    (key_sum, value_sum), query_grads = lax.scan(
        back_block, (zero_sum, zero_sum), (query_blocks, grad_blocks, log_total, block_starts)
    )
    return (
        query_grads.reshape(seq_rows, local_width),
        key_sum.astype(jnp.bfloat16).reshape(key_count, local_width),
        value_sum.astype(jnp.bfloat16).reshape(key_count, local_width),
    )


def attend_groups(queries, key_rows, value_rows, rules, block_rows):
    results, totals = ([], [])
    for which_group, rule in enumerate(rules):
        mixed, log_total = attend_forward(queries, key_rows, value_rows, rule, block_rows)
        results.append(mixed)
        totals.append(log_total)
    return (results[0], totals)


def back_groups(queries, key_rows, value_rows, out_grad, totals, rules, block_rows):
    query_list, key_list, value_list = ([], [], [])
    for which_group, rule in enumerate(rules):
        query_grad, key_grad, value_grad = attend_backward(
            queries, key_rows, value_rows, out_grad, totals[which_group], rule, block_rows
        )
        query_list.append(query_grad)
        key_list.append(key_grad)
        value_list.append(value_grad)
    return (query_list[0], key_list[0], value_list[0])


def shards(
    tokens,
    enc_states,
    enc_len,
    cont_lengths,
    cotangent,
    self_qkv,
    self_out,
    cross_qkv,
    cross_out,
    ff_in,
    ff_out,
    head_bias,
    ff_bias,
    vec_params,
):
    gathered = (
        lax.all_gather(self_qkv, "dp", axis=1, tiled=True),
        lax.all_gather(self_out, "dp", axis=1, tiled=True),
        lax.all_gather(cross_qkv, "dp", axis=1, tiled=True),
        lax.all_gather(cross_out, "dp", axis=1, tiled=True),
        lax.all_gather(ff_in, "dp", axis=0, tiled=True),
        lax.all_gather(ff_out, "dp", axis=1, tiled=True),
        lax.all_gather(head_bias, "dp", axis=1, tiled=True),
        lax.all_gather(ff_bias, "dp", axis=0, tiled=True),
        lax.all_gather(vec_params, "dp", axis=1, tiled=True),
    )
    (
        w_self,
        w_self_out,
        w_cross,
        w_cross_out,
        w_hidden_in,
        w_hidden_out,
        bias_heads,
        bias_hidden,
        vectors,
    ) = gathered
    vectors = vectors.astype(jnp.float32)
    bias_heads = bias_heads.astype(jnp.float32)
    bias_hidden = bias_hidden.astype(jnp.float32)
    seq_rows = PROMPT + CONT_TOK
    block_rows = min(512, seq_rows)
    scaling = HD ** (-0.5)
    rows_dev = tokens.shape[0]

    def self_rule(which_group):
        bounds = PROMPT + jnp.cumsum(cont_lengths[which_group])
        positions = jnp.arange(seq_rows, dtype=jnp.int32)
        segment = jnp.sum((positions[:, None] >= bounds[None, :]).astype(jnp.int32), axis=1)

        def self_allowed(offset, number):
            row_ids = offset + jnp.arange(number, dtype=jnp.int32)
            row_segment = lax.dynamic_slice_in_dim(segment, offset, number)
            return (positions[None, :] <= row_ids[:, None]) & (
                (positions[None, :] < PROMPT) | (segment[None, :] == row_segment[:, None])
            )

        return self_allowed

    def cross_rule(which_group):
        usable = jnp.arange(ENC, dtype=jnp.int32) < enc_len[which_group]

        def cross_allowed(offset, number):
            return jnp.broadcast_to(usable[None, :], (number, ENC))

        return cross_allowed

    def spread(low_rows):
        return lax.all_gather(low_rows, "tensor", axis=0, tiled=True)

    def head_branch(values, weight):

        def term(offset, number):
            return product(values, weight)

        return lax.psum_scatter(
            term(jnp.int32(0), rows_dev * lax.axis_size("tensor")),
            "tensor",
            scatter_dimension=0,
            tiled=True,
        )

    def widen(low_rows):
        return lax.all_gather(low_rows, "tensor", axis=0, tiled=True)

    def narrow(term):
        return lax.psum_scatter(
            term(jnp.int32(0), rows_dev * lax.axis_size("tensor")),
            "tensor",
            scatter_dimension=0,
            tiled=True,
        )

    self_rules = [self_rule(0)]
    cross_rules = [cross_rule(0)]
    resid = tokens.astype(jnp.float32)
    enc_full = lax.all_gather(enc_states, "tensor", axis=0, tiled=True)
    normed_in, hat_one, inv_one = norm_forward(resid, vectors[0], vectors[3])
    attn_low = normed_in.astype(jnp.bfloat16)
    attn_full = spread(attn_low)
    queries = ((product(attn_full, w_self[0]) + bias_heads[0]) * scaling).astype(jnp.bfloat16)
    key_rows = product(attn_full, w_self[1]).astype(jnp.bfloat16)
    value_rows = (product(attn_full, w_self[2]) + bias_heads[1]).astype(jnp.bfloat16)
    mixed, self_totals = attend_groups(queries, key_rows, value_rows, self_rules, block_rows)
    after_one = resid + (head_branch(mixed, w_self_out) + vectors[6])
    normed_mid, hat_two, inv_two = norm_forward(after_one, vectors[1], vectors[4])
    cross_low = normed_mid.astype(jnp.bfloat16)
    cross_full = spread(cross_low)
    cross_queries = ((product(cross_full, w_cross[0]) + bias_heads[2]) * scaling).astype(
        jnp.bfloat16
    )
    cross_keys = product(enc_full, w_cross[1]).astype(jnp.bfloat16)
    cross_values = (product(enc_full, w_cross[2]) + bias_heads[3]).astype(jnp.bfloat16)
    cross_mixed, cross_totals = attend_groups(
        cross_queries, cross_keys, cross_values, cross_rules, block_rows
    )
    after_two = after_one + (head_branch(cross_mixed, w_cross_out) + vectors[7])
    normed_out, hat_three, inv_three = norm_forward(after_two, vectors[2], vectors[5])
    hidden_low = normed_out.astype(jnp.bfloat16)
    hidden_full = spread(hidden_low)
    pre_act = product(hidden_full, w_hidden_in) + bias_hidden
    activation = gelu_value(pre_act).astype(jnp.bfloat16)

    def term(offset, number):
        return product(activation, w_hidden_out)

    after_three = after_two + (
        lax.psum_scatter(
            term(jnp.int32(0), rows_dev * lax.axis_size("tensor")),
            "tensor",
            scatter_dimension=0,
            tiled=True,
        )
        + vectors[8]
    )
    layer_out = after_three.astype(jnp.bfloat16)
    gradient = cotangent.astype(jnp.float32)
    grad_low = gradient.astype(jnp.bfloat16)
    bias_out_three = jnp.sum(grad_low.astype(jnp.float32), axis=0)
    grad_full = widen(grad_low)
    act_grad = (product_right_t(grad_full, w_hidden_out) * gelu_slope(pre_act)).astype(jnp.bfloat16)
    grad_hidden_out = product_left_t(activation, grad_full)
    grad_hidden_in = product_left_t(hidden_full, act_grad)
    grad_bias_hidden = jnp.sum(act_grad.astype(jnp.float32), axis=0)

    def hidden_term(offset, number):
        return product_right_t(act_grad, w_hidden_in)

    input_part, gain_three, shift_three = norm_backward(
        narrow(hidden_term), hat_three, inv_three, vectors[2]
    )
    gradient = gradient + input_part
    grad_low = gradient.astype(jnp.bfloat16)
    bias_out_two = jnp.sum(grad_low.astype(jnp.float32), axis=0)
    grad_full = widen(grad_low)
    grad_cross_out = product_left_t(cross_mixed, grad_full)
    mixed_grad = product_right_t(grad_full, w_cross_out).astype(jnp.bfloat16)
    cross_query_grad, cross_key_grad, cross_value_grad = back_groups(
        cross_queries, cross_keys, cross_values, mixed_grad, cross_totals, cross_rules, block_rows
    )
    grad_cross = jnp.stack(
        [
            product_left_t(cross_full, cross_query_grad) * scaling,
            product_left_t(enc_full, cross_key_grad),
            product_left_t(enc_full, cross_value_grad),
        ]
    )
    bias_cross_query = jnp.sum(cross_query_grad.astype(jnp.float32), axis=0) * scaling
    bias_cross_value = jnp.sum(cross_value_grad.astype(jnp.float32), axis=0)
    enc_grad = lax.psum_scatter(
        product_right_t(cross_key_grad, w_cross[1]) + product_right_t(cross_value_grad, w_cross[2]),
        "tensor",
        scatter_dimension=0,
        tiled=True,
    )

    def cross_term(offset, number):
        return product_right_t(cross_query_grad, w_cross[0]) * scaling

    input_part, gain_two, shift_two = norm_backward(
        narrow(cross_term), hat_two, inv_two, vectors[1]
    )
    gradient = gradient + input_part
    grad_low = gradient.astype(jnp.bfloat16)
    bias_out_one = jnp.sum(grad_low.astype(jnp.float32), axis=0)
    grad_full = widen(grad_low)
    grad_self_out = product_left_t(mixed, grad_full)
    self_mixed_grad = product_right_t(grad_full, w_self_out).astype(jnp.bfloat16)
    query_grad, key_grad, value_grad = back_groups(
        queries, key_rows, value_rows, self_mixed_grad, self_totals, self_rules, block_rows
    )
    grad_self = jnp.stack(
        [
            product_left_t(attn_full, query_grad) * scaling,
            product_left_t(attn_full, key_grad),
            product_left_t(attn_full, value_grad),
        ]
    )
    bias_self_query = jnp.sum(query_grad.astype(jnp.float32), axis=0) * scaling
    bias_self_value = jnp.sum(value_grad.astype(jnp.float32), axis=0)

    def self_term(offset, number):
        return (
            product_right_t(query_grad, w_self[0]) * scaling
            + product_right_t(key_grad, w_self[1])
            + product_right_t(value_grad, w_self[2])
        )

    input_part, gain_one, shift_one = norm_backward(narrow(self_term), hat_one, inv_one, vectors[0])
    input_grad = gradient + input_part
    vector_grads = jnp.stack(
        [
            gain_one,
            gain_two,
            gain_three,
            shift_one,
            shift_two,
            shift_three,
            bias_out_one,
            bias_out_two,
            bias_out_three,
        ]
    )
    head_grads = jnp.stack([bias_self_query, bias_self_value, bias_cross_query, bias_cross_value])
    results = (
        lax.psum_scatter(grad_self, "dp", scatter_dimension=1, tiled=True),
        lax.psum_scatter(grad_self_out, "dp", scatter_dimension=1, tiled=True),
        lax.psum_scatter(grad_cross, "dp", scatter_dimension=1, tiled=True),
        lax.psum_scatter(grad_cross_out, "dp", scatter_dimension=1, tiled=True),
        lax.psum_scatter(grad_hidden_in, "dp", scatter_dimension=0, tiled=True),
        lax.psum_scatter(grad_hidden_out, "dp", scatter_dimension=1, tiled=True),
        lax.psum_scatter(head_grads, "dp", scatter_dimension=1, tiled=True),
        lax.psum_scatter(grad_bias_hidden, "dp", scatter_dimension=0, tiled=True),
        lax.psum_scatter(vector_grads, "dp", scatter_dimension=1, tiled=True),
    )
    vector_total = lax.psum(results[8], "tensor")
    return (
        layer_out,
        input_grad,
        enc_grad,
        results[0],
        results[1],
        results[2],
        results[3],
        results[4],
        results[5],
        results[6],
        results[7],
        vector_total,
    )


def hidden_kernel(x_ref, e_ref, w_in_ref, w_out_ref, bias_ref, act_ref, grad_ref, sum_ref):
    chunk = 256
    sum_ref[...] = jnp.zeros_like(sum_ref)

    def step(index, carry):
        rows = pl.ds(pl.multiple_of(index * chunk, chunk), chunk)
        value = dot_nn(x_ref[rows, :], w_in_ref[...]) + bias_ref[...]
        upper = dot_nn(e_ref[rows, :], w_out_ref[...])
        square = value * value
        inner = jnp.tanh(value * (GELU_C + (GELU_C * GELU_A) * square))
        half = 0.5 + 0.5 * inner
        act_ref[rows, :] = (value * half).astype(act_ref.dtype)
        slope = half + (value * (half * (1.0 - inner))) * (GELU_C + (3.0 * GELU_C * GELU_A) * square)
        grad = (upper * slope).astype(grad_ref.dtype)
        grad_ref[rows, :] = grad
        sum_ref[...] += jnp.sum(grad.astype(jnp.float32), axis=0, keepdims=True)
        return carry

    lax.fori_loop(0, x_ref.shape[0] // chunk, step, 0, unroll=2)


def hidden_units(rows, grads, weights, bias, tile=512):
    count, model = rows.shape
    width = weights.shape[1] // 2
    tiles = width // tile
    whole = pl.BlockSpec((count, model), lambda i: (0, 0))
    weight = pl.BlockSpec((model, tile), lambda i: (0, i))
    weight_out = pl.BlockSpec((model, tile), lambda i: (0, tiles + i))
    line = pl.BlockSpec((1, tile), lambda i: (0, i))
    out = pl.BlockSpec((count, tile), lambda i: (0, i))
    return pl.pallas_call(
        hidden_kernel,
        grid=(width // tile,),
        in_specs=[whole, whole, weight, weight_out, line],
        out_specs=[out, out, line],
        out_shape=[
            jax.ShapeDtypeStruct((count, width), jnp.bfloat16),
            jax.ShapeDtypeStruct((count, width), jnp.bfloat16),
            jax.ShapeDtypeStruct((1, width), jnp.float32),
        ],
        cost_estimate=pl.CostEstimate(
            flops=4 * count * model * width,
            bytes_accessed=4 * (count * model + model * width + count * width),
            transcendentals=count * width,
        ),
    )(rows, grads, weights, weights, bias)


MESH = pl.DeviceIdType.MESH
LINKS = ("core", "x", "y", "zhi", "zlo")


def start_kernel(
    tokens,
    enc,
    w_self,
    w_cross,
    w_in,
    w_out,
    small,
    token_rows,
    attn,
    g_self,
    cross_rows,
    hidden,
    enc_full,
    small_all,
    held,
    normed,
    gathered,
    send,
    recv,
    local,
):
    y, x, core, zhi, zlo = (lax.axis_index(axis) for axis in AXES)
    crossing = core != zhi
    rows = tokens.shape[0]
    part = w_self.shape[1]
    counts = {"sent": 0, "local": 0}

    def push(source, target, axis):
        index = counts["sent"]
        counts["sent"] += 1
        copy = pltpu.make_async_remote_copy(
            src_ref=source,
            dst_ref=target,
            send_sem=send.at[index],
            recv_sem=recv.at[index],
            device_id={axis: 1 - lax.axis_index(axis)},
            device_id_type=MESH,
        )
        copy.start()
        return copy

    def keep(source, target):
        index = counts["local"]
        counts["local"] += 1
        copy = pltpu.make_async_copy(source, target, local.at[index])
        copy.start()
        return copy

    def moving(source, target, source_here, target_here):
        index, index_here = counts["sent"], counts["local"]
        counts["sent"] += 1
        counts["local"] += 1

        def remote():
            return pltpu.make_async_remote_copy(
                src_ref=source,
                dst_ref=target,
                send_sem=send.at[index],
                recv_sem=recv.at[index],
                device_id={"core": zhi, "zhi": core},
                device_id_type=MESH,
            )

        def here():
            return pltpu.make_async_copy(source_here, target_here, local.at[index_here])

        @pl.when(crossing)
        def _():
            remote().start()

        @pl.when(jnp.logical_not(crossing))
        def _():
            here().start()

        def wait():
            @pl.when(crossing)
            def _():
                remote().wait()

            @pl.when(jnp.logical_not(crossing))
            def _():
                here().wait()

        return wait

    def lanes(block, size):
        return pl.ds(pl.multiple_of(block * size, size), size)

    barrier = pltpu.get_barrier_semaphore()
    for axis in LINKS:
        pl.semaphore_signal(barrier, inc=1, device_id={axis: 1 - lax.axis_index(axis)}, device_id_type=MESH)

    @pl.when(crossing)
    def _():
        pl.semaphore_signal(barrier, inc=1, device_id={"core": zhi, "zhi": core}, device_id_type=MESH)

    pl.semaphore_wait(barrier, len(LINKS) + crossing.astype(jnp.int32))

    wait_tokens = moving(tokens, held, tokens, held)
    own_small = keep(small, gathered.at[y, x, core, zhi, zlo])
    own_rows = pl.ds(pl.multiple_of(core * part, part), part)
    quarter = 2 * zhi + zlo

    def from_shard(shard, target, block, size):
        own = keep(shard.at[:, :, lanes(core, size)], target.at[:, y, x, own_rows, lanes(block, size)])
        other = push(
            shard.at[:, :, lanes(1 - core, size)], target.at[:, y, x, own_rows, lanes(block, size)], "core"
        )
        return own, other

    self_width = w_self.shape[2] // 2
    hidden_width = w_in.shape[1] // 2
    cross_core = []
    for plane in range(4):
        target = cross_rows.at[own_rows, lanes(4 * plane + quarter, self_width)]
        cross_core.append(keep(w_cross.at[plane, :, lanes(core, self_width)], target))
        cross_core.append(push(w_cross.at[plane, :, lanes(1 - core, self_width)], target, "core"))
    own_small.wait()
    small_core = push(gathered.at[y, x, core, zhi, zlo], gathered.at[y, x, core, zhi, zlo], "core")
    self_core = from_shard(w_self, g_self, zhi, self_width)
    hidden_core = []
    for plane, shard in enumerate((w_in, w_out)):
        target = hidden.at[plane, own_rows]
        hidden_core.append(keep(shard.at[:, lanes(core, hidden_width)], target))
        hidden_core.append(push(shard.at[:, lanes(1 - core, hidden_width)], target, "core"))
    for copy in cross_core:
        copy.wait()
    regions = [cross_rows.at[:, lanes(4 * plane + quarter, self_width)] for plane in range(4)]
    cross_zlo = [push(region, region, "zlo") for region in regions]
    small_core.wait()
    region = gathered.at[y, x, :, zhi, zlo]
    small_x = push(region, region, "x")
    for copy in self_core:
        copy.wait()
    small_x.wait()
    region = gathered.at[y, :, :, zhi, zlo]
    small_y = push(region, region, "y")
    for copy in cross_zlo:
        copy.wait()
    small_y.wait()

    def over_plane(target, width):
        first, second = pl.ds(0, width), pl.ds(width, width)
        region_a, region_b = target.at[:, y, x, :, first], target.at[:, y, x, :, second]
        steps = (push(region_a, region_a, "x"), push(region_b, region_b, "y"))

        def second_steps():
            steps[0].wait()
            region_a = target.at[:, y, :, :, first]
            step_a = push(region_a, region_a, "y")
            steps[1].wait()
            region_b = target.at[:, :, x, :, second]
            return step_a, push(region_b, region_b, "x")

        return second_steps

    wait_tokens()
    keep_tokens = keep(held, token_rows)
    region = gathered.at[:, :, :, zhi, zlo]
    small_zhi = push(region, region, "zhi")
    region = g_self.at[:, y, x, :, lanes(zhi, self_width)]
    self_zhi = push(region, region, "zhi")
    wait_enc = moving(enc, enc_full.at[2 * zhi + zlo], enc, enc_full.at[2 * core + zlo])
    regions = [cross_rows.at[:, lanes(2 * plane + zhi, 2 * self_width)] for plane in range(4)]
    cross_zhi = [push(region, region, "zhi") for region in regions]
    gain = jnp.concatenate([gathered[d // 4, d // 2 % 2, d % 2, zhi, zlo, 0:1, :] for d in range(8)], axis=1)
    shift = jnp.concatenate([gathered[d // 4, d // 2 % 2, d % 2, zhi, zlo, 3:4, :] for d in range(8)], axis=1)

    def norm_step(step, carry):
        block = pl.ds(pl.multiple_of(step * 64, 64), 64)
        values = held[block, :].astype(jnp.float32)
        centred = values - jnp.mean(values, axis=1, keepdims=True)
        inverse = lax.rsqrt(jnp.mean(centred * centred, axis=1, keepdims=True) + EPSILON)
        normed[block, :] = (centred * inverse * gain + shift).astype(normed.dtype)
        return carry

    lax.fori_loop(0, rows // 64, norm_step, 0)
    attn_zlo = push(normed, attn.at[pl.ds(2 * rows, rows)], "zlo")
    attn_core = push(normed, attn.at[pl.ds(rows, rows)], "core")
    attn_own = keep(normed, attn.at[pl.ds(0, rows)])

    wait_enc()
    region = enc_full.at[2 * core + zlo]
    enc_zlo = push(region, region, "zlo")
    enc_core = push(region, region, "core")
    self_zhi.wait()
    self_second = over_plane(g_self, self_width)
    self_last = self_second()
    small_zhi.wait()
    region = gathered.at[:, :, :, :, zlo]
    small_zlo = push(region, region, "zlo")
    enc_zlo.wait()
    region = enc_full.at[2 * core + 1 - zlo]
    enc_diagonal = push(region, region, "core")
    attn_zlo.wait()
    attn_diagonal = push(attn.at[pl.ds(2 * rows, rows)], attn.at[pl.ds(3 * rows, rows)], "core")
    small_zlo.wait()
    keep_small = keep(gathered, small_all)
    for copy in (
        *self_last,
        *cross_zhi,
        *hidden_core,
        attn_core,
        attn_diagonal,
        enc_core,
        enc_diagonal,
        attn_own,
        keep_tokens,
        keep_small,
    ):
        copy.wait()


def start_exchange(tokens, enc, w_self, w_cross, w_in, w_out, small):
    rows, model = tokens.shape
    part = w_self.shape[1]
    low_type = tokens.dtype
    shapes = [
        jax.ShapeDtypeStruct((rows, model), low_type),
        jax.ShapeDtypeStruct((4 * rows, model), low_type),
        jax.ShapeDtypeStruct((4, 2, 2, 2 * part, w_self.shape[2]), low_type),
        jax.ShapeDtypeStruct((2 * part, 8 * w_cross.shape[2]), low_type),
        jax.ShapeDtypeStruct((2, 2 * part, w_in.shape[1] // 2), low_type),
        jax.ShapeDtypeStruct((4, enc.shape[0], model), low_type),
        jax.ShapeDtypeStruct((2,) * 5 + small.shape, small.dtype),
    ]
    anywhere = pl.BlockSpec(memory_space=pl.ANY)
    return pl.pallas_call(
        start_kernel,
        out_shape=shapes,
        in_specs=[anywhere] * 7,
        out_specs=[anywhere] * len(shapes),
        scratch_shapes=[
            pltpu.VMEM((rows, model), low_type),
            pltpu.VMEM((rows, model), low_type),
            pltpu.VMEM((2,) * 5 + small.shape, small.dtype),
            pltpu.SemaphoreType.DMA((40,)),
            pltpu.SemaphoreType.DMA((40,)),
            pltpu.SemaphoreType.DMA((20,)),
        ],
        compiler_params=pltpu.CompilerParams(collective_id=0, has_side_effects=True),
    )(tokens, enc, w_self, w_cross, w_in, w_out, small)


def finish_kernel(
    ff_in,
    ff_out,
    cross,
    cross_beyond,
    self_q,
    self_k,
    self_v,
    self_o,
    enc_part,
    small,
    ff_in_out,
    ff_out_out,
    cross_qkv_out,
    cross_out_out,
    self_qkv_out,
    self_out_out,
    enc_out,
    small_out,
    cross_own,
    cross_got,
    cross_low,
    cross_got_low,
    cross_total,
    enc_own,
    enc_got,
    enc_sum,
    enc_far,
    enc_low,
    self_own,
    self_got,
    low_a,
    low_b,
    self_got_low,
    self_total,
    self_last,
    small_sum,
    small_got_0,
    small_got_1,
    small_got_2,
    small_got_3,
    small_got_4,
    send,
    recv,
    local,
):
    y, x, core, zhi, zlo = (lax.axis_index(axis) for axis in AXES)
    crossing = core != zhi
    small_got = (small_got_0, small_got_1, small_got_2, small_got_3, small_got_4)
    counts = {"sent": 0, "local": 0}

    def push(source, target, axis):
        index = counts["sent"]
        counts["sent"] += 1
        copy = pltpu.make_async_remote_copy(
            src_ref=source,
            dst_ref=target,
            send_sem=send.at[index],
            recv_sem=recv.at[index],
            device_id={axis: 1 - lax.axis_index(axis)},
            device_id_type=MESH,
        )
        copy.start()
        return copy

    def keep(source, target):
        index = counts["local"]
        counts["local"] += 1
        copy = pltpu.make_async_copy(source, target, local.at[index])
        copy.start()
        return copy

    def moving(source, target, source_here, target_here):
        index, index_here = counts["sent"], counts["local"]
        counts["sent"] += 1
        counts["local"] += 1

        def remote():
            return pltpu.make_async_remote_copy(
                src_ref=source,
                dst_ref=target,
                send_sem=send.at[index],
                recv_sem=recv.at[index],
                device_id={"core": zhi, "zhi": core},
                device_id_type=MESH,
            )

        def here():
            return pltpu.make_async_copy(source_here, target_here, local.at[index_here])

        @pl.when(crossing)
        def _():
            remote().start()

        @pl.when(jnp.logical_not(crossing))
        def _():
            here().start()

        def wait():
            @pl.when(crossing)
            def _():
                remote().wait()

            @pl.when(jnp.logical_not(crossing))
            def _():
                here().wait()

        return wait

    def lanes(block, size):
        return pl.ds(pl.multiple_of(block * size, size), size)

    def add(target, *terms):
        def step(index, carry):
            rows = pl.ds(pl.multiple_of(index * 64, 64), 64)
            value = sum(term[rows, :].astype(jnp.float32) for term in terms)
            target[rows, :] = value.astype(target.dtype)
            return carry

        lax.fori_loop(0, target.shape[0] // 64, step, 0)

    barrier = pltpu.get_barrier_semaphore()
    for axis in LINKS:
        pl.semaphore_signal(barrier, inc=1, device_id={axis: 1 - lax.axis_index(axis)}, device_id_type=MESH)

    @pl.when(crossing)
    def _():
        pl.semaphore_signal(barrier, inc=1, device_id={"core": zhi, "zhi": core}, device_id_type=MESH)

    pl.semaphore_wait(barrier, len(LINKS) + crossing.astype(jnp.int32))

    last = []
    half = self_q.shape[3] // 2

    def to_cores(values, out):
        part, width = values.shape[0] // 2, values.shape[1]
        there, here = lanes(1 - core, part), lanes(core, part)
        last.append(push(values.at[there], out.at[:, lanes(core, width)], "core"))
        last.append(keep(values.at[here], out.at[:, lanes(core, width)]))

    def planes_to_cores(values, qkv_out, out_out):
        part = values.shape[0] // 2
        there, here = lanes(1 - core, part), lanes(core, part)
        for plane in range(4):
            columns_of = pl.ds(plane * half, half)
            out = qkv_out.at[plane, :, lanes(core, half)] if plane < 3 else out_out.at[:, lanes(core, half)]
            last.append(push(values.at[there, columns_of], out, "core"))
            last.append(keep(values.at[here, columns_of], out))

    cross_keep = [keep(cross, cross_own), keep(cross_beyond, cross_got)]

    first, second = pl.ds(0, half), pl.ds(half, half)
    parts = (self_q, self_k, self_v, self_o)
    self_x, self_y, own_a, own_b = [], [], [], []
    for plane, partial in enumerate(parts):
        columns_of = pl.ds(plane * half, half)
        self_x.append(push(partial.at[:, 1 - x, :, first], self_got.at[0, :, :, columns_of], "x"))
        self_y.append(push(partial.at[1 - y, :, :, second], self_got.at[1, :, :, columns_of], "y"))
        own_a.append(keep(partial.at[:, x, :, first], self_own.at[0, :, :, columns_of]))
        own_b.append(keep(partial.at[y, :, :, second], self_own.at[1, :, :, columns_of]))
    enc_core = push(enc_part.at[1 - core], enc_got, "core")
    enc_keep = keep(enc_part.at[core], enc_own)

    to_cores(ff_in, ff_in_out)
    to_cores(ff_out, ff_out_out)

    small_first, small_size = 0, 32

    def small_send(stage):
        rows = small_size // 2
        away = small_first + (1 - lax.axis_index(AXES[stage])) * rows
        return push(small_sum.at[pl.ds(away, rows)], small_got[stage], AXES[stage])

    def small_add(stage, copy):
        copy.wait()
        rows, got = small_size // 2, small_got[stage]
        mine = small_first + lax.axis_index(AXES[stage]) * rows

        def step(index, carry):
            small_sum[mine + index] += got[index]
            return carry

        lax.fori_loop(0, rows, step, 0)
        return mine, rows

    keep(small, small_sum).wait()
    small_copy = small_send(0)
    for copy in cross_keep:
        copy.wait()

    def cross_step(target, which, *others):
        def step(index, carry):
            rows = pl.ds(pl.multiple_of(index * 64, 64), 64)
            for plane in range(4):
                source = pl.ds(pl.multiple_of((2 * plane + which) * half, half), half)
                columns_of = pl.ds(plane * half, half)
                value = cross_own[rows, source].astype(jnp.float32) + cross_got[rows, source].astype(jnp.float32)
                for other in others:
                    value += other[rows, columns_of].astype(jnp.float32)
                target[rows, columns_of] = value.astype(target.dtype)
            return carry

        lax.fori_loop(0, target.shape[0] // 64, step, 0)

    cross_step(cross_low, 1 - zlo)
    cross_zlo = push(cross_low, cross_got_low, "zlo")
    enc_core.wait()
    enc_keep.wait()
    add(enc_sum, enc_own.at[1 - zlo], enc_got.at[1 - zlo])
    enc_zlo = push(enc_sum, enc_far, "zlo")
    small_first, small_size = small_add(0, small_copy)
    small_copy = small_send(1)
    for copy in own_a + self_x:
        copy.wait()
    add(low_a, self_own.at[0, 1 - y], self_got.at[0, 1 - y])
    a_second = push(low_a, self_got_low.at[0], "y")
    for copy in own_b + self_y:
        copy.wait()
    add(low_b, self_own.at[1, 1 - x], self_got.at[1, 1 - x])
    b_second = push(low_b, self_got_low.at[1], "x")
    small_first, small_size = small_add(1, small_copy)
    small_copy = small_send(2)
    add(self_total.at[0], self_own.at[0, y], self_got.at[0, y])
    add(self_total.at[1], self_own.at[1, x], self_got.at[1, x])
    enc_zlo.wait()
    add(enc_low, enc_own.at[zlo], enc_got.at[zlo], enc_far)
    small_first, small_size = small_add(2, small_copy)
    small_copy = small_send(3)
    a_second.wait()
    add(self_total.at[0], self_total.at[0], self_got_low.at[0])
    b_second.wait()
    add(self_total.at[1], self_total.at[1], self_got_low.at[1])
    add(low_a, self_total.at[1 - zhi])
    self_zhi = push(low_a, self_last, "zhi")
    wait_enc = moving(enc_low, enc_out, enc_low, enc_out)
    cross_zlo.wait()
    cross_step(cross_total, zlo, cross_got_low)
    planes_to_cores(cross_total, cross_qkv_out, cross_out_out)
    small_first, small_size = small_add(3, small_copy)
    small_copy = small_send(4)
    self_zhi.wait()
    add(self_total.at[zhi], self_total.at[zhi], self_last)
    planes_to_cores(self_total.at[zhi], self_qkv_out, self_out_out)
    small_first, small_size = small_add(4, small_copy)
    keep(small_sum.at[small_first], small_out).wait()
    wait_enc()
    for copy in last:
        copy.wait()


def finish(ff_in, ff_out, cross, cross_beyond, self_parts, enc, small):
    rows, width = ff_in.shape
    part, half = self_parts[0].shape[2], self_parts[0].shape[3] // 2
    low_type, enc_shape = enc.dtype, enc.shape[2:]
    wide = 4 * half

    def full(*shape):
        return jax.ShapeDtypeStruct(shape, jnp.float32)

    shapes = [
        full(rows // 2, 2 * width),
        full(rows // 2, 2 * width),
        full(3, part // 2, 2 * half),
        full(part // 2, 2 * half),
        full(3, part // 2, 2 * half),
        full(part // 2, 2 * half),
        jax.ShapeDtypeStruct(enc_shape, low_type),
        jax.ShapeDtypeStruct(small.shape[1:], small.dtype),
    ]
    anywhere = pl.BlockSpec(memory_space=pl.ANY)
    return pl.pallas_call(
        finish_kernel,
        out_shape=shapes,
        in_specs=[anywhere] * 10,
        out_specs=[anywhere] * len(shapes),
        scratch_shapes=[
            pltpu.VMEM((part, 2 * wide), low_type),
            pltpu.VMEM((part, 2 * wide), low_type),
            pltpu.VMEM((part, wide), low_type),
            pltpu.VMEM((part, wide), low_type),
            pltpu.VMEM((part, wide), jnp.float32),
            pltpu.VMEM((2, *enc_shape), low_type),
            pltpu.VMEM((2, *enc_shape), low_type),
            pltpu.VMEM(enc_shape, low_type),
            pltpu.VMEM(enc_shape, low_type),
            pltpu.VMEM(enc_shape, low_type),
            pltpu.VMEM((2, 2, part, wide), low_type),
            pltpu.VMEM((2, 2, part, wide), low_type),
            pltpu.VMEM((part, wide), low_type),
            pltpu.VMEM((part, wide), low_type),
            pltpu.VMEM((2, part, wide), low_type),
            pltpu.VMEM((2, part, wide), jnp.float32),
            pltpu.VMEM((part, wide), low_type),
            pltpu.VMEM(small.shape, small.dtype),
        ]
        + [pltpu.VMEM((32 >> stage, *small.shape[1:]), small.dtype) for stage in range(1, 6)]
        + [pltpu.SemaphoreType.DMA((40,))] * 3,
        compiler_params=pltpu.CompilerParams(collective_id=1, has_side_effects=True),
        cost_estimate=pl.CostEstimate(flops=40_000_000_000, bytes_accessed=0, transcendentals=0),
    )(ff_in, ff_out, cross, cross_beyond, *self_parts, enc, small)


def trade(rows, axis, name="trade"):
    with jax.named_scope(name):
        return lax.ppermute(rows, axis, [(0, 1), (1, 0)])


def after(value, *others):
    return lax.optimization_barrier((value, *others))[0]


def regroup(rows, name="regroup"):
    with jax.named_scope("re_" + name):
        moved = lax.ppermute(rows, ("core", "zhi"), [(1, 2), (2, 1)])
        return jnp.where(lax.axis_index("core") == lax.axis_index("zhi"), rows, moved)


def in_order(index, own, other, axis):
    return jnp.concatenate(
        [jnp.where(index == 0, own, other), jnp.where(index == 0, other, own)], axis=axis
    )


def low(values):
    return values.astype(jnp.bfloat16)


def half_of(values, index, axis):
    size = values.shape[axis] // 2
    return lax.dynamic_slice_in_dim(values, index * size, size, axis)


def over_chips(rows):
    return lax.all_gather(rows, ("y", "x"), axis=0, tiled=True)


def sum_over_chips(partial):
    return lax.psum_scatter(partial, ("y", "x"), scatter_dimension=0, tiled=True)


def spread_rows(rows, name):
    beyond = trade(rows, "zlo", name + "_z")
    return (
        jnp.concatenate([rows, trade(rows, "core", name + "_c")], axis=0),
        jnp.concatenate([beyond, trade(beyond, "core", name + "_zc")], axis=0),
    )


def sum_rows(near, far, term, name):
    size = near.shape[0] // 2
    far_sum = term(far[:size]) + trade(low(term(far[size:])), "core", name + "_zc")
    from_far = trade(low(far_sum), "zlo", name + "_z")
    near_other = trade(low(term(near[size:])), "core", name + "_c")
    return term(near[:size]) + near_other + from_far


def fast_layer(
    tokens,
    enc_states,
    enc_len,
    cont_lengths,
    cotangent,
    self_qkv,
    self_out,
    cross_qkv,
    cross_out,
    ff_in,
    ff_out,
    head_bias,
    ff_bias,
    vec_params,
):
    core, zhi, zlo = lax.axis_index("core"), lax.axis_index("zhi"), lax.axis_index("zlo")
    scaling = HD**-0.5
    model = tokens.shape[1]
    segments = cont_lengths.shape[1]

    flat = jnp.concatenate([vec_params.reshape(-1), head_bias.reshape(-1), ff_bias]).astype(jnp.float32)
    sizes = (vec_params.size, head_bias.size, ff_bias.size)
    flat = jnp.pad(flat.reshape(-1, 128), ((0, 4), (0, 0)))
    token_rows, attn_rows, w_self, w_cross, hidden, enc_full, small = start_exchange(
        tokens,
        enc_states,
        jnp.concatenate([self_qkv, self_out.T[None]], axis=0),
        jnp.concatenate([cross_qkv, cross_out.T[None]], axis=0),
        ff_in,
        ff_out.T,
        flat,
    )
    w_self = w_self.reshape(4, model, -1)
    w_cross = over_chips(w_cross)
    cross_width = w_cross.shape[1] // 4
    hidden_beyond = trade(hidden, "zhi", "wh_zhi")
    w_qkv, w_so = jnp.concatenate([w_self[0], w_self[1], w_self[2]], axis=1), w_self[3]
    w_cq, w_ckv, w_co = jnp.split(w_cross, [cross_width, 3 * cross_width], axis=1)
    rows_of = model // 4
    width = w_self.shape[2]
    pairs, cross_pairs = width // PAIR, cross_width // PAIR
    enc_full = enc_full.reshape(-1, model)
    attn_near, attn_far = attn_rows[: attn_rows.shape[0] // 2], attn_rows[attn_rows.shape[0] // 2 :]
    small = small.reshape(8, 4, -1)
    vec_part, head_part, ff_part = jnp.split(
        small[:, :, : sum(sizes)], [sizes[0], sizes[0] + sizes[1]], axis=2
    )
    vectors = vec_part[:, 0].reshape(8, 9, -1).transpose(1, 0, 2).reshape(9, model)
    heads = head_part.reshape(8, 4, 4, -1).transpose(2, 1, 0, 3).reshape(4, 2, 2, 2, -1)
    self_bias = lax.dynamic_index_in_dim(
        lax.dynamic_index_in_dim(heads[:2], zlo, 2, False), core, 2, False
    ).reshape(2, -1)
    cross_bias = lax.dynamic_index_in_dim(heads[2:], core, 3, False).reshape(2, -1)
    hidden_bias = ff_part.transpose(1, 0, 2).reshape(2, 2, 2, -1)
    hidden_bias = lax.dynamic_index_in_dim(
        lax.dynamic_index_in_dim(hidden_bias, zlo, 1, False), core, 1, False
    ).reshape(-1)

    lengths = regroup(jnp.concatenate([cont_lengths[0], enc_len]))
    places = jnp.stack(
        [512 * ((core != block // 2) + 2 * (zlo != block % 2)) for block in range(4)]
    ).astype(jnp.int32)
    bounds = PROMPT + jnp.concatenate(
        [jnp.zeros((1,), jnp.int32), jnp.cumsum(lengths[:segments]).astype(jnp.int32)]
    )
    self_meta = jnp.concatenate([places, bounds])
    cross_meta = lengths[segments:]

    resid = token_rows.astype(jnp.float32)
    _, hat_one, inv_one = norm_forward(resid, vectors[0], vectors[3])
    qkv_bias = jnp.concatenate([self_bias[0], jnp.zeros((width,), jnp.float32), self_bias[1]])
    qkv_scale = jnp.concatenate([jnp.full((width,), scaling), jnp.ones((2 * width,))]).astype(jnp.float32)
    def project(rows):
        return low((product(rows, w_qkv) + qkv_bias) * qkv_scale)

    qkv = project(attn_rows)
    count = qkv.shape[0]
    self_plan = functools.partial(self_sections, segments=segments)
    mixed, self_lse = attend(self_plan, self_meta, qkv, 0, qkv, pairs, 2 * pairs, pairs, 1152)
    mixed = after(mixed, hidden_beyond)
    hidden = in_order(zhi, hidden, after(hidden_beyond, mixed), 2).transpose(1, 0, 2)
    w_hidden = over_chips(hidden.reshape(hidden.shape[0], -1))
    w_in, w_out = jnp.split(w_hidden, 2, axis=1)
    near, far = mixed[: count // 2], mixed[count // 2 :]
    so_far = low(
        product_right_t(far[: count // 4], w_so)
        + trade(low(product_right_t(far[count // 4 :], w_so)), "core", "so_zc")
    )
    so_near_other = low(product_right_t(near[count // 4 :], w_so))
    so_near = product_right_t(near[: count // 4], w_so)
    grad_rows = regroup(after(cotangent, mixed), "cotangent")
    cross_kv = low(
        product(after(enc_full, grad_rows, so_far), w_ckv)
        + jnp.concatenate([jnp.zeros((cross_width,), jnp.float32), cross_bias[1]])
    )
    branch = so_near + trade(so_near_other, "core", "so_c") + after(trade(so_far, "zlo", "so_z"), cross_kv)
    after_one = resid + (branch + vectors[6])

    cot_beyond = trade(after(grad_rows, after_one), "zlo", "cot_z")
    cot_near = jnp.concatenate([grad_rows, trade(grad_rows, "core", "cot_c")], axis=0)

    normed_mid, hat_two, inv_two = norm_forward(after_one, vectors[1], vectors[4])
    cross_low = low(normed_mid)
    cross_rows = jnp.concatenate([cross_low, trade(cross_low, "core", "cin")], axis=0)
    own_rows = cross_low.shape[0]
    cross_q = low((product(cross_rows, w_cq) + cross_bias[0]) * scaling)
    cross_plan = functools.partial(cross_sections, blocks=cross_q.shape[0] // BLOCK)
    cross_mixed, cross_lse = attend(
        cross_plan, cross_meta, cross_q, 0, cross_kv, 0, cross_pairs, cross_pairs, ENC
    )
    cross_mixed = after(cross_mixed, cot_beyond)
    other = trade(low(product_right_t(cross_mixed[own_rows:], w_co)), "core", "co_c")
    branch = product_right_t(cross_mixed[:own_rows], w_co) + other
    after_two = after_one + (branch + vectors[7])

    normed_out, hat_three, inv_three = norm_forward(after_two, vectors[2], vectors[5])
    mlp_in = low(normed_out)
    beyond = trade(mlp_in, "zlo", "mlp_z")
    mlp_near = jnp.concatenate([mlp_in, trade(mlp_in, "core", "mlp_c")], axis=0)
    act_near, dpre_near, sum_near = hidden_units(mlp_near, cot_near, w_hidden, hidden_bias[None])
    beyond = after(beyond, act_near)
    mlp_far = jnp.concatenate([beyond, trade(beyond, "core", "mlp_zc")], axis=0)
    cot_far = jnp.concatenate([cot_beyond, trade(cot_beyond, "core", "cot_zc")], axis=0)
    act_far, dpre_far, sum_far = hidden_units(mlp_far, cot_far, w_hidden, hidden_bias[None])
    gradient = grad_rows.astype(jnp.float32)
    bias_out_three = jnp.sum(gradient, axis=0)
    dmlp_far = low(
        product_right_t(dpre_far[:own_rows], w_in)
        + trade(low(product_right_t(dpre_far[own_rows:], w_in)), "core", "dmlp_zc")
    )
    mlp_term = product_right_t(dpre_near[:own_rows], w_in) + trade(
        low(product_right_t(dpre_near[own_rows:], w_in)), "core", "dmlp_c"
    )
    act_near, act_far = after(act_near, dmlp_far, mlp_term), after(act_far, dmlp_far, mlp_term)
    out_parts = [
        low(product_right_t(act_far[own_rows:], w_out)),
        product_right_t(act_far[:own_rows], w_out),
        low(product_right_t(act_near[own_rows:], w_out)),
        product_right_t(act_near[:own_rows], w_out),
    ]
    out_far = low(out_parts[1] + trade(out_parts[0], "core", "out_zc"))
    out_branch = out_parts[3] + trade(out_parts[2], "core", "out_c")
    grad_w_out = low(product_left_t(cot_near, act_near) + product_left_t(cot_far, act_far))
    mlp_near, mlp_far = after(mlp_near, grad_w_out), after(mlp_far, grad_w_out)
    grad_w_in = low(product_left_t(mlp_near, dpre_near) + product_left_t(mlp_far, dpre_far))
    mlp_term = mlp_term + after(trade(dmlp_far, "zlo", "dmlp_z"), grad_w_in, grad_w_out)
    out_far = trade(after(out_far, mlp_term), "zlo", "out_z")
    part, gain_three, shift_three = norm_backward(mlp_term, hat_three, inv_three, vectors[2])
    gradient = gradient + part

    grad_low = low(gradient)
    bias_out_two = jnp.sum(grad_low.astype(jnp.float32), axis=0)
    grad_both = jnp.concatenate([grad_low, trade(grad_low, "core", "e2")], axis=0)
    cross_mixed_grad = low(product(grad_both, w_co))
    cross_dq, cross_dk, cross_dv = attend_back(
        cross_plan,
        cross_meta,
        cross_q,
        0,
        cross_kv,
        0,
        cross_pairs,
        cross_mixed,
        cross_mixed_grad,
        cross_lse,
        cross_pairs,
        ENC,
    )
    cross_dq = after(cross_dq, out_far)
    other = trade(low(product_right_t(cross_dq[own_rows:], w_cq)), "core", "dcin")
    part, gain_two, shift_two = norm_backward(
        product_right_t(cross_dq[:own_rows], w_cq) + other, hat_two, inv_two, vectors[1]
    )
    gradient = gradient + part

    grad_low = low(gradient)
    bias_out_one = jnp.sum(grad_low.astype(jnp.float32), axis=0)
    def zhi_sum(partial, axis, name):
        mine, theirs = half_of(partial, zhi, axis), half_of(partial, 1 - zhi, axis)
        return mine.astype(jnp.float32) + trade(theirs, "zhi", name).astype(jnp.float32)

    beyond = trade(grad_low, "zlo", "e1_z")
    grad_near = jnp.concatenate([grad_low, trade(grad_low, "core", "e1_c")], axis=0)
    mixed_grad = low(product(grad_near, w_so))
    cross_parts = [
        low(product_left_t(cross_rows, after(cross_dq, grad_low))),
        low(product_left_t(enc_full, after(cross_dk, grad_low))),
        low(product_left_t(enc_full, after(cross_dv, grad_low))),
        low(product_left_t(after(grad_both, grad_low), cross_mixed)),
    ]
    grad_cross = jnp.concatenate(cross_parts, axis=1)
    layer_out = low(after_two + (out_branch + after(out_far, grad_low) + vectors[8]))
    beyond = after(beyond, mixed_grad, grad_cross, layer_out)
    cross_sum = sum_over_chips(grad_cross)
    grad_far = jnp.concatenate([beyond, trade(beyond, "core", "e1_zc")], axis=0)
    mixed_grad = jnp.concatenate([mixed_grad, low(product(grad_far, w_so))], axis=0)

    out_sum = zhi_sum(sum_over_chips(grad_w_out), 1, "go_zhi")
    in_sum = zhi_sum(sum_over_chips(grad_w_in), 1, "gi_zhi")
    dq, dk, dv = attend_back(
        self_plan, self_meta, qkv, 0, qkv, pairs, 2 * pairs, mixed, mixed_grad, self_lse, pairs, 1152
    )
    dq, dk, dv = after(dq, in_sum, out_sum), after(dk, in_sum, out_sum), after(dv, in_sum, out_sum)
    layer_out = regroup(after(layer_out, dq), "out")
    dqkv = jnp.concatenate([dq, dk, dv], axis=1)
    d_near, d_far = dqkv[: count // 2], dqkv[count // 2 :]
    dx_far = low(
        product_right_t(d_far[: count // 4], w_qkv)
        + trade(low(product_right_t(d_far[count // 4 :], w_qkv)), "core", "dx_zc")
    )
    dx = product_right_t(d_near[: count // 4], w_qkv) + trade(
        low(product_right_t(d_near[count // 4 :], w_qkv)), "core", "dx_c"
    )
    dq, dk, dv = after(dq, dx_far), after(dk, dx_far), after(dv, dx_far)
    self_parts = [
        low(product_left_t(attn_rows, dq)),
        low(product_left_t(attn_rows, dk)),
        low(product_left_t(attn_rows, dv)),
        low(product_left_t(grad_near, near) + product_left_t(grad_far, far)),
    ]
    enc_part = low(
        product_right_t(after(cross_dk, dq), w_ckv[:, :cross_width])
        + product_right_t(after(cross_dv, dq), w_ckv[:, cross_width:])
    )
    cross_sum = after(cross_sum, dq).reshape(rows_of, 4, 2, -1)
    cross_kept = half_of(cross_sum, zhi, 2).reshape(rows_of, -1)
    cross_beyond = trade(half_of(cross_sum, 1 - zhi, 2).reshape(rows_of, -1), "zhi", "gc_zhi")
    dx = dx + after(trade(dx_far, "zlo", "dx_z"), enc_part, layer_out, cross_beyond, *self_parts)
    part, gain_one, shift_one = norm_backward(dx, hat_one, inv_one, vectors[0])
    input_part = low(gradient + part)
    input_grad = regroup(input_part, "dgrad").astype(jnp.float32)

    bias_self_query = jnp.sum(dq.astype(jnp.float32), axis=0)
    bias_self_value = jnp.sum(dv.astype(jnp.float32), axis=0)
    bias_cross_query = jnp.sum(cross_dq.astype(jnp.float32), axis=0)
    bias_cross_value = jnp.sum(cross_dv.astype(jnp.float32), axis=0)
    grad_hidden_bias = (sum_near + sum_far)[0]
    vec_sums = jnp.stack(
        [
            gain_one,
            gain_two,
            gain_three,
            shift_one,
            shift_two,
            shift_three,
            bias_out_one,
            bias_out_two,
            bias_out_three,
        ]
    )
    at_zlo = (jnp.arange(2) == zlo).astype(jnp.float32)
    at_core = (jnp.arange(2) == core).astype(jnp.float32)
    quarter = (at_zlo[:, None] * at_core[None, :])[:, :, None]
    self_sums = jnp.stack([bias_self_query, bias_self_value]).reshape(2, 2, 1, 1, -1) * quarter
    cross_sums = jnp.stack([bias_cross_query, bias_cross_value]).reshape(2, 2, 2, 1, -1) * at_core[:, None]
    head_sums = jnp.concatenate([self_sums, cross_sums], axis=0)
    hidden_sums = grad_hidden_bias.reshape(2, 1, 1, -1) * quarter
    vec_sums = vec_sums.reshape(9, 8, -1).transpose(1, 0, 2).reshape(8, 1, -1)
    sums = jnp.concatenate(
        [
            jnp.broadcast_to(vec_sums, (8, 4, sizes[0])),
            head_sums.reshape(4, 4, 8, -1).transpose(2, 1, 0, 3).reshape(8, 4, -1),
            hidden_sums.reshape(4, 8, -1).transpose(1, 0, 2),
        ],
        axis=2,
    )
    sums = jnp.pad(after(sums, input_part).reshape(32, -1, 128), ((0, 0), (0, 4), (0, 0)))
    ff_in_grad, ff_out_grad, cross_qkv_grad, cross_out_grad, self_qkv_grad, self_out_grad, enc_grad, sums = finish(
        in_sum,
        out_sum,
        cross_kept,
        cross_beyond,
        [part.reshape(2, 2, rows_of, -1) for part in self_parts],
        enc_part.reshape(2, 2, -1, model),
        sums,
    )
    sums = sums.reshape(-1)[: sum(sizes)]
    vec_grad, head_grad, ff_bias_grad = jnp.split(sums, [sizes[0], sizes[0] + sizes[1]])
    return (
        layer_out,
        input_grad,
        enc_grad.astype(jnp.float32),
        self_qkv_grad,
        self_out_grad.T,
        cross_qkv_grad,
        cross_out_grad.T,
        ff_in_grad,
        ff_out_grad.T,
        head_grad.reshape(head_bias.shape),
        ff_bias_grad,
        vec_grad.reshape(vec_params.shape),
    )


def solution(mesh):
    fast = tuple(mesh.shape[axis] for axis in ("dp", "tensor")) == (8, 4)
    dp, tensor = (AXES[:3], AXES[3:]) if fast else (("dp",), ("tensor",))
    both = dp + tensor
    rows = P(both, None)
    qkv = P(None, dp, tensor)
    out = P(tensor, dp)
    in_specs = (
        rows,
        rows,
        P(dp),
        P(dp, None),
        rows,
        qkv,
        out,
        qkv,
        out,
        P(dp, tensor),
        out,
        P(None, tensor + dp),
        P(tensor + dp),
        P(None, dp),
    )
    out_specs = (
        rows,
        rows,
        rows,
        qkv,
        out,
        qkv,
        out,
        P(dp, tensor),
        out,
        P(None, tensor + dp),
        P(tensor + dp),
        P(None, dp),
    )
    if fast:
        mesh = Mesh(mesh.devices.reshape(2, 2, 2, 2, 2), AXES)
    return jax.shard_map(
        fast_layer if fast else shards, mesh=mesh, in_specs=in_specs, out_specs=out_specs, check_vma=False
    )
```

```python
import functools
import math

import jax
import jax.numpy as jnp
from jax import lax
from jax.experimental import pallas as pl
from jax.experimental.pallas import tpu as pltpu
from jax.sharding import Mesh
from jax.sharding import PartitionSpec as P

HD = 64
PROMPT = 1024
CONT_TOK = 1024
ENC = 512
BLOCK = 256
PAIR = 2 * HD
AXES = ("y", "x", "core", "zhi", "zlo")


def lane_half():
    return lax.broadcasted_iota(jnp.int32, (1, PAIR), 1) < HD


def one_head(rows, head):
    keep = lane_half() if head == 0 else jnp.logical_not(lane_half())
    return rows * jnp.where(keep, 1.0, 0.0).astype(rows.dtype)


def dot_nt(left, right):
    return lax.dot_general(left, right, (((1,), (1,)), ((), ())), preferred_element_type=jnp.float32)


def dot_nn(left, right):
    return jnp.dot(left, right, preferred_element_type=jnp.float32)


def dot_tn(left, right):
    return lax.dot_general(left, right, (((0,), (0,)), ((), ())), preferred_element_type=jnp.float32)


def self_sections(meta_ref, segments):
    def at(block):
        return pl.multiple_of(meta_ref[block], 512)

    def place(index):
        return pl.multiple_of(meta_ref[index >> 1] + (index & 1) * BLOCK, BLOCK)

    def causal(row, col):
        return col <= row

    def banded(row, col):
        start = jnp.full(row.shape, meta_ref[4], jnp.int32)
        for segment in range(1, segments):
            bound = meta_ref[4 + segment]
            start = jnp.where(row >= bound, bound, start)
        return (col <= row) & (col >= start)

    def early(index):
        return [(at(0), 512, 0, causal)]

    def middle(index):
        return [(at(0), 512, 0, None), (at(1), 512, 512, causal)]

    def late(index):
        return [
            (at(0), 512, 0, None),
            (at(1), 512, 512, None),
            (place(index - 1), BLOCK, (index - 1) * BLOCK, banded),
            (place(index), BLOCK, index * BLOCK, banded),
        ]

    return place, ((0, 2, early), (2, 4, middle), (4, 8, late))


def cross_sections(meta_ref, blocks):
    def place(index):
        return pl.multiple_of(index * BLOCK, BLOCK)

    def usable(row, col):
        return col < meta_ref[0]

    def every(index):
        return [(0, ENC, 0, usable)]

    return place, ((0, blocks, every),)


def forward_kernel(sections, meta_ref, q_ref, k_ref, v_ref, o_ref, lse_ref):
    place, ranges = sections(meta_ref)

    for low, high, parts_of in ranges:

        def step(index, carry, parts_of=parts_of):
            rows = pl.ds(place(index), BLOCK)
            parts = parts_of(index)
            queries = q_ref[rows, :]
            row = index * BLOCK + lax.broadcasted_iota(jnp.int32, (BLOCK, 1), 0)
            allowed = [
                None if rule is None else rule(row, first + lax.broadcasted_iota(jnp.int32, (1, size), 1))
                for _, size, first, rule in parts
            ]
            outs, totals = [], []
            for head in range(2):
                query = one_head(queries, head)
                scores = []
                for (where, size, _, _), ok in zip(parts, allowed):
                    score = dot_nt(query, k_ref[pl.ds(where, size), :])
                    scores.append(score if ok is None else jnp.where(ok, score, -1e30))
                top = functools.reduce(jnp.maximum, [jnp.max(s, axis=1, keepdims=True) for s in scores])
                exps = [jnp.exp(s - top) for s in scores]
                total = sum(jnp.sum(e, axis=1, keepdims=True) for e in exps)
                mixed = sum(
                    dot_nn(e.astype(jnp.bfloat16), v_ref[pl.ds(where, size), :])
                    for (where, size, _, _), e in zip(parts, exps)
                )
                outs.append(mixed * (1.0 / total))
                totals.append(top + jnp.log(total))
            o_ref[rows, :] = jnp.where(lane_half(), outs[0], outs[1]).astype(o_ref.dtype)
            lse_ref[rows, :] = jnp.where(lane_half(), totals[0], totals[1])
            return carry

        lax.fori_loop(low, high, step, 0)


def backward_kernel(
    sections, meta_ref, q_ref, k_ref, v_ref, o_ref, do_ref, lse_ref, dq_ref, dk_ref, dv_ref, dk_sum, dv_sum
):
    place, ranges = sections(meta_ref)
    dk_sum[...] = jnp.zeros_like(dk_sum)
    dv_sum[...] = jnp.zeros_like(dv_sum)

    for low, high, parts_of in ranges:

        def step(index, carry, parts_of=parts_of):
            rows = pl.ds(place(index), BLOCK)
            parts = parts_of(index)
            queries, grads = q_ref[rows, :], do_ref[rows, :]
            row = index * BLOCK + lax.broadcasted_iota(jnp.int32, (1, BLOCK), 1)
            allowed = [
                None if rule is None else rule(row, first + lax.broadcasted_iota(jnp.int32, (size, 1), 0))
                for _, size, first, rule in parts
            ]
            logs = jnp.transpose(lse_ref[rows, :])
            spread = jnp.transpose(grads.astype(jnp.float32) * o_ref[rows, :].astype(jnp.float32))
            key_parts = [k_ref[pl.ds(where, size), :] for where, size, _, _ in parts]
            value_parts = [v_ref[pl.ds(where, size), :] for where, size, _, _ in parts]
            query_grads = []
            for head in range(2):
                query, grad = one_head(queries, head), one_head(grads, head)
                log = logs[head * HD : head * HD + 1, :]
                delta = jnp.sum(spread[head * HD : (head + 1) * HD, :], axis=0, keepdims=True)
                query_grad = None
                for (where, size, _, _), ok, keys, values in zip(parts, allowed, key_parts, value_parts):
                    score = dot_nt(keys, query)
                    if ok is not None:
                        score = jnp.where(ok, score, -1e30)
                    probs = jnp.exp(score - log)
                    score_grad = (probs * (dot_nt(values, grad) - delta)).astype(jnp.bfloat16)
                    dv_sum[pl.ds(where, size), :] += dot_nn(probs.astype(jnp.bfloat16), grad)
                    dk_sum[pl.ds(where, size), :] += dot_nn(score_grad, query)
                    term = dot_tn(score_grad, keys)
                    query_grad = term if query_grad is None else query_grad + term
                query_grads.append(query_grad)
            both = jnp.where(lane_half(), query_grads[0], query_grads[1])
            dq_ref[rows, :] = both.astype(jnp.bfloat16) * jnp.asarray(HD**-0.5, jnp.bfloat16)
            return carry

        lax.fori_loop(low, high, step, 0)
    dk_ref[...] = dk_sum[...].astype(dk_ref.dtype)
    dv_ref[...] = dv_sum[...].astype(dv_ref.dtype)


def columns(rows, first):
    return pl.BlockSpec((rows, PAIR), lambda pair, meta: (0, first + pair))


def attend(sections, meta, q, q_at, keys, k_at, v_at, pairs, weight):
    count, key_rows = q.shape[0], keys.shape[0]
    return pl.pallas_call(
        functools.partial(forward_kernel, sections),
        grid_spec=pltpu.PrefetchScalarGridSpec(
            num_scalar_prefetch=1,
            grid=(pairs,),
            in_specs=[columns(count, q_at), columns(key_rows, k_at), columns(key_rows, v_at)],
            out_specs=[columns(count, 0), columns(count, 0)],
        ),
        out_shape=[
            jax.ShapeDtypeStruct((count, pairs * PAIR), jnp.bfloat16),
            jax.ShapeDtypeStruct((count, pairs * PAIR), jnp.float32),
        ],
        cost_estimate=pl.CostEstimate(
            flops=2 * 4 * 4 * count * weight * pairs * PAIR,
            bytes_accessed=10 * count * pairs * PAIR,
            transcendentals=2 * pairs * count * weight,
        ),
    )(meta, q, keys, keys)


def attend_back(sections, meta, q, q_at, keys, k_at, v_at, out, out_grad, lse, pairs, weight):
    count, key_rows = q.shape[0], keys.shape[0]
    return pl.pallas_call(
        functools.partial(backward_kernel, sections),
        grid_spec=pltpu.PrefetchScalarGridSpec(
            num_scalar_prefetch=1,
            grid=(pairs,),
            in_specs=[
                columns(count, q_at),
                columns(key_rows, k_at),
                columns(key_rows, v_at),
                columns(count, 0),
                columns(count, 0),
                columns(count, 0),
            ],
            out_specs=[columns(count, 0), columns(key_rows, 0), columns(key_rows, 0)],
            scratch_shapes=[pltpu.VMEM((key_rows, PAIR), jnp.float32)] * 2,
        ),
        out_shape=[
            jax.ShapeDtypeStruct((count, pairs * PAIR), jnp.bfloat16),
            jax.ShapeDtypeStruct((key_rows, pairs * PAIR), jnp.bfloat16),
            jax.ShapeDtypeStruct((key_rows, pairs * PAIR), jnp.bfloat16),
        ],
        cost_estimate=pl.CostEstimate(
            flops=5 * 4 * 4 * count * weight * pairs * PAIR,
            bytes_accessed=20 * count * pairs * PAIR,
            transcendentals=2 * pairs * count * weight,
        ),
    )(meta, q, keys, keys, out, out_grad, lse)


EPSILON = 1e-05
MASKED = 1e30
GELU_C = math.sqrt(2.0 / math.pi)
GELU_A = 0.044715


def gelu_value(values):
    inner = jnp.tanh(GELU_C * (values + GELU_A * values * values * values))
    return 0.5 * values * (1.0 + inner)


def gelu_slope(values):
    inner = jnp.tanh(GELU_C * (values + GELU_A * values * values * values))
    return 0.5 * (1.0 + inner) + 0.5 * values * (1.0 - inner * inner) * GELU_C * (
        1.0 + 3.0 * GELU_A * values * values
    )


def norm_forward(values, gain_vec, shift_vec):
    row_mean = jnp.mean(values, axis=1, keepdims=True)
    centred = values - row_mean
    inverse = lax.rsqrt(jnp.mean(centred * centred, axis=1, keepdims=True) + EPSILON)
    normed = centred * inverse
    return (normed * gain_vec + shift_vec, normed, inverse)


def norm_backward(gradient, normed, inverse, gain_vec):
    scaled = gradient * gain_vec
    inner = (
        scaled
        - jnp.mean(scaled, axis=1, keepdims=True)
        - normed * jnp.mean(scaled * normed, axis=1, keepdims=True)
    )
    return (inner * inverse, jnp.sum(gradient * normed, axis=0), jnp.sum(gradient, axis=0))


def product(left, right):
    return jnp.dot(left, right, preferred_element_type=jnp.float32)


def product_left_t(left, right):
    return lax.dot_general(
        left, right, (((0,), (0,)), ((), ())), preferred_element_type=jnp.float32
    )


def product_right_t(left, right):
    return lax.dot_general(
        left, right, (((1,), (1,)), ((), ())), preferred_element_type=jnp.float32
    )


def attend_forward(queries, key_rows, value_rows, rule, block_rows):
    seq_rows, local_width = queries.shape
    local_heads = local_width // HD
    query_blocks = queries.reshape(seq_rows // block_rows, block_rows, local_heads, HD)
    key_heads = key_rows.reshape(-1, local_heads, HD)
    value_heads = value_rows.reshape(-1, local_heads, HD)
    block_starts = jnp.arange(seq_rows // block_rows, dtype=jnp.int32) * block_rows

    def attend_block(pieces):
        query_block, offset = pieces
        scores = jnp.einsum(
            "qhd,khd->hqk", query_block, key_heads, preferred_element_type=jnp.float32
        )
        scores = jnp.where(rule(offset, block_rows)[None], scores, -MASKED)
        row_max = jnp.max(scores, axis=2, keepdims=True)
        exponent = jnp.exp(scores - row_max)
        row_total = jnp.sum(exponent, axis=2, keepdims=True)
        probs_low = (exponent / row_total).astype(jnp.bfloat16)
        mixed = jnp.einsum(
            "hqk,khd->qhd", probs_low, value_heads, preferred_element_type=jnp.float32
        )
        return (
            mixed.astype(jnp.bfloat16).reshape(block_rows, local_width),
            (row_max + jnp.log(row_total))[:, :, 0],
        )

    outputs, log_total = lax.map(attend_block, (query_blocks, block_starts))
    return (outputs.reshape(seq_rows, local_width), log_total)


def attend_backward(queries, key_rows, value_rows, out_grad, log_total, rule, block_rows):
    seq_rows, local_width = queries.shape
    local_heads = local_width // HD
    key_count = key_rows.shape[0]
    query_blocks = queries.reshape(seq_rows // block_rows, block_rows, local_heads, HD)
    grad_blocks = out_grad.reshape(seq_rows // block_rows, block_rows, local_heads, HD)
    key_heads = key_rows.reshape(key_count, local_heads, HD)
    value_heads = value_rows.reshape(key_count, local_heads, HD)
    block_starts = jnp.arange(seq_rows // block_rows, dtype=jnp.int32) * block_rows

    def back_block(running, pieces):
        key_sum, value_sum = running
        query_block, grad_block, block_total, offset = pieces
        scores = jnp.einsum(
            "qhd,khd->hqk", query_block, key_heads, preferred_element_type=jnp.float32
        )
        probs = jnp.where(
            rule(offset, block_rows)[None], jnp.exp(scores - block_total[:, :, None]), 0.0
        )
        probs_low = probs.astype(jnp.bfloat16)
        prob_grad = jnp.einsum(
            "qhd,khd->hqk", grad_block, value_heads, preferred_element_type=jnp.float32
        )
        row_delta = jnp.sum(probs * prob_grad, axis=2, keepdims=True)
        score_grad = (probs * (prob_grad - row_delta)).astype(jnp.bfloat16)
        query_grad = jnp.einsum(
            "hqk,khd->qhd", score_grad, key_heads, preferred_element_type=jnp.float32
        )
        key_sum = key_sum + jnp.einsum(
            "hqk,qhd->khd", score_grad, query_block, preferred_element_type=jnp.float32
        )
        value_sum = value_sum + jnp.einsum(
            "hqk,qhd->khd", probs_low, grad_block, preferred_element_type=jnp.float32
        )
        return (
            (key_sum, value_sum),
            query_grad.astype(jnp.bfloat16).reshape(block_rows, local_width),
        )

    zero_sum = jnp.zeros((key_count, local_heads, HD), jnp.float32)
    (key_sum, value_sum), query_grads = lax.scan(
        back_block, (zero_sum, zero_sum), (query_blocks, grad_blocks, log_total, block_starts)
    )
    return (
        query_grads.reshape(seq_rows, local_width),
        key_sum.astype(jnp.bfloat16).reshape(key_count, local_width),
        value_sum.astype(jnp.bfloat16).reshape(key_count, local_width),
    )


def attend_groups(queries, key_rows, value_rows, rules, block_rows):
    results, totals = ([], [])
    for which_group, rule in enumerate(rules):
        mixed, log_total = attend_forward(queries, key_rows, value_rows, rule, block_rows)
        results.append(mixed)
        totals.append(log_total)
    return (results[0], totals)


def back_groups(queries, key_rows, value_rows, out_grad, totals, rules, block_rows):
    query_list, key_list, value_list = ([], [], [])
    for which_group, rule in enumerate(rules):
        query_grad, key_grad, value_grad = attend_backward(
            queries, key_rows, value_rows, out_grad, totals[which_group], rule, block_rows
        )
        query_list.append(query_grad)
        key_list.append(key_grad)
        value_list.append(value_grad)
    return (query_list[0], key_list[0], value_list[0])


def shards(
    tokens,
    enc_states,
    enc_len,
    cont_lengths,
    cotangent,
    self_qkv,
    self_out,
    cross_qkv,
    cross_out,
    ff_in,
    ff_out,
    head_bias,
    ff_bias,
    vec_params,
):
    gathered = (
        lax.all_gather(self_qkv, "dp", axis=1, tiled=True),
        lax.all_gather(self_out, "dp", axis=1, tiled=True),
        lax.all_gather(cross_qkv, "dp", axis=1, tiled=True),
        lax.all_gather(cross_out, "dp", axis=1, tiled=True),
        lax.all_gather(ff_in, "dp", axis=0, tiled=True),
        lax.all_gather(ff_out, "dp", axis=1, tiled=True),
        lax.all_gather(head_bias, "dp", axis=1, tiled=True),
        lax.all_gather(ff_bias, "dp", axis=0, tiled=True),
        lax.all_gather(vec_params, "dp", axis=1, tiled=True),
    )
    (
        w_self,
        w_self_out,
        w_cross,
        w_cross_out,
        w_hidden_in,
        w_hidden_out,
        bias_heads,
        bias_hidden,
        vectors,
    ) = gathered
    vectors = vectors.astype(jnp.float32)
    bias_heads = bias_heads.astype(jnp.float32)
    bias_hidden = bias_hidden.astype(jnp.float32)
    seq_rows = PROMPT + CONT_TOK
    block_rows = min(512, seq_rows)
    scaling = HD ** (-0.5)
    rows_dev = tokens.shape[0]

    def self_rule(which_group):
        bounds = PROMPT + jnp.cumsum(cont_lengths[which_group])
        positions = jnp.arange(seq_rows, dtype=jnp.int32)
        segment = jnp.sum((positions[:, None] >= bounds[None, :]).astype(jnp.int32), axis=1)

        def self_allowed(offset, number):
            row_ids = offset + jnp.arange(number, dtype=jnp.int32)
            row_segment = lax.dynamic_slice_in_dim(segment, offset, number)
            return (positions[None, :] <= row_ids[:, None]) & (
                (positions[None, :] < PROMPT) | (segment[None, :] == row_segment[:, None])
            )

        return self_allowed

    def cross_rule(which_group):
        usable = jnp.arange(ENC, dtype=jnp.int32) < enc_len[which_group]

        def cross_allowed(offset, number):
            return jnp.broadcast_to(usable[None, :], (number, ENC))

        return cross_allowed

    def spread(low_rows):
        return lax.all_gather(low_rows, "tensor", axis=0, tiled=True)

    def head_branch(values, weight):

        def term(offset, number):
            return product(values, weight)

        return lax.psum_scatter(
            term(jnp.int32(0), rows_dev * lax.axis_size("tensor")),
            "tensor",
            scatter_dimension=0,
            tiled=True,
        )

    def widen(low_rows):
        return lax.all_gather(low_rows, "tensor", axis=0, tiled=True)

    def narrow(term):
        return lax.psum_scatter(
            term(jnp.int32(0), rows_dev * lax.axis_size("tensor")),
            "tensor",
            scatter_dimension=0,
            tiled=True,
        )

    self_rules = [self_rule(0)]
    cross_rules = [cross_rule(0)]
    resid = tokens.astype(jnp.float32)
    enc_full = lax.all_gather(enc_states, "tensor", axis=0, tiled=True)
    normed_in, hat_one, inv_one = norm_forward(resid, vectors[0], vectors[3])
    attn_low = normed_in.astype(jnp.bfloat16)
    attn_full = spread(attn_low)
    queries = ((product(attn_full, w_self[0]) + bias_heads[0]) * scaling).astype(jnp.bfloat16)
    key_rows = product(attn_full, w_self[1]).astype(jnp.bfloat16)
    value_rows = (product(attn_full, w_self[2]) + bias_heads[1]).astype(jnp.bfloat16)
    mixed, self_totals = attend_groups(queries, key_rows, value_rows, self_rules, block_rows)
    after_one = resid + (head_branch(mixed, w_self_out) + vectors[6])
    normed_mid, hat_two, inv_two = norm_forward(after_one, vectors[1], vectors[4])
    cross_low = normed_mid.astype(jnp.bfloat16)
    cross_full = spread(cross_low)
    cross_queries = ((product(cross_full, w_cross[0]) + bias_heads[2]) * scaling).astype(
        jnp.bfloat16
    )
    cross_keys = product(enc_full, w_cross[1]).astype(jnp.bfloat16)
    cross_values = (product(enc_full, w_cross[2]) + bias_heads[3]).astype(jnp.bfloat16)
    cross_mixed, cross_totals = attend_groups(
        cross_queries, cross_keys, cross_values, cross_rules, block_rows
    )
    after_two = after_one + (head_branch(cross_mixed, w_cross_out) + vectors[7])
    normed_out, hat_three, inv_three = norm_forward(after_two, vectors[2], vectors[5])
    hidden_low = normed_out.astype(jnp.bfloat16)
    hidden_full = spread(hidden_low)
    pre_act = product(hidden_full, w_hidden_in) + bias_hidden
    activation = gelu_value(pre_act).astype(jnp.bfloat16)

    def term(offset, number):
        return product(activation, w_hidden_out)

    after_three = after_two + (
        lax.psum_scatter(
            term(jnp.int32(0), rows_dev * lax.axis_size("tensor")),
            "tensor",
            scatter_dimension=0,
            tiled=True,
        )
        + vectors[8]
    )
    layer_out = after_three.astype(jnp.bfloat16)
    gradient = cotangent.astype(jnp.float32)
    grad_low = gradient.astype(jnp.bfloat16)
    bias_out_three = jnp.sum(grad_low.astype(jnp.float32), axis=0)
    grad_full = widen(grad_low)
    act_grad = (product_right_t(grad_full, w_hidden_out) * gelu_slope(pre_act)).astype(jnp.bfloat16)
    grad_hidden_out = product_left_t(activation, grad_full)
    grad_hidden_in = product_left_t(hidden_full, act_grad)
    grad_bias_hidden = jnp.sum(act_grad.astype(jnp.float32), axis=0)

    def hidden_term(offset, number):
        return product_right_t(act_grad, w_hidden_in)

    input_part, gain_three, shift_three = norm_backward(
        narrow(hidden_term), hat_three, inv_three, vectors[2]
    )
    gradient = gradient + input_part
    grad_low = gradient.astype(jnp.bfloat16)
    bias_out_two = jnp.sum(grad_low.astype(jnp.float32), axis=0)
    grad_full = widen(grad_low)
    grad_cross_out = product_left_t(cross_mixed, grad_full)
    mixed_grad = product_right_t(grad_full, w_cross_out).astype(jnp.bfloat16)
    cross_query_grad, cross_key_grad, cross_value_grad = back_groups(
        cross_queries, cross_keys, cross_values, mixed_grad, cross_totals, cross_rules, block_rows
    )
    grad_cross = jnp.stack(
        [
            product_left_t(cross_full, cross_query_grad) * scaling,
            product_left_t(enc_full, cross_key_grad),
            product_left_t(enc_full, cross_value_grad),
        ]
    )
    bias_cross_query = jnp.sum(cross_query_grad.astype(jnp.float32), axis=0) * scaling
    bias_cross_value = jnp.sum(cross_value_grad.astype(jnp.float32), axis=0)
    enc_grad = lax.psum_scatter(
        product_right_t(cross_key_grad, w_cross[1]) + product_right_t(cross_value_grad, w_cross[2]),
        "tensor",
        scatter_dimension=0,
        tiled=True,
    )

    def cross_term(offset, number):
        return product_right_t(cross_query_grad, w_cross[0]) * scaling

    input_part, gain_two, shift_two = norm_backward(
        narrow(cross_term), hat_two, inv_two, vectors[1]
    )
    gradient = gradient + input_part
    grad_low = gradient.astype(jnp.bfloat16)
    bias_out_one = jnp.sum(grad_low.astype(jnp.float32), axis=0)
    grad_full = widen(grad_low)
    grad_self_out = product_left_t(mixed, grad_full)
    self_mixed_grad = product_right_t(grad_full, w_self_out).astype(jnp.bfloat16)
    query_grad, key_grad, value_grad = back_groups(
        queries, key_rows, value_rows, self_mixed_grad, self_totals, self_rules, block_rows
    )
    grad_self = jnp.stack(
        [
            product_left_t(attn_full, query_grad) * scaling,
            product_left_t(attn_full, key_grad),
            product_left_t(attn_full, value_grad),
        ]
    )
    bias_self_query = jnp.sum(query_grad.astype(jnp.float32), axis=0) * scaling
    bias_self_value = jnp.sum(value_grad.astype(jnp.float32), axis=0)

    def self_term(offset, number):
        return (
            product_right_t(query_grad, w_self[0]) * scaling
            + product_right_t(key_grad, w_self[1])
            + product_right_t(value_grad, w_self[2])
        )

    input_part, gain_one, shift_one = norm_backward(narrow(self_term), hat_one, inv_one, vectors[0])
    input_grad = gradient + input_part
    vector_grads = jnp.stack(
        [
            gain_one,
            gain_two,
            gain_three,
            shift_one,
            shift_two,
            shift_three,
            bias_out_one,
            bias_out_two,
            bias_out_three,
        ]
    )
    head_grads = jnp.stack([bias_self_query, bias_self_value, bias_cross_query, bias_cross_value])
    results = (
        lax.psum_scatter(grad_self, "dp", scatter_dimension=1, tiled=True),
        lax.psum_scatter(grad_self_out, "dp", scatter_dimension=1, tiled=True),
        lax.psum_scatter(grad_cross, "dp", scatter_dimension=1, tiled=True),
        lax.psum_scatter(grad_cross_out, "dp", scatter_dimension=1, tiled=True),
        lax.psum_scatter(grad_hidden_in, "dp", scatter_dimension=0, tiled=True),
        lax.psum_scatter(grad_hidden_out, "dp", scatter_dimension=1, tiled=True),
        lax.psum_scatter(head_grads, "dp", scatter_dimension=1, tiled=True),
        lax.psum_scatter(grad_bias_hidden, "dp", scatter_dimension=0, tiled=True),
        lax.psum_scatter(vector_grads, "dp", scatter_dimension=1, tiled=True),
    )
    vector_total = lax.psum(results[8], "tensor")
    return (
        layer_out,
        input_grad,
        enc_grad,
        results[0],
        results[1],
        results[2],
        results[3],
        results[4],
        results[5],
        results[6],
        results[7],
        vector_total,
    )


def hidden_kernel(x0_ref, x1_ref, e0_ref, e1_ref, w_in_ref, w_out_ref, bias_ref, act_ref, grad_ref, sum_ref):
    chunk = 256
    sum_ref[...] = jnp.zeros_like(sum_ref)
    count = x0_ref.shape[0]

    for which, (x_ref, e_ref) in enumerate(((x0_ref, e0_ref), (x1_ref, e1_ref))):

        def step(index, carry, which=which, x_ref=x_ref, e_ref=e_ref):
            rows = pl.ds(pl.multiple_of(index * chunk, chunk), chunk)
            out_rows = pl.ds(pl.multiple_of(which * count + index * chunk, chunk), chunk)
            value = dot_nn(x_ref[rows, :], w_in_ref[...]) + bias_ref[...]
            upper = dot_nn(e_ref[rows, :], w_out_ref[...])
            square = value * value
            inner = jnp.tanh(value * (GELU_C + (GELU_C * GELU_A) * square))
            half = 0.5 + 0.5 * inner
            act_ref[out_rows, :] = (value * half).astype(act_ref.dtype)
            slope = half + (value * (half * (1.0 - inner))) * (GELU_C + (3.0 * GELU_C * GELU_A) * square)
            grad = (upper * slope).astype(grad_ref.dtype)
            grad_ref[out_rows, :] = grad
            sum_ref[...] += jnp.sum(grad.astype(jnp.float32), axis=0, keepdims=True)
            return carry

        lax.fori_loop(0, count // chunk, step, 0, unroll=2)


def hidden_units(rows, grads, weights, bias, tile=512):
    count, model = rows[0].shape
    width = weights.shape[1] // 2
    tiles = width // tile
    whole = pl.BlockSpec((count, model), lambda i: (0, 0))
    weight = pl.BlockSpec((model, tile), lambda i: (0, i))
    weight_out = pl.BlockSpec((model, tile), lambda i: (0, tiles + i))
    line = pl.BlockSpec((1, tile), lambda i: (0, i))
    out = pl.BlockSpec((2 * count, tile), lambda i: (0, i))
    return pl.pallas_call(
        hidden_kernel,
        grid=(tiles,),
        in_specs=[whole] * 4 + [weight, weight_out, line],
        out_specs=[out, out, line],
        out_shape=[
            jax.ShapeDtypeStruct((2 * count, width), jnp.bfloat16),
            jax.ShapeDtypeStruct((2 * count, width), jnp.bfloat16),
            jax.ShapeDtypeStruct((1, width), jnp.float32),
        ],
        cost_estimate=pl.CostEstimate(
            flops=8 * count * model * width,
            bytes_accessed=4 * (2 * count * model + model * width + 2 * count * width),
            transcendentals=2 * count * width,
        ),
    )(*rows, *grads, weights, weights, bias)


MESH = pl.DeviceIdType.MESH


def weight_grad_kernel(*refs):
    rows_ref, refs = refs[0], refs[1:]
    sides, (rows_out, *outs, turned, send, recv) = (refs[:6], refs[6:12]), refs[12:]
    count, depth = sides[0][0].shape[0], sides[0][4].shape[0]
    step_of, tiles = pl.program_id(0), pl.num_programs(0) // 2

    def copy():
        return pltpu.make_async_remote_copy(
            src_ref=rows_ref,
            dst_ref=rows_out,
            send_sem=send,
            recv_sem=recv,
            device_id={"zlo": 1 - lax.axis_index("zlo")},
            device_id_type=MESH,
        )

    @pl.when(step_of == 0)
    def _():
        barrier = pltpu.get_barrier_semaphore()
        pl.semaphore_signal(
            barrier, inc=1, device_id={"zlo": 1 - lax.axis_index("zlo")}, device_id_type=MESH
        )
        pl.semaphore_wait(barrier, 1)
        copy().start()

    for half, ((x0_ref, x1_ref, x2_ref, x3_ref, near_ref, far_ref), out_ref) in enumerate(zip(sides, outs)):

        @pl.when(step_of == half * tiles)
        def _(blocks=(x0_ref, x1_ref, x2_ref, x3_ref)):
            for which, x_ref in enumerate(blocks):
                turned[:, which * count : (which + 1) * count] = jnp.transpose(x_ref[...])

        @pl.when(step_of // tiles == half)
        def _(near_ref=near_ref, far_ref=far_ref, out_ref=out_ref):
            def step(index, carry):
                rows = pl.ds(pl.multiple_of(index * 256, 256), 256)
                total = dot_nn(turned[rows, :depth], near_ref[...]) + dot_nn(turned[rows, depth:], far_ref[...])
                out_ref[rows, :] = total.astype(out_ref.dtype)
                return carry

            lax.fori_loop(0, out_ref.shape[0] // 256, step, 0, unroll=2)

    @pl.when(step_of == 2 * tiles - 1)
    def _():
        copy().wait()


def weight_grads(rows, first, second, collective_id, tile=512):
    blocks, near, _ = first
    (count, model), (depth, width) = blocks[0].shape, near.shape
    tiles = width // tile
    anywhere = pl.BlockSpec(memory_space=pl.ANY)
    whole = pl.BlockSpec((count, model), lambda i: (0, 0))

    def early(size):
        return pl.BlockSpec((size, tile), lambda i: (0, jnp.minimum(i, tiles - 1)))

    def late(size):
        return pl.BlockSpec((size, tile), lambda i: (0, jnp.maximum(i - tiles, 0)))

    shape = jax.ShapeDtypeStruct((model, width), near.dtype)
    return pl.pallas_call(
        weight_grad_kernel,
        grid=(2 * tiles,),
        in_specs=[anywhere] + [whole] * 4 + [early(depth)] * 2 + [whole] * 4 + [late(depth)] * 2,
        out_specs=[anywhere, early(model), late(model)],
        out_shape=[jax.ShapeDtypeStruct(rows.shape, rows.dtype), shape, shape],
        scratch_shapes=[
            pltpu.VMEM((model, 4 * count), near.dtype),
            pltpu.SemaphoreType.DMA,
            pltpu.SemaphoreType.DMA,
        ],
        compiler_params=pltpu.CompilerParams(collective_id=collective_id, has_side_effects=True),
        cost_estimate=pl.CostEstimate(flops=16 * count * model * width, bytes_accessed=0, transcendentals=0),
    )(rows, *first[0], *first[1:], *second[0], *second[1:])


LINKS = ("core", "x", "y", "zhi", "zlo")


def start_kernel(
    tokens,
    enc,
    w_self,
    w_cross,
    w_in,
    w_out,
    small,
    token_rows,
    attn,
    g_self,
    cross_rows,
    hidden,
    enc_full,
    small_all,
    held,
    normed,
    gathered,
    send,
    recv,
    local,
):
    y, x, core, zhi, zlo = (lax.axis_index(axis) for axis in AXES)
    crossing = core != zhi
    rows = tokens.shape[0]
    part = w_self.shape[1]
    counts = {"sent": 0, "local": 0}

    def push(source, target, axis):
        index = counts["sent"]
        counts["sent"] += 1
        copy = pltpu.make_async_remote_copy(
            src_ref=source,
            dst_ref=target,
            send_sem=send.at[index],
            recv_sem=recv.at[index],
            device_id={axis: 1 - lax.axis_index(axis)},
            device_id_type=MESH,
        )
        copy.start()
        return copy

    def keep(source, target):
        index = counts["local"]
        counts["local"] += 1
        copy = pltpu.make_async_copy(source, target, local.at[index])
        copy.start()
        return copy

    def moving(source, target, source_here, target_here):
        index, index_here = counts["sent"], counts["local"]
        counts["sent"] += 1
        counts["local"] += 1

        def remote():
            return pltpu.make_async_remote_copy(
                src_ref=source,
                dst_ref=target,
                send_sem=send.at[index],
                recv_sem=recv.at[index],
                device_id={"core": zhi, "zhi": core},
                device_id_type=MESH,
            )

        def here():
            return pltpu.make_async_copy(source_here, target_here, local.at[index_here])

        @pl.when(crossing)
        def _():
            remote().start()

        @pl.when(jnp.logical_not(crossing))
        def _():
            here().start()

        def wait():
            @pl.when(crossing)
            def _():
                remote().wait()

            @pl.when(jnp.logical_not(crossing))
            def _():
                here().wait()

        return wait

    def lanes(block, size):
        return pl.ds(pl.multiple_of(block * size, size), size)

    barrier = pltpu.get_barrier_semaphore()
    for axis in LINKS:
        pl.semaphore_signal(barrier, inc=1, device_id={axis: 1 - lax.axis_index(axis)}, device_id_type=MESH)

    @pl.when(crossing)
    def _():
        pl.semaphore_signal(barrier, inc=1, device_id={"core": zhi, "zhi": core}, device_id_type=MESH)

    pl.semaphore_wait(barrier, len(LINKS) + crossing.astype(jnp.int32))

    wait_tokens = moving(tokens, held, tokens, held)
    own_small = keep(small, gathered.at[y, x, core, zhi, zlo])
    own_rows = pl.ds(pl.multiple_of(core * part, part), part)
    quarter = 2 * zhi + zlo

    def from_shard(shard, target, block, size):
        own = keep(shard.at[:, :, lanes(core, size)], target.at[:, y, x, own_rows, lanes(block, size)])
        other = push(
            shard.at[:, :, lanes(1 - core, size)], target.at[:, y, x, own_rows, lanes(block, size)], "core"
        )
        return own, other

    self_width = w_self.shape[2] // 2
    hidden_width = w_in.shape[1] // 2
    cross_core = []
    for plane in range(4):
        target = cross_rows.at[own_rows, lanes(4 * plane + quarter, self_width)]
        cross_core.append(keep(w_cross.at[plane, :, lanes(core, self_width)], target))
        cross_core.append(push(w_cross.at[plane, :, lanes(1 - core, self_width)], target, "core"))
    own_small.wait()
    small_core = push(gathered.at[y, x, core, zhi, zlo], gathered.at[y, x, core, zhi, zlo], "core")
    self_core = from_shard(w_self, g_self, zhi, self_width)
    hidden_core = []
    for plane, shard in enumerate((w_in, w_out)):
        target = hidden.at[plane, own_rows]
        hidden_core.append(keep(shard.at[:, lanes(core, hidden_width)], target))
        hidden_core.append(push(shard.at[:, lanes(1 - core, hidden_width)], target, "core"))
    for copy in cross_core:
        copy.wait()
    regions = [cross_rows.at[:, lanes(4 * plane + quarter, self_width)] for plane in range(4)]
    cross_zlo = [push(region, region, "zlo") for region in regions]
    small_core.wait()
    region = gathered.at[y, x, :, zhi, zlo]
    small_x = push(region, region, "x")
    for copy in self_core:
        copy.wait()
    small_x.wait()
    region = gathered.at[y, :, :, zhi, zlo]
    small_y = push(region, region, "y")
    for copy in cross_zlo:
        copy.wait()
    small_y.wait()

    def over_plane(target, width):
        first, second = pl.ds(0, width), pl.ds(width, width)
        region_a, region_b = target.at[:, y, x, :, first], target.at[:, y, x, :, second]
        steps = (push(region_a, region_a, "x"), push(region_b, region_b, "y"))

        def second_steps():
            steps[0].wait()
            region_a = target.at[:, y, :, :, first]
            step_a = push(region_a, region_a, "y")
            steps[1].wait()
            region_b = target.at[:, :, x, :, second]
            return step_a, push(region_b, region_b, "x")

        return second_steps

    wait_tokens()
    keep_tokens = keep(held, token_rows)
    region = gathered.at[:, :, :, zhi, zlo]
    small_zhi = push(region, region, "zhi")
    region = g_self.at[:, y, x, :, lanes(zhi, self_width)]
    self_zhi = push(region, region, "zhi")
    wait_enc = moving(enc, enc_full.at[2 * zhi + zlo], enc, enc_full.at[2 * core + zlo])
    regions = [cross_rows.at[:, lanes(2 * plane + zhi, 2 * self_width)] for plane in range(4)]
    cross_zhi = [push(region, region, "zhi") for region in regions]
    gain = jnp.concatenate([gathered[d // 4, d // 2 % 2, d % 2, zhi, zlo, 0:1, :] for d in range(8)], axis=1)
    shift = jnp.concatenate([gathered[d // 4, d // 2 % 2, d % 2, zhi, zlo, 3:4, :] for d in range(8)], axis=1)

    def norm_step(step, carry):
        block = pl.ds(pl.multiple_of(step * 64, 64), 64)
        values = held[block, :].astype(jnp.float32)
        centred = values - jnp.mean(values, axis=1, keepdims=True)
        inverse = lax.rsqrt(jnp.mean(centred * centred, axis=1, keepdims=True) + EPSILON)
        normed[block, :] = (centred * inverse * gain + shift).astype(normed.dtype)
        return carry

    lax.fori_loop(0, rows // 64, norm_step, 0)
    attn_zlo = push(normed, attn.at[pl.ds(2 * rows, rows)], "zlo")
    attn_core = push(normed, attn.at[pl.ds(rows, rows)], "core")
    attn_own = keep(normed, attn.at[pl.ds(0, rows)])

    wait_enc()
    region = enc_full.at[2 * core + zlo]
    enc_zlo = push(region, region, "zlo")
    enc_core = push(region, region, "core")
    self_zhi.wait()
    self_second = over_plane(g_self, self_width)
    self_last = self_second()
    small_zhi.wait()
    region = gathered.at[:, :, :, :, zlo]
    small_zlo = push(region, region, "zlo")
    enc_zlo.wait()
    region = enc_full.at[2 * core + 1 - zlo]
    enc_diagonal = push(region, region, "core")
    attn_zlo.wait()
    attn_diagonal = push(attn.at[pl.ds(2 * rows, rows)], attn.at[pl.ds(3 * rows, rows)], "core")
    small_zlo.wait()
    keep_small = keep(gathered, small_all)
    for copy in (
        *self_last,
        *cross_zhi,
        *hidden_core,
        attn_core,
        attn_diagonal,
        enc_core,
        enc_diagonal,
        attn_own,
        keep_tokens,
        keep_small,
    ):
        copy.wait()


def start_exchange(tokens, enc, w_self, w_cross, w_in, w_out, small):
    rows, model = tokens.shape
    part = w_self.shape[1]
    low_type = tokens.dtype
    shapes = [
        jax.ShapeDtypeStruct((rows, model), low_type),
        jax.ShapeDtypeStruct((4 * rows, model), low_type),
        jax.ShapeDtypeStruct((4, 2, 2, 2 * part, w_self.shape[2]), low_type),
        jax.ShapeDtypeStruct((2 * part, 8 * w_cross.shape[2]), low_type),
        jax.ShapeDtypeStruct((2, 2 * part, w_in.shape[1] // 2), low_type),
        jax.ShapeDtypeStruct((4, enc.shape[0], model), low_type),
        jax.ShapeDtypeStruct((2,) * 5 + small.shape, small.dtype),
    ]
    anywhere = pl.BlockSpec(memory_space=pl.ANY)
    return pl.pallas_call(
        start_kernel,
        out_shape=shapes,
        in_specs=[anywhere] * 7,
        out_specs=[anywhere] * len(shapes),
        scratch_shapes=[
            pltpu.VMEM((rows, model), low_type),
            pltpu.VMEM((rows, model), low_type),
            pltpu.VMEM((2,) * 5 + small.shape, small.dtype),
            pltpu.SemaphoreType.DMA((40,)),
            pltpu.SemaphoreType.DMA((40,)),
            pltpu.SemaphoreType.DMA((20,)),
        ],
        compiler_params=pltpu.CompilerParams(collective_id=0, has_side_effects=True),
    )(tokens, enc, w_self, w_cross, w_in, w_out, small)


def finish_kernel(
    ff_in,
    ff_out,
    cross,
    cross_beyond,
    self_q,
    self_k,
    self_v,
    self_o,
    enc_part,
    small,
    ff_in_out,
    ff_out_out,
    cross_qkv_out,
    cross_out_out,
    self_qkv_out,
    self_out_out,
    enc_out,
    small_out,
    cross_own,
    cross_got,
    cross_low,
    cross_got_low,
    cross_total,
    enc_own,
    enc_got,
    enc_sum,
    enc_far,
    enc_low,
    self_own,
    self_got,
    low_a,
    low_b,
    self_got_low,
    self_total,
    self_last,
    small_sum,
    small_got_0,
    small_got_1,
    small_got_2,
    small_got_3,
    small_got_4,
    send,
    recv,
    local,
):
    y, x, core, zhi, zlo = (lax.axis_index(axis) for axis in AXES)
    crossing = core != zhi
    small_got = (small_got_0, small_got_1, small_got_2, small_got_3, small_got_4)
    counts = {"sent": 0, "local": 0}

    def push(source, target, axis):
        index = counts["sent"]
        counts["sent"] += 1
        copy = pltpu.make_async_remote_copy(
            src_ref=source,
            dst_ref=target,
            send_sem=send.at[index],
            recv_sem=recv.at[index],
            device_id={axis: 1 - lax.axis_index(axis)},
            device_id_type=MESH,
        )
        copy.start()
        return copy

    def keep(source, target):
        index = counts["local"]
        counts["local"] += 1
        copy = pltpu.make_async_copy(source, target, local.at[index])
        copy.start()
        return copy

    def moving(source, target, source_here, target_here):
        index, index_here = counts["sent"], counts["local"]
        counts["sent"] += 1
        counts["local"] += 1

        def remote():
            return pltpu.make_async_remote_copy(
                src_ref=source,
                dst_ref=target,
                send_sem=send.at[index],
                recv_sem=recv.at[index],
                device_id={"core": zhi, "zhi": core},
                device_id_type=MESH,
            )

        def here():
            return pltpu.make_async_copy(source_here, target_here, local.at[index_here])

        @pl.when(crossing)
        def _():
            remote().start()

        @pl.when(jnp.logical_not(crossing))
        def _():
            here().start()

        def wait():
            @pl.when(crossing)
            def _():
                remote().wait()

            @pl.when(jnp.logical_not(crossing))
            def _():
                here().wait()

        return wait

    def lanes(block, size):
        return pl.ds(pl.multiple_of(block * size, size), size)

    def add(target, *terms):
        def step(index, carry):
            rows = pl.ds(pl.multiple_of(index * 64, 64), 64)
            value = sum(term[rows, :].astype(jnp.float32) for term in terms)
            target[rows, :] = value.astype(target.dtype)
            return carry

        lax.fori_loop(0, target.shape[0] // 64, step, 0)

    barrier = pltpu.get_barrier_semaphore()
    for axis in LINKS:
        pl.semaphore_signal(barrier, inc=1, device_id={axis: 1 - lax.axis_index(axis)}, device_id_type=MESH)

    @pl.when(crossing)
    def _():
        pl.semaphore_signal(barrier, inc=1, device_id={"core": zhi, "zhi": core}, device_id_type=MESH)

    pl.semaphore_wait(barrier, len(LINKS) + crossing.astype(jnp.int32))

    last = []
    half = self_q.shape[3] // 2

    def to_cores(values, out):
        part, width = values.shape[0] // 2, values.shape[1]
        there, here = lanes(1 - core, part), lanes(core, part)
        last.append(push(values.at[there], out.at[:, lanes(core, width)], "core"))
        last.append(keep(values.at[here], out.at[:, lanes(core, width)]))

    def planes_to_cores(values, qkv_out, out_out):
        part = values.shape[0] // 2
        there, here = lanes(1 - core, part), lanes(core, part)
        for plane in range(4):
            columns_of = pl.ds(plane * half, half)
            out = qkv_out.at[plane, :, lanes(core, half)] if plane < 3 else out_out.at[:, lanes(core, half)]
            last.append(push(values.at[there, columns_of], out, "core"))
            last.append(keep(values.at[here, columns_of], out))

    cross_keep = [keep(cross, cross_own), keep(cross_beyond, cross_got)]

    first, second = pl.ds(0, half), pl.ds(half, half)
    parts = (self_q, self_k, self_v, self_o)
    self_x, self_y, own_a, own_b = [], [], [], []
    for plane, partial in enumerate(parts):
        columns_of = pl.ds(plane * half, half)
        self_x.append(push(partial.at[:, 1 - x, :, first], self_got.at[0, :, :, columns_of], "x"))
        self_y.append(push(partial.at[1 - y, :, :, second], self_got.at[1, :, :, columns_of], "y"))
        own_a.append(keep(partial.at[:, x, :, first], self_own.at[0, :, :, columns_of]))
        own_b.append(keep(partial.at[y, :, :, second], self_own.at[1, :, :, columns_of]))
    enc_core = push(enc_part.at[1 - core], enc_got, "core")
    enc_keep = keep(enc_part.at[core], enc_own)

    to_cores(ff_in, ff_in_out)
    to_cores(ff_out, ff_out_out)

    small_first, small_size = 0, 32

    def small_send(stage):
        rows = small_size // 2
        away = small_first + (1 - lax.axis_index(AXES[stage])) * rows
        return push(small_sum.at[pl.ds(away, rows)], small_got[stage], AXES[stage])

    def small_add(stage, copy):
        copy.wait()
        rows, got = small_size // 2, small_got[stage]
        mine = small_first + lax.axis_index(AXES[stage]) * rows

        def step(index, carry):
            small_sum[mine + index] += got[index]
            return carry

        lax.fori_loop(0, rows, step, 0)
        return mine, rows

    keep(small, small_sum).wait()
    small_copy = small_send(0)
    for copy in cross_keep:
        copy.wait()

    def cross_step(target, which, *others):
        def step(index, carry):
            rows = pl.ds(pl.multiple_of(index * 64, 64), 64)
            for plane in range(4):
                source = pl.ds(pl.multiple_of((2 * plane + which) * half, half), half)
                columns_of = pl.ds(plane * half, half)
                value = cross_own[rows, source].astype(jnp.float32) + cross_got[rows, source].astype(jnp.float32)
                for other in others:
                    value += other[rows, columns_of].astype(jnp.float32)
                target[rows, columns_of] = value.astype(target.dtype)
            return carry

        lax.fori_loop(0, target.shape[0] // 64, step, 0)

    cross_step(cross_low, 1 - zlo)
    cross_zlo = push(cross_low, cross_got_low, "zlo")
    enc_core.wait()
    enc_keep.wait()
    add(enc_sum, enc_own.at[1 - zlo], enc_got.at[1 - zlo])
    enc_zlo = push(enc_sum, enc_far, "zlo")
    small_first, small_size = small_add(0, small_copy)
    small_copy = small_send(1)
    for copy in own_a + self_x:
        copy.wait()
    add(low_a, self_own.at[0, 1 - y], self_got.at[0, 1 - y])
    a_second = push(low_a, self_got_low.at[0], "y")
    for copy in own_b + self_y:
        copy.wait()
    add(low_b, self_own.at[1, 1 - x], self_got.at[1, 1 - x])
    b_second = push(low_b, self_got_low.at[1], "x")
    small_first, small_size = small_add(1, small_copy)
    small_copy = small_send(2)
    add(self_total.at[0], self_own.at[0, y], self_got.at[0, y])
    add(self_total.at[1], self_own.at[1, x], self_got.at[1, x])
    enc_zlo.wait()
    add(enc_low, enc_own.at[zlo], enc_got.at[zlo], enc_far)
    small_first, small_size = small_add(2, small_copy)
    small_copy = small_send(3)
    a_second.wait()
    add(self_total.at[0], self_total.at[0], self_got_low.at[0])
    b_second.wait()
    add(self_total.at[1], self_total.at[1], self_got_low.at[1])
    add(low_a, self_total.at[1 - zhi])
    self_zhi = push(low_a, self_last, "zhi")
    wait_enc = moving(enc_low, enc_out, enc_low, enc_out)
    cross_zlo.wait()
    cross_step(cross_total, zlo, cross_got_low)
    planes_to_cores(cross_total, cross_qkv_out, cross_out_out)
    small_first, small_size = small_add(3, small_copy)
    small_copy = small_send(4)
    self_zhi.wait()
    add(self_total.at[zhi], self_total.at[zhi], self_last)
    planes_to_cores(self_total.at[zhi], self_qkv_out, self_out_out)
    small_first, small_size = small_add(4, small_copy)
    keep(small_sum.at[small_first], small_out).wait()
    wait_enc()
    for copy in last:
        copy.wait()


def finish(ff_in, ff_out, cross, cross_beyond, self_parts, enc, small):
    rows, width = ff_in.shape
    part, half = self_parts[0].shape[2], self_parts[0].shape[3] // 2
    low_type, enc_shape = enc.dtype, enc.shape[2:]
    wide = 4 * half

    def full(*shape):
        return jax.ShapeDtypeStruct(shape, jnp.float32)

    shapes = [
        full(rows // 2, 2 * width),
        full(rows // 2, 2 * width),
        full(3, part // 2, 2 * half),
        full(part // 2, 2 * half),
        full(3, part // 2, 2 * half),
        full(part // 2, 2 * half),
        jax.ShapeDtypeStruct(enc_shape, low_type),
        jax.ShapeDtypeStruct(small.shape[1:], small.dtype),
    ]
    anywhere = pl.BlockSpec(memory_space=pl.ANY)
    return pl.pallas_call(
        finish_kernel,
        out_shape=shapes,
        in_specs=[anywhere] * 10,
        out_specs=[anywhere] * len(shapes),
        scratch_shapes=[
            pltpu.VMEM((part, 2 * wide), low_type),
            pltpu.VMEM((part, 2 * wide), low_type),
            pltpu.VMEM((part, wide), low_type),
            pltpu.VMEM((part, wide), low_type),
            pltpu.VMEM((part, wide), jnp.float32),
            pltpu.VMEM((2, *enc_shape), low_type),
            pltpu.VMEM((2, *enc_shape), low_type),
            pltpu.VMEM(enc_shape, low_type),
            pltpu.VMEM(enc_shape, low_type),
            pltpu.VMEM(enc_shape, low_type),
            pltpu.VMEM((2, 2, part, wide), low_type),
            pltpu.VMEM((2, 2, part, wide), low_type),
            pltpu.VMEM((part, wide), low_type),
            pltpu.VMEM((part, wide), low_type),
            pltpu.VMEM((2, part, wide), low_type),
            pltpu.VMEM((2, part, wide), jnp.float32),
            pltpu.VMEM((part, wide), low_type),
            pltpu.VMEM(small.shape, small.dtype),
        ]
        + [pltpu.VMEM((32 >> stage, *small.shape[1:]), small.dtype) for stage in range(1, 6)]
        + [pltpu.SemaphoreType.DMA((40,))] * 3,
        compiler_params=pltpu.CompilerParams(collective_id=1, has_side_effects=True),
        cost_estimate=pl.CostEstimate(flops=40_000_000_000, bytes_accessed=0, transcendentals=0),
    )(ff_in, ff_out, cross, cross_beyond, *self_parts, enc, small)


def trade(rows, axis, name="trade"):
    with jax.named_scope(name):
        return lax.ppermute(rows, axis, [(0, 1), (1, 0)])


def after(value, *others):
    return lax.optimization_barrier((value, *others))[0]


def regroup(rows, name="regroup"):
    with jax.named_scope("re_" + name):
        moved = lax.ppermute(rows, ("core", "zhi"), [(1, 2), (2, 1)])
        return jnp.where(lax.axis_index("core") == lax.axis_index("zhi"), rows, moved)


def in_order(index, own, other, axis):
    return jnp.concatenate(
        [jnp.where(index == 0, own, other), jnp.where(index == 0, other, own)], axis=axis
    )


def low(values):
    return values.astype(jnp.bfloat16)


def half_of(values, index, axis):
    size = values.shape[axis] // 2
    return lax.dynamic_slice_in_dim(values, index * size, size, axis)


def over_chips(rows):
    return lax.all_gather(rows, ("y", "x"), axis=0, tiled=True)


def sum_over_chips(partial):
    return lax.psum_scatter(partial, ("y", "x"), scatter_dimension=0, tiled=True)


def spread_rows(rows, name):
    beyond = trade(rows, "zlo", name + "_z")
    return (
        jnp.concatenate([rows, trade(rows, "core", name + "_c")], axis=0),
        jnp.concatenate([beyond, trade(beyond, "core", name + "_zc")], axis=0),
    )


def sum_rows(near, far, term, name):
    size = near.shape[0] // 2
    far_sum = term(far[:size]) + trade(low(term(far[size:])), "core", name + "_zc")
    from_far = trade(low(far_sum), "zlo", name + "_z")
    near_other = trade(low(term(near[size:])), "core", name + "_c")
    return term(near[:size]) + near_other + from_far


def fast_layer(
    tokens,
    enc_states,
    enc_len,
    cont_lengths,
    cotangent,
    self_qkv,
    self_out,
    cross_qkv,
    cross_out,
    ff_in,
    ff_out,
    head_bias,
    ff_bias,
    vec_params,
):
    core, zhi, zlo = lax.axis_index("core"), lax.axis_index("zhi"), lax.axis_index("zlo")
    scaling = HD**-0.5
    model = tokens.shape[1]
    segments = cont_lengths.shape[1]

    flat = jnp.concatenate([vec_params.reshape(-1), head_bias.reshape(-1), ff_bias]).astype(jnp.float32)
    sizes = (vec_params.size, head_bias.size, ff_bias.size)
    flat = jnp.pad(flat.reshape(-1, 128), ((0, 4), (0, 0)))
    token_rows, attn_rows, w_self, w_cross, hidden, enc_full, small = start_exchange(
        tokens,
        enc_states,
        jnp.concatenate([self_qkv, self_out.T[None]], axis=0),
        jnp.concatenate([cross_qkv, cross_out.T[None]], axis=0),
        ff_in,
        ff_out.T,
        flat,
    )
    w_self = w_self.reshape(4, model, -1)
    w_cross = over_chips(w_cross)
    cross_width = w_cross.shape[1] // 4
    hidden_beyond = trade(hidden, "zhi", "wh_zhi")
    w_qkv, w_so = jnp.concatenate([w_self[0], w_self[1], w_self[2]], axis=1), w_self[3]
    w_cq, w_ckv, w_co = jnp.split(w_cross, [cross_width, 3 * cross_width], axis=1)
    rows_of = model // 4
    width = w_self.shape[2]
    pairs, cross_pairs = width // PAIR, cross_width // PAIR
    enc_full = enc_full.reshape(-1, model)
    attn_near, attn_far = attn_rows[: attn_rows.shape[0] // 2], attn_rows[attn_rows.shape[0] // 2 :]
    small = small.reshape(8, 4, -1)
    vec_part, head_part, ff_part = jnp.split(
        small[:, :, : sum(sizes)], [sizes[0], sizes[0] + sizes[1]], axis=2
    )
    vectors = vec_part[:, 0].reshape(8, 9, -1).transpose(1, 0, 2).reshape(9, model)
    heads = head_part.reshape(8, 4, 4, -1).transpose(2, 1, 0, 3).reshape(4, 2, 2, 2, -1)
    self_bias = lax.dynamic_index_in_dim(
        lax.dynamic_index_in_dim(heads[:2], zlo, 2, False), core, 2, False
    ).reshape(2, -1)
    cross_bias = lax.dynamic_index_in_dim(heads[2:], core, 3, False).reshape(2, -1)
    hidden_bias = ff_part.transpose(1, 0, 2).reshape(2, 2, 2, -1)
    hidden_bias = lax.dynamic_index_in_dim(
        lax.dynamic_index_in_dim(hidden_bias, zlo, 1, False), core, 1, False
    ).reshape(-1)

    lengths = regroup(jnp.concatenate([cont_lengths[0], enc_len]))
    places = jnp.stack(
        [512 * ((core != block // 2) + 2 * (zlo != block % 2)) for block in range(4)]
    ).astype(jnp.int32)
    bounds = PROMPT + jnp.concatenate(
        [jnp.zeros((1,), jnp.int32), jnp.cumsum(lengths[:segments]).astype(jnp.int32)]
    )
    self_meta = jnp.concatenate([places, bounds])
    cross_meta = lengths[segments:]

    resid = token_rows.astype(jnp.float32)
    _, hat_one, inv_one = norm_forward(resid, vectors[0], vectors[3])
    qkv_bias = jnp.concatenate([self_bias[0], jnp.zeros((width,), jnp.float32), self_bias[1]])
    qkv_scale = jnp.concatenate([jnp.full((width,), scaling), jnp.ones((2 * width,))]).astype(jnp.float32)
    def project(rows):
        return low((product(rows, w_qkv) + qkv_bias) * qkv_scale)

    qkv = project(attn_rows)
    count = qkv.shape[0]
    self_plan = functools.partial(self_sections, segments=segments)
    mixed, self_lse = attend(self_plan, self_meta, qkv, 0, qkv, pairs, 2 * pairs, pairs, 1152)
    mixed = after(mixed, hidden_beyond)
    hidden = in_order(zhi, hidden, after(hidden_beyond, mixed), 2).transpose(1, 0, 2)
    w_hidden = over_chips(hidden.reshape(hidden.shape[0], -1))
    w_in, w_out = jnp.split(w_hidden, 2, axis=1)
    near, far = mixed[: count // 2], mixed[count // 2 :]
    so_far = low(
        product_right_t(far[: count // 4], w_so)
        + trade(low(product_right_t(far[count // 4 :], w_so)), "core", "so_zc")
    )
    so_near_other = low(product_right_t(near[count // 4 :], w_so))
    so_near = product_right_t(near[: count // 4], w_so)
    grad_rows = regroup(after(cotangent, mixed), "cotangent")
    cross_kv = low(
        product(after(enc_full, grad_rows, so_far), w_ckv)
        + jnp.concatenate([jnp.zeros((cross_width,), jnp.float32), cross_bias[1]])
    )
    branch = so_near + trade(so_near_other, "core", "so_c") + after(trade(so_far, "zlo", "so_z"), cross_kv)
    after_one = resid + (branch + vectors[6])

    cot_beyond = trade(after(grad_rows, after_one), "zlo", "cot_z")
    cot_near = [grad_rows, trade(grad_rows, "core", "cot_c")]

    normed_mid, hat_two, inv_two = norm_forward(after_one, vectors[1], vectors[4])
    cross_low = low(normed_mid)
    cross_rows = jnp.concatenate([cross_low, trade(cross_low, "core", "cin")], axis=0)
    own_rows = cross_low.shape[0]
    cross_q = low((product(cross_rows, w_cq) + cross_bias[0]) * scaling)
    cross_plan = functools.partial(cross_sections, blocks=cross_q.shape[0] // BLOCK)
    cross_mixed, cross_lse = attend(
        cross_plan, cross_meta, cross_q, 0, cross_kv, 0, cross_pairs, cross_pairs, ENC
    )
    cross_mixed = after(cross_mixed, cot_beyond)
    other = trade(low(product_right_t(cross_mixed[own_rows:], w_co)), "core", "co_c")
    branch = product_right_t(cross_mixed[:own_rows], w_co) + other
    after_two = after_one + (branch + vectors[7])

    normed_out, hat_three, inv_three = norm_forward(after_two, vectors[2], vectors[5])
    mlp_in = low(normed_out)
    beyond = trade(mlp_in, "zlo", "mlp_z")
    mlp_near = [mlp_in, trade(mlp_in, "core", "mlp_c")]
    act_near, dpre_near, sum_near = hidden_units(mlp_near, cot_near, w_hidden, hidden_bias[None])
    beyond = after(beyond, act_near)
    mlp_far = [beyond, trade(beyond, "core", "mlp_zc")]
    cot_far = [cot_beyond, trade(cot_beyond, "core", "cot_zc")]
    act_far, dpre_far, sum_far = hidden_units(mlp_far, cot_far, w_hidden, hidden_bias[None])
    gradient = grad_rows.astype(jnp.float32)
    bias_out_three = jnp.sum(gradient, axis=0)
    dmlp_far = low(
        product_right_t(dpre_far[:own_rows], w_in)
        + trade(low(product_right_t(dpre_far[own_rows:], w_in)), "core", "dmlp_zc")
    )
    mlp_term = product_right_t(dpre_near[:own_rows], w_in) + trade(
        low(product_right_t(dpre_near[own_rows:], w_in)), "core", "dmlp_c"
    )
    act_near, act_far = after(act_near, dmlp_far, mlp_term), after(act_far, dmlp_far, mlp_term)
    out_parts = [
        low(product_right_t(act_far[own_rows:], w_out)),
        product_right_t(act_far[:own_rows], w_out),
        low(product_right_t(act_near[own_rows:], w_out)),
        product_right_t(act_near[:own_rows], w_out),
    ]
    out_far = low(out_parts[1] + trade(out_parts[0], "core", "out_zc"))
    out_branch = out_parts[3] + trade(out_parts[2], "core", "out_c")
    dmlp_beyond, grad_w_out, grad_w_in = weight_grads(
        dmlp_far, (cot_near + cot_far, act_near, act_far), (mlp_near + mlp_far, dpre_near, dpre_far), 2
    )
    mlp_term = mlp_term + dmlp_beyond
    out_far = trade(after(out_far, mlp_term), "zlo", "out_z")
    part, gain_three, shift_three = norm_backward(mlp_term, hat_three, inv_three, vectors[2])
    gradient = gradient + part

    grad_low = low(gradient)
    bias_out_two = jnp.sum(grad_low.astype(jnp.float32), axis=0)
    grad_both = jnp.concatenate([grad_low, trade(grad_low, "core", "e2")], axis=0)
    cross_mixed_grad = low(product(grad_both, w_co))
    cross_dq, cross_dk, cross_dv = attend_back(
        cross_plan,
        cross_meta,
        cross_q,
        0,
        cross_kv,
        0,
        cross_pairs,
        cross_mixed,
        cross_mixed_grad,
        cross_lse,
        cross_pairs,
        ENC,
    )
    cross_dq = after(cross_dq, out_far)
    other = trade(low(product_right_t(cross_dq[own_rows:], w_cq)), "core", "dcin")
    part, gain_two, shift_two = norm_backward(
        product_right_t(cross_dq[:own_rows], w_cq) + other, hat_two, inv_two, vectors[1]
    )
    gradient = gradient + part

    grad_low = low(gradient)
    bias_out_one = jnp.sum(grad_low.astype(jnp.float32), axis=0)
    def zhi_sum(partial, axis, name):
        mine, theirs = half_of(partial, zhi, axis), half_of(partial, 1 - zhi, axis)
        return mine.astype(jnp.float32) + trade(theirs, "zhi", name).astype(jnp.float32)

    beyond = trade(grad_low, "zlo", "e1_z")
    grad_near = jnp.concatenate([grad_low, trade(grad_low, "core", "e1_c")], axis=0)
    mixed_grad = low(product(grad_near, w_so))
    cross_parts = [
        low(product_left_t(cross_rows, after(cross_dq, grad_low))),
        low(product_left_t(enc_full, after(cross_dk, grad_low))),
        low(product_left_t(enc_full, after(cross_dv, grad_low))),
        low(product_left_t(after(grad_both, grad_low), cross_mixed)),
    ]
    grad_cross = jnp.concatenate(cross_parts, axis=1)
    layer_out = low(after_two + (out_branch + after(out_far, grad_low) + vectors[8]))
    beyond = after(beyond, mixed_grad, grad_cross, layer_out)
    cross_sum = sum_over_chips(grad_cross)
    grad_far = jnp.concatenate([beyond, trade(beyond, "core", "e1_zc")], axis=0)
    mixed_grad = jnp.concatenate([mixed_grad, low(product(grad_far, w_so))], axis=0)

    out_sum = zhi_sum(sum_over_chips(grad_w_out), 1, "go_zhi")
    in_sum = zhi_sum(sum_over_chips(grad_w_in), 1, "gi_zhi")
    dq, dk, dv = attend_back(
        self_plan, self_meta, qkv, 0, qkv, pairs, 2 * pairs, mixed, mixed_grad, self_lse, pairs, 1152
    )
    dq, dk, dv = after(dq, in_sum, out_sum), after(dk, in_sum, out_sum), after(dv, in_sum, out_sum)
    layer_out = regroup(after(layer_out, dq), "out")
    dqkv = jnp.concatenate([dq, dk, dv], axis=1)
    d_near, d_far = dqkv[: count // 2], dqkv[count // 2 :]
    dx_far = low(
        product_right_t(d_far[: count // 4], w_qkv)
        + trade(low(product_right_t(d_far[count // 4 :], w_qkv)), "core", "dx_zc")
    )
    dx = product_right_t(d_near[: count // 4], w_qkv) + trade(
        low(product_right_t(d_near[count // 4 :], w_qkv)), "core", "dx_c"
    )
    dq, dk, dv = after(dq, dx_far), after(dk, dx_far), after(dv, dx_far)
    self_parts = [
        low(product_left_t(attn_rows, dq)),
        low(product_left_t(attn_rows, dk)),
        low(product_left_t(attn_rows, dv)),
        low(product_left_t(grad_near, near) + product_left_t(grad_far, far)),
    ]
    enc_part = low(
        product_right_t(after(cross_dk, dq), w_ckv[:, :cross_width])
        + product_right_t(after(cross_dv, dq), w_ckv[:, cross_width:])
    )
    cross_sum = after(cross_sum, dq).reshape(rows_of, 4, 2, -1)
    cross_kept = half_of(cross_sum, zhi, 2).reshape(rows_of, -1)
    cross_beyond = trade(half_of(cross_sum, 1 - zhi, 2).reshape(rows_of, -1), "zhi", "gc_zhi")
    dx = dx + after(trade(dx_far, "zlo", "dx_z"), enc_part, layer_out, cross_beyond, *self_parts)
    part, gain_one, shift_one = norm_backward(dx, hat_one, inv_one, vectors[0])
    input_part = low(gradient + part)
    input_grad = regroup(input_part, "dgrad").astype(jnp.float32)

    bias_self_query = jnp.sum(dq.astype(jnp.float32), axis=0)
    bias_self_value = jnp.sum(dv.astype(jnp.float32), axis=0)
    bias_cross_query = jnp.sum(cross_dq.astype(jnp.float32), axis=0)
    bias_cross_value = jnp.sum(cross_dv.astype(jnp.float32), axis=0)
    grad_hidden_bias = (sum_near + sum_far)[0]
    vec_sums = jnp.stack(
        [
            gain_one,
            gain_two,
            gain_three,
            shift_one,
            shift_two,
            shift_three,
            bias_out_one,
            bias_out_two,
            bias_out_three,
        ]
    )
    at_zlo = (jnp.arange(2) == zlo).astype(jnp.float32)
    at_core = (jnp.arange(2) == core).astype(jnp.float32)
    quarter = (at_zlo[:, None] * at_core[None, :])[:, :, None]
    self_sums = jnp.stack([bias_self_query, bias_self_value]).reshape(2, 2, 1, 1, -1) * quarter
    cross_sums = jnp.stack([bias_cross_query, bias_cross_value]).reshape(2, 2, 2, 1, -1) * at_core[:, None]
    head_sums = jnp.concatenate([self_sums, cross_sums], axis=0)
    hidden_sums = grad_hidden_bias.reshape(2, 1, 1, -1) * quarter
    vec_sums = vec_sums.reshape(9, 8, -1).transpose(1, 0, 2).reshape(8, 1, -1)
    sums = jnp.concatenate(
        [
            jnp.broadcast_to(vec_sums, (8, 4, sizes[0])),
            head_sums.reshape(4, 4, 8, -1).transpose(2, 1, 0, 3).reshape(8, 4, -1),
            hidden_sums.reshape(4, 8, -1).transpose(1, 0, 2),
        ],
        axis=2,
    )
    sums = jnp.pad(after(sums, input_part).reshape(32, -1, 128), ((0, 0), (0, 4), (0, 0)))
    ff_in_grad, ff_out_grad, cross_qkv_grad, cross_out_grad, self_qkv_grad, self_out_grad, enc_grad, sums = finish(
        in_sum,
        out_sum,
        cross_kept,
        cross_beyond,
        [part.reshape(2, 2, rows_of, -1) for part in self_parts],
        enc_part.reshape(2, 2, -1, model),
        sums,
    )
    sums = sums.reshape(-1)[: sum(sizes)]
    vec_grad, head_grad, ff_bias_grad = jnp.split(sums, [sizes[0], sizes[0] + sizes[1]])
    return (
        layer_out,
        input_grad,
        enc_grad.astype(jnp.float32),
        self_qkv_grad,
        self_out_grad.T,
        cross_qkv_grad,
        cross_out_grad.T,
        ff_in_grad,
        ff_out_grad.T,
        head_grad.reshape(head_bias.shape),
        ff_bias_grad,
        vec_grad.reshape(vec_params.shape),
    )


def solution(mesh):
    fast = tuple(mesh.shape[axis] for axis in ("dp", "tensor")) == (8, 4)
    dp, tensor = (AXES[:3], AXES[3:]) if fast else (("dp",), ("tensor",))
    both = dp + tensor
    rows = P(both, None)
    qkv = P(None, dp, tensor)
    out = P(tensor, dp)
    in_specs = (
        rows,
        rows,
        P(dp),
        P(dp, None),
        rows,
        qkv,
        out,
        qkv,
        out,
        P(dp, tensor),
        out,
        P(None, tensor + dp),
        P(tensor + dp),
        P(None, dp),
    )
    out_specs = (
        rows,
        rows,
        rows,
        qkv,
        out,
        qkv,
        out,
        P(dp, tensor),
        out,
        P(None, tensor + dp),
        P(tensor + dp),
        P(None, dp),
    )
    if fast:
        mesh = Mesh(mesh.devices.reshape(2, 2, 2, 2, 2), AXES)
    return jax.shard_map(
        fast_layer if fast else shards, mesh=mesh, in_specs=in_specs, out_specs=out_specs, check_vma=False
    )
```

```python
import functools
import math

import jax
import jax.numpy as jnp
from jax import lax
from jax.experimental import pallas as pl
from jax.experimental.pallas import tpu as pltpu
from jax.sharding import Mesh
from jax.sharding import PartitionSpec as P

HD = 64
PROMPT = 1024
CONT_TOK = 1024
ENC = 512
BLOCK = 256
PAIR = 2 * HD
AXES = ("y", "x", "core", "zhi", "zlo")


def lane_half():
    return lax.broadcasted_iota(jnp.int32, (1, PAIR), 1) < HD


def one_head(rows, head):
    keep = lane_half() if head == 0 else jnp.logical_not(lane_half())
    return rows * jnp.where(keep, 1.0, 0.0).astype(rows.dtype)


def dot_nt(left, right):
    return lax.dot_general(left, right, (((1,), (1,)), ((), ())), preferred_element_type=jnp.float32)


def dot_nn(left, right):
    return jnp.dot(left, right, preferred_element_type=jnp.float32)


def dot_tn(left, right):
    return lax.dot_general(left, right, (((0,), (0,)), ((), ())), preferred_element_type=jnp.float32)


def self_sections(meta_ref, segments):
    def at(block):
        return pl.multiple_of(meta_ref[block], 512)

    def place(index):
        return pl.multiple_of(meta_ref[index >> 1] + (index & 1) * BLOCK, BLOCK)

    def causal(row, col):
        return col <= row

    def banded(row, col):
        start = jnp.full(row.shape, meta_ref[4], jnp.int32)
        for segment in range(1, segments):
            bound = meta_ref[4 + segment]
            start = jnp.where(row >= bound, bound, start)
        return (col <= row) & (col >= start)

    def early(index):
        return [(at(0), 512, 0, causal)]

    def middle(index):
        return [(at(0), 512, 0, None), (at(1), 512, 512, causal)]

    def late(index):
        return [
            (at(0), 512, 0, None),
            (at(1), 512, 512, None),
            (place(index - 1), BLOCK, (index - 1) * BLOCK, banded),
            (place(index), BLOCK, index * BLOCK, banded),
        ]

    return place, ((0, 2, early), (2, 4, middle), (4, 8, late))


def cross_sections(meta_ref, blocks):
    def place(index):
        return pl.multiple_of(index * BLOCK, BLOCK)

    def usable(row, col):
        return col < meta_ref[0]

    def every(index):
        return [(0, ENC, 0, usable)]

    return place, ((0, blocks, every),)


def forward_kernel(sections, meta_ref, q_ref, k_ref, v_ref, o_ref, lse_ref):
    place, ranges = sections(meta_ref)

    for low, high, parts_of in ranges:

        def step(index, carry, parts_of=parts_of):
            rows = pl.ds(place(index), BLOCK)
            parts = parts_of(index)
            queries = q_ref[rows, :]
            row = index * BLOCK + lax.broadcasted_iota(jnp.int32, (BLOCK, 1), 0)
            allowed = [
                None if rule is None else rule(row, first + lax.broadcasted_iota(jnp.int32, (1, size), 1))
                for _, size, first, rule in parts
            ]
            outs, totals = [], []
            for head in range(2):
                query = one_head(queries, head)
                scores = []
                for (where, size, _, _), ok in zip(parts, allowed):
                    score = dot_nt(query, k_ref[pl.ds(where, size), :])
                    scores.append(score if ok is None else jnp.where(ok, score, -1e30))
                top = functools.reduce(jnp.maximum, [jnp.max(s, axis=1, keepdims=True) for s in scores])
                exps = [jnp.exp(s - top) for s in scores]
                total = sum(jnp.sum(e, axis=1, keepdims=True) for e in exps)
                mixed = sum(
                    dot_nn(e.astype(jnp.bfloat16), v_ref[pl.ds(where, size), :])
                    for (where, size, _, _), e in zip(parts, exps)
                )
                outs.append(mixed * (1.0 / total))
                totals.append(top + jnp.log(total))
            o_ref[rows, :] = jnp.where(lane_half(), outs[0], outs[1]).astype(o_ref.dtype)
            lse_ref[rows, :] = jnp.where(lane_half(), totals[0], totals[1])
            return carry

        lax.fori_loop(low, high, step, 0)


def backward_kernel(
    sections, meta_ref, q_ref, k_ref, v_ref, o_ref, do_ref, lse_ref, dq_ref, dk_ref, dv_ref, dk_sum, dv_sum
):
    place, ranges = sections(meta_ref)
    dk_sum[...] = jnp.zeros_like(dk_sum)
    dv_sum[...] = jnp.zeros_like(dv_sum)

    for low, high, parts_of in ranges:

        def step(index, carry, parts_of=parts_of):
            rows = pl.ds(place(index), BLOCK)
            parts = parts_of(index)
            queries, grads = q_ref[rows, :], do_ref[rows, :]
            row = index * BLOCK + lax.broadcasted_iota(jnp.int32, (1, BLOCK), 1)
            allowed = [
                None if rule is None else rule(row, first + lax.broadcasted_iota(jnp.int32, (size, 1), 0))
                for _, size, first, rule in parts
            ]
            logs = jnp.transpose(lse_ref[rows, :])
            spread = jnp.transpose(grads.astype(jnp.float32) * o_ref[rows, :].astype(jnp.float32))
            key_parts = [k_ref[pl.ds(where, size), :] for where, size, _, _ in parts]
            value_parts = [v_ref[pl.ds(where, size), :] for where, size, _, _ in parts]
            query_grads = []
            for head in range(2):
                query, grad = one_head(queries, head), one_head(grads, head)
                log = logs[head * HD : head * HD + 1, :]
                delta = jnp.sum(spread[head * HD : (head + 1) * HD, :], axis=0, keepdims=True)
                query_grad = None
                for (where, size, _, _), ok, keys, values in zip(parts, allowed, key_parts, value_parts):
                    score = dot_nt(keys, query)
                    if ok is not None:
                        score = jnp.where(ok, score, -1e30)
                    probs = jnp.exp(score - log)
                    score_grad = (probs * (dot_nt(values, grad) - delta)).astype(jnp.bfloat16)
                    dv_sum[pl.ds(where, size), :] += dot_nn(probs.astype(jnp.bfloat16), grad)
                    dk_sum[pl.ds(where, size), :] += dot_nn(score_grad, query)
                    term = dot_tn(score_grad, keys)
                    query_grad = term if query_grad is None else query_grad + term
                query_grads.append(query_grad)
            both = jnp.where(lane_half(), query_grads[0], query_grads[1])
            dq_ref[rows, :] = both.astype(jnp.bfloat16) * jnp.asarray(HD**-0.5, jnp.bfloat16)
            return carry

        lax.fori_loop(low, high, step, 0)
    dk_ref[...] = dk_sum[...].astype(dk_ref.dtype)
    dv_ref[...] = dv_sum[...].astype(dv_ref.dtype)


def columns(rows, first):
    return pl.BlockSpec((rows, PAIR), lambda pair, meta: (0, first + pair))


def attend(sections, meta, q, q_at, keys, k_at, v_at, pairs, weight):
    count, key_rows = q.shape[0], keys.shape[0]
    return pl.pallas_call(
        functools.partial(forward_kernel, sections),
        grid_spec=pltpu.PrefetchScalarGridSpec(
            num_scalar_prefetch=1,
            grid=(pairs,),
            in_specs=[columns(count, q_at), columns(key_rows, k_at), columns(key_rows, v_at)],
            out_specs=[columns(count, 0), columns(count, 0)],
        ),
        out_shape=[
            jax.ShapeDtypeStruct((count, pairs * PAIR), jnp.bfloat16),
            jax.ShapeDtypeStruct((count, pairs * PAIR), jnp.float32),
        ],
        cost_estimate=pl.CostEstimate(
            flops=2 * 4 * 4 * count * weight * pairs * PAIR,
            bytes_accessed=10 * count * pairs * PAIR,
            transcendentals=2 * pairs * count * weight,
        ),
    )(meta, q, keys, keys)


def attend_back(sections, meta, q, q_at, keys, k_at, v_at, out, out_grad, lse, pairs, weight):
    count, key_rows = q.shape[0], keys.shape[0]
    return pl.pallas_call(
        functools.partial(backward_kernel, sections),
        grid_spec=pltpu.PrefetchScalarGridSpec(
            num_scalar_prefetch=1,
            grid=(pairs,),
            in_specs=[
                columns(count, q_at),
                columns(key_rows, k_at),
                columns(key_rows, v_at),
                columns(count, 0),
                columns(count, 0),
                columns(count, 0),
            ],
            out_specs=[columns(count, 0), columns(key_rows, 0), columns(key_rows, 0)],
            scratch_shapes=[pltpu.VMEM((key_rows, PAIR), jnp.float32)] * 2,
        ),
        out_shape=[
            jax.ShapeDtypeStruct((count, pairs * PAIR), jnp.bfloat16),
            jax.ShapeDtypeStruct((key_rows, pairs * PAIR), jnp.bfloat16),
            jax.ShapeDtypeStruct((key_rows, pairs * PAIR), jnp.bfloat16),
        ],
        cost_estimate=pl.CostEstimate(
            flops=5 * 4 * 4 * count * weight * pairs * PAIR,
            bytes_accessed=20 * count * pairs * PAIR,
            transcendentals=2 * pairs * count * weight,
        ),
    )(meta, q, keys, keys, out, out_grad, lse)


EPSILON = 1e-05
MASKED = 1e30
GELU_C = math.sqrt(2.0 / math.pi)
GELU_A = 0.044715


def gelu_value(values):
    inner = jnp.tanh(GELU_C * (values + GELU_A * values * values * values))
    return 0.5 * values * (1.0 + inner)


def gelu_slope(values):
    inner = jnp.tanh(GELU_C * (values + GELU_A * values * values * values))
    return 0.5 * (1.0 + inner) + 0.5 * values * (1.0 - inner * inner) * GELU_C * (
        1.0 + 3.0 * GELU_A * values * values
    )


def norm_forward(values, gain_vec, shift_vec):
    row_mean = jnp.mean(values, axis=1, keepdims=True)
    centred = values - row_mean
    inverse = lax.rsqrt(jnp.mean(centred * centred, axis=1, keepdims=True) + EPSILON)
    normed = centred * inverse
    return (normed * gain_vec + shift_vec, normed, inverse)


def norm_backward(gradient, normed, inverse, gain_vec):
    scaled = gradient * gain_vec
    inner = (
        scaled
        - jnp.mean(scaled, axis=1, keepdims=True)
        - normed * jnp.mean(scaled * normed, axis=1, keepdims=True)
    )
    return (inner * inverse, jnp.sum(gradient * normed, axis=0), jnp.sum(gradient, axis=0))


def product(left, right):
    return jnp.dot(left, right, preferred_element_type=jnp.float32)


def product_left_t(left, right):
    return lax.dot_general(
        left, right, (((0,), (0,)), ((), ())), preferred_element_type=jnp.float32
    )


def product_right_t(left, right):
    return lax.dot_general(
        left, right, (((1,), (1,)), ((), ())), preferred_element_type=jnp.float32
    )


def attend_forward(queries, key_rows, value_rows, rule, block_rows):
    seq_rows, local_width = queries.shape
    local_heads = local_width // HD
    query_blocks = queries.reshape(seq_rows // block_rows, block_rows, local_heads, HD)
    key_heads = key_rows.reshape(-1, local_heads, HD)
    value_heads = value_rows.reshape(-1, local_heads, HD)
    block_starts = jnp.arange(seq_rows // block_rows, dtype=jnp.int32) * block_rows

    def attend_block(pieces):
        query_block, offset = pieces
        scores = jnp.einsum(
            "qhd,khd->hqk", query_block, key_heads, preferred_element_type=jnp.float32
        )
        scores = jnp.where(rule(offset, block_rows)[None], scores, -MASKED)
        row_max = jnp.max(scores, axis=2, keepdims=True)
        exponent = jnp.exp(scores - row_max)
        row_total = jnp.sum(exponent, axis=2, keepdims=True)
        probs_low = (exponent / row_total).astype(jnp.bfloat16)
        mixed = jnp.einsum(
            "hqk,khd->qhd", probs_low, value_heads, preferred_element_type=jnp.float32
        )
        return (
            mixed.astype(jnp.bfloat16).reshape(block_rows, local_width),
            (row_max + jnp.log(row_total))[:, :, 0],
        )

    outputs, log_total = lax.map(attend_block, (query_blocks, block_starts))
    return (outputs.reshape(seq_rows, local_width), log_total)


def attend_backward(queries, key_rows, value_rows, out_grad, log_total, rule, block_rows):
    seq_rows, local_width = queries.shape
    local_heads = local_width // HD
    key_count = key_rows.shape[0]
    query_blocks = queries.reshape(seq_rows // block_rows, block_rows, local_heads, HD)
    grad_blocks = out_grad.reshape(seq_rows // block_rows, block_rows, local_heads, HD)
    key_heads = key_rows.reshape(key_count, local_heads, HD)
    value_heads = value_rows.reshape(key_count, local_heads, HD)
    block_starts = jnp.arange(seq_rows // block_rows, dtype=jnp.int32) * block_rows

    def back_block(running, pieces):
        key_sum, value_sum = running
        query_block, grad_block, block_total, offset = pieces
        scores = jnp.einsum(
            "qhd,khd->hqk", query_block, key_heads, preferred_element_type=jnp.float32
        )
        probs = jnp.where(
            rule(offset, block_rows)[None], jnp.exp(scores - block_total[:, :, None]), 0.0
        )
        probs_low = probs.astype(jnp.bfloat16)
        prob_grad = jnp.einsum(
            "qhd,khd->hqk", grad_block, value_heads, preferred_element_type=jnp.float32
        )
        row_delta = jnp.sum(probs * prob_grad, axis=2, keepdims=True)
        score_grad = (probs * (prob_grad - row_delta)).astype(jnp.bfloat16)
        query_grad = jnp.einsum(
            "hqk,khd->qhd", score_grad, key_heads, preferred_element_type=jnp.float32
        )
        key_sum = key_sum + jnp.einsum(
            "hqk,qhd->khd", score_grad, query_block, preferred_element_type=jnp.float32
        )
        value_sum = value_sum + jnp.einsum(
            "hqk,qhd->khd", probs_low, grad_block, preferred_element_type=jnp.float32
        )
        return (
            (key_sum, value_sum),
            query_grad.astype(jnp.bfloat16).reshape(block_rows, local_width),
        )

    zero_sum = jnp.zeros((key_count, local_heads, HD), jnp.float32)
    (key_sum, value_sum), query_grads = lax.scan(
        back_block, (zero_sum, zero_sum), (query_blocks, grad_blocks, log_total, block_starts)
    )
    return (
        query_grads.reshape(seq_rows, local_width),
        key_sum.astype(jnp.bfloat16).reshape(key_count, local_width),
        value_sum.astype(jnp.bfloat16).reshape(key_count, local_width),
    )


def attend_groups(queries, key_rows, value_rows, rules, block_rows):
    results, totals = ([], [])
    for which_group, rule in enumerate(rules):
        mixed, log_total = attend_forward(queries, key_rows, value_rows, rule, block_rows)
        results.append(mixed)
        totals.append(log_total)
    return (results[0], totals)


def back_groups(queries, key_rows, value_rows, out_grad, totals, rules, block_rows):
    query_list, key_list, value_list = ([], [], [])
    for which_group, rule in enumerate(rules):
        query_grad, key_grad, value_grad = attend_backward(
            queries, key_rows, value_rows, out_grad, totals[which_group], rule, block_rows
        )
        query_list.append(query_grad)
        key_list.append(key_grad)
        value_list.append(value_grad)
    return (query_list[0], key_list[0], value_list[0])


def shards(
    tokens,
    enc_states,
    enc_len,
    cont_lengths,
    cotangent,
    self_qkv,
    self_out,
    cross_qkv,
    cross_out,
    ff_in,
    ff_out,
    head_bias,
    ff_bias,
    vec_params,
):
    gathered = (
        lax.all_gather(self_qkv, "dp", axis=1, tiled=True),
        lax.all_gather(self_out, "dp", axis=1, tiled=True),
        lax.all_gather(cross_qkv, "dp", axis=1, tiled=True),
        lax.all_gather(cross_out, "dp", axis=1, tiled=True),
        lax.all_gather(ff_in, "dp", axis=0, tiled=True),
        lax.all_gather(ff_out, "dp", axis=1, tiled=True),
        lax.all_gather(head_bias, "dp", axis=1, tiled=True),
        lax.all_gather(ff_bias, "dp", axis=0, tiled=True),
        lax.all_gather(vec_params, "dp", axis=1, tiled=True),
    )
    (
        w_self,
        w_self_out,
        w_cross,
        w_cross_out,
        w_hidden_in,
        w_hidden_out,
        bias_heads,
        bias_hidden,
        vectors,
    ) = gathered
    vectors = vectors.astype(jnp.float32)
    bias_heads = bias_heads.astype(jnp.float32)
    bias_hidden = bias_hidden.astype(jnp.float32)
    seq_rows = PROMPT + CONT_TOK
    block_rows = min(512, seq_rows)
    scaling = HD ** (-0.5)
    rows_dev = tokens.shape[0]

    def self_rule(which_group):
        bounds = PROMPT + jnp.cumsum(cont_lengths[which_group])
        positions = jnp.arange(seq_rows, dtype=jnp.int32)
        segment = jnp.sum((positions[:, None] >= bounds[None, :]).astype(jnp.int32), axis=1)

        def self_allowed(offset, number):
            row_ids = offset + jnp.arange(number, dtype=jnp.int32)
            row_segment = lax.dynamic_slice_in_dim(segment, offset, number)
            return (positions[None, :] <= row_ids[:, None]) & (
                (positions[None, :] < PROMPT) | (segment[None, :] == row_segment[:, None])
            )

        return self_allowed

    def cross_rule(which_group):
        usable = jnp.arange(ENC, dtype=jnp.int32) < enc_len[which_group]

        def cross_allowed(offset, number):
            return jnp.broadcast_to(usable[None, :], (number, ENC))

        return cross_allowed

    def spread(low_rows):
        return lax.all_gather(low_rows, "tensor", axis=0, tiled=True)

    def head_branch(values, weight):

        def term(offset, number):
            return product(values, weight)

        return lax.psum_scatter(
            term(jnp.int32(0), rows_dev * lax.axis_size("tensor")),
            "tensor",
            scatter_dimension=0,
            tiled=True,
        )

    def widen(low_rows):
        return lax.all_gather(low_rows, "tensor", axis=0, tiled=True)

    def narrow(term):
        return lax.psum_scatter(
            term(jnp.int32(0), rows_dev * lax.axis_size("tensor")),
            "tensor",
            scatter_dimension=0,
            tiled=True,
        )

    self_rules = [self_rule(0)]
    cross_rules = [cross_rule(0)]
    resid = tokens.astype(jnp.float32)
    enc_full = lax.all_gather(enc_states, "tensor", axis=0, tiled=True)
    normed_in, hat_one, inv_one = norm_forward(resid, vectors[0], vectors[3])
    attn_low = normed_in.astype(jnp.bfloat16)
    attn_full = spread(attn_low)
    queries = ((product(attn_full, w_self[0]) + bias_heads[0]) * scaling).astype(jnp.bfloat16)
    key_rows = product(attn_full, w_self[1]).astype(jnp.bfloat16)
    value_rows = (product(attn_full, w_self[2]) + bias_heads[1]).astype(jnp.bfloat16)
    mixed, self_totals = attend_groups(queries, key_rows, value_rows, self_rules, block_rows)
    after_one = resid + (head_branch(mixed, w_self_out) + vectors[6])
    normed_mid, hat_two, inv_two = norm_forward(after_one, vectors[1], vectors[4])
    cross_low = normed_mid.astype(jnp.bfloat16)
    cross_full = spread(cross_low)
    cross_queries = ((product(cross_full, w_cross[0]) + bias_heads[2]) * scaling).astype(
        jnp.bfloat16
    )
    cross_keys = product(enc_full, w_cross[1]).astype(jnp.bfloat16)
    cross_values = (product(enc_full, w_cross[2]) + bias_heads[3]).astype(jnp.bfloat16)
    cross_mixed, cross_totals = attend_groups(
        cross_queries, cross_keys, cross_values, cross_rules, block_rows
    )
    after_two = after_one + (head_branch(cross_mixed, w_cross_out) + vectors[7])
    normed_out, hat_three, inv_three = norm_forward(after_two, vectors[2], vectors[5])
    hidden_low = normed_out.astype(jnp.bfloat16)
    hidden_full = spread(hidden_low)
    pre_act = product(hidden_full, w_hidden_in) + bias_hidden
    activation = gelu_value(pre_act).astype(jnp.bfloat16)

    def term(offset, number):
        return product(activation, w_hidden_out)

    after_three = after_two + (
        lax.psum_scatter(
            term(jnp.int32(0), rows_dev * lax.axis_size("tensor")),
            "tensor",
            scatter_dimension=0,
            tiled=True,
        )
        + vectors[8]
    )
    layer_out = after_three.astype(jnp.bfloat16)
    gradient = cotangent.astype(jnp.float32)
    grad_low = gradient.astype(jnp.bfloat16)
    bias_out_three = jnp.sum(grad_low.astype(jnp.float32), axis=0)
    grad_full = widen(grad_low)
    act_grad = (product_right_t(grad_full, w_hidden_out) * gelu_slope(pre_act)).astype(jnp.bfloat16)
    grad_hidden_out = product_left_t(activation, grad_full)
    grad_hidden_in = product_left_t(hidden_full, act_grad)
    grad_bias_hidden = jnp.sum(act_grad.astype(jnp.float32), axis=0)

    def hidden_term(offset, number):
        return product_right_t(act_grad, w_hidden_in)

    input_part, gain_three, shift_three = norm_backward(
        narrow(hidden_term), hat_three, inv_three, vectors[2]
    )
    gradient = gradient + input_part
    grad_low = gradient.astype(jnp.bfloat16)
    bias_out_two = jnp.sum(grad_low.astype(jnp.float32), axis=0)
    grad_full = widen(grad_low)
    grad_cross_out = product_left_t(cross_mixed, grad_full)
    mixed_grad = product_right_t(grad_full, w_cross_out).astype(jnp.bfloat16)
    cross_query_grad, cross_key_grad, cross_value_grad = back_groups(
        cross_queries, cross_keys, cross_values, mixed_grad, cross_totals, cross_rules, block_rows
    )
    grad_cross = jnp.stack(
        [
            product_left_t(cross_full, cross_query_grad) * scaling,
            product_left_t(enc_full, cross_key_grad),
            product_left_t(enc_full, cross_value_grad),
        ]
    )
    bias_cross_query = jnp.sum(cross_query_grad.astype(jnp.float32), axis=0) * scaling
    bias_cross_value = jnp.sum(cross_value_grad.astype(jnp.float32), axis=0)
    enc_grad = lax.psum_scatter(
        product_right_t(cross_key_grad, w_cross[1]) + product_right_t(cross_value_grad, w_cross[2]),
        "tensor",
        scatter_dimension=0,
        tiled=True,
    )

    def cross_term(offset, number):
        return product_right_t(cross_query_grad, w_cross[0]) * scaling

    input_part, gain_two, shift_two = norm_backward(
        narrow(cross_term), hat_two, inv_two, vectors[1]
    )
    gradient = gradient + input_part
    grad_low = gradient.astype(jnp.bfloat16)
    bias_out_one = jnp.sum(grad_low.astype(jnp.float32), axis=0)
    grad_full = widen(grad_low)
    grad_self_out = product_left_t(mixed, grad_full)
    self_mixed_grad = product_right_t(grad_full, w_self_out).astype(jnp.bfloat16)
    query_grad, key_grad, value_grad = back_groups(
        queries, key_rows, value_rows, self_mixed_grad, self_totals, self_rules, block_rows
    )
    grad_self = jnp.stack(
        [
            product_left_t(attn_full, query_grad) * scaling,
            product_left_t(attn_full, key_grad),
            product_left_t(attn_full, value_grad),
        ]
    )
    bias_self_query = jnp.sum(query_grad.astype(jnp.float32), axis=0) * scaling
    bias_self_value = jnp.sum(value_grad.astype(jnp.float32), axis=0)

    def self_term(offset, number):
        return (
            product_right_t(query_grad, w_self[0]) * scaling
            + product_right_t(key_grad, w_self[1])
            + product_right_t(value_grad, w_self[2])
        )

    input_part, gain_one, shift_one = norm_backward(narrow(self_term), hat_one, inv_one, vectors[0])
    input_grad = gradient + input_part
    vector_grads = jnp.stack(
        [
            gain_one,
            gain_two,
            gain_three,
            shift_one,
            shift_two,
            shift_three,
            bias_out_one,
            bias_out_two,
            bias_out_three,
        ]
    )
    head_grads = jnp.stack([bias_self_query, bias_self_value, bias_cross_query, bias_cross_value])
    results = (
        lax.psum_scatter(grad_self, "dp", scatter_dimension=1, tiled=True),
        lax.psum_scatter(grad_self_out, "dp", scatter_dimension=1, tiled=True),
        lax.psum_scatter(grad_cross, "dp", scatter_dimension=1, tiled=True),
        lax.psum_scatter(grad_cross_out, "dp", scatter_dimension=1, tiled=True),
        lax.psum_scatter(grad_hidden_in, "dp", scatter_dimension=0, tiled=True),
        lax.psum_scatter(grad_hidden_out, "dp", scatter_dimension=1, tiled=True),
        lax.psum_scatter(head_grads, "dp", scatter_dimension=1, tiled=True),
        lax.psum_scatter(grad_bias_hidden, "dp", scatter_dimension=0, tiled=True),
        lax.psum_scatter(vector_grads, "dp", scatter_dimension=1, tiled=True),
    )
    vector_total = lax.psum(results[8], "tensor")
    return (
        layer_out,
        input_grad,
        enc_grad,
        results[0],
        results[1],
        results[2],
        results[3],
        results[4],
        results[5],
        results[6],
        results[7],
        vector_total,
    )


def hidden_kernel(x0_ref, x1_ref, e0_ref, e1_ref, w_in_ref, w_out_ref, bias_ref, act_ref, grad_ref, sum_ref):
    chunk = 256
    sum_ref[...] = jnp.zeros_like(sum_ref)
    count = x0_ref.shape[0]

    for which, (x_ref, e_ref) in enumerate(((x0_ref, e0_ref), (x1_ref, e1_ref))):

        def step(index, carry, which=which, x_ref=x_ref, e_ref=e_ref):
            rows = pl.ds(pl.multiple_of(index * chunk, chunk), chunk)
            out_rows = pl.ds(pl.multiple_of(which * count + index * chunk, chunk), chunk)
            value = dot_nn(x_ref[rows, :], w_in_ref[...]) + bias_ref[...]
            upper = dot_nn(e_ref[rows, :], w_out_ref[...])
            square = value * value
            inner = jnp.tanh(value * (GELU_C + (GELU_C * GELU_A) * square))
            half = 0.5 + 0.5 * inner
            act_ref[out_rows, :] = (value * half).astype(act_ref.dtype)
            slope = half + (value * (half * (1.0 - inner))) * (GELU_C + (3.0 * GELU_C * GELU_A) * square)
            grad = (upper * slope).astype(grad_ref.dtype)
            grad_ref[out_rows, :] = grad
            sum_ref[...] += jnp.sum(grad.astype(jnp.float32), axis=0, keepdims=True)
            return carry

        lax.fori_loop(0, count // chunk, step, 0, unroll=2)


def hidden_units(rows, grads, weights, bias, tile=512):
    count, model = rows[0].shape
    width = weights.shape[1] // 2
    tiles = width // tile
    whole = pl.BlockSpec((count, model), lambda i: (0, 0))
    weight = pl.BlockSpec((model, tile), lambda i: (0, i))
    weight_out = pl.BlockSpec((model, tile), lambda i: (0, tiles + i))
    line = pl.BlockSpec((1, tile), lambda i: (0, i))
    out = pl.BlockSpec((2 * count, tile), lambda i: (0, i))
    return pl.pallas_call(
        hidden_kernel,
        grid=(tiles,),
        in_specs=[whole] * 4 + [weight, weight_out, line],
        out_specs=[out, out, line],
        out_shape=[
            jax.ShapeDtypeStruct((2 * count, width), jnp.bfloat16),
            jax.ShapeDtypeStruct((2 * count, width), jnp.bfloat16),
            jax.ShapeDtypeStruct((1, width), jnp.float32),
        ],
        cost_estimate=pl.CostEstimate(
            flops=8 * count * model * width,
            bytes_accessed=4 * (2 * count * model + model * width + 2 * count * width),
            transcendentals=2 * count * width,
        ),
    )(*rows, *grads, weights, weights, bias)


MESH = pl.DeviceIdType.MESH


def weight_grad_kernel(*refs):
    rows_ref, refs = refs[0], refs[1:]
    sides, (rows_out, out_ref, turned, send, recv) = (refs[:6], refs[6:12]), refs[12:]
    count, depth = sides[0][0].shape[0], sides[0][4].shape[0]
    step_of, tiles = pl.program_id(0), pl.num_programs(0) // 2

    def copy():
        return pltpu.make_async_remote_copy(
            src_ref=rows_ref,
            dst_ref=rows_out,
            send_sem=send,
            recv_sem=recv,
            device_id={"zlo": 1 - lax.axis_index("zlo")},
            device_id_type=MESH,
        )

    @pl.when(step_of == 0)
    def _():
        barrier = pltpu.get_barrier_semaphore()
        pl.semaphore_signal(
            barrier, inc=1, device_id={"zlo": 1 - lax.axis_index("zlo")}, device_id_type=MESH
        )
        pl.semaphore_wait(barrier, 1)
        copy().start()

    for half, (x0_ref, x1_ref, x2_ref, x3_ref, near_ref, far_ref) in enumerate(sides):

        @pl.when(step_of == half * tiles)
        def _(blocks=(x0_ref, x1_ref, x2_ref, x3_ref)):
            for which, x_ref in enumerate(blocks):
                turned[:, which * count : (which + 1) * count] = jnp.transpose(x_ref[...])

        @pl.when(step_of // tiles == half)
        def _(near_ref=near_ref, far_ref=far_ref):
            def step(index, carry):
                rows = pl.ds(pl.multiple_of(index * 256, 256), 256)
                total = dot_nn(turned[rows, :depth], near_ref[...]) + dot_nn(turned[rows, depth:], far_ref[...])
                out_ref[rows, :] = total.astype(out_ref.dtype)
                return carry

            lax.fori_loop(0, out_ref.shape[0] // 256, step, 0, unroll=2)

    @pl.when(step_of == 2 * tiles - 1)
    def _():
        copy().wait()


def weight_grads(rows, first, second, collective_id, tile=512):
    blocks, near, _ = first
    (count, model), (depth, width) = blocks[0].shape, near.shape
    tiles = width // tile
    anywhere = pl.BlockSpec(memory_space=pl.ANY)
    whole = pl.BlockSpec((count, model), lambda i: (0, 0))

    def early(size):
        return pl.BlockSpec((size, tile), lambda i: (0, jnp.minimum(i, tiles - 1)))

    def late(size):
        return pl.BlockSpec((size, tile), lambda i: (0, jnp.maximum(i - tiles, 0)))

    return pl.pallas_call(
        weight_grad_kernel,
        grid=(2 * tiles,),
        in_specs=[anywhere] + [whole] * 4 + [early(depth)] * 2 + [whole] * 4 + [late(depth)] * 2,
        out_specs=[anywhere, pl.BlockSpec((model, tile), lambda i: (0, i))],
        out_shape=[
            jax.ShapeDtypeStruct(rows.shape, rows.dtype),
            jax.ShapeDtypeStruct((model, 2 * width), near.dtype),
        ],
        scratch_shapes=[
            pltpu.VMEM((model, 4 * count), near.dtype),
            pltpu.SemaphoreType.DMA,
            pltpu.SemaphoreType.DMA,
        ],
        compiler_params=pltpu.CompilerParams(collective_id=collective_id, has_side_effects=True),
        cost_estimate=pl.CostEstimate(flops=16 * count * model * width, bytes_accessed=0, transcendentals=0),
    )(rows, *first[0], *first[1:], *second[0], *second[1:])


LINKS = ("core", "x", "y", "zhi", "zlo")


def start_kernel(
    tokens,
    enc,
    self_qkv,
    self_out,
    cross_qkv,
    cross_out,
    w_in,
    w_out,
    small,
    token_rows,
    attn,
    g_self,
    cross_rows,
    hidden,
    enc_full,
    small_all,
    held,
    normed,
    gathered,
    send,
    recv,
    local,
):
    y, x, core, zhi, zlo = (lax.axis_index(axis) for axis in AXES)
    crossing = core != zhi
    rows = tokens.shape[0]
    part = self_out.shape[0]
    counts = {"sent": 0, "local": 0}

    def push(source, target, axis):
        index = counts["sent"]
        counts["sent"] += 1
        copy = pltpu.make_async_remote_copy(
            src_ref=source,
            dst_ref=target,
            send_sem=send.at[index],
            recv_sem=recv.at[index],
            device_id={axis: 1 - lax.axis_index(axis)},
            device_id_type=MESH,
        )
        copy.start()
        return copy

    def keep(source, target):
        index = counts["local"]
        counts["local"] += 1
        copy = pltpu.make_async_copy(source, target, local.at[index])
        copy.start()
        return copy

    def moving(source, target, source_here, target_here):
        index, index_here = counts["sent"], counts["local"]
        counts["sent"] += 1
        counts["local"] += 1

        def remote():
            return pltpu.make_async_remote_copy(
                src_ref=source,
                dst_ref=target,
                send_sem=send.at[index],
                recv_sem=recv.at[index],
                device_id={"core": zhi, "zhi": core},
                device_id_type=MESH,
            )

        def here():
            return pltpu.make_async_copy(source_here, target_here, local.at[index_here])

        @pl.when(crossing)
        def _():
            remote().start()

        @pl.when(jnp.logical_not(crossing))
        def _():
            here().start()

        def wait():
            @pl.when(crossing)
            def _():
                remote().wait()

            @pl.when(jnp.logical_not(crossing))
            def _():
                here().wait()

        return wait

    def lanes(block, size):
        return pl.ds(pl.multiple_of(block * size, size), size)

    barrier = pltpu.get_barrier_semaphore()
    for axis in LINKS:
        pl.semaphore_signal(barrier, inc=1, device_id={axis: 1 - lax.axis_index(axis)}, device_id_type=MESH)

    @pl.when(crossing)
    def _():
        pl.semaphore_signal(barrier, inc=1, device_id={"core": zhi, "zhi": core}, device_id_type=MESH)

    pl.semaphore_wait(barrier, len(LINKS) + crossing.astype(jnp.int32))

    wait_tokens = moving(tokens, held, tokens, held)
    own_small = keep(small, gathered.at[y, x, core, zhi, zlo])
    own_rows = pl.ds(pl.multiple_of(core * part, part), part)
    quarter = 2 * zhi + zlo

    self_width = self_out.shape[1] // 2
    hidden_width = w_in.shape[1] // 2
    cross_core = []
    for plane in range(4):
        target = cross_rows.at[own_rows, lanes(4 * plane + quarter, self_width)]
        shard = cross_qkv.at[plane] if plane < 3 else cross_out
        cross_core.append(keep(shard.at[:, lanes(core, self_width)], target))
        cross_core.append(push(shard.at[:, lanes(1 - core, self_width)], target, "core"))
    own_small.wait()
    small_core = push(gathered.at[y, x, core, zhi, zlo], gathered.at[y, x, core, zhi, zlo], "core")
    target = g_self.at[pl.ds(0, 3), y, x, own_rows, lanes(zhi, self_width)]
    target_out = g_self.at[3, y, x, own_rows, lanes(zhi, self_width)]
    self_core = [
        keep(self_qkv.at[:, :, lanes(core, self_width)], target),
        push(self_qkv.at[:, :, lanes(1 - core, self_width)], target, "core"),
        keep(self_out.at[:, lanes(core, self_width)], target_out),
        push(self_out.at[:, lanes(1 - core, self_width)], target_out, "core"),
    ]
    hidden_core = []
    for plane, shard in enumerate((w_in, w_out)):
        target = hidden.at[plane, own_rows]
        hidden_core.append(keep(shard.at[:, lanes(core, hidden_width)], target))
        hidden_core.append(push(shard.at[:, lanes(1 - core, hidden_width)], target, "core"))
    for copy in cross_core:
        copy.wait()
    regions = [cross_rows.at[:, lanes(4 * plane + quarter, self_width)] for plane in range(4)]
    cross_zlo = [push(region, region, "zlo") for region in regions]
    small_core.wait()
    region = gathered.at[y, x, :, zhi, zlo]
    small_x = push(region, region, "x")
    for copy in self_core:
        copy.wait()
    small_x.wait()
    region = gathered.at[y, :, :, zhi, zlo]
    small_y = push(region, region, "y")
    for copy in cross_zlo:
        copy.wait()
    small_y.wait()

    def over_plane(target, width):
        first, second = pl.ds(0, width), pl.ds(width, width)
        region_a, region_b = target.at[:, y, x, :, first], target.at[:, y, x, :, second]
        steps = (push(region_a, region_a, "x"), push(region_b, region_b, "y"))

        def second_steps():
            steps[0].wait()
            region_a = target.at[:, y, :, :, first]
            step_a = push(region_a, region_a, "y")
            steps[1].wait()
            region_b = target.at[:, :, x, :, second]
            return step_a, push(region_b, region_b, "x")

        return second_steps

    wait_tokens()
    keep_tokens = keep(held, token_rows)
    region = gathered.at[:, :, :, zhi, zlo]
    small_zhi = push(region, region, "zhi")
    region = g_self.at[:, y, x, :, lanes(zhi, self_width)]
    self_zhi = push(region, region, "zhi")
    wait_enc = moving(enc, enc_full.at[2 * zhi + zlo], enc, enc_full.at[2 * core + zlo])
    regions = [cross_rows.at[:, lanes(2 * plane + zhi, 2 * self_width)] for plane in range(4)]
    cross_zhi = [push(region, region, "zhi") for region in regions]
    gain = jnp.concatenate([gathered[d // 4, d // 2 % 2, d % 2, zhi, zlo, 0:1, :] for d in range(8)], axis=1)
    shift = jnp.concatenate([gathered[d // 4, d // 2 % 2, d % 2, zhi, zlo, 3:4, :] for d in range(8)], axis=1)

    def norm_step(step, carry):
        block = pl.ds(pl.multiple_of(step * 64, 64), 64)
        values = held[block, :].astype(jnp.float32)
        centred = values - jnp.mean(values, axis=1, keepdims=True)
        inverse = lax.rsqrt(jnp.mean(centred * centred, axis=1, keepdims=True) + EPSILON)
        normed[block, :] = (centred * inverse * gain + shift).astype(normed.dtype)
        return carry

    lax.fori_loop(0, rows // 64, norm_step, 0)
    attn_zlo = push(normed, attn.at[pl.ds(2 * rows, rows)], "zlo")
    attn_core = push(normed, attn.at[pl.ds(rows, rows)], "core")
    attn_own = keep(normed, attn.at[pl.ds(0, rows)])

    wait_enc()
    region = enc_full.at[2 * core + zlo]
    enc_zlo = push(region, region, "zlo")
    enc_core = push(region, region, "core")
    self_zhi.wait()
    self_second = over_plane(g_self, self_width)
    self_last = self_second()
    small_zhi.wait()
    region = gathered.at[:, :, :, :, zlo]
    small_zlo = push(region, region, "zlo")
    enc_zlo.wait()
    region = enc_full.at[2 * core + 1 - zlo]
    enc_diagonal = push(region, region, "core")
    attn_zlo.wait()
    attn_diagonal = push(attn.at[pl.ds(2 * rows, rows)], attn.at[pl.ds(3 * rows, rows)], "core")
    small_zlo.wait()
    keep_small = keep(gathered, small_all)
    for copy in (
        *self_last,
        *cross_zhi,
        *hidden_core,
        attn_core,
        attn_diagonal,
        enc_core,
        enc_diagonal,
        attn_own,
        keep_tokens,
        keep_small,
    ):
        copy.wait()


def start_exchange(tokens, enc, self_qkv, self_out, cross_qkv, cross_out, w_in, w_out, small):
    rows, model = tokens.shape
    part, shard = self_out.shape
    low_type = tokens.dtype
    shapes = [
        jax.ShapeDtypeStruct((rows, model), low_type),
        jax.ShapeDtypeStruct((4 * rows, model), low_type),
        jax.ShapeDtypeStruct((4, 2, 2, 2 * part, shard), low_type),
        jax.ShapeDtypeStruct((2 * part, 8 * shard), low_type),
        jax.ShapeDtypeStruct((2, 2 * part, w_in.shape[1] // 2), low_type),
        jax.ShapeDtypeStruct((4, enc.shape[0], model), low_type),
        jax.ShapeDtypeStruct((2,) * 5 + small.shape, small.dtype),
    ]
    anywhere = pl.BlockSpec(memory_space=pl.ANY)
    return pl.pallas_call(
        start_kernel,
        out_shape=shapes,
        in_specs=[anywhere] * 9,
        out_specs=[anywhere] * len(shapes),
        scratch_shapes=[
            pltpu.VMEM((rows, model), low_type),
            pltpu.VMEM((rows, model), low_type),
            pltpu.VMEM((2,) * 5 + small.shape, small.dtype),
            pltpu.SemaphoreType.DMA((40,)),
            pltpu.SemaphoreType.DMA((40,)),
            pltpu.SemaphoreType.DMA((20,)),
        ],
        compiler_params=pltpu.CompilerParams(collective_id=0, has_side_effects=True),
    )(tokens, enc, self_qkv, self_out, cross_qkv, cross_out, w_in, w_out, small)


def finish_kernel(
    ff_in,
    ff_out,
    cross,
    cross_beyond,
    self_q,
    self_k,
    self_v,
    self_o,
    enc_part,
    small,
    ff_in_out,
    ff_out_out,
    cross_qkv_out,
    cross_out_out,
    self_qkv_out,
    self_out_out,
    enc_out,
    small_out,
    cross_own,
    cross_got,
    cross_low,
    cross_got_low,
    cross_total,
    enc_own,
    enc_got,
    enc_sum,
    enc_far,
    enc_low,
    self_own,
    self_got,
    low_a,
    low_b,
    self_got_low,
    self_total,
    self_last,
    small_sum,
    small_got_0,
    small_got_1,
    small_got_2,
    small_got_3,
    small_got_4,
    send,
    recv,
    local,
):
    y, x, core, zhi, zlo = (lax.axis_index(axis) for axis in AXES)
    crossing = core != zhi
    small_got = (small_got_0, small_got_1, small_got_2, small_got_3, small_got_4)
    counts = {"sent": 0, "local": 0}

    def push(source, target, axis):
        index = counts["sent"]
        counts["sent"] += 1
        copy = pltpu.make_async_remote_copy(
            src_ref=source,
            dst_ref=target,
            send_sem=send.at[index],
            recv_sem=recv.at[index],
            device_id={axis: 1 - lax.axis_index(axis)},
            device_id_type=MESH,
        )
        copy.start()
        return copy

    def keep(source, target):
        index = counts["local"]
        counts["local"] += 1
        copy = pltpu.make_async_copy(source, target, local.at[index])
        copy.start()
        return copy

    def moving(source, target, source_here, target_here):
        index, index_here = counts["sent"], counts["local"]
        counts["sent"] += 1
        counts["local"] += 1

        def remote():
            return pltpu.make_async_remote_copy(
                src_ref=source,
                dst_ref=target,
                send_sem=send.at[index],
                recv_sem=recv.at[index],
                device_id={"core": zhi, "zhi": core},
                device_id_type=MESH,
            )

        def here():
            return pltpu.make_async_copy(source_here, target_here, local.at[index_here])

        @pl.when(crossing)
        def _():
            remote().start()

        @pl.when(jnp.logical_not(crossing))
        def _():
            here().start()

        def wait():
            @pl.when(crossing)
            def _():
                remote().wait()

            @pl.when(jnp.logical_not(crossing))
            def _():
                here().wait()

        return wait

    def lanes(block, size):
        return pl.ds(pl.multiple_of(block * size, size), size)

    def add(target, *terms):
        def step(index, carry):
            rows = pl.ds(pl.multiple_of(index * 64, 64), 64)
            value = sum(term[rows, :].astype(jnp.float32) for term in terms)
            target[rows, :] = value.astype(target.dtype)
            return carry

        lax.fori_loop(0, target.shape[0] // 64, step, 0)

    barrier = pltpu.get_barrier_semaphore()
    for axis in LINKS:
        pl.semaphore_signal(barrier, inc=1, device_id={axis: 1 - lax.axis_index(axis)}, device_id_type=MESH)

    @pl.when(crossing)
    def _():
        pl.semaphore_signal(barrier, inc=1, device_id={"core": zhi, "zhi": core}, device_id_type=MESH)

    pl.semaphore_wait(barrier, len(LINKS) + crossing.astype(jnp.int32))

    last = []
    half = self_q.shape[3] // 2

    def to_cores(values, out):
        part, width = values.shape[0] // 2, values.shape[1]
        there, here = lanes(1 - core, part), lanes(core, part)
        last.append(push(values.at[there], out.at[:, lanes(core, width)], "core"))
        last.append(keep(values.at[here], out.at[:, lanes(core, width)]))

    def planes_to_cores(values, qkv_out, out_out):
        part = values.shape[0] // 2
        there, here = lanes(1 - core, part), lanes(core, part)
        for plane in range(4):
            columns_of = pl.ds(plane * half, half)
            out = qkv_out.at[plane, :, lanes(core, half)] if plane < 3 else out_out.at[:, lanes(core, half)]
            last.append(push(values.at[there, columns_of], out, "core"))
            last.append(keep(values.at[here, columns_of], out))

    cross_keep = [keep(cross, cross_own), keep(cross_beyond, cross_got)]

    first, second = pl.ds(0, half), pl.ds(half, half)
    parts = (self_q, self_k, self_v, self_o)
    self_x, self_y, own_a, own_b = [], [], [], []
    for plane, partial in enumerate(parts):
        columns_of = pl.ds(plane * half, half)
        self_x.append(push(partial.at[:, 1 - x, :, first], self_got.at[0, :, :, columns_of], "x"))
        self_y.append(push(partial.at[1 - y, :, :, second], self_got.at[1, :, :, columns_of], "y"))
        own_a.append(keep(partial.at[:, x, :, first], self_own.at[0, :, :, columns_of]))
        own_b.append(keep(partial.at[y, :, :, second], self_own.at[1, :, :, columns_of]))
    enc_core = push(enc_part.at[1 - core], enc_got, "core")
    enc_keep = keep(enc_part.at[core], enc_own)

    to_cores(ff_in, ff_in_out)
    to_cores(ff_out, ff_out_out)

    small_first, small_size = 0, 32

    def small_send(stage):
        rows = small_size // 2
        away = small_first + (1 - lax.axis_index(AXES[stage])) * rows
        return push(small_sum.at[pl.ds(away, rows)], small_got[stage], AXES[stage])

    def small_add(stage, copy):
        copy.wait()
        rows, got = small_size // 2, small_got[stage]
        mine = small_first + lax.axis_index(AXES[stage]) * rows

        def step(index, carry):
            small_sum[mine + index] += got[index]
            return carry

        lax.fori_loop(0, rows, step, 0)
        return mine, rows

    keep(small, small_sum).wait()
    small_copy = small_send(0)
    for copy in cross_keep:
        copy.wait()

    def cross_step(target, which, *others):
        def step(index, carry):
            rows = pl.ds(pl.multiple_of(index * 64, 64), 64)
            for plane in range(4):
                source = pl.ds(pl.multiple_of((2 * plane + which) * half, half), half)
                columns_of = pl.ds(plane * half, half)
                value = cross_own[rows, source].astype(jnp.float32) + cross_got[rows, source].astype(jnp.float32)
                for other in others:
                    value += other[rows, columns_of].astype(jnp.float32)
                target[rows, columns_of] = value.astype(target.dtype)
            return carry

        lax.fori_loop(0, target.shape[0] // 64, step, 0)

    cross_step(cross_low, 1 - zlo)
    cross_zlo = push(cross_low, cross_got_low, "zlo")
    enc_core.wait()
    enc_keep.wait()
    add(enc_sum, enc_own.at[1 - zlo], enc_got.at[1 - zlo])
    enc_zlo = push(enc_sum, enc_far, "zlo")
    small_first, small_size = small_add(0, small_copy)
    small_copy = small_send(1)
    for copy in own_a + self_x:
        copy.wait()
    add(low_a, self_own.at[0, 1 - y], self_got.at[0, 1 - y])
    a_second = push(low_a, self_got_low.at[0], "y")
    for copy in own_b + self_y:
        copy.wait()
    add(low_b, self_own.at[1, 1 - x], self_got.at[1, 1 - x])
    b_second = push(low_b, self_got_low.at[1], "x")
    small_first, small_size = small_add(1, small_copy)
    small_copy = small_send(2)
    add(self_total.at[0], self_own.at[0, y], self_got.at[0, y])
    add(self_total.at[1], self_own.at[1, x], self_got.at[1, x])
    enc_zlo.wait()
    add(enc_low, enc_own.at[zlo], enc_got.at[zlo], enc_far)
    small_first, small_size = small_add(2, small_copy)
    small_copy = small_send(3)
    a_second.wait()
    add(self_total.at[0], self_total.at[0], self_got_low.at[0])
    b_second.wait()
    add(self_total.at[1], self_total.at[1], self_got_low.at[1])
    add(low_a, self_total.at[1 - zhi])
    self_zhi = push(low_a, self_last, "zhi")
    wait_enc = moving(enc_low, enc_out, enc_low, enc_out)
    cross_zlo.wait()
    cross_step(cross_total, zlo, cross_got_low)
    planes_to_cores(cross_total, cross_qkv_out, cross_out_out)
    small_first, small_size = small_add(3, small_copy)
    small_copy = small_send(4)
    self_zhi.wait()
    add(self_total.at[zhi], self_total.at[zhi], self_last)
    planes_to_cores(self_total.at[zhi], self_qkv_out, self_out_out)
    small_first, small_size = small_add(4, small_copy)
    keep(small_sum.at[small_first], small_out).wait()
    wait_enc()
    for copy in last:
        copy.wait()


def finish(ff_in, ff_out, cross, cross_beyond, self_parts, enc, small):
    rows, width = ff_in.shape
    part, half = self_parts[0].shape[2], self_parts[0].shape[3] // 2
    low_type, enc_shape = enc.dtype, enc.shape[2:]
    wide = 4 * half

    def full(*shape):
        return jax.ShapeDtypeStruct(shape, jnp.float32)

    shapes = [
        full(rows // 2, 2 * width),
        full(rows // 2, 2 * width),
        full(3, part // 2, 2 * half),
        full(part // 2, 2 * half),
        full(3, part // 2, 2 * half),
        full(part // 2, 2 * half),
        jax.ShapeDtypeStruct(enc_shape, low_type),
        jax.ShapeDtypeStruct(small.shape[1:], small.dtype),
    ]
    anywhere = pl.BlockSpec(memory_space=pl.ANY)
    return pl.pallas_call(
        finish_kernel,
        out_shape=shapes,
        in_specs=[anywhere] * 10,
        out_specs=[anywhere] * len(shapes),
        scratch_shapes=[
            pltpu.VMEM((part, 2 * wide), low_type),
            pltpu.VMEM((part, 2 * wide), low_type),
            pltpu.VMEM((part, wide), low_type),
            pltpu.VMEM((part, wide), low_type),
            pltpu.VMEM((part, wide), jnp.float32),
            pltpu.VMEM((2, *enc_shape), low_type),
            pltpu.VMEM((2, *enc_shape), low_type),
            pltpu.VMEM(enc_shape, low_type),
            pltpu.VMEM(enc_shape, low_type),
            pltpu.VMEM(enc_shape, low_type),
            pltpu.VMEM((2, 2, part, wide), low_type),
            pltpu.VMEM((2, 2, part, wide), low_type),
            pltpu.VMEM((part, wide), low_type),
            pltpu.VMEM((part, wide), low_type),
            pltpu.VMEM((2, part, wide), low_type),
            pltpu.VMEM((2, part, wide), jnp.float32),
            pltpu.VMEM((part, wide), low_type),
            pltpu.VMEM(small.shape, small.dtype),
        ]
        + [pltpu.VMEM((32 >> stage, *small.shape[1:]), small.dtype) for stage in range(1, 6)]
        + [pltpu.SemaphoreType.DMA((40,))] * 3,
        compiler_params=pltpu.CompilerParams(collective_id=1, has_side_effects=True),
        cost_estimate=pl.CostEstimate(flops=40_000_000_000, bytes_accessed=0, transcendentals=0),
    )(ff_in, ff_out, cross, cross_beyond, *self_parts, enc, small)


def trade(rows, axis, name="trade"):
    with jax.named_scope(name):
        return lax.ppermute(rows, axis, [(0, 1), (1, 0)])


def after(value, *others):
    return lax.optimization_barrier((value, *others))[0]


def regroup_sent(rows, name):
    with jax.named_scope("re_" + name):
        return lax.ppermute(rows, ("core", "zhi"), [(1, 2), (2, 1)])


def regroup_done(rows, moved):
    return jnp.where(lax.axis_index("core") == lax.axis_index("zhi"), rows, moved)


def regroup(rows, name="regroup"):
    return regroup_done(rows, regroup_sent(rows, name))


def in_order(index, own, other, axis):
    return jnp.concatenate(
        [jnp.where(index == 0, own, other), jnp.where(index == 0, other, own)], axis=axis
    )


def low(values):
    return values.astype(jnp.bfloat16)


def half_of(values, index, axis):
    size = values.shape[axis] // 2
    return lax.dynamic_slice_in_dim(values, index * size, size, axis)


def over_chips(rows):
    return lax.all_gather(rows, ("y", "x"), axis=0, tiled=True)


def sum_over_chips(partial):
    return lax.psum_scatter(partial, ("y", "x"), scatter_dimension=0, tiled=True)


def spread_rows(rows, name):
    beyond = trade(rows, "zlo", name + "_z")
    return (
        jnp.concatenate([rows, trade(rows, "core", name + "_c")], axis=0),
        jnp.concatenate([beyond, trade(beyond, "core", name + "_zc")], axis=0),
    )


def sum_rows(near, far, term, name):
    size = near.shape[0] // 2
    far_sum = term(far[:size]) + trade(low(term(far[size:])), "core", name + "_zc")
    from_far = trade(low(far_sum), "zlo", name + "_z")
    near_other = trade(low(term(near[size:])), "core", name + "_c")
    return term(near[:size]) + near_other + from_far


def fast_layer(
    tokens,
    enc_states,
    enc_len,
    cont_lengths,
    cotangent,
    self_qkv,
    self_out,
    cross_qkv,
    cross_out,
    ff_in,
    ff_out,
    head_bias,
    ff_bias,
    vec_params,
):
    core, zhi, zlo = lax.axis_index("core"), lax.axis_index("zhi"), lax.axis_index("zlo")
    scaling = HD**-0.5
    model = tokens.shape[1]
    segments = cont_lengths.shape[1]

    flat = jnp.concatenate([vec_params.reshape(-1), head_bias.reshape(-1), ff_bias]).astype(jnp.float32)
    sizes = (vec_params.size, head_bias.size, ff_bias.size)
    flat = jnp.pad(flat.reshape(-1, 128), ((0, 4), (0, 0)))
    token_rows, attn_rows, w_self, w_cross, hidden, enc_full, small = start_exchange(
        tokens,
        enc_states,
        self_qkv,
        self_out.T,
        cross_qkv,
        cross_out.T,
        ff_in,
        ff_out.T,
        flat,
    )
    w_self = w_self.reshape(4, model, -1)
    w_cross = over_chips(w_cross)
    cross_width = w_cross.shape[1] // 4
    hidden_beyond = trade(hidden, "zhi", "wh_zhi")
    w_qkv, w_so = jnp.concatenate([w_self[0], w_self[1], w_self[2]], axis=1), w_self[3]
    w_cq, w_ckv, w_co = jnp.split(w_cross, [cross_width, 3 * cross_width], axis=1)
    rows_of = model // 4
    width = w_self.shape[2]
    pairs, cross_pairs = width // PAIR, cross_width // PAIR
    enc_full = enc_full.reshape(-1, model)
    attn_near, attn_far = attn_rows[: attn_rows.shape[0] // 2], attn_rows[attn_rows.shape[0] // 2 :]
    small = small.reshape(8, 4, -1)
    vec_part, head_part, ff_part = jnp.split(
        small[:, :, : sum(sizes)], [sizes[0], sizes[0] + sizes[1]], axis=2
    )
    vectors = vec_part[:, 0].reshape(8, 9, -1).transpose(1, 0, 2).reshape(9, model)
    heads = head_part.reshape(8, 4, 4, -1).transpose(2, 1, 0, 3).reshape(4, 2, 2, 2, -1)
    self_bias = lax.dynamic_index_in_dim(
        lax.dynamic_index_in_dim(heads[:2], zlo, 2, False), core, 2, False
    ).reshape(2, -1)
    cross_bias = lax.dynamic_index_in_dim(heads[2:], core, 3, False).reshape(2, -1)
    hidden_bias = ff_part.transpose(1, 0, 2).reshape(2, 2, 2, -1)
    hidden_bias = lax.dynamic_index_in_dim(
        lax.dynamic_index_in_dim(hidden_bias, zlo, 1, False), core, 1, False
    ).reshape(-1)

    lengths = regroup(jnp.concatenate([cont_lengths[0], enc_len]))
    places = jnp.stack(
        [512 * ((core != block // 2) + 2 * (zlo != block % 2)) for block in range(4)]
    ).astype(jnp.int32)
    bounds = PROMPT + jnp.concatenate(
        [jnp.zeros((1,), jnp.int32), jnp.cumsum(lengths[:segments]).astype(jnp.int32)]
    )
    self_meta = jnp.concatenate([places, bounds])
    cross_meta = lengths[segments:]

    resid = token_rows.astype(jnp.float32)
    _, hat_one, inv_one = norm_forward(resid, vectors[0], vectors[3])
    qkv_bias = jnp.concatenate([self_bias[0], jnp.zeros((width,), jnp.float32), self_bias[1]])
    qkv_scale = jnp.concatenate([jnp.full((width,), scaling), jnp.ones((2 * width,))]).astype(jnp.float32)
    def project(rows):
        return low((product(rows, w_qkv) + qkv_bias) * qkv_scale)

    qkv = project(attn_rows)
    count = qkv.shape[0]
    self_plan = functools.partial(self_sections, segments=segments)
    mixed, self_lse = attend(self_plan, self_meta, qkv, 0, qkv, pairs, 2 * pairs, pairs, 1152)
    mixed = after(mixed, hidden_beyond)
    hidden = in_order(zhi, hidden, after(hidden_beyond, mixed), 2).transpose(1, 0, 2)
    w_hidden = over_chips(hidden.reshape(hidden.shape[0], -1))
    w_in, w_out = jnp.split(w_hidden, 2, axis=1)
    near, far = mixed[: count // 2], mixed[count // 2 :]
    so_far = low(
        product_right_t(far[: count // 4], w_so)
        + trade(low(product_right_t(far[count // 4 :], w_so)), "core", "so_zc")
    )
    so_near_other = low(product_right_t(near[count // 4 :], w_so))
    so_near = product_right_t(near[: count // 4], w_so)
    grad_rows = regroup(after(cotangent, mixed), "cotangent")
    cross_kv = low(
        product(after(enc_full, grad_rows, so_far), w_ckv)
        + jnp.concatenate([jnp.zeros((cross_width,), jnp.float32), cross_bias[1]])
    )
    branch = so_near + trade(so_near_other, "core", "so_c") + after(trade(so_far, "zlo", "so_z"), cross_kv)
    after_one = resid + (branch + vectors[6])

    cot_beyond = trade(after(grad_rows, after_one), "zlo", "cot_z")
    cot_near = [grad_rows, trade(grad_rows, "core", "cot_c")]

    normed_mid, hat_two, inv_two = norm_forward(after_one, vectors[1], vectors[4])
    cross_low = low(normed_mid)
    cross_rows = jnp.concatenate([cross_low, trade(cross_low, "core", "cin")], axis=0)
    own_rows = cross_low.shape[0]
    cross_q = low((product(cross_rows, w_cq) + cross_bias[0]) * scaling)
    cross_plan = functools.partial(cross_sections, blocks=cross_q.shape[0] // BLOCK)
    cross_mixed, cross_lse = attend(
        cross_plan, cross_meta, cross_q, 0, cross_kv, 0, cross_pairs, cross_pairs, ENC
    )
    cross_mixed = after(cross_mixed, cot_beyond)
    other = trade(low(product_right_t(cross_mixed[own_rows:], w_co)), "core", "co_c")
    branch = product_right_t(cross_mixed[:own_rows], w_co) + other
    after_two = after_one + (branch + vectors[7])

    normed_out, hat_three, inv_three = norm_forward(after_two, vectors[2], vectors[5])
    mlp_in = low(normed_out)
    beyond = trade(mlp_in, "zlo", "mlp_z")
    mlp_near = [mlp_in, trade(mlp_in, "core", "mlp_c")]
    act_near, dpre_near, sum_near = hidden_units(mlp_near, cot_near, w_hidden, hidden_bias[None])
    bias_out_three = jnp.sum(grad_rows.astype(jnp.float32), axis=0)
    beyond = after(beyond, act_near, bias_out_three)
    mlp_far = [beyond, trade(beyond, "core", "mlp_zc")]
    cot_far = [cot_beyond, trade(cot_beyond, "core", "cot_zc")]
    act_far, dpre_far, sum_far = hidden_units(mlp_far, cot_far, w_hidden, hidden_bias[None])
    gradient = grad_rows.astype(jnp.float32)
    dmlp_far = low(
        product_right_t(dpre_far[:own_rows], w_in)
        + trade(low(product_right_t(dpre_far[own_rows:], w_in)), "core", "dmlp_zc")
    )
    mlp_term = product_right_t(dpre_near[:own_rows], w_in) + trade(
        low(product_right_t(dpre_near[own_rows:], w_in)), "core", "dmlp_c"
    )
    act_near, act_far = after(act_near, dmlp_far, mlp_term), after(act_far, dmlp_far, mlp_term)
    out_parts = [
        low(product_right_t(act_far[own_rows:], w_out)),
        product_right_t(act_far[:own_rows], w_out),
    ]
    out_far = low(out_parts[1] + trade(out_parts[0], "core", "out_zc"))
    dmlp_beyond, grad_hidden = weight_grads(
        dmlp_far, (cot_near + cot_far, act_near, act_far), (mlp_near + mlp_far, dpre_near, dpre_far), 2
    )
    mlp_term = mlp_term + dmlp_beyond
    out_far = trade(after(out_far, mlp_term), "zlo", "out_z")
    part, gain_three, shift_three = norm_backward(mlp_term, hat_three, inv_three, vectors[2])
    gradient = gradient + part

    grad_low = low(gradient)
    bias_out_two = jnp.sum(grad_low.astype(jnp.float32), axis=0)
    grad_both = jnp.concatenate([grad_low, trade(grad_low, "core", "e2")], axis=0)
    cross_mixed_grad = low(product(grad_both, w_co))
    cross_dq, cross_dk, cross_dv = attend_back(
        cross_plan,
        cross_meta,
        cross_q,
        0,
        cross_kv,
        0,
        cross_pairs,
        cross_mixed,
        cross_mixed_grad,
        cross_lse,
        cross_pairs,
        ENC,
    )
    cross_dq = after(cross_dq, out_far)
    other = trade(low(product_right_t(cross_dq[own_rows:], w_cq)), "core", "dcin")
    part, gain_two, shift_two = norm_backward(
        product_right_t(cross_dq[:own_rows], w_cq) + other, hat_two, inv_two, vectors[1]
    )
    gradient = gradient + part

    grad_low = low(gradient)
    bias_out_one = jnp.sum(grad_low.astype(jnp.float32), axis=0)
    beyond = trade(grad_low, "zlo", "e1_z")
    grad_near = jnp.concatenate([grad_low, trade(grad_low, "core", "e1_c")], axis=0)
    mixed_grad = low(product(grad_near, w_so))
    cross_parts = [
        low(product_left_t(cross_rows, after(cross_dq, grad_low))),
        low(product_left_t(enc_full, after(cross_dk, grad_low))),
        low(product_left_t(enc_full, after(cross_dv, grad_low))),
        low(product_left_t(after(grad_both, grad_low), cross_mixed)),
    ]
    grad_cross = jnp.concatenate(cross_parts, axis=1)
    act_near = after(act_near, grad_low)
    out_branch = product_right_t(act_near[:own_rows], w_out) + trade(
        low(product_right_t(act_near[own_rows:], w_out)), "core", "out_c"
    )
    layer_out = low(after_two + (out_branch + after(out_far, grad_low) + vectors[8]))
    beyond = after(beyond, mixed_grad, grad_cross, layer_out)
    cross_sum = sum_over_chips(grad_cross)
    grad_far = jnp.concatenate([beyond, trade(beyond, "core", "e1_zc")], axis=0)
    mixed_grad = jnp.concatenate([mixed_grad, low(product(grad_far, w_so))], axis=0)

    hidden_sum = sum_over_chips(grad_hidden)
    sides = [hidden_sum[:, : hidden_sum.shape[1] // 2], hidden_sum[:, hidden_sum.shape[1] // 2 :]]
    sent = jnp.concatenate([half_of(side, 1 - zhi, 1) for side in sides], axis=1)
    hidden_beyond = jnp.split(trade(sent, "zhi", "gf_zhi"), 2, axis=1)
    out_sum, in_sum = (
        half_of(side, zhi, 1).astype(jnp.float32) + beyond.astype(jnp.float32)
        for side, beyond in zip(sides, hidden_beyond)
    )
    dq, dk, dv = attend_back(
        self_plan, self_meta, qkv, 0, qkv, pairs, 2 * pairs, mixed, mixed_grad, self_lse, pairs, 1152
    )
    dq, dk, dv = after(dq, in_sum, out_sum), after(dk, in_sum, out_sum), after(dv, in_sum, out_sum)
    layer_moved = regroup_sent(after(layer_out, dq), "out")
    dqkv = jnp.concatenate([dq, dk, dv], axis=1)
    d_near, d_far = dqkv[: count // 2], dqkv[count // 2 :]
    dx_far = low(
        product_right_t(d_far[: count // 4], w_qkv)
        + trade(low(product_right_t(d_far[count // 4 :], w_qkv)), "core", "dx_zc")
    )
    dx = product_right_t(d_near[: count // 4], w_qkv) + trade(
        low(product_right_t(d_near[count // 4 :], w_qkv)), "core", "dx_c"
    )
    cross_sum = after(cross_sum, dx_far).reshape(rows_of, 4, 2, -1)
    cross_kept = half_of(cross_sum, zhi, 2).reshape(rows_of, -1)
    cross_sent = half_of(cross_sum, 1 - zhi, 2).reshape(rows_of, -1)
    cross_beyond = trade(cross_sent, "zhi", "gc_zhi")
    dq, dk, dv = (after(part, dx_far, cross_sent, cross_kept) for part in (dq, dk, dv))
    self_parts = [
        low(product_left_t(attn_rows, dq)),
        low(product_left_t(attn_rows, dk)),
        low(product_left_t(attn_rows, dv)),
        low(product_left_t(grad_near, near) + product_left_t(grad_far, far)),
    ]
    enc_part = low(
        product_right_t(after(cross_dk, dq), w_ckv[:, :cross_width])
        + product_right_t(after(cross_dv, dq), w_ckv[:, cross_width:])
    )
    layer_out = regroup_done(layer_out, after(layer_moved, *self_parts))
    dx = dx + after(trade(dx_far, "zlo", "dx_z"), enc_part, layer_out, cross_beyond, *self_parts)
    part, gain_one, shift_one = norm_backward(dx, hat_one, inv_one, vectors[0])
    input_part = low(gradient + part)
    input_grad = regroup(input_part, "dgrad").astype(jnp.float32)

    bias_self_query = jnp.sum(dq.astype(jnp.float32), axis=0)
    bias_self_value = jnp.sum(dv.astype(jnp.float32), axis=0)
    bias_cross_query = jnp.sum(cross_dq.astype(jnp.float32), axis=0)
    bias_cross_value = jnp.sum(cross_dv.astype(jnp.float32), axis=0)
    grad_hidden_bias = (sum_near + sum_far)[0]
    vec_sums = jnp.stack(
        [
            gain_one,
            gain_two,
            gain_three,
            shift_one,
            shift_two,
            shift_three,
            bias_out_one,
            bias_out_two,
            bias_out_three,
        ]
    )
    at_zlo = (jnp.arange(2) == zlo).astype(jnp.float32)
    at_core = (jnp.arange(2) == core).astype(jnp.float32)
    quarter = (at_zlo[:, None] * at_core[None, :])[:, :, None]
    self_sums = jnp.stack([bias_self_query, bias_self_value]).reshape(2, 2, 1, 1, -1) * quarter
    cross_sums = jnp.stack([bias_cross_query, bias_cross_value]).reshape(2, 2, 2, 1, -1) * at_core[:, None]
    head_sums = jnp.concatenate([self_sums, cross_sums], axis=0)
    hidden_sums = grad_hidden_bias.reshape(2, 1, 1, -1) * quarter
    vec_sums = vec_sums.reshape(9, 8, -1).transpose(1, 0, 2).reshape(8, 1, -1)
    sums = jnp.concatenate(
        [
            jnp.broadcast_to(vec_sums, (8, 4, sizes[0])),
            head_sums.reshape(4, 4, 8, -1).transpose(2, 1, 0, 3).reshape(8, 4, -1),
            hidden_sums.reshape(4, 8, -1).transpose(1, 0, 2),
        ],
        axis=2,
    )
    sums = jnp.pad(after(sums, input_part).reshape(32, -1, 128), ((0, 0), (0, 4), (0, 0)))
    ff_in_grad, ff_out_grad, cross_qkv_grad, cross_out_grad, self_qkv_grad, self_out_grad, enc_grad, sums = finish(
        in_sum,
        out_sum,
        cross_kept,
        cross_beyond,
        [part.reshape(2, 2, rows_of, -1) for part in self_parts],
        enc_part.reshape(2, 2, -1, model),
        sums,
    )
    sums = sums.reshape(-1)[: sum(sizes)]
    vec_grad, head_grad, ff_bias_grad = jnp.split(sums, [sizes[0], sizes[0] + sizes[1]])
    return (
        layer_out,
        input_grad,
        enc_grad.astype(jnp.float32),
        self_qkv_grad,
        self_out_grad.T,
        cross_qkv_grad,
        cross_out_grad.T,
        ff_in_grad,
        ff_out_grad.T,
        head_grad.reshape(head_bias.shape),
        ff_bias_grad,
        vec_grad.reshape(vec_params.shape),
    )


def solution(mesh):
    fast = tuple(mesh.shape[axis] for axis in ("dp", "tensor")) == (8, 4)
    dp, tensor = (AXES[:3], AXES[3:]) if fast else (("dp",), ("tensor",))
    both = dp + tensor
    rows = P(both, None)
    qkv = P(None, dp, tensor)
    out = P(tensor, dp)
    in_specs = (
        rows,
        rows,
        P(dp),
        P(dp, None),
        rows,
        qkv,
        out,
        qkv,
        out,
        P(dp, tensor),
        out,
        P(None, tensor + dp),
        P(tensor + dp),
        P(None, dp),
    )
    out_specs = (
        rows,
        rows,
        rows,
        qkv,
        out,
        qkv,
        out,
        P(dp, tensor),
        out,
        P(None, tensor + dp),
        P(tensor + dp),
        P(None, dp),
    )
    if fast:
        mesh = Mesh(mesh.devices.reshape(2, 2, 2, 2, 2), AXES)
    return jax.shard_map(
        fast_layer if fast else shards, mesh=mesh, in_specs=in_specs, out_specs=out_specs, check_vma=False
    )
```

```python
import functools
import math

import jax
import jax.numpy as jnp
from jax import lax
from jax.experimental import pallas as pl
from jax.experimental.pallas import tpu as pltpu
from jax.sharding import Mesh
from jax.sharding import PartitionSpec as P

HD = 64
PROMPT = 1024
CONT_TOK = 1024
ENC = 512
BLOCK = 256
PAIR = 2 * HD
AXES = ("y", "x", "core", "zhi", "zlo")


def lane_half():
    return lax.broadcasted_iota(jnp.int32, (1, PAIR), 1) < HD


def one_head(rows, head):
    keep = lane_half() if head == 0 else jnp.logical_not(lane_half())
    return rows * jnp.where(keep, 1.0, 0.0).astype(rows.dtype)


def dot_nt(left, right):
    return lax.dot_general(left, right, (((1,), (1,)), ((), ())), preferred_element_type=jnp.float32)


def dot_nn(left, right):
    return jnp.dot(left, right, preferred_element_type=jnp.float32)


def dot_tn(left, right):
    return lax.dot_general(left, right, (((0,), (0,)), ((), ())), preferred_element_type=jnp.float32)


def self_sections(meta_ref, segments):
    def at(block):
        return pl.multiple_of(meta_ref[block], 512)

    def place(index):
        return pl.multiple_of(meta_ref[index >> 1] + (index & 1) * BLOCK, BLOCK)

    def causal(row, col):
        return col <= row

    def banded(row, col):
        start = jnp.full(row.shape, meta_ref[4], jnp.int32)
        for segment in range(1, segments):
            bound = meta_ref[4 + segment]
            start = jnp.where(row >= bound, bound, start)
        return (col <= row) & (col >= start)

    def early(index):
        return [(at(0), 512, 0, causal)]

    def middle(index):
        return [(at(0), 512, 0, None), (at(1), 512, 512, causal)]

    def late(index):
        return [
            (at(0), 512, 0, None),
            (at(1), 512, 512, None),
            (place(index - 1), BLOCK, (index - 1) * BLOCK, banded),
            (place(index), BLOCK, index * BLOCK, banded),
        ]

    return place, ((0, 2, early), (2, 4, middle), (4, 8, late))


def cross_sections(meta_ref, blocks):
    def place(index):
        return pl.multiple_of(index * BLOCK, BLOCK)

    def usable(row, col):
        return col < meta_ref[0]

    def every(index):
        return [(0, ENC, 0, usable)]

    return place, ((0, blocks, every),)


def forward_kernel(sections, meta_ref, q_ref, k_ref, v_ref, o_ref, lse_ref):
    place, ranges = sections(meta_ref)

    for low, high, parts_of in ranges:

        def step(index, carry, parts_of=parts_of):
            rows = pl.ds(place(index), BLOCK)
            parts = parts_of(index)
            queries = q_ref[rows, :]
            row = index * BLOCK + lax.broadcasted_iota(jnp.int32, (BLOCK, 1), 0)
            allowed = [
                None if rule is None else rule(row, first + lax.broadcasted_iota(jnp.int32, (1, size), 1))
                for _, size, first, rule in parts
            ]
            outs, totals = [], []
            for head in range(2):
                query = one_head(queries, head)
                scores = []
                for (where, size, _, _), ok in zip(parts, allowed):
                    score = dot_nt(query, k_ref[pl.ds(where, size), :])
                    scores.append(score if ok is None else jnp.where(ok, score, -1e30))
                top = functools.reduce(jnp.maximum, [jnp.max(s, axis=1, keepdims=True) for s in scores])
                exps = [jnp.exp(s - top) for s in scores]
                total = sum(jnp.sum(e, axis=1, keepdims=True) for e in exps)
                mixed = sum(
                    dot_nn(e.astype(jnp.bfloat16), v_ref[pl.ds(where, size), :])
                    for (where, size, _, _), e in zip(parts, exps)
                )
                outs.append(mixed * (1.0 / total))
                totals.append(top + jnp.log(total))
            o_ref[rows, :] = jnp.where(lane_half(), outs[0], outs[1]).astype(o_ref.dtype)
            lse_ref[rows, :] = jnp.where(lane_half(), totals[0], totals[1])
            return carry

        lax.fori_loop(low, high, step, 0)


def backward_kernel(
    sections, meta_ref, q_ref, k_ref, v_ref, o_ref, do_ref, lse_ref, dq_ref, dk_ref, dv_ref, dk_sum, dv_sum
):
    place, ranges = sections(meta_ref)
    dk_sum[...] = jnp.zeros_like(dk_sum)
    dv_sum[...] = jnp.zeros_like(dv_sum)

    for low, high, parts_of in ranges:

        def step(index, carry, parts_of=parts_of):
            rows = pl.ds(place(index), BLOCK)
            parts = parts_of(index)
            queries, grads = q_ref[rows, :], do_ref[rows, :]
            row = index * BLOCK + lax.broadcasted_iota(jnp.int32, (1, BLOCK), 1)
            allowed = [
                None if rule is None else rule(row, first + lax.broadcasted_iota(jnp.int32, (size, 1), 0))
                for _, size, first, rule in parts
            ]
            logs = jnp.transpose(lse_ref[rows, :])
            spread = jnp.transpose(grads.astype(jnp.float32) * o_ref[rows, :].astype(jnp.float32))
            key_parts = [k_ref[pl.ds(where, size), :] for where, size, _, _ in parts]
            value_parts = [v_ref[pl.ds(where, size), :] for where, size, _, _ in parts]
            query_grads = []
            for head in range(2):
                query, grad = one_head(queries, head), one_head(grads, head)
                log = logs[head * HD : head * HD + 1, :]
                delta = jnp.sum(spread[head * HD : (head + 1) * HD, :], axis=0, keepdims=True)
                query_grad = None
                for (where, size, _, _), ok, keys, values in zip(parts, allowed, key_parts, value_parts):
                    score = dot_nt(keys, query)
                    if ok is not None:
                        score = jnp.where(ok, score, -1e30)
                    probs = jnp.exp(score - log)
                    score_grad = (probs * (dot_nt(values, grad) - delta)).astype(jnp.bfloat16)
                    dv_sum[pl.ds(where, size), :] += dot_nn(probs.astype(jnp.bfloat16), grad)
                    dk_sum[pl.ds(where, size), :] += dot_nn(score_grad, query)
                    term = dot_tn(score_grad, keys)
                    query_grad = term if query_grad is None else query_grad + term
                query_grads.append(query_grad)
            both = jnp.where(lane_half(), query_grads[0], query_grads[1])
            dq_ref[rows, :] = both.astype(jnp.bfloat16) * jnp.asarray(HD**-0.5, jnp.bfloat16)
            return carry

        lax.fori_loop(low, high, step, 0)
    dk_ref[...] = dk_sum[...].astype(dk_ref.dtype)
    dv_ref[...] = dv_sum[...].astype(dv_ref.dtype)


def columns(rows, first):
    return pl.BlockSpec((rows, PAIR), lambda pair, meta: (0, first + pair))


def attend(sections, meta, q, q_at, keys, k_at, v_at, pairs, weight):
    count, key_rows = q.shape[0], keys.shape[0]
    return pl.pallas_call(
        functools.partial(forward_kernel, sections),
        grid_spec=pltpu.PrefetchScalarGridSpec(
            num_scalar_prefetch=1,
            grid=(pairs,),
            in_specs=[columns(count, q_at), columns(key_rows, k_at), columns(key_rows, v_at)],
            out_specs=[columns(count, 0), columns(count, 0)],
        ),
        out_shape=[
            jax.ShapeDtypeStruct((count, pairs * PAIR), jnp.bfloat16),
            jax.ShapeDtypeStruct((count, pairs * PAIR), jnp.float32),
        ],
        cost_estimate=pl.CostEstimate(
            flops=2 * 4 * 4 * count * weight * pairs * PAIR,
            bytes_accessed=10 * count * pairs * PAIR,
            transcendentals=2 * pairs * count * weight,
        ),
    )(meta, q, keys, keys)


def attend_back(sections, meta, q, q_at, keys, k_at, v_at, out, out_grad, lse, pairs, weight):
    count, key_rows = q.shape[0], keys.shape[0]
    return pl.pallas_call(
        functools.partial(backward_kernel, sections),
        grid_spec=pltpu.PrefetchScalarGridSpec(
            num_scalar_prefetch=1,
            grid=(pairs,),
            in_specs=[
                columns(count, q_at),
                columns(key_rows, k_at),
                columns(key_rows, v_at),
                columns(count, 0),
                columns(count, 0),
                columns(count, 0),
            ],
            out_specs=[columns(count, 0), columns(key_rows, 0), columns(key_rows, 0)],
            scratch_shapes=[pltpu.VMEM((key_rows, PAIR), jnp.float32)] * 2,
        ),
        out_shape=[
            jax.ShapeDtypeStruct((count, pairs * PAIR), jnp.bfloat16),
            jax.ShapeDtypeStruct((key_rows, pairs * PAIR), jnp.bfloat16),
            jax.ShapeDtypeStruct((key_rows, pairs * PAIR), jnp.bfloat16),
        ],
        cost_estimate=pl.CostEstimate(
            flops=5 * 4 * 4 * count * weight * pairs * PAIR,
            bytes_accessed=20 * count * pairs * PAIR,
            transcendentals=2 * pairs * count * weight,
        ),
    )(meta, q, keys, keys, out, out_grad, lse)


EPSILON = 1e-05
MASKED = 1e30
GELU_C = math.sqrt(2.0 / math.pi)
GELU_A = 0.044715


def gelu_value(values):
    inner = jnp.tanh(GELU_C * (values + GELU_A * values * values * values))
    return 0.5 * values * (1.0 + inner)


def gelu_slope(values):
    inner = jnp.tanh(GELU_C * (values + GELU_A * values * values * values))
    return 0.5 * (1.0 + inner) + 0.5 * values * (1.0 - inner * inner) * GELU_C * (
        1.0 + 3.0 * GELU_A * values * values
    )


def norm_forward(values, gain_vec, shift_vec):
    row_mean = jnp.mean(values, axis=1, keepdims=True)
    centred = values - row_mean
    inverse = lax.rsqrt(jnp.mean(centred * centred, axis=1, keepdims=True) + EPSILON)
    normed = centred * inverse
    return (normed * gain_vec + shift_vec, normed, inverse)


def norm_backward(gradient, normed, inverse, gain_vec):
    scaled = gradient * gain_vec
    inner = (
        scaled
        - jnp.mean(scaled, axis=1, keepdims=True)
        - normed * jnp.mean(scaled * normed, axis=1, keepdims=True)
    )
    return (inner * inverse, jnp.sum(gradient * normed, axis=0), jnp.sum(gradient, axis=0))


def product(left, right):
    return jnp.dot(left, right, preferred_element_type=jnp.float32)


def product_left_t(left, right):
    return lax.dot_general(
        left, right, (((0,), (0,)), ((), ())), preferred_element_type=jnp.float32
    )


def product_right_t(left, right):
    return lax.dot_general(
        left, right, (((1,), (1,)), ((), ())), preferred_element_type=jnp.float32
    )


def attend_forward(queries, key_rows, value_rows, rule, block_rows):
    seq_rows, local_width = queries.shape
    local_heads = local_width // HD
    query_blocks = queries.reshape(seq_rows // block_rows, block_rows, local_heads, HD)
    key_heads = key_rows.reshape(-1, local_heads, HD)
    value_heads = value_rows.reshape(-1, local_heads, HD)
    block_starts = jnp.arange(seq_rows // block_rows, dtype=jnp.int32) * block_rows

    def attend_block(pieces):
        query_block, offset = pieces
        scores = jnp.einsum(
            "qhd,khd->hqk", query_block, key_heads, preferred_element_type=jnp.float32
        )
        scores = jnp.where(rule(offset, block_rows)[None], scores, -MASKED)
        row_max = jnp.max(scores, axis=2, keepdims=True)
        exponent = jnp.exp(scores - row_max)
        row_total = jnp.sum(exponent, axis=2, keepdims=True)
        probs_low = (exponent / row_total).astype(jnp.bfloat16)
        mixed = jnp.einsum(
            "hqk,khd->qhd", probs_low, value_heads, preferred_element_type=jnp.float32
        )
        return (
            mixed.astype(jnp.bfloat16).reshape(block_rows, local_width),
            (row_max + jnp.log(row_total))[:, :, 0],
        )

    outputs, log_total = lax.map(attend_block, (query_blocks, block_starts))
    return (outputs.reshape(seq_rows, local_width), log_total)


def attend_backward(queries, key_rows, value_rows, out_grad, log_total, rule, block_rows):
    seq_rows, local_width = queries.shape
    local_heads = local_width // HD
    key_count = key_rows.shape[0]
    query_blocks = queries.reshape(seq_rows // block_rows, block_rows, local_heads, HD)
    grad_blocks = out_grad.reshape(seq_rows // block_rows, block_rows, local_heads, HD)
    key_heads = key_rows.reshape(key_count, local_heads, HD)
    value_heads = value_rows.reshape(key_count, local_heads, HD)
    block_starts = jnp.arange(seq_rows // block_rows, dtype=jnp.int32) * block_rows

    def back_block(running, pieces):
        key_sum, value_sum = running
        query_block, grad_block, block_total, offset = pieces
        scores = jnp.einsum(
            "qhd,khd->hqk", query_block, key_heads, preferred_element_type=jnp.float32
        )
        probs = jnp.where(
            rule(offset, block_rows)[None], jnp.exp(scores - block_total[:, :, None]), 0.0
        )
        probs_low = probs.astype(jnp.bfloat16)
        prob_grad = jnp.einsum(
            "qhd,khd->hqk", grad_block, value_heads, preferred_element_type=jnp.float32
        )
        row_delta = jnp.sum(probs * prob_grad, axis=2, keepdims=True)
        score_grad = (probs * (prob_grad - row_delta)).astype(jnp.bfloat16)
        query_grad = jnp.einsum(
            "hqk,khd->qhd", score_grad, key_heads, preferred_element_type=jnp.float32
        )
        key_sum = key_sum + jnp.einsum(
            "hqk,qhd->khd", score_grad, query_block, preferred_element_type=jnp.float32
        )
        value_sum = value_sum + jnp.einsum(
            "hqk,qhd->khd", probs_low, grad_block, preferred_element_type=jnp.float32
        )
        return (
            (key_sum, value_sum),
            query_grad.astype(jnp.bfloat16).reshape(block_rows, local_width),
        )

    zero_sum = jnp.zeros((key_count, local_heads, HD), jnp.float32)
    (key_sum, value_sum), query_grads = lax.scan(
        back_block, (zero_sum, zero_sum), (query_blocks, grad_blocks, log_total, block_starts)
    )
    return (
        query_grads.reshape(seq_rows, local_width),
        key_sum.astype(jnp.bfloat16).reshape(key_count, local_width),
        value_sum.astype(jnp.bfloat16).reshape(key_count, local_width),
    )


def attend_groups(queries, key_rows, value_rows, rules, block_rows):
    results, totals = ([], [])
    for which_group, rule in enumerate(rules):
        mixed, log_total = attend_forward(queries, key_rows, value_rows, rule, block_rows)
        results.append(mixed)
        totals.append(log_total)
    return (results[0], totals)


def back_groups(queries, key_rows, value_rows, out_grad, totals, rules, block_rows):
    query_list, key_list, value_list = ([], [], [])
    for which_group, rule in enumerate(rules):
        query_grad, key_grad, value_grad = attend_backward(
            queries, key_rows, value_rows, out_grad, totals[which_group], rule, block_rows
        )
        query_list.append(query_grad)
        key_list.append(key_grad)
        value_list.append(value_grad)
    return (query_list[0], key_list[0], value_list[0])


def shards(
    tokens,
    enc_states,
    enc_len,
    cont_lengths,
    cotangent,
    self_qkv,
    self_out,
    cross_qkv,
    cross_out,
    ff_in,
    ff_out,
    head_bias,
    ff_bias,
    vec_params,
):
    gathered = (
        lax.all_gather(self_qkv, "dp", axis=1, tiled=True),
        lax.all_gather(self_out, "dp", axis=1, tiled=True),
        lax.all_gather(cross_qkv, "dp", axis=1, tiled=True),
        lax.all_gather(cross_out, "dp", axis=1, tiled=True),
        lax.all_gather(ff_in, "dp", axis=0, tiled=True),
        lax.all_gather(ff_out, "dp", axis=1, tiled=True),
        lax.all_gather(head_bias, "dp", axis=1, tiled=True),
        lax.all_gather(ff_bias, "dp", axis=0, tiled=True),
        lax.all_gather(vec_params, "dp", axis=1, tiled=True),
    )
    (
        w_self,
        w_self_out,
        w_cross,
        w_cross_out,
        w_hidden_in,
        w_hidden_out,
        bias_heads,
        bias_hidden,
        vectors,
    ) = gathered
    vectors = vectors.astype(jnp.float32)
    bias_heads = bias_heads.astype(jnp.float32)
    bias_hidden = bias_hidden.astype(jnp.float32)
    seq_rows = PROMPT + CONT_TOK
    block_rows = min(512, seq_rows)
    scaling = HD ** (-0.5)
    rows_dev = tokens.shape[0]

    def self_rule(which_group):
        bounds = PROMPT + jnp.cumsum(cont_lengths[which_group])
        positions = jnp.arange(seq_rows, dtype=jnp.int32)
        segment = jnp.sum((positions[:, None] >= bounds[None, :]).astype(jnp.int32), axis=1)

        def self_allowed(offset, number):
            row_ids = offset + jnp.arange(number, dtype=jnp.int32)
            row_segment = lax.dynamic_slice_in_dim(segment, offset, number)
            return (positions[None, :] <= row_ids[:, None]) & (
                (positions[None, :] < PROMPT) | (segment[None, :] == row_segment[:, None])
            )

        return self_allowed

    def cross_rule(which_group):
        usable = jnp.arange(ENC, dtype=jnp.int32) < enc_len[which_group]

        def cross_allowed(offset, number):
            return jnp.broadcast_to(usable[None, :], (number, ENC))

        return cross_allowed

    def spread(low_rows):
        return lax.all_gather(low_rows, "tensor", axis=0, tiled=True)

    def head_branch(values, weight):

        def term(offset, number):
            return product(values, weight)

        return lax.psum_scatter(
            term(jnp.int32(0), rows_dev * lax.axis_size("tensor")),
            "tensor",
            scatter_dimension=0,
            tiled=True,
        )

    def widen(low_rows):
        return lax.all_gather(low_rows, "tensor", axis=0, tiled=True)

    def narrow(term):
        return lax.psum_scatter(
            term(jnp.int32(0), rows_dev * lax.axis_size("tensor")),
            "tensor",
            scatter_dimension=0,
            tiled=True,
        )

    self_rules = [self_rule(0)]
    cross_rules = [cross_rule(0)]
    resid = tokens.astype(jnp.float32)
    enc_full = lax.all_gather(enc_states, "tensor", axis=0, tiled=True)
    normed_in, hat_one, inv_one = norm_forward(resid, vectors[0], vectors[3])
    attn_low = normed_in.astype(jnp.bfloat16)
    attn_full = spread(attn_low)
    queries = ((product(attn_full, w_self[0]) + bias_heads[0]) * scaling).astype(jnp.bfloat16)
    key_rows = product(attn_full, w_self[1]).astype(jnp.bfloat16)
    value_rows = (product(attn_full, w_self[2]) + bias_heads[1]).astype(jnp.bfloat16)
    mixed, self_totals = attend_groups(queries, key_rows, value_rows, self_rules, block_rows)
    after_one = resid + (head_branch(mixed, w_self_out) + vectors[6])
    normed_mid, hat_two, inv_two = norm_forward(after_one, vectors[1], vectors[4])
    cross_low = normed_mid.astype(jnp.bfloat16)
    cross_full = spread(cross_low)
    cross_queries = ((product(cross_full, w_cross[0]) + bias_heads[2]) * scaling).astype(
        jnp.bfloat16
    )
    cross_keys = product(enc_full, w_cross[1]).astype(jnp.bfloat16)
    cross_values = (product(enc_full, w_cross[2]) + bias_heads[3]).astype(jnp.bfloat16)
    cross_mixed, cross_totals = attend_groups(
        cross_queries, cross_keys, cross_values, cross_rules, block_rows
    )
    after_two = after_one + (head_branch(cross_mixed, w_cross_out) + vectors[7])
    normed_out, hat_three, inv_three = norm_forward(after_two, vectors[2], vectors[5])
    hidden_low = normed_out.astype(jnp.bfloat16)
    hidden_full = spread(hidden_low)
    pre_act = product(hidden_full, w_hidden_in) + bias_hidden
    activation = gelu_value(pre_act).astype(jnp.bfloat16)

    def term(offset, number):
        return product(activation, w_hidden_out)

    after_three = after_two + (
        lax.psum_scatter(
            term(jnp.int32(0), rows_dev * lax.axis_size("tensor")),
            "tensor",
            scatter_dimension=0,
            tiled=True,
        )
        + vectors[8]
    )
    layer_out = after_three.astype(jnp.bfloat16)
    gradient = cotangent.astype(jnp.float32)
    grad_low = gradient.astype(jnp.bfloat16)
    bias_out_three = jnp.sum(grad_low.astype(jnp.float32), axis=0)
    grad_full = widen(grad_low)
    act_grad = (product_right_t(grad_full, w_hidden_out) * gelu_slope(pre_act)).astype(jnp.bfloat16)
    grad_hidden_out = product_left_t(activation, grad_full)
    grad_hidden_in = product_left_t(hidden_full, act_grad)
    grad_bias_hidden = jnp.sum(act_grad.astype(jnp.float32), axis=0)

    def hidden_term(offset, number):
        return product_right_t(act_grad, w_hidden_in)

    input_part, gain_three, shift_three = norm_backward(
        narrow(hidden_term), hat_three, inv_three, vectors[2]
    )
    gradient = gradient + input_part
    grad_low = gradient.astype(jnp.bfloat16)
    bias_out_two = jnp.sum(grad_low.astype(jnp.float32), axis=0)
    grad_full = widen(grad_low)
    grad_cross_out = product_left_t(cross_mixed, grad_full)
    mixed_grad = product_right_t(grad_full, w_cross_out).astype(jnp.bfloat16)
    cross_query_grad, cross_key_grad, cross_value_grad = back_groups(
        cross_queries, cross_keys, cross_values, mixed_grad, cross_totals, cross_rules, block_rows
    )
    grad_cross = jnp.stack(
        [
            product_left_t(cross_full, cross_query_grad) * scaling,
            product_left_t(enc_full, cross_key_grad),
            product_left_t(enc_full, cross_value_grad),
        ]
    )
    bias_cross_query = jnp.sum(cross_query_grad.astype(jnp.float32), axis=0) * scaling
    bias_cross_value = jnp.sum(cross_value_grad.astype(jnp.float32), axis=0)
    enc_grad = lax.psum_scatter(
        product_right_t(cross_key_grad, w_cross[1]) + product_right_t(cross_value_grad, w_cross[2]),
        "tensor",
        scatter_dimension=0,
        tiled=True,
    )

    def cross_term(offset, number):
        return product_right_t(cross_query_grad, w_cross[0]) * scaling

    input_part, gain_two, shift_two = norm_backward(
        narrow(cross_term), hat_two, inv_two, vectors[1]
    )
    gradient = gradient + input_part
    grad_low = gradient.astype(jnp.bfloat16)
    bias_out_one = jnp.sum(grad_low.astype(jnp.float32), axis=0)
    grad_full = widen(grad_low)
    grad_self_out = product_left_t(mixed, grad_full)
    self_mixed_grad = product_right_t(grad_full, w_self_out).astype(jnp.bfloat16)
    query_grad, key_grad, value_grad = back_groups(
        queries, key_rows, value_rows, self_mixed_grad, self_totals, self_rules, block_rows
    )
    grad_self = jnp.stack(
        [
            product_left_t(attn_full, query_grad) * scaling,
            product_left_t(attn_full, key_grad),
            product_left_t(attn_full, value_grad),
        ]
    )
    bias_self_query = jnp.sum(query_grad.astype(jnp.float32), axis=0) * scaling
    bias_self_value = jnp.sum(value_grad.astype(jnp.float32), axis=0)

    def self_term(offset, number):
        return (
            product_right_t(query_grad, w_self[0]) * scaling
            + product_right_t(key_grad, w_self[1])
            + product_right_t(value_grad, w_self[2])
        )

    input_part, gain_one, shift_one = norm_backward(narrow(self_term), hat_one, inv_one, vectors[0])
    input_grad = gradient + input_part
    vector_grads = jnp.stack(
        [
            gain_one,
            gain_two,
            gain_three,
            shift_one,
            shift_two,
            shift_three,
            bias_out_one,
            bias_out_two,
            bias_out_three,
        ]
    )
    head_grads = jnp.stack([bias_self_query, bias_self_value, bias_cross_query, bias_cross_value])
    results = (
        lax.psum_scatter(grad_self, "dp", scatter_dimension=1, tiled=True),
        lax.psum_scatter(grad_self_out, "dp", scatter_dimension=1, tiled=True),
        lax.psum_scatter(grad_cross, "dp", scatter_dimension=1, tiled=True),
        lax.psum_scatter(grad_cross_out, "dp", scatter_dimension=1, tiled=True),
        lax.psum_scatter(grad_hidden_in, "dp", scatter_dimension=0, tiled=True),
        lax.psum_scatter(grad_hidden_out, "dp", scatter_dimension=1, tiled=True),
        lax.psum_scatter(head_grads, "dp", scatter_dimension=1, tiled=True),
        lax.psum_scatter(grad_bias_hidden, "dp", scatter_dimension=0, tiled=True),
        lax.psum_scatter(vector_grads, "dp", scatter_dimension=1, tiled=True),
    )
    vector_total = lax.psum(results[8], "tensor")
    return (
        layer_out,
        input_grad,
        enc_grad,
        results[0],
        results[1],
        results[2],
        results[3],
        results[4],
        results[5],
        results[6],
        results[7],
        vector_total,
    )


def hidden_kernel(x0_ref, x1_ref, e0_ref, e1_ref, w_in_ref, w_out_ref, bias_ref, act_ref, grad_ref, sum_ref):
    chunk = 256
    sum_ref[...] = jnp.zeros_like(sum_ref)
    count = x0_ref.shape[0]

    for which, (x_ref, e_ref) in enumerate(((x0_ref, e0_ref), (x1_ref, e1_ref))):

        def step(index, carry, which=which, x_ref=x_ref, e_ref=e_ref):
            rows = pl.ds(pl.multiple_of(index * chunk, chunk), chunk)
            out_rows = pl.ds(pl.multiple_of(which * count + index * chunk, chunk), chunk)
            value = dot_nn(x_ref[rows, :], w_in_ref[...]) + bias_ref[...]
            upper = dot_nn(e_ref[rows, :], w_out_ref[...])
            square = value * value
            inner = jnp.tanh(value * (GELU_C + (GELU_C * GELU_A) * square))
            half = 0.5 + 0.5 * inner
            act_ref[out_rows, :] = (value * half).astype(act_ref.dtype)
            slope = half + (value * (half * (1.0 - inner))) * (GELU_C + (3.0 * GELU_C * GELU_A) * square)
            grad = (upper * slope).astype(grad_ref.dtype)
            grad_ref[out_rows, :] = grad
            sum_ref[...] += jnp.sum(grad.astype(jnp.float32), axis=0, keepdims=True)
            return carry

        lax.fori_loop(0, count // chunk, step, 0, unroll=2)


def hidden_units(rows, grads, weights, bias, tile=512):
    count, model = rows[0].shape
    width = weights.shape[1] // 2
    tiles = width // tile
    whole = pl.BlockSpec((count, model), lambda i: (0, 0))
    weight = pl.BlockSpec((model, tile), lambda i: (0, i))
    weight_out = pl.BlockSpec((model, tile), lambda i: (0, tiles + i))
    line = pl.BlockSpec((1, tile), lambda i: (0, i))
    out = pl.BlockSpec((2 * count, tile), lambda i: (0, i))
    return pl.pallas_call(
        hidden_kernel,
        grid=(tiles,),
        in_specs=[whole] * 4 + [weight, weight_out, line],
        out_specs=[out, out, line],
        out_shape=[
            jax.ShapeDtypeStruct((2 * count, width), jnp.bfloat16),
            jax.ShapeDtypeStruct((2 * count, width), jnp.bfloat16),
            jax.ShapeDtypeStruct((1, width), jnp.float32),
        ],
        cost_estimate=pl.CostEstimate(
            flops=8 * count * model * width,
            bytes_accessed=4 * (2 * count * model + model * width + 2 * count * width),
            transcendentals=2 * count * width,
        ),
    )(*rows, *grads, weights, weights, bias)


MESH = pl.DeviceIdType.MESH


def weight_grad_kernel(*refs):
    rows_ref, refs = refs[0], refs[1:]
    sides, (rows_out, out_ref, turned, send, recv) = (refs[:6], refs[6:12]), refs[12:]
    count, depth = sides[0][0].shape[0], sides[0][4].shape[0]
    step_of, tiles = pl.program_id(0), pl.num_programs(0) // 2

    def copy():
        return pltpu.make_async_remote_copy(
            src_ref=rows_ref,
            dst_ref=rows_out,
            send_sem=send,
            recv_sem=recv,
            device_id={"zlo": 1 - lax.axis_index("zlo")},
            device_id_type=MESH,
        )

    @pl.when(step_of == 0)
    def _():
        barrier = pltpu.get_barrier_semaphore()
        pl.semaphore_signal(
            barrier, inc=1, device_id={"zlo": 1 - lax.axis_index("zlo")}, device_id_type=MESH
        )
        pl.semaphore_wait(barrier, 1)
        copy().start()

    for half, (x0_ref, x1_ref, x2_ref, x3_ref, near_ref, far_ref) in enumerate(sides):

        @pl.when(step_of == half * tiles)
        def _(blocks=(x0_ref, x1_ref, x2_ref, x3_ref)):
            for which, x_ref in enumerate(blocks):
                turned[:, which * count : (which + 1) * count] = jnp.transpose(x_ref[...])

        @pl.when(step_of // tiles == half)
        def _(near_ref=near_ref, far_ref=far_ref):
            def step(index, carry):
                rows = pl.ds(pl.multiple_of(index * 256, 256), 256)
                total = dot_nn(turned[rows, :depth], near_ref[...]) + dot_nn(turned[rows, depth:], far_ref[...])
                out_ref[rows, :] = total.astype(out_ref.dtype)
                return carry

            lax.fori_loop(0, out_ref.shape[0] // 256, step, 0, unroll=2)

    @pl.when(step_of == 2 * tiles - 1)
    def _():
        copy().wait()


def weight_grads(rows, first, second, collective_id, tile=512):
    blocks, near, _ = first
    (count, model), (depth, width) = blocks[0].shape, near.shape
    tiles = width // tile
    anywhere = pl.BlockSpec(memory_space=pl.ANY)
    whole = pl.BlockSpec((count, model), lambda i: (0, 0))

    def early(size):
        return pl.BlockSpec((size, tile), lambda i: (0, jnp.minimum(i, tiles - 1)))

    def late(size):
        return pl.BlockSpec((size, tile), lambda i: (0, jnp.maximum(i - tiles, 0)))

    return pl.pallas_call(
        weight_grad_kernel,
        grid=(2 * tiles,),
        in_specs=[anywhere] + [whole] * 4 + [early(depth)] * 2 + [whole] * 4 + [late(depth)] * 2,
        out_specs=[anywhere, pl.BlockSpec((model, tile), lambda i: (0, i))],
        out_shape=[
            jax.ShapeDtypeStruct(rows.shape, rows.dtype),
            jax.ShapeDtypeStruct((model, 2 * width), near.dtype),
        ],
        scratch_shapes=[
            pltpu.VMEM((model, 4 * count), near.dtype),
            pltpu.SemaphoreType.DMA,
            pltpu.SemaphoreType.DMA,
        ],
        compiler_params=pltpu.CompilerParams(collective_id=collective_id, has_side_effects=True),
        cost_estimate=pl.CostEstimate(flops=16 * count * model * width, bytes_accessed=0, transcendentals=0),
    )(rows, *first[0], *first[1:], *second[0], *second[1:])


LINKS = ("core", "x", "y", "zhi", "zlo")


def start_kernel(
    tokens,
    enc,
    self_qkv,
    self_out,
    cross_qkv,
    cross_out,
    w_in,
    w_out,
    small,
    token_rows,
    attn,
    g_self,
    cross_rows,
    hidden,
    enc_full,
    small_all,
    held,
    normed,
    gathered,
    send,
    recv,
    local,
):
    y, x, core, zhi, zlo = (lax.axis_index(axis) for axis in AXES)
    crossing = core != zhi
    rows = tokens.shape[0]
    part = self_out.shape[0]
    counts = {"sent": 0, "local": 0}

    def push(source, target, axis):
        index = counts["sent"]
        counts["sent"] += 1
        copy = pltpu.make_async_remote_copy(
            src_ref=source,
            dst_ref=target,
            send_sem=send.at[index],
            recv_sem=recv.at[index],
            device_id={axis: 1 - lax.axis_index(axis)},
            device_id_type=MESH,
        )
        copy.start()
        return copy

    def keep(source, target):
        index = counts["local"]
        counts["local"] += 1
        copy = pltpu.make_async_copy(source, target, local.at[index])
        copy.start()
        return copy

    def moving(source, target, source_here, target_here):
        index, index_here = counts["sent"], counts["local"]
        counts["sent"] += 1
        counts["local"] += 1

        def remote():
            return pltpu.make_async_remote_copy(
                src_ref=source,
                dst_ref=target,
                send_sem=send.at[index],
                recv_sem=recv.at[index],
                device_id={"core": zhi, "zhi": core},
                device_id_type=MESH,
            )

        def here():
            return pltpu.make_async_copy(source_here, target_here, local.at[index_here])

        @pl.when(crossing)
        def _():
            remote().start()

        @pl.when(jnp.logical_not(crossing))
        def _():
            here().start()

        def wait():
            @pl.when(crossing)
            def _():
                remote().wait()

            @pl.when(jnp.logical_not(crossing))
            def _():
                here().wait()

        return wait

    def lanes(block, size):
        return pl.ds(pl.multiple_of(block * size, size), size)

    barrier = pltpu.get_barrier_semaphore()
    for axis in LINKS:
        pl.semaphore_signal(barrier, inc=1, device_id={axis: 1 - lax.axis_index(axis)}, device_id_type=MESH)

    @pl.when(crossing)
    def _():
        pl.semaphore_signal(barrier, inc=1, device_id={"core": zhi, "zhi": core}, device_id_type=MESH)

    pl.semaphore_wait(barrier, len(LINKS) + crossing.astype(jnp.int32))

    wait_tokens = moving(tokens, held, tokens, held)
    own_small = keep(small, gathered.at[y, x, core, zhi, zlo])
    own_rows = pl.ds(pl.multiple_of(core * part, part), part)
    quarter = 2 * zhi + zlo

    self_width = self_out.shape[1] // 2
    hidden_width = w_in.shape[1] // 2
    cross_core = []
    for plane in range(4):
        target = cross_rows.at[own_rows, lanes(4 * plane + quarter, self_width)]
        shard = cross_qkv.at[plane] if plane < 3 else cross_out
        cross_core.append(keep(shard.at[:, lanes(core, self_width)], target))
        cross_core.append(push(shard.at[:, lanes(1 - core, self_width)], target, "core"))
    own_small.wait()
    small_core = push(gathered.at[y, x, core, zhi, zlo], gathered.at[y, x, core, zhi, zlo], "core")
    target = g_self.at[pl.ds(0, 3), y, x, own_rows, lanes(zhi, self_width)]
    target_out = g_self.at[3, y, x, own_rows, lanes(zhi, self_width)]
    self_core = [
        keep(self_qkv.at[:, :, lanes(core, self_width)], target),
        push(self_qkv.at[:, :, lanes(1 - core, self_width)], target, "core"),
        keep(self_out.at[:, lanes(core, self_width)], target_out),
        push(self_out.at[:, lanes(1 - core, self_width)], target_out, "core"),
    ]
    hidden_core = []
    for plane, shard in enumerate((w_in, w_out)):
        target = hidden.at[plane, own_rows]
        hidden_core.append(keep(shard.at[:, lanes(core, hidden_width)], target))
        hidden_core.append(push(shard.at[:, lanes(1 - core, hidden_width)], target, "core"))
    for copy in cross_core:
        copy.wait()
    regions = [cross_rows.at[:, lanes(4 * plane + quarter, self_width)] for plane in range(4)]
    cross_zlo = [push(region, region, "zlo") for region in regions]
    small_core.wait()
    region = gathered.at[y, x, :, zhi, zlo]
    small_x = push(region, region, "x")
    for copy in self_core:
        copy.wait()
    small_x.wait()
    region = gathered.at[y, :, :, zhi, zlo]
    small_y = push(region, region, "y")
    for copy in cross_zlo:
        copy.wait()
    small_y.wait()

    def over_plane(target, width):
        first, second = pl.ds(0, width), pl.ds(width, width)
        region_a, region_b = target.at[:, y, x, :, first], target.at[:, y, x, :, second]
        steps = (push(region_a, region_a, "x"), push(region_b, region_b, "y"))

        def second_steps():
            steps[0].wait()
            region_a = target.at[:, y, :, :, first]
            step_a = push(region_a, region_a, "y")
            steps[1].wait()
            region_b = target.at[:, :, x, :, second]
            return step_a, push(region_b, region_b, "x")

        return second_steps

    wait_tokens()
    keep_tokens = keep(held, token_rows)
    region = gathered.at[:, :, :, zhi, zlo]
    small_zhi = push(region, region, "zhi")
    region = g_self.at[:, y, x, :, lanes(zhi, self_width)]
    self_zhi = push(region, region, "zhi")
    wait_enc = moving(enc, enc_full.at[2 * zhi + zlo], enc, enc_full.at[2 * core + zlo])
    regions = [cross_rows.at[:, lanes(2 * plane + zhi, 2 * self_width)] for plane in range(4)]
    cross_zhi = [push(region, region, "zhi") for region in regions]
    gain = jnp.concatenate([gathered[d // 4, d // 2 % 2, d % 2, zhi, zlo, 0:1, :] for d in range(8)], axis=1)
    shift = jnp.concatenate([gathered[d // 4, d // 2 % 2, d % 2, zhi, zlo, 3:4, :] for d in range(8)], axis=1)

    def norm_step(step, carry):
        block = pl.ds(pl.multiple_of(step * 64, 64), 64)
        values = held[block, :].astype(jnp.float32)
        centred = values - jnp.mean(values, axis=1, keepdims=True)
        inverse = lax.rsqrt(jnp.mean(centred * centred, axis=1, keepdims=True) + EPSILON)
        normed[block, :] = (centred * inverse * gain + shift).astype(normed.dtype)
        return carry

    lax.fori_loop(0, rows // 64, norm_step, 0)
    attn_zlo = push(normed, attn.at[pl.ds(2 * rows, rows)], "zlo")
    attn_core = push(normed, attn.at[pl.ds(rows, rows)], "core")
    attn_own = keep(normed, attn.at[pl.ds(0, rows)])

    wait_enc()
    region = enc_full.at[2 * core + zlo]
    enc_zlo = push(region, region, "zlo")
    enc_core = push(region, region, "core")
    self_zhi.wait()
    self_second = over_plane(g_self, self_width)
    self_last = self_second()
    small_zhi.wait()
    region = gathered.at[:, :, :, :, zlo]
    small_zlo = push(region, region, "zlo")
    enc_zlo.wait()
    region = enc_full.at[2 * core + 1 - zlo]
    enc_diagonal = push(region, region, "core")
    attn_zlo.wait()
    attn_diagonal = push(attn.at[pl.ds(2 * rows, rows)], attn.at[pl.ds(3 * rows, rows)], "core")
    small_zlo.wait()
    keep_small = keep(gathered, small_all)
    for copy in (
        *self_last,
        *cross_zhi,
        *hidden_core,
        attn_core,
        attn_diagonal,
        enc_core,
        enc_diagonal,
        attn_own,
        keep_tokens,
        keep_small,
    ):
        copy.wait()


def start_exchange(tokens, enc, self_qkv, self_out, cross_qkv, cross_out, w_in, w_out, small):
    rows, model = tokens.shape
    part, shard = self_out.shape
    low_type = tokens.dtype
    shapes = [
        jax.ShapeDtypeStruct((rows, model), low_type),
        jax.ShapeDtypeStruct((4 * rows, model), low_type),
        jax.ShapeDtypeStruct((4, 2, 2, 2 * part, shard), low_type),
        jax.ShapeDtypeStruct((2 * part, 8 * shard), low_type),
        jax.ShapeDtypeStruct((2, 2 * part, w_in.shape[1] // 2), low_type),
        jax.ShapeDtypeStruct((4, enc.shape[0], model), low_type),
        jax.ShapeDtypeStruct((2,) * 5 + small.shape, small.dtype),
    ]
    anywhere = pl.BlockSpec(memory_space=pl.ANY)
    return pl.pallas_call(
        start_kernel,
        out_shape=shapes,
        in_specs=[anywhere] * 9,
        out_specs=[anywhere] * len(shapes),
        scratch_shapes=[
            pltpu.VMEM((rows, model), low_type),
            pltpu.VMEM((rows, model), low_type),
            pltpu.VMEM((2,) * 5 + small.shape, small.dtype),
            pltpu.SemaphoreType.DMA((40,)),
            pltpu.SemaphoreType.DMA((40,)),
            pltpu.SemaphoreType.DMA((20,)),
        ],
        compiler_params=pltpu.CompilerParams(collective_id=0, has_side_effects=True),
    )(tokens, enc, self_qkv, self_out, cross_qkv, cross_out, w_in, w_out, small)


def finish_kernel(
    ff_in,
    ff_out,
    cross,
    cross_beyond,
    self_q,
    self_k,
    self_v,
    self_o,
    enc_part,
    small,
    ff_in_out,
    ff_out_out,
    cross_qkv_out,
    cross_out_out,
    self_qkv_out,
    self_out_out,
    enc_out,
    small_out,
    cross_own,
    cross_got,
    cross_low,
    cross_got_low,
    cross_total,
    enc_own,
    enc_got,
    enc_sum,
    enc_far,
    enc_low,
    self_own,
    self_got,
    low_a,
    low_b,
    self_got_low,
    self_total,
    self_last,
    small_sum,
    small_got_0,
    small_got_1,
    small_got_2,
    small_got_3,
    small_got_4,
    send,
    recv,
    local,
):
    y, x, core, zhi, zlo = (lax.axis_index(axis) for axis in AXES)
    crossing = core != zhi
    small_got = (small_got_0, small_got_1, small_got_2, small_got_3, small_got_4)
    counts = {"sent": 0, "local": 0}

    def push(source, target, axis):
        index = counts["sent"]
        counts["sent"] += 1
        copy = pltpu.make_async_remote_copy(
            src_ref=source,
            dst_ref=target,
            send_sem=send.at[index],
            recv_sem=recv.at[index],
            device_id={axis: 1 - lax.axis_index(axis)},
            device_id_type=MESH,
        )
        copy.start()
        return copy

    def keep(source, target):
        index = counts["local"]
        counts["local"] += 1
        copy = pltpu.make_async_copy(source, target, local.at[index])
        copy.start()
        return copy

    def moving(source, target, source_here, target_here):
        index, index_here = counts["sent"], counts["local"]
        counts["sent"] += 1
        counts["local"] += 1

        def remote():
            return pltpu.make_async_remote_copy(
                src_ref=source,
                dst_ref=target,
                send_sem=send.at[index],
                recv_sem=recv.at[index],
                device_id={"core": zhi, "zhi": core},
                device_id_type=MESH,
            )

        def here():
            return pltpu.make_async_copy(source_here, target_here, local.at[index_here])

        @pl.when(crossing)
        def _():
            remote().start()

        @pl.when(jnp.logical_not(crossing))
        def _():
            here().start()

        def wait():
            @pl.when(crossing)
            def _():
                remote().wait()

            @pl.when(jnp.logical_not(crossing))
            def _():
                here().wait()

        return wait

    def lanes(block, size):
        return pl.ds(pl.multiple_of(block * size, size), size)

    def add(target, *terms):
        def step(index, carry):
            rows = pl.ds(pl.multiple_of(index * 64, 64), 64)
            value = sum(term[rows, :].astype(jnp.float32) for term in terms)
            target[rows, :] = value.astype(target.dtype)
            return carry

        lax.fori_loop(0, target.shape[0] // 64, step, 0)

    barrier = pltpu.get_barrier_semaphore()
    for axis in LINKS:
        pl.semaphore_signal(barrier, inc=1, device_id={axis: 1 - lax.axis_index(axis)}, device_id_type=MESH)

    @pl.when(crossing)
    def _():
        pl.semaphore_signal(barrier, inc=1, device_id={"core": zhi, "zhi": core}, device_id_type=MESH)

    pl.semaphore_wait(barrier, len(LINKS) + crossing.astype(jnp.int32))

    last = []
    half = self_q.shape[3] // 2

    def to_cores(values, out):
        part, width = values.shape[0] // 2, values.shape[1]
        there, here = lanes(1 - core, part), lanes(core, part)
        last.append(push(values.at[there], out.at[:, lanes(core, width)], "core"))
        last.append(keep(values.at[here], out.at[:, lanes(core, width)]))

    def planes_to_cores(values, qkv_out, out_out):
        part = values.shape[0] // 2
        there, here = lanes(1 - core, part), lanes(core, part)
        for plane in range(4):
            columns_of = pl.ds(plane * half, half)
            out = qkv_out.at[plane, :, lanes(core, half)] if plane < 3 else out_out.at[:, lanes(core, half)]
            last.append(push(values.at[there, columns_of], out, "core"))
            last.append(keep(values.at[here, columns_of], out))

    cross_keep = [keep(cross, cross_own), keep(cross_beyond, cross_got)]

    first, second = pl.ds(0, half), pl.ds(half, half)
    parts = (self_q, self_k, self_v, self_o)
    self_x, self_y, own_a, own_b = [], [], [], []
    for plane, partial in enumerate(parts):
        columns_of = pl.ds(plane * half, half)
        self_x.append(push(partial.at[:, 1 - x, :, first], self_got.at[0, :, :, columns_of], "x"))
        self_y.append(push(partial.at[1 - y, :, :, second], self_got.at[1, :, :, columns_of], "y"))
        own_a.append(keep(partial.at[:, x, :, first], self_own.at[0, :, :, columns_of]))
        own_b.append(keep(partial.at[y, :, :, second], self_own.at[1, :, :, columns_of]))
    enc_core = push(enc_part.at[1 - core], enc_got, "core")
    enc_keep = keep(enc_part.at[core], enc_own)

    to_cores(ff_in, ff_in_out)
    to_cores(ff_out, ff_out_out)

    small_first, small_size = 0, 32

    def small_send(stage):
        rows = small_size // 2
        away = small_first + (1 - lax.axis_index(AXES[stage])) * rows
        return push(small_sum.at[pl.ds(away, rows)], small_got[stage], AXES[stage])

    def small_add(stage, copy):
        copy.wait()
        rows, got = small_size // 2, small_got[stage]
        mine = small_first + lax.axis_index(AXES[stage]) * rows

        def step(index, carry):
            small_sum[mine + index] += got[index]
            return carry

        lax.fori_loop(0, rows, step, 0)
        return mine, rows

    keep(small, small_sum).wait()
    small_copy = small_send(0)
    for copy in cross_keep:
        copy.wait()

    def cross_step(target, which, *others):
        def step(index, carry):
            rows = pl.ds(pl.multiple_of(index * 64, 64), 64)
            for plane in range(4):
                source = pl.ds(pl.multiple_of((2 * plane + which) * half, half), half)
                columns_of = pl.ds(plane * half, half)
                value = cross_own[rows, source].astype(jnp.float32) + cross_got[rows, source].astype(jnp.float32)
                for other in others:
                    value += other[rows, columns_of].astype(jnp.float32)
                target[rows, columns_of] = value.astype(target.dtype)
            return carry

        lax.fori_loop(0, target.shape[0] // 64, step, 0)

    cross_step(cross_low, 1 - zlo)
    cross_zlo = push(cross_low, cross_got_low, "zlo")
    enc_core.wait()
    enc_keep.wait()
    add(enc_sum, enc_own.at[1 - zlo], enc_got.at[1 - zlo])
    enc_zlo = push(enc_sum, enc_far, "zlo")
    small_first, small_size = small_add(0, small_copy)
    small_copy = small_send(1)
    for copy in own_a + self_x:
        copy.wait()
    add(low_a, self_own.at[0, 1 - y], self_got.at[0, 1 - y])
    a_second = push(low_a, self_got_low.at[0], "y")
    for copy in own_b + self_y:
        copy.wait()
    add(low_b, self_own.at[1, 1 - x], self_got.at[1, 1 - x])
    b_second = push(low_b, self_got_low.at[1], "x")
    small_first, small_size = small_add(1, small_copy)
    small_copy = small_send(2)
    add(self_total.at[0], self_own.at[0, y], self_got.at[0, y])
    add(self_total.at[1], self_own.at[1, x], self_got.at[1, x])
    enc_zlo.wait()
    add(enc_low, enc_own.at[zlo], enc_got.at[zlo], enc_far)
    small_first, small_size = small_add(2, small_copy)
    small_copy = small_send(3)
    a_second.wait()
    add(self_total.at[0], self_total.at[0], self_got_low.at[0])
    b_second.wait()
    add(self_total.at[1], self_total.at[1], self_got_low.at[1])
    add(low_a, self_total.at[1 - zhi])
    self_zhi = push(low_a, self_last, "zhi")
    wait_enc = moving(enc_low, enc_out, enc_low, enc_out)
    cross_zlo.wait()
    cross_step(cross_total, zlo, cross_got_low)
    planes_to_cores(cross_total, cross_qkv_out, cross_out_out)
    small_first, small_size = small_add(3, small_copy)
    small_copy = small_send(4)
    self_zhi.wait()
    add(self_total.at[zhi], self_total.at[zhi], self_last)
    planes_to_cores(self_total.at[zhi], self_qkv_out, self_out_out)
    small_first, small_size = small_add(4, small_copy)
    keep(small_sum.at[small_first], small_out).wait()
    wait_enc()
    for copy in last:
        copy.wait()


def finish(ff_in, ff_out, cross, cross_beyond, self_parts, enc, small):
    rows, width = ff_in.shape
    part, half = self_parts[0].shape[2], self_parts[0].shape[3] // 2
    low_type, enc_shape = enc.dtype, enc.shape[2:]
    wide = 4 * half

    def full(*shape):
        return jax.ShapeDtypeStruct(shape, jnp.float32)

    shapes = [
        full(rows // 2, 2 * width),
        full(rows // 2, 2 * width),
        full(3, part // 2, 2 * half),
        full(part // 2, 2 * half),
        full(3, part // 2, 2 * half),
        full(part // 2, 2 * half),
        jax.ShapeDtypeStruct(enc_shape, low_type),
        jax.ShapeDtypeStruct(small.shape[1:], small.dtype),
    ]
    anywhere = pl.BlockSpec(memory_space=pl.ANY)
    return pl.pallas_call(
        finish_kernel,
        out_shape=shapes,
        in_specs=[anywhere] * 10,
        out_specs=[anywhere] * len(shapes),
        scratch_shapes=[
            pltpu.VMEM((part, 2 * wide), low_type),
            pltpu.VMEM((part, 2 * wide), low_type),
            pltpu.VMEM((part, wide), low_type),
            pltpu.VMEM((part, wide), low_type),
            pltpu.VMEM((part, wide), jnp.float32),
            pltpu.VMEM((2, *enc_shape), low_type),
            pltpu.VMEM((2, *enc_shape), low_type),
            pltpu.VMEM(enc_shape, low_type),
            pltpu.VMEM(enc_shape, low_type),
            pltpu.VMEM(enc_shape, low_type),
            pltpu.VMEM((2, 2, part, wide), low_type),
            pltpu.VMEM((2, 2, part, wide), low_type),
            pltpu.VMEM((part, wide), low_type),
            pltpu.VMEM((part, wide), low_type),
            pltpu.VMEM((2, part, wide), low_type),
            pltpu.VMEM((2, part, wide), jnp.float32),
            pltpu.VMEM((part, wide), low_type),
            pltpu.VMEM(small.shape, small.dtype),
        ]
        + [pltpu.VMEM((32 >> stage, *small.shape[1:]), small.dtype) for stage in range(1, 6)]
        + [pltpu.SemaphoreType.DMA((40,))] * 3,
        compiler_params=pltpu.CompilerParams(collective_id=1, has_side_effects=True),
        cost_estimate=pl.CostEstimate(flops=40_000_000_000, bytes_accessed=0, transcendentals=0),
    )(ff_in, ff_out, cross, cross_beyond, *self_parts, enc, small)


def trade(rows, axis, name="trade"):
    with jax.named_scope(name):
        return lax.ppermute(rows, axis, [(0, 1), (1, 0)])


def after(value, *others):
    return lax.optimization_barrier((value, *others))[0]


def regroup_sent(rows, name):
    with jax.named_scope("re_" + name):
        return lax.ppermute(rows, ("core", "zhi"), [(1, 2), (2, 1)])


def regroup_done(rows, moved):
    return jnp.where(lax.axis_index("core") == lax.axis_index("zhi"), rows, moved)


def regroup(rows, name="regroup"):
    return regroup_done(rows, regroup_sent(rows, name))


def in_order(index, own, other, axis):
    return jnp.concatenate(
        [jnp.where(index == 0, own, other), jnp.where(index == 0, other, own)], axis=axis
    )


def low(values):
    return values.astype(jnp.bfloat16)


def half_of(values, index, axis):
    size = values.shape[axis] // 2
    return lax.dynamic_slice_in_dim(values, index * size, size, axis)


def over_chips(rows):
    return lax.all_gather(rows, ("y", "x"), axis=0, tiled=True)


def sum_over_chips(partial):
    return lax.psum_scatter(partial, ("y", "x"), scatter_dimension=0, tiled=True)


def spread_rows(rows, name):
    beyond = trade(rows, "zlo", name + "_z")
    return (
        jnp.concatenate([rows, trade(rows, "core", name + "_c")], axis=0),
        jnp.concatenate([beyond, trade(beyond, "core", name + "_zc")], axis=0),
    )


def sum_rows(near, far, term, name):
    size = near.shape[0] // 2
    far_sum = term(far[:size]) + trade(low(term(far[size:])), "core", name + "_zc")
    from_far = trade(low(far_sum), "zlo", name + "_z")
    near_other = trade(low(term(near[size:])), "core", name + "_c")
    return term(near[:size]) + near_other + from_far


def fast_layer(
    tokens,
    enc_states,
    enc_len,
    cont_lengths,
    cotangent,
    self_qkv,
    self_out,
    cross_qkv,
    cross_out,
    ff_in,
    ff_out,
    head_bias,
    ff_bias,
    vec_params,
):
    core, zhi, zlo = lax.axis_index("core"), lax.axis_index("zhi"), lax.axis_index("zlo")
    scaling = HD**-0.5
    model = tokens.shape[1]
    segments = cont_lengths.shape[1]

    flat = jnp.concatenate([vec_params.reshape(-1), head_bias.reshape(-1), ff_bias]).astype(jnp.float32)
    sizes = (vec_params.size, head_bias.size, ff_bias.size)
    flat = jnp.pad(flat.reshape(-1, 128), ((0, 4), (0, 0)))
    token_rows, attn_rows, w_self, w_cross, hidden, enc_full, small = start_exchange(
        tokens,
        enc_states,
        self_qkv,
        self_out.T,
        cross_qkv,
        cross_out.T,
        ff_in,
        ff_out.T,
        flat,
    )
    w_self = w_self.reshape(4, model, -1)
    w_cross = over_chips(w_cross)
    cross_width = w_cross.shape[1] // 4
    hidden_beyond = trade(hidden, "zhi", "wh_zhi")
    w_qkv, w_so = jnp.concatenate([w_self[0], w_self[1], w_self[2]], axis=1), w_self[3]
    w_cq, w_ckv, w_co = jnp.split(w_cross, [cross_width, 3 * cross_width], axis=1)
    rows_of = model // 4
    width = w_self.shape[2]
    pairs, cross_pairs = width // PAIR, cross_width // PAIR
    enc_full = enc_full.reshape(-1, model)
    attn_near, attn_far = attn_rows[: attn_rows.shape[0] // 2], attn_rows[attn_rows.shape[0] // 2 :]
    small = small.reshape(8, 4, -1)
    vec_part, head_part, ff_part = jnp.split(
        small[:, :, : sum(sizes)], [sizes[0], sizes[0] + sizes[1]], axis=2
    )
    vectors = vec_part[:, 0].reshape(8, 9, -1).transpose(1, 0, 2).reshape(9, model)
    heads = head_part.reshape(8, 4, 4, -1).transpose(2, 1, 0, 3).reshape(4, 2, 2, 2, -1)
    self_bias = lax.dynamic_index_in_dim(
        lax.dynamic_index_in_dim(heads[:2], zlo, 2, False), core, 2, False
    ).reshape(2, -1)
    cross_bias = lax.dynamic_index_in_dim(heads[2:], core, 3, False).reshape(2, -1)
    hidden_bias = ff_part.transpose(1, 0, 2).reshape(2, 2, 2, -1)
    hidden_bias = lax.dynamic_index_in_dim(
        lax.dynamic_index_in_dim(hidden_bias, zlo, 1, False), core, 1, False
    ).reshape(-1)

    lengths = regroup(jnp.concatenate([cont_lengths[0], enc_len]))
    places = jnp.stack(
        [512 * ((core != block // 2) + 2 * (zlo != block % 2)) for block in range(4)]
    ).astype(jnp.int32)
    bounds = PROMPT + jnp.concatenate(
        [jnp.zeros((1,), jnp.int32), jnp.cumsum(lengths[:segments]).astype(jnp.int32)]
    )
    self_meta = jnp.concatenate([places, bounds])
    cross_meta = lengths[segments:]

    resid = token_rows.astype(jnp.float32)
    _, hat_one, inv_one = norm_forward(resid, vectors[0], vectors[3])
    qkv_bias = jnp.concatenate([self_bias[0], jnp.zeros((width,), jnp.float32), self_bias[1]])
    qkv_scale = jnp.concatenate([jnp.full((width,), scaling), jnp.ones((2 * width,))]).astype(jnp.float32)
    def project(rows):
        return low((product(rows, w_qkv) + qkv_bias) * qkv_scale)

    qkv = project(attn_rows)
    count = qkv.shape[0]
    self_plan = functools.partial(self_sections, segments=segments)
    mixed, self_lse = attend(self_plan, self_meta, qkv, 0, qkv, pairs, 2 * pairs, pairs, 1152)
    mixed = after(mixed, hidden_beyond)
    hidden = in_order(zhi, hidden, after(hidden_beyond, mixed), 2).transpose(1, 0, 2)
    w_hidden = over_chips(hidden.reshape(hidden.shape[0], -1))
    w_in, w_out = jnp.split(w_hidden, 2, axis=1)
    near, far = mixed[: count // 2], mixed[count // 2 :]
    so_far = low(
        product_right_t(far[: count // 4], w_so)
        + trade(low(product_right_t(far[count // 4 :], w_so)), "core", "so_zc")
    )
    so_near_other = low(product_right_t(near[count // 4 :], w_so))
    so_near = product_right_t(near[: count // 4], w_so)
    grad_rows = regroup(after(cotangent, mixed), "cotangent")
    cross_kv = low(
        product(after(enc_full, grad_rows, so_far), w_ckv)
        + jnp.concatenate([jnp.zeros((cross_width,), jnp.float32), cross_bias[1]])
    )
    branch = so_near + trade(so_near_other, "core", "so_c") + after(trade(so_far, "zlo", "so_z"), cross_kv)
    after_one = resid + (branch + vectors[6])

    cot_beyond = trade(after(grad_rows, after_one), "zlo", "cot_z")
    cot_near = [grad_rows, trade(grad_rows, "core", "cot_c")]

    normed_mid, hat_two, inv_two = norm_forward(after_one, vectors[1], vectors[4])
    cross_low = low(normed_mid)
    cross_rows = jnp.concatenate([cross_low, trade(cross_low, "core", "cin")], axis=0)
    own_rows = cross_low.shape[0]
    cross_q = low((product(cross_rows, w_cq) + cross_bias[0]) * scaling)
    cross_plan = functools.partial(cross_sections, blocks=cross_q.shape[0] // BLOCK)
    cross_mixed, cross_lse = attend(
        cross_plan, cross_meta, cross_q, 0, cross_kv, 0, cross_pairs, cross_pairs, ENC
    )
    cross_mixed = after(cross_mixed, cot_beyond)
    other = trade(low(product_right_t(cross_mixed[own_rows:], w_co)), "core", "co_c")
    branch = product_right_t(cross_mixed[:own_rows], w_co) + other
    after_two = after_one + (branch + vectors[7])

    normed_out, hat_three, inv_three = norm_forward(after_two, vectors[2], vectors[5])
    mlp_in = low(normed_out)
    beyond = trade(mlp_in, "zlo", "mlp_z")
    mlp_near = [mlp_in, trade(mlp_in, "core", "mlp_c")]
    act_near, dpre_near, sum_near = hidden_units(mlp_near, cot_near, w_hidden, hidden_bias[None])
    bias_out_three = jnp.sum(grad_rows.astype(jnp.float32), axis=0)
    beyond = after(beyond, act_near, bias_out_three)
    mlp_far = [beyond, trade(beyond, "core", "mlp_zc")]
    cot_far = [cot_beyond, trade(cot_beyond, "core", "cot_zc")]
    act_far, dpre_far, sum_far = hidden_units(mlp_far, cot_far, w_hidden, hidden_bias[None])
    gradient = grad_rows.astype(jnp.float32)
    dmlp_far = low(
        product_right_t(dpre_far[:own_rows], w_in)
        + trade(low(product_right_t(dpre_far[own_rows:], w_in)), "core", "dmlp_zc")
    )
    mlp_term = product_right_t(dpre_near[:own_rows], w_in) + trade(
        low(product_right_t(dpre_near[own_rows:], w_in)), "core", "dmlp_c"
    )
    act_near, act_far = after(act_near, dmlp_far, mlp_term), after(act_far, dmlp_far, mlp_term)
    out_parts = [
        low(product_right_t(act_far[own_rows:], w_out)),
        product_right_t(act_far[:own_rows], w_out),
    ]
    out_far = low(out_parts[1] + trade(out_parts[0], "core", "out_zc"))
    dmlp_beyond, grad_hidden = weight_grads(
        dmlp_far, (cot_near + cot_far, act_near, act_far), (mlp_near + mlp_far, dpre_near, dpre_far), 2
    )
    mlp_term = mlp_term + dmlp_beyond
    out_far = trade(after(out_far, mlp_term), "zlo", "out_z")
    part, gain_three, shift_three = norm_backward(mlp_term, hat_three, inv_three, vectors[2])
    gradient = gradient + part

    grad_low = low(gradient)
    bias_out_two = jnp.sum(grad_low.astype(jnp.float32), axis=0)
    grad_both = jnp.concatenate([grad_low, trade(grad_low, "core", "e2")], axis=0)
    cross_mixed_grad = low(product(grad_both, w_co))
    cross_dq, cross_dk, cross_dv = attend_back(
        cross_plan,
        cross_meta,
        cross_q,
        0,
        cross_kv,
        0,
        cross_pairs,
        cross_mixed,
        cross_mixed_grad,
        cross_lse,
        cross_pairs,
        ENC,
    )
    cross_dq = after(cross_dq, out_far)
    other = trade(low(product_right_t(cross_dq[own_rows:], w_cq)), "core", "dcin")
    part, gain_two, shift_two = norm_backward(
        product_right_t(cross_dq[:own_rows], w_cq) + other, hat_two, inv_two, vectors[1]
    )
    gradient = gradient + part

    grad_low = low(gradient)
    bias_out_one = jnp.sum(grad_low.astype(jnp.float32), axis=0)
    beyond = trade(grad_low, "zlo", "e1_z")
    grad_near = jnp.concatenate([grad_low, trade(grad_low, "core", "e1_c")], axis=0)
    mixed_grad = low(product(grad_near, w_so))
    cross_parts = [
        low(product_left_t(cross_rows, after(cross_dq, grad_low))),
        low(product_left_t(enc_full, after(cross_dk, grad_low))),
        low(product_left_t(enc_full, after(cross_dv, grad_low))),
        low(product_left_t(after(grad_both, grad_low), cross_mixed)),
    ]
    grad_cross = jnp.concatenate(cross_parts, axis=1)
    act_near = after(act_near, grad_low)
    out_branch = product_right_t(act_near[:own_rows], w_out) + trade(
        low(product_right_t(act_near[own_rows:], w_out)), "core", "out_c"
    )
    layer_out = low(after_two + (out_branch + after(out_far, grad_low) + vectors[8]))
    beyond = after(beyond, mixed_grad, grad_cross, layer_out)
    cross_sum = sum_over_chips(grad_cross)
    grad_far = jnp.concatenate([beyond, trade(beyond, "core", "e1_zc")], axis=0)
    mixed_grad = jnp.concatenate([mixed_grad, low(product(grad_far, w_so))], axis=0)

    hidden_sum = sum_over_chips(grad_hidden)
    sides = [hidden_sum[:, : hidden_sum.shape[1] // 2], hidden_sum[:, hidden_sum.shape[1] // 2 :]]
    sent = jnp.concatenate([half_of(side, 1 - zhi, 1) for side in sides], axis=1)
    hidden_beyond = jnp.split(trade(sent, "zhi", "gf_zhi"), 2, axis=1)
    out_sum, in_sum = (
        half_of(side, zhi, 1).astype(jnp.float32) + beyond.astype(jnp.float32)
        for side, beyond in zip(sides, hidden_beyond)
    )
    dq, dk, dv = attend_back(
        self_plan, self_meta, qkv, 0, qkv, pairs, 2 * pairs, mixed, mixed_grad, self_lse, pairs, 1152
    )
    dq, dk, dv = (after(part, *hidden_beyond) for part in (dq, dk, dv))
    layer_moved = regroup_sent(after(layer_out, dq), "out")
    dqkv = jnp.concatenate([dq, dk, dv], axis=1)
    d_near, d_far = dqkv[: count // 2], dqkv[count // 2 :]
    dx_far = low(
        product_right_t(d_far[: count // 4], w_qkv)
        + trade(low(product_right_t(d_far[count // 4 :], w_qkv)), "core", "dx_zc")
    )
    dx = product_right_t(d_near[: count // 4], w_qkv) + trade(
        low(product_right_t(d_near[count // 4 :], w_qkv)), "core", "dx_c"
    )
    cross_sum = after(cross_sum, dx_far).reshape(rows_of, 4, 2, -1)
    cross_kept = half_of(cross_sum, zhi, 2).reshape(rows_of, -1)
    cross_sent = half_of(cross_sum, 1 - zhi, 2).reshape(rows_of, -1)
    cross_beyond = trade(cross_sent, "zhi", "gc_zhi")
    dq, dk, dv = (after(part, dx_far, cross_sent, cross_kept) for part in (dq, dk, dv))
    self_parts = [
        low(product_left_t(attn_rows, dq)),
        low(product_left_t(attn_rows, dk)),
        low(product_left_t(attn_rows, dv)),
        low(product_left_t(grad_near, near) + product_left_t(grad_far, far)),
    ]
    enc_part = low(
        product_right_t(after(cross_dk, dq), w_ckv[:, :cross_width])
        + product_right_t(after(cross_dv, dq), w_ckv[:, cross_width:])
    )
    layer_out = regroup_done(layer_out, after(layer_moved, *self_parts))
    dx = dx + after(trade(dx_far, "zlo", "dx_z"), enc_part, layer_out, cross_beyond, *self_parts)
    part, gain_one, shift_one = norm_backward(dx, hat_one, inv_one, vectors[0])
    input_part = low(gradient + part)
    input_grad = regroup(input_part, "dgrad").astype(jnp.float32)

    bias_self_query = jnp.sum(dq.astype(jnp.float32), axis=0)
    bias_self_value = jnp.sum(dv.astype(jnp.float32), axis=0)
    bias_cross_query = jnp.sum(cross_dq.astype(jnp.float32), axis=0)
    bias_cross_value = jnp.sum(cross_dv.astype(jnp.float32), axis=0)
    grad_hidden_bias = (sum_near + sum_far)[0]
    vec_sums = jnp.stack(
        [
            gain_one,
            gain_two,
            gain_three,
            shift_one,
            shift_two,
            shift_three,
            bias_out_one,
            bias_out_two,
            bias_out_three,
        ]
    )
    at_zlo = (jnp.arange(2) == zlo).astype(jnp.float32)
    at_core = (jnp.arange(2) == core).astype(jnp.float32)
    quarter = (at_zlo[:, None] * at_core[None, :])[:, :, None]
    self_sums = jnp.stack([bias_self_query, bias_self_value]).reshape(2, 2, 1, 1, -1) * quarter
    cross_sums = jnp.stack([bias_cross_query, bias_cross_value]).reshape(2, 2, 2, 1, -1) * at_core[:, None]
    head_sums = jnp.concatenate([self_sums, cross_sums], axis=0)
    hidden_sums = grad_hidden_bias.reshape(2, 1, 1, -1) * quarter
    vec_sums = vec_sums.reshape(9, 8, -1).transpose(1, 0, 2).reshape(8, 1, -1)
    sums = jnp.concatenate(
        [
            jnp.broadcast_to(vec_sums, (8, 4, sizes[0])),
            head_sums.reshape(4, 4, 8, -1).transpose(2, 1, 0, 3).reshape(8, 4, -1),
            hidden_sums.reshape(4, 8, -1).transpose(1, 0, 2),
        ],
        axis=2,
    )
    sums = jnp.pad(after(sums, input_part).reshape(32, -1, 128), ((0, 0), (0, 4), (0, 0)))
    ff_in_grad, ff_out_grad, cross_qkv_grad, cross_out_grad, self_qkv_grad, self_out_grad, enc_grad, sums = finish(
        in_sum,
        out_sum,
        cross_kept,
        cross_beyond,
        [part.reshape(2, 2, rows_of, -1) for part in self_parts],
        enc_part.reshape(2, 2, -1, model),
        sums,
    )
    sums = sums.reshape(-1)[: sum(sizes)]
    vec_grad, head_grad, ff_bias_grad = jnp.split(sums, [sizes[0], sizes[0] + sizes[1]])
    return (
        layer_out,
        input_grad,
        enc_grad.astype(jnp.float32),
        self_qkv_grad,
        self_out_grad.T,
        cross_qkv_grad,
        cross_out_grad.T,
        ff_in_grad,
        ff_out_grad.T,
        head_grad.reshape(head_bias.shape),
        ff_bias_grad,
        vec_grad.reshape(vec_params.shape),
    )


def solution(mesh):
    fast = tuple(mesh.shape[axis] for axis in ("dp", "tensor")) == (8, 4)
    dp, tensor = (AXES[:3], AXES[3:]) if fast else (("dp",), ("tensor",))
    both = dp + tensor
    rows = P(both, None)
    qkv = P(None, dp, tensor)
    out = P(tensor, dp)
    in_specs = (
        rows,
        rows,
        P(dp),
        P(dp, None),
        rows,
        qkv,
        out,
        qkv,
        out,
        P(dp, tensor),
        out,
        P(None, tensor + dp),
        P(tensor + dp),
        P(None, dp),
    )
    out_specs = (
        rows,
        rows,
        rows,
        qkv,
        out,
        qkv,
        out,
        P(dp, tensor),
        out,
        P(None, tensor + dp),
        P(tensor + dp),
        P(None, dp),
    )
    if fast:
        mesh = Mesh(mesh.devices.reshape(2, 2, 2, 2, 2), AXES)
    return jax.shard_map(
        fast_layer if fast else shards, mesh=mesh, in_specs=in_specs, out_specs=out_specs, check_vma=False
    )
```
